32 devices in a mesh: dp: 2 (over core), fsdp: 16 (over z, y, x).
Axes of the slice: x: 2, y: 2, z: 4, core: 2. Of those that a mesh axis runs over, the one named last changes fastest.
Arguments:
- features: bfloat16 [2, 128, 64, 2048], P('dp', 'fsdp'), may hold values from -6 to 6
- cotangent: bfloat16 [3, 2, 128, 64, 256], P(None, 'dp', 'fsdp'), may hold values from -6 to 6
- crop_heights: int32 [2, 4], replicated, may hold values from 1 to 64, 128 in all within a row
- task_scale: float32 [3], replicated, may hold values from 0.5 to 2
- w_reduce: float32 [2048, 512], P('fsdp'), may hold values from -0.125 to 0.125
- w_dilated: float32 [4608, 512], P('fsdp'), may hold values from -0.09375 to 0.09375
- w_expand: float32 [512, 2048], P(None, 'fsdp'), may hold values from -0.25 to 0.25
- w_heads: float32 [3, 18432, 256], P(None, 'fsdp'), may hold values from -0.046875 to 0.046875
- norm_params: float32 [2, 3840], replicated, may hold values from -1 to 1.3, as said below
- m_reduce: float32 [2048, 512], P('fsdp'), may hold values from -96 to 96
- m_dilated: float32 [4608, 512], P('fsdp'), may hold values from -96 to 96
- m_expand: float32 [512, 2048], P(None, 'fsdp'), may hold values from -96 to 96
- m_heads: float32 [3, 18432, 256], P(None, 'fsdp'), may hold values from -96 to 96
- norm_moment: float32 [2, 3840], replicated, may hold values from -96 to 96
Outputs:
- features_grad: float32 [2, 128, 64, 2048], P('dp', 'fsdp')
- w_reduce_new: float32 [2048, 512], P('fsdp')
- m_reduce_new: float32 [2048, 512], P('fsdp')
- w_dilated_new: float32 [4608, 512], P('fsdp')
- m_dilated_new: float32 [4608, 512], P('fsdp')
- w_expand_new: float32 [512, 2048], P(None, 'fsdp')
- m_expand_new: float32 [512, 2048], P(None, 'fsdp')
- w_heads_new: float32 [3, 18432, 256], P(None, 'fsdp')
- m_heads_new: float32 [3, 18432, 256], P(None, 'fsdp')
- norm_params_new: float32 [2, 3840], replicated
- norm_moment_new: float32 [2, 3840], replicated
The draws below stay inside these ranges and needn't reach their ends.
Inputs may be any that keep to these rules, and one draw needn't show every extreme that they name: `crop_heights`: row g lists the sides of 4 square crops stacked down group g's canvas of 128 rows; the sides sum to 128 and the largest is 64. `norm_params`: row 0 holds the norm gains near one, row 1 the norm biases.
All inputs are finite; a program needn't handle non-finite values.
Results may differ from the reference program's by a relative error of at most 0.018.
Values may be sent and summed in bfloat16 or wider, within the bound.
A program may use at most 320 MiB of HBM per device.

```python
import math
import jax
import jax.numpy as jnp
import numpy as np
from jax import lax

C = 2048
MID = 512
HEAD = 256
HEADS = 3
W = 64
ROWS_DEV = 8
GROUPS = 2
ROWS = 128
CROPS = 4
NORM_W = 3840
N_FSDP = 16


def draw_norm_params(key, part):
    gain_key = jax.random.fold_in(key, 11)
    bias_key = jax.random.fold_in(key, 23)
    gain_values = 1.0 + 0.3 * jax.random.uniform(gain_key, (NORM_W,), jnp.float32, -1.0, 1.0)
    bias_values = jnp.clip(0.4 * jax.random.normal(bias_key, (NORM_W,), jnp.float32), -1.0, 1.0)
    return jnp.stack([gain_values, bias_values]).astype(jnp.float32)


def raised(values, stream_key, source, target, blocks, factor):
    owner, partner = [(jnp.arange(values.shape[position]) // (values.shape[position] // blocks)).reshape([-1 if axis == position else 1 for axis in range(values.ndim)]) for position in (source, target)]
    chosen = jax.random.permutation(stream_key, blocks)[partner]
    strong = (owner == chosen) | (owner == (partner + blocks // 2) % blocks)
    return jnp.where(strong, factor * values, values)


def levels(key, dims, cuts, least, top_value):
    level = 1.0
    for position, blocks in cuts:
        heights = jax.random.uniform(jax.random.fold_in(jax.random.fold_in(key, 6), position), (blocks,), jnp.float32, least / len(cuts), top_value / len(cuts))
        level = level * jnp.repeat(jnp.exp(heights), dims[position] // blocks).reshape((-1,) + (1,) * (len(dims) - 1 - position))
    return level


def profile(number_of, total, bound, slope):
    weights = [(1 << 20) // math.isqrt(rank ** slope) + 1 for rank in range(2, number_of + 1)]
    rest, holding = total - bound - (number_of - 1), [1] * (number_of - 1)
    while rest > 0:
        free = [i for i in range(number_of - 1) if holding[i] < bound]
        pool, left = sum([weights[i] for i in free]), rest
        for i in free:
            more = min(bound - holding[i], max(1, left * weights[i] // pool), rest)
            holding[i] = holding[i] + more
            rest = rest - more
    return np.array([bound] + holding)


def ragged_sizes(stream_key, amount, total, bound, lean):
    if amount == 2:
        one = jax.random.randint(stream_key, (), max(1, total - bound), min(bound, total - 1) + 1)
        return jnp.stack([one, total - one])
    sizes = jnp.asarray(profile(amount, total, bound, lean), jnp.int32)
    twos = (amount - 1) // 2
    giver, taker = sizes[1:1 + 2 * twos:2], sizes[2:2 + 2 * twos:2]
    slack = jnp.minimum(giver - 1, bound - taker)
    passed = jax.random.randint(jax.random.fold_in(stream_key, 1), (twos,), 0, 1 << 20) % (slack + 1)
    sizes = sizes.at[1:1 + 2 * twos:2].set(giver - passed).at[2:2 + 2 * twos:2].set(taker + passed)
    return sizes[jax.random.permutation(jax.random.fold_in(stream_key, 2), amount)]


def noise(key, extent, spread, bound, cuts=(), kind=jnp.bfloat16):
    values = spread * jax.random.normal(key, extent, jnp.float32)
    if cuts:
        values = values * levels(key, extent, cuts, -0.22, 0.18)
    return jnp.clip(values, -bound, bound).astype(kind)


def gaussian_with(own_key, extent, deviation, bound, cuts, heavy, kind=jnp.bfloat16):
    values = deviation * jax.random.normal(own_key, extent, jnp.float32)
    if cuts:
        values = values * levels(own_key, extent, cuts, -0.22, 0.18)
    return jnp.clip(raised(values, jax.random.fold_in(own_key, 3), *heavy), -bound, bound).astype(kind)


def setup_inputs(seed: int = 0) -> dict:
    splits = jax.random.split(jax.random.key(seed), 15)
    features = gaussian_with(splits[0], (GROUPS, ROWS, W, C), 1.0, 6.0, ((0, 2), (1, 16)), (1, 3, 16, 2.0))
    cotangent = noise(splits[1], (HEADS, GROUPS, ROWS, W, HEAD), 1.0, 6.0, ((1, 2), (2, 16)))
    crop_heights = jax.vmap(lambda own: ragged_sizes(own, CROPS, ROWS_DEV * N_FSDP, W, 1))(jax.random.split(splits[2], GROUPS)).reshape((GROUPS, CROPS)).astype(jnp.int32)
    task_scale = jnp.clip(jnp.exp(jax.random.uniform(splits[3], (HEADS,), jnp.float32, math.log(0.5), math.log(2.0))), 0.5, 2.0)
    w_reduce = noise(splits[4], (C, MID), C ** -0.5, 0.125, ((0, 16),), jnp.float32)
    w_dilated = noise(splits[5], (9 * MID, MID), (9 * MID) ** -0.5, 0.09375, ((0, 16),), jnp.float32)
    w_expand = noise(splits[6], (MID, C), MID ** -0.5, 0.25, ((1, 16),), jnp.float32)
    w_heads = noise(splits[7], (HEADS, 9 * C, HEAD), (9 * C) ** -0.5, 0.046875, ((1, 16),), jnp.float32)
    norm_params = draw_norm_params(jax.random.fold_in(splits[14], 71), 0)
    m_reduce = noise(splits[9], (C, MID), 16.0, 96.0, ((0, 16),), jnp.float32)
    m_dilated = noise(splits[10], (9 * MID, MID), 16.0, 96.0, ((0, 16),), jnp.float32)
    m_expand = noise(splits[11], (MID, C), 16.0, 96.0, ((1, 16),), jnp.float32)
    m_heads = noise(splits[12], (HEADS, 9 * C, HEAD), 16.0, 96.0, ((1, 16),), jnp.float32)
    norm_moment = noise(splits[13], (2, NORM_W), 16.0, 96.0, (), jnp.float32)
    return dict(features=features, cotangent=cotangent, crop_heights=crop_heights, task_scale=task_scale, w_reduce=w_reduce, w_dilated=w_dilated, w_expand=w_expand, w_heads=w_heads, norm_params=norm_params, m_reduce=m_reduce, m_dilated=m_dilated, m_expand=m_expand, m_heads=m_heads, norm_moment=norm_moment)


norm_epsilon = 1e-05
task_epsilon = 1e-06
momentum_decay = 0.9
step_rate = 0.01
trunk_rate = 4
head_rates = (12, 24, 36)

@jax.custom_vjp
def low(v):
    return lax.optimization_barrier(v.astype(jnp.bfloat16)).astype(jnp.float32)

@jax.custom_vjp
def low_back(v):
    return v

def low_keep(v):
    return (low(v), None)

def low_pass(kept, grad):
    return (grad,)

def back_keep(v):
    return (v, None)

def back_low(kept, grad):
    return (low(grad),)
low.defvjp(low_keep, low_pass)
low_back.defvjp(back_keep, back_low)

def row_layout(crop_heights):
    crop_ends = jnp.cumsum(crop_heights, axis=1, dtype=jnp.int32)
    crop_starts = crop_ends - crop_heights
    row_ids = jnp.arange(ROWS, dtype=jnp.int32)
    member = (row_ids[None, :, None] >= crop_starts[:, None, :]) & (row_ids[None, :, None] < crop_ends[:, None, :])
    row_top = lax.optimization_barrier(jnp.sum(jnp.where(member, crop_starts[:, None, :], 0), axis=2, dtype=jnp.int32))
    row_bottom = lax.optimization_barrier(jnp.sum(jnp.where(member, crop_ends[:, None, :], 0), axis=2, dtype=jnp.int32))
    row_side = lax.optimization_barrier(jnp.sum(jnp.where(member, crop_heights[:, None, :], 0), axis=2, dtype=jnp.int32))
    return (row_ids, row_top, row_bottom, row_side)

def shift_along(values, offset, axis_number):
    if offset == 0:
        return values
    length = values.shape[axis_number]
    pad_shape = list(values.shape)
    pad_shape[axis_number] = abs(offset)
    zero_block = jnp.zeros(pad_shape, values.dtype)
    if offset > 0:
        return jnp.concatenate([lax.slice_in_dim(values, offset, length, axis=axis_number), zero_block], axis_number)
    return jnp.concatenate([zero_block, lax.slice_in_dim(values, 0, length + offset, axis=axis_number)], axis_number)

def dilated(inputs, weight, rate, layout):
    row_ids, row_top, row_bottom, row_side = layout
    in_width = inputs.shape[-1]
    out_width = weight.shape[-1]
    tap_weights = weight.reshape(3, 3, in_width, out_width)
    columns = jnp.arange(W, dtype=jnp.int32)
    result = jnp.zeros(inputs.shape[:-1] + (out_width,), jnp.float32)
    for row_step in range(3):
        down = (row_step - 1) * rate
        inside = (row_ids[None, :] + down >= row_top) & (row_ids[None, :] + down < row_bottom)
        moved_rows = shift_along(inputs, down, 1)
        for col_step in range(3):
            across = (col_step - 1) * rate
            keep_mask = inside[:, :, None] & (columns[None, None, :] + across >= 0) & (columns[None, None, :] + across < row_side[:, :, None])
            source = shift_along(moved_rows, across, 2) * keep_mask[..., None].astype(jnp.float32)
            result = result + jnp.einsum('grwc,co->grwo', source, tap_weights[row_step, col_step], precision=lax.Precision.HIGHEST)
    return result

def normalize(values, gain_row, bias_row, valid_mask, valid_count):
    weighted = values * valid_mask[..., None]
    mean_value = lax.optimization_barrier(jnp.sum(weighted, axis=(0, 1, 2))) / valid_count
    variance = lax.optimization_barrier(jnp.sum(weighted * values, axis=(0, 1, 2))) / valid_count - mean_value * mean_value
    return (values - mean_value) * lax.rsqrt(variance + norm_epsilon) * gain_row + bias_row

def trunk(features, w_reduce, w_dilated, w_expand, norm_params, layout, valid_mask, valid_count):
    gain_values = norm_params[0]
    bias_values = norm_params[1]
    first = low_back(jnp.einsum('grwc,cm->grwm', features, low(w_reduce), precision=lax.Precision.HIGHEST))
    hidden_one = low(jax.nn.silu(normalize(first, gain_values[:MID], bias_values[:MID], valid_mask, valid_count)))
    conv_trunk = jax.checkpoint(lambda inputs, weight: dilated(inputs, weight, trunk_rate, layout))
    second = low_back(conv_trunk(hidden_one, low(w_dilated)))
    hidden_two = low(jax.nn.silu(normalize(second, gain_values[MID:2 * MID], bias_values[MID:2 * MID], valid_mask, valid_count)))
    third = low_back(jnp.einsum('grwm,mc->grwc', hidden_two, low(w_expand), precision=lax.Precision.HIGHEST))
    normed = normalize(third, gain_values[2 * MID:2 * MID + C], bias_values[2 * MID:2 * MID + C], valid_mask, valid_count)
    return low(jax.nn.silu(features + normed))

def head(trunk_out, w_heads, norm_params, head_index, layout, valid_mask, valid_count):
    start = 2 * MID + C + head_index * HEAD
    conv_head = jax.checkpoint(lambda inputs, weight: dilated(inputs, weight, head_rates[head_index], layout))
    response = low_back(conv_head(trunk_out, low(w_heads[head_index])))
    return jax.nn.silu(normalize(response, norm_params[0, start:start + HEAD], norm_params[1, start:start + HEAD], valid_mask, valid_count))

def reference(features, cotangent, crop_heights, task_scale, w_reduce, w_dilated, w_expand, w_heads, norm_params, m_reduce, m_dilated, m_expand, m_heads, norm_moment):
    layout = row_layout(crop_heights)
    valid_mask = (jnp.arange(W, dtype=jnp.int32)[None, None, :] < layout[3][:, :, None]).astype(jnp.float32)
    valid_count = jnp.sum(crop_heights * crop_heights).astype(jnp.float32)
    features_float = features.astype(jnp.float32)

    def trunk_call(inputs, weight_one, weight_two, weight_three, params):
        return trunk(inputs, weight_one, weight_two, weight_three, params, layout, valid_mask, valid_count)
    trunk_out, trunk_back = jax.vjp(trunk_call, features_float, w_reduce, w_dilated, w_expand, norm_params)
    head_results = []
    for head_index in range(HEADS):

        def head_call(inputs, weights, params, head_index=head_index):
            return head(inputs, weights, params, head_index, layout, valid_mask, valid_count)
        head_value, head_back = jax.vjp(head_call, trunk_out, w_heads, norm_params)
        head_results.append(head_back(cotangent[head_index].astype(jnp.float32) * valid_mask[..., None]))
    task_rms = jnp.stack([jnp.sqrt(jnp.sum(item[0] * item[0]) / (valid_count * C) + task_epsilon) for item in head_results])
    task_weight = task_scale / task_rms
    trunk_grad = jnp.zeros_like(trunk_out)
    heads_grad = jnp.zeros_like(w_heads)
    norm_grad_heads = jnp.zeros_like(norm_params)
    for head_index in range(HEADS):
        trunk_grad = trunk_grad + task_weight[head_index] * head_results[head_index][0]
        heads_grad = heads_grad + task_weight[head_index] * head_results[head_index][1]
        norm_grad_heads = norm_grad_heads + task_weight[head_index] * head_results[head_index][2]
    features_grad, grad_reduce, grad_dilated, grad_expand, norm_grad = trunk_back(trunk_grad)
    norm_grad = norm_grad + norm_grad_heads

    def update(param, moment, grad):
        moment_new = momentum_decay * moment + grad
        return (param - step_rate * moment_new, moment_new)
    w_reduce_new, m_reduce_new = update(w_reduce, m_reduce, grad_reduce)
    w_dilated_new, m_dilated_new = update(w_dilated, m_dilated, grad_dilated)
    w_expand_new, m_expand_new = update(w_expand, m_expand, grad_expand)
    w_heads_new, m_heads_new = update(w_heads, m_heads, heads_grad)
    norm_params_new, norm_moment_new = update(norm_params, norm_moment, norm_grad)
    return (features_grad, w_reduce_new, m_reduce_new, w_dilated_new, m_dilated_new, w_expand_new, m_expand_new, w_heads_new, m_heads_new, norm_params_new, norm_moment_new)
```

```python
import jax
import jax.numpy as jnp
from jax import lax
from jax.sharding import PartitionSpec as P

norm_epsilon = 1e-05
task_epsilon = 1e-06
momentum_decay = 0.9
step_rate = 0.01
trunk_rate = 4
head_rates = (12, 24, 36)


def shifted(shard, axis, by):
    count = lax.axis_size(axis)
    pairs = [(i, i + by) for i in range(count) if 0 <= i + by < count]
    return lax.ppermute(shard, axis, pairs)


def silu_slope(values):
    sigmoid_value = jax.nn.sigmoid(values)
    return sigmoid_value * (1.0 + values * (1.0 - sigmoid_value))


def shift_along(values, offset, axis_number):
    if offset == 0:
        return values
    length = values.shape[axis_number]
    pad_shape = list(values.shape)
    pad_shape[axis_number] = abs(offset)
    zero_block = jnp.zeros(pad_shape, values.dtype)
    if offset > 0:
        return jnp.concatenate(
            [lax.slice_in_dim(values, offset, length, axis=axis_number), zero_block], axis_number
        )
    return jnp.concatenate(
        [zero_block, lax.slice_in_dim(values, 0, length + offset, axis=axis_number)], axis_number
    )


def move_sums(piece, distance):
    return shifted(piece.astype(jnp.bfloat16), "fsdp", -distance).astype(piece.dtype)


def move_grads(piece, distance):
    return shifted(piece, "fsdp", -distance)


def pull_rows(values, offset, row_count, mover):
    first_step = offset // row_count
    remainder = offset % row_count
    pieces = []
    for distance, lower, upper in (
        (first_step, remainder, row_count),
        (first_step + 1, 0, remainder),
    ):
        if upper > lower:
            piece = values[lower:upper]
            pieces.append(piece if distance == 0 else mover(piece, distance))
    return jnp.concatenate(pieces, 0)


def inside_rows(layout, offset):
    row_ids, row_top, row_bottom, row_side = layout
    return (row_ids + offset >= row_top) & (row_ids + offset < row_bottom)


def inside_cols(layout, offset, col_count):
    row_ids, row_top, row_bottom, row_side = layout
    columns = jnp.arange(col_count, dtype=jnp.int32)
    return (columns[None, :] + offset >= 0) & (columns[None, :] + offset < row_side[:, None])


def dilated_forward(inputs, weight, rate, layout):
    row_count, col_count, in_width = inputs.shape
    out_width = weight.shape[-1]
    tap_weights = weight.reshape(3, 3, in_width, out_width)
    result = jnp.zeros((row_count, col_count, out_width), jnp.float32)
    for row_step in range(3):
        down = (row_step - 1) * rate
        products = jnp.einsum(
            "rwc,kco->krwo", inputs, tap_weights[row_step], preferred_element_type=jnp.float32
        )
        summed = jnp.zeros((row_count, col_count, out_width), jnp.float32)
        for col_step in range(3):
            across = (col_step - 1) * rate
            summed = summed + inside_cols(layout, across, col_count)[:, :, None].astype(
                jnp.float32
            ) * shift_along(products[col_step], across, 1)
        pulled = pull_rows(summed, down, row_count, move_sums)
        result = result + inside_rows(layout, down)[:, None, None].astype(jnp.float32) * pulled
    return result


def dilated_backward(inputs, weight, grad_out, rate, layout):
    row_count, col_count, in_width = inputs.shape
    out_width = weight.shape[-1]
    tap_weights = weight.reshape(3, 3, in_width, out_width)
    grad_inputs = jnp.zeros((row_count, col_count, in_width), jnp.float32)
    blocks = []
    for row_step in range(3):
        down = (row_step - 1) * rate
        masked = grad_out * inside_rows(layout, down)[:, None, None].astype(jnp.bfloat16)
        arrived = pull_rows(masked, -down, row_count, move_grads)
        stacked = jnp.stack(
            [
                shift_along(
                    arrived
                    * inside_cols(layout, (col_step - 1) * rate, col_count)[:, :, None].astype(
                        jnp.bfloat16
                    ),
                    -(col_step - 1) * rate,
                    1,
                )
                for col_step in range(3)
            ]
        )
        grad_inputs = grad_inputs + jnp.einsum(
            "krwo,kco->rwc", stacked, tap_weights[row_step], preferred_element_type=jnp.float32
        )
        blocks.append(
            jnp.einsum("rwc,krwo->kco", inputs, stacked, preferred_element_type=jnp.float32)
        )
    return (grad_inputs, jnp.stack(blocks).reshape(9 * in_width, out_width))


def spread(stat):
    return stat.reshape(stat.shape[:-1] + (1, 1) + stat.shape[-1:])


def moments(values, valid_mask):
    weighted = values * valid_mask[..., None]
    return lax.psum(
        (jnp.sum(weighted, axis=(-3, -2)), jnp.sum(weighted * values, axis=(-3, -2))),
        ("dp", "fsdp"),
    )


def normalize(values, sums, valid_count, gain_row, bias_row):
    mean_value = sums[0] / valid_count
    variance = sums[1] / valid_count - mean_value * mean_value
    inverse = lax.rsqrt(variance + norm_epsilon)
    scaled = (values - spread(mean_value)) * spread(inverse)
    return (scaled, inverse, scaled * spread(gain_row) + spread(bias_row))


def norm_backward(grad_norm, scaled, inverse, gain_row, valid_mask, valid_count):
    masked = grad_norm * valid_mask[..., None]
    sums = lax.psum(
        (jnp.sum(masked, axis=(-3, -2)), jnp.sum(masked * scaled, axis=(-3, -2))), ("dp", "fsdp")
    )
    grad_values = (
        valid_mask[..., None]
        * spread(inverse * gain_row)
        * (masked - spread(sums[0] / valid_count) - scaled * spread(sums[1] / valid_count))
    )
    return (grad_values, sums)


def update(param, moment, grad):
    moment_new = momentum_decay * moment + grad
    return (param - step_rate * moment_new, moment_new)


def local(
    features,
    cotangent,
    crop_heights,
    task_scale,
    w_reduce,
    w_dilated,
    w_expand,
    w_heads,
    norm_params,
    m_reduce,
    m_dilated,
    m_expand,
    m_heads,
    norm_moment,
):
    row_count = features.shape[1]
    col_count = features.shape[2]
    channels = features.shape[3]
    middle = w_reduce.shape[1]
    head_width = w_heads.shape[2]
    head_total = w_heads.shape[0]
    group_index = lax.axis_index("dp")
    place_index = lax.axis_index("fsdp")
    group_heights = lax.dynamic_index_in_dim(crop_heights, group_index, 0, keepdims=False)
    crop_order = jnp.arange(group_heights.shape[0], dtype=jnp.int32)
    crop_ends = jnp.sum(
        jnp.where(crop_order[None, :] <= crop_order[:, None], group_heights[None, :], 0),
        axis=1,
        dtype=jnp.int32,
    )
    crop_starts = crop_ends - group_heights
    row_ids = place_index * row_count + jnp.arange(row_count, dtype=jnp.int32)
    member = (row_ids[:, None] >= crop_starts[None, :]) & (row_ids[:, None] < crop_ends[None, :])
    row_top = jnp.sum(jnp.where(member, crop_starts[None, :], 0), axis=1, dtype=jnp.int32)
    row_bottom = jnp.sum(jnp.where(member, crop_ends[None, :], 0), axis=1, dtype=jnp.int32)
    row_side = jnp.sum(jnp.where(member, group_heights[None, :], 0), axis=1, dtype=jnp.int32)
    layout = (row_ids, row_top, row_bottom, row_side)
    valid_mask = (jnp.arange(col_count, dtype=jnp.int32)[None, :] < row_side[:, None]).astype(
        jnp.float32
    )
    valid_count = jnp.sum(crop_heights * crop_heights).astype(jnp.float32)
    gain_values = norm_params[0]
    bias_values = norm_params[1]
    trunk_end = 2 * middle + channels
    inputs = features[0]
    inputs_float = inputs.astype(jnp.float32)
    fetched = (
        lax.all_gather(w_reduce.astype(jnp.bfloat16), "fsdp", axis=0, tiled=True),
        lax.all_gather(w_dilated.astype(jnp.bfloat16), "fsdp", axis=0, tiled=True),
        lax.all_gather(w_expand.astype(jnp.bfloat16), "fsdp", axis=1, tiled=True),
    )
    reduce_low, dilated_low, expand_low = fetched
    first = jnp.einsum("rwc,cm->rwm", inputs, reduce_low, preferred_element_type=jnp.float32)
    scaled_one, inverse_one, normed_one = normalize(
        first, moments(first, valid_mask), valid_count, gain_values[:middle], bias_values[:middle]
    )
    hidden_one = jax.nn.silu(normed_one).astype(jnp.bfloat16)
    second = dilated_forward(hidden_one, dilated_low, trunk_rate, layout)
    scaled_two, inverse_two, normed_two = normalize(
        second,
        moments(second, valid_mask),
        valid_count,
        gain_values[middle : 2 * middle],
        bias_values[middle : 2 * middle],
    )
    hidden_two = jax.nn.silu(normed_two).astype(jnp.bfloat16)
    third = jnp.einsum("rwm,mc->rwc", hidden_two, expand_low, preferred_element_type=jnp.float32)
    scaled_three, inverse_three, normed_three = normalize(
        third,
        moments(third, valid_mask),
        valid_count,
        gain_values[2 * middle : trunk_end],
        bias_values[2 * middle : trunk_end],
    )
    pre_act = inputs_float + normed_three
    trunk_out = jax.nn.silu(pre_act).astype(jnp.bfloat16)
    heads_low = lax.all_gather(w_heads.astype(jnp.bfloat16), "fsdp", axis=1, tiled=True)
    responses = jnp.stack(
        [
            dilated_forward(trunk_out, heads_low[head_index], head_rates[head_index], layout)
            for head_index in range(head_total)
        ]
    )
    head_gain = gain_values[trunk_end:].reshape(head_total, head_width)
    head_bias = bias_values[trunk_end:].reshape(head_total, head_width)
    head_scaled, head_inverse, head_normed = normalize(
        responses, moments(responses, valid_mask), valid_count, head_gain, head_bias
    )
    grad_normed = cotangent[:, 0].astype(jnp.float32) * silu_slope(head_normed)
    grad_responses, head_sums = norm_backward(
        grad_normed, head_scaled, head_inverse, head_gain, valid_mask, valid_count
    )
    grad_responses = grad_responses.astype(jnp.bfloat16)
    heads_back = lax.all_gather(w_heads.astype(jnp.bfloat16), "fsdp", axis=1, tiled=True)
    head_parts = [
        dilated_backward(
            trunk_out,
            heads_back[head_index],
            grad_responses[head_index],
            head_rates[head_index],
            layout,
        )
        for head_index in range(head_total)
    ]
    squares = lax.psum(
        jnp.stack([jnp.sum(part[0] * part[0]) for part in head_parts]), ("dp", "fsdp")
    )
    task_rms = jnp.sqrt(squares / (valid_count * channels) + task_epsilon)
    task_weight = task_scale / task_rms
    grad_trunk = jnp.zeros((row_count, col_count, channels), jnp.float32)
    for head_index in range(head_total):
        grad_trunk = grad_trunk + task_weight[head_index] * head_parts[head_index][0]
    weighted_heads = jnp.stack(
        [task_weight[head_index] * head_parts[head_index][1] for head_index in range(head_total)]
    )
    heads_shard = lax.psum_scatter(weighted_heads, "fsdp", scatter_dimension=1, tiled=True)
    grad_pre = grad_trunk * silu_slope(pre_act)
    grad_third, sums_three = norm_backward(
        grad_pre,
        scaled_three,
        inverse_three,
        gain_values[2 * middle : trunk_end],
        valid_mask,
        valid_count,
    )
    grad_third = grad_third.astype(jnp.bfloat16)
    reduce_back, dilated_back, expand_back = (
        lax.all_gather(w_reduce.astype(jnp.bfloat16), "fsdp", axis=0, tiled=True),
        lax.all_gather(w_dilated.astype(jnp.bfloat16), "fsdp", axis=0, tiled=True),
        lax.all_gather(w_expand.astype(jnp.bfloat16), "fsdp", axis=1, tiled=True),
    )
    grad_expand = jnp.einsum(
        "rwm,rwc->mc", hidden_two, grad_third, preferred_element_type=jnp.float32
    )
    grad_hidden_two = jnp.einsum(
        "rwc,mc->rwm", grad_third, expand_back, preferred_element_type=jnp.float32
    )
    grad_second, sums_two = norm_backward(
        grad_hidden_two * silu_slope(normed_two),
        scaled_two,
        inverse_two,
        gain_values[middle : 2 * middle],
        valid_mask,
        valid_count,
    )
    grad_hidden_one, grad_dilated = dilated_backward(
        hidden_one, dilated_back, grad_second.astype(jnp.bfloat16), trunk_rate, layout
    )
    grad_first, sums_one = norm_backward(
        grad_hidden_one * silu_slope(normed_one),
        scaled_one,
        inverse_one,
        gain_values[:middle],
        valid_mask,
        valid_count,
    )
    grad_first = grad_first.astype(jnp.bfloat16)
    grad_reduce = jnp.einsum("rwc,rwm->cm", inputs, grad_first, preferred_element_type=jnp.float32)
    features_grad = (
        jnp.einsum("rwm,cm->rwc", grad_first, reduce_back, preferred_element_type=jnp.float32)
        + grad_pre
    )
    trunk_shards = (
        lax.psum_scatter(grad_reduce, "fsdp", scatter_dimension=0, tiled=True),
        lax.psum_scatter(grad_dilated, "fsdp", scatter_dimension=0, tiled=True),
        lax.psum_scatter(grad_expand, "fsdp", scatter_dimension=1, tiled=True),
    )
    totals = (
        lax.psum(trunk_shards[0].astype(jnp.bfloat16), "dp").astype(jnp.float32),
        lax.psum(trunk_shards[1].astype(jnp.bfloat16), "dp").astype(jnp.float32),
        lax.psum(trunk_shards[2].astype(jnp.bfloat16), "dp").astype(jnp.float32),
        lax.psum(heads_shard.astype(jnp.bfloat16), "dp").astype(jnp.float32),
    )
    gain_grad = jnp.concatenate(
        [sums_one[1], sums_two[1], sums_three[1], (task_weight[:, None] * head_sums[1]).reshape(-1)]
    )
    bias_grad = jnp.concatenate(
        [sums_one[0], sums_two[0], sums_three[0], (task_weight[:, None] * head_sums[0]).reshape(-1)]
    )
    norm_grad = jnp.stack([gain_grad, bias_grad])
    w_reduce_new, m_reduce_new = update(w_reduce, m_reduce, totals[0])
    w_dilated_new, m_dilated_new = update(w_dilated, m_dilated, totals[1])
    w_expand_new, m_expand_new = update(w_expand, m_expand, totals[2])
    w_heads_new, m_heads_new = update(w_heads, m_heads, totals[3])
    norm_params_new, norm_moment_new = update(norm_params, norm_moment, norm_grad)
    return (
        features_grad[None],
        w_reduce_new,
        m_reduce_new,
        w_dilated_new,
        m_dilated_new,
        w_expand_new,
        m_expand_new,
        w_heads_new,
        m_heads_new,
        norm_params_new,
        norm_moment_new,
    )


def solution(mesh):
    placed = (
        P("dp", "fsdp", None, None),
        P(None, "dp", "fsdp", None, None),
        P(),
        P(),
        P("fsdp", None),
        P("fsdp", None),
        P(None, "fsdp"),
        P(None, "fsdp", None),
        P(),
        P("fsdp", None),
        P("fsdp", None),
        P(None, "fsdp"),
        P(None, "fsdp", None),
        P(),
    )
    return jax.shard_map(
        local,
        mesh=mesh,
        in_specs=placed,
        out_specs=(
            P("dp", "fsdp", None, None),
            P("fsdp", None),
            P("fsdp", None),
            P("fsdp", None),
            P("fsdp", None),
            P(None, "fsdp"),
            P(None, "fsdp"),
            P(None, "fsdp", None),
            P(None, "fsdp", None),
            P(),
            P(),
        ),
        check_vma=False,
    )
```

```python
import functools

import jax
import jax.numpy as jnp
from jax import lax
from jax.experimental import pallas as pl
from jax.experimental.pallas import tpu as pltpu
from jax.sharding import PartitionSpec as P

MESH = pl.DeviceIdType.MESH
norm_epsilon = 1e-05
task_epsilon = 1e-06
momentum_decay = 0.9
step_rate = 0.01
trunk_rate = 4
head_rates = (12, 24, 36)

class Tree:
    def __init__(self):
        self.core = lax.axis_index("dp")
        self.place = lax.axis_index("fsdp")
        self.count = lax.axis_size("fsdp")
        self.line = self.count // 4
        self.z = self.place // 4
        self.low = self.place % 4
        self.step_a = 1 + self.core
        self.step_b = 2 - self.core
        self.move_a = self.step_a * (1 - 2 * ((self.low // self.step_a) % 2))
        self.move_b = self.step_b * (1 - 2 * ((self.low // self.step_b) % 2))

    def at(self, place):
        return (self.core, place)

    @property
    def partner(self):
        return (1 - self.core, self.place)

    @property
    def a(self):
        return self.at(self.place + self.move_a)

    @property
    def b(self):
        return self.at(self.place + self.move_b)

    @property
    def down(self):
        return self.at(self.place - 4)

    @property
    def up(self):
        return self.at(self.place + 4)

    def greet(self):
        barrier = pltpu.get_barrier_semaphore()
        for peer in (self.partner, self.a, self.b):
            pl.semaphore_signal(barrier, inc=1, device_id=peer, device_id_type=MESH)

        @pl.when(self.z > 0)
        def _():
            pl.semaphore_signal(barrier, inc=1, device_id=self.down, device_id_type=MESH)

        @pl.when(self.z < self.line - 1)
        def _():
            pl.semaphore_signal(barrier, inc=1, device_id=self.up, device_id_type=MESH)

        pl.semaphore_wait(
            barrier,
            3
            + jnp.where(self.z > 0, 1, 0)
            + jnp.where(self.z < self.line - 1, 1, 0),
        )


def gather_kernel(count, *refs):
    shards, outs = refs[:count], refs[count : 2 * count]
    own_sem, sends, arrives, shares = refs[2 * count :]
    t = Tree()
    t.greet()
    line = t.line

    def half(ref, core):
        rows = ref.shape[-2] // 2
        return pl.ds(pl.multiple_of(core * rows, 8), rows)

    def copy(k, kind, block, peer, own=False, shared=False):
        dst = outs[k].at[block, half(outs[k], t.core)]
        src = shards[k].at[half(shards[k], t.core)] if own else dst
        return pltpu.make_async_remote_copy(
            src_ref=src,
            dst_ref=dst,
            send_sem=sends.at[k, kind, block],
            recv_sem=(shares if shared else arrives).at[k, block],
            device_id=peer,
            device_id_type=MESH,
        )

    def arrive(k, block):
        copy(k, 0, block, t.partner).wait_recv()

    def fan(k, block, own, go_down, go_up, to_a, to_b, finish):
        def act(c):
            c.wait_send() if finish else c.start()

        if go_down:
            pl.when(t.z > 0)(lambda: act(copy(k, 0, block, t.down, own)))
        if go_up:
            pl.when(t.z < line - 1)(lambda: act(copy(k, 1, block, t.up, own)))
        if to_a:
            act(copy(k, 2, block, t.a, own))
        if to_b:
            act(copy(k, 3, block, t.b, own))
        act(copy(k, 4, block, t.partner, own, shared=True))

    def walk(finish):
        def own():
            for k in range(count):
                here = outs[k].at[t.place]
                c = pltpu.make_async_copy(
                    shards[k].at[half(shards[k], t.core)],
                    outs[k].at[t.place, half(outs[k], t.core)],
                    own_sem.at[k],
                )
                c.wait() if finish else c.start()
                fan(k, t.place, True, True, True, True, True, finish)

        def along(s):
            for k in range(count):
                @pl.when(t.z - s >= 0)
                def _():
                    block = t.place - 4 * s
                    if not finish:
                        arrive(k, block)
                    fan(k, block, False, False, True, True, True, finish)

                @pl.when(t.z + s < line)
                def _():
                    block = t.place + 4 * s
                    if not finish:
                        arrive(k, block)
                    fan(k, block, False, True, False, True, True, finish)

        def side(s, move, to_b):
            for k in range(count):
                @pl.when(t.z - s >= 0)
                def _():
                    block = t.place - 4 * s + move
                    if not finish:
                        arrive(k, block)
                    fan(k, block, False, False, False, False, to_b, finish)

                if s:
                    @pl.when(t.z + s < line)
                    def _():
                        block = t.place + 4 * s + move
                        if not finish:
                            arrive(k, block)
                        fan(k, block, False, False, False, False, to_b, finish)

        own()
        for s in range(line):
            if s:
                along(s)
            if s >= 1:
                side(s - 1, t.move_a, True)
        side(line - 1, t.move_a, True)
        for s in range(line):
            side(s, t.move_b, False)
            side(s, t.move_a + t.move_b, False)

    walk(False)

    @pl.loop(0, t.count)
    def _(block):
        for k in range(count):
            other = outs[k].at[block, half(outs[k], 1 - t.core)]
            pltpu.make_async_remote_copy(
                src_ref=other,
                dst_ref=other,
                send_sem=sends.at[k, 4, block],
                recv_sem=shares.at[k, block],
                device_id=t.partner,
                device_id_type=MESH,
            ).wait_recv()

    walk(True)


def gather(shards, number):
    n = lax.axis_size("fsdp")
    count = len(shards)
    return pl.pallas_call(
        functools.partial(gather_kernel, count),
        out_shape=tuple(jax.ShapeDtypeStruct((n,) + s.shape, s.dtype) for s in shards),
        in_specs=[pl.BlockSpec(memory_space=pl.ANY)] * count,
        out_specs=tuple([pl.BlockSpec(memory_space=pl.ANY)] * count),
        scratch_shapes=[
            pltpu.SemaphoreType.DMA((count,)),
            pltpu.SemaphoreType.DMA((count, 5, n)),
            pltpu.SemaphoreType.DMA((count, n)),
            pltpu.SemaphoreType.DMA((count, n)),
        ],
        compiler_params=pltpu.CompilerParams(collective_id=number, has_side_effects=True),
    )(*shards)


def plane_sum_kernel(line, x_ref, o_ref, near, part, far, n_send, n_recv, f_send, f_recv):
    core = lax.axis_index("dp")
    place = lax.axis_index("fsdp")
    z, low = place // 4, place % 4
    me = low * 2 + core

    def beside(s):
        other = (me + s) % 8
        return (other % 2, z * 4 + other // 2)

    def away(s):
        return (core, ((z + s) % line) * 4 + low)

    barrier = pltpu.get_barrier_semaphore()
    for s in range(1, 8):
        pl.semaphore_signal(barrier, inc=1, device_id=beside(s), device_id_type=MESH)

    @pl.loop(1, line)
    def _(s):
        pl.semaphore_signal(barrier, inc=1, device_id=away(s), device_id_type=MESH)

    near[me] = x_ref[...]
    pl.semaphore_wait(barrier, 7 + line - 1)

    def to_beside(s):
        return pltpu.make_async_remote_copy(src_ref=x_ref, dst_ref=near.at[me], send_sem=n_send.at[s], recv_sem=n_recv, device_id=beside(s), device_id_type=MESH)

    def to_away(s):
        return pltpu.make_async_remote_copy(src_ref=part, dst_ref=far.at[z], send_sem=f_send.at[s], recv_sem=f_recv, device_id=away(s), device_id_type=MESH)

    for s in range(1, 8):
        to_beside(s).start()
    seven = near.at[pl.ds(0, 7)]
    pltpu.make_async_copy(seven, seven, n_recv).wait()
    total = jnp.sum(near[...], axis=0)
    part[...] = total
    pl.loop(1, line)(lambda s: to_away(s).start())
    far[z] = total
    rest = far.at[pl.ds(0, line - 1)]
    pltpu.make_async_copy(rest, rest, f_recv).wait()
    o_ref[...] = jnp.sum(far[...], axis=0)
    for s in range(1, 8):
        to_beside(s).wait_send()
    pl.loop(1, line)(lambda s: to_away(s).wait_send())


def all_sum(x, number):
    line = lax.axis_size("fsdp") // 4
    dma = pltpu.SemaphoreType.DMA
    return pl.pallas_call(
        functools.partial(plane_sum_kernel, line),
        out_shape=jax.ShapeDtypeStruct(x.shape, x.dtype),
        in_specs=[pl.BlockSpec(memory_space=pltpu.VMEM)],
        out_specs=pl.BlockSpec(memory_space=pltpu.VMEM),
        scratch_shapes=[
            pltpu.VMEM((8,) + x.shape, x.dtype), pltpu.VMEM(x.shape, x.dtype), pltpu.VMEM((line,) + x.shape, x.dtype),
            dma((8,)), dma, dma((line,)), dma,
        ],
        compiler_params=pltpu.CompilerParams(collective_id=number, has_side_effects=True),
    )(x)


def reduce_kernel(kinds, *refs):
    count = len(kinds)
    parts, outs = refs[:count], refs[count : 2 * count]
    scratch = refs[2 * count :]
    accs, prx, brx, arx, zrx = (scratch[k * count : (k + 1) * count] for k in range(5))
    load_sem, p_send, p_recv, b_send, b_recv, a_send, a_recv, z_send, z_recv, s_send, s_recv = scratch[5 * count :]
    t = Tree()
    t.greet()
    line, z, low = t.line, t.z, t.low

    def rows_of(k, core):
        rows = kinds[k][1] // 2
        return pl.ds(pl.multiple_of(core * rows, 16), rows)

    def remote(src, dst, send, recv, peer):
        return pltpu.make_async_remote_copy(src_ref=src, dst_ref=dst, send_sem=send, recv_sem=recv, device_id=peer, device_id_type=MESH)

    def load(k, block):
        return pltpu.make_async_copy(parts[k].at[:, block, rows_of(k, t.core)], accs[k].at[block], load_sem.at[k, block])

    def to_partner(k, block):
        return remote(parts[k].at[:, block, rows_of(k, 1 - t.core)], prx[k].at[block], p_send.at[k, block], p_recv.at[k, block], t.partner)

    upper = z >= line // 2
    own_spot = jnp.where(upper, z, line - 1 - z)

    def spot(j):
        q = j + jnp.where(j >= own_spot, 1, 0)
        other = jnp.where(upper, q, line - 1 - q)
        return jnp.where(j == line - 1, z, other)

    lows = (low + t.move_b, low + t.move_a + t.move_b, low + t.move_a, low)

    def to_b(k, zz, which):
        return remote(accs[k].at[zz * 4 + lows[which]], brx[k].at[zz * 2 + which], b_send.at[k, zz * 2 + which], b_recv.at[k, zz * 2 + which], t.b)

    def to_a(k, zz):
        return remote(accs[k].at[zz * 4 + lows[2]], arx[k].at[zz], a_send.at[k, zz], a_recv.at[k, zz], t.a)

    def along(k, zz, up):
        w = 1 if up else 0
        return remote(accs[k].at[zz * 4 + low], zrx[k].at[w, zz], z_send.at[k, w, zz], z_recv.at[k, w, zz], t.up if up else t.down)

    def add(k, block, ref):
        lead = kinds[k][0]

        @pl.loop(0, lead)
        def _(h):
            accs[k][block, h] = accs[k][block, h] + ref[h]

    def begin(j):
        zz = spot(j)
        for w in range(4):
            for k in range(count):
                to_partner(k, zz * 4 + lows[w]).start()
                load(k, zz * 4 + lows[w]).start()

    def stage_b(j):
        zz = spot(j)
        for w in range(4):
            for k in range(count):
                block = zz * 4 + lows[w]
                load(k, block).wait()
                to_partner(k, block).wait_recv()
                add(k, block, prx[k].at[block])
                if w < 2:
                    to_b(k, zz, w).start()

    def stage_a(j):
        zz = spot(j)
        for w in (1, 0):
            for k in range(count):
                to_b(k, zz, w).wait_recv()
                add(k, zz * 4 + lows[3 - w if w == 0 else 2], brx[k].at[zz * 2 + w])
                if w == 1:
                    to_a(k, zz).start()

    def stage_z(j):
        zz = spot(j)
        for k in range(count):
            to_a(k, zz).wait_recv()
            add(k, zz * 4 + low, arx[k].at[zz])

            @pl.when(jnp.logical_and(zz >= z, z > 0))
            def _():
                along(k, zz, True).wait_recv()
                add(k, zz * 4 + low, zrx[k].at[1, zz])

            @pl.when(jnp.logical_and(zz <= z, z < line - 1))
            def _():
                along(k, zz, False).wait_recv()
                add(k, zz * 4 + low, zrx[k].at[0, zz])

            @pl.when(zz > z)
            def _():
                along(k, zz, True).start()

            @pl.when(zz < z)
            def _():
                along(k, zz, False).start()

    pl.loop(0, line)(begin)

    @pl.loop(0, line + 2)
    def _(j):
        pl.when(j < line)(lambda: stage_b(j))
        pl.when(jnp.logical_and(j >= 1, j < line + 1))(lambda: stage_a(j - 1))
        pl.when(j >= 2)(lambda: stage_z(j - 2))

    def share(k):
        return remote(accs[k].at[t.place], outs[k].at[:, rows_of(k, t.core)], s_send.at[k], s_recv.at[k], t.partner)

    def keep(k):
        return pltpu.make_async_copy(accs[k].at[t.place], outs[k].at[:, rows_of(k, t.core)], load_sem.at[k, 0])

    for k in range(count):
        share(k).start()
        keep(k).start()

    @pl.loop(0, line)
    def _(j):
        zz = spot(j)
        for k in range(count):
            for w in range(4):
                to_partner(k, zz * 4 + lows[w]).wait_send()
            to_b(k, zz, 0).wait_send()
            to_b(k, zz, 1).wait_send()
            to_a(k, zz).wait_send()
            pl.when(zz > z)(lambda: along(k, zz, True).wait_send())
            pl.when(zz < z)(lambda: along(k, zz, False).wait_send())

    for k in range(count):
        keep(k).wait()
        other = outs[k].at[:, rows_of(k, 1 - t.core)]
        remote(other, other, s_send.at[k], s_recv.at[k], t.partner).wait_recv()
        share(k).wait_send()


def reduce_shards(parts, number):
    n = lax.axis_size("fsdp")
    line = n // 4
    kinds = [(p.shape[0], p.shape[2], p.shape[3]) for p in parts]
    bf = jnp.bfloat16
    count = len(parts)
    dma = pltpu.SemaphoreType.DMA

    def room(*lead):
        return [pltpu.VMEM(tuple(lead) + (l, r // 2, c), bf) for l, r, c in kinds]

    return pl.pallas_call(
        functools.partial(reduce_kernel, kinds),
        out_shape=tuple(jax.ShapeDtypeStruct((l, r, c), bf) for l, r, c in kinds),
        in_specs=[pl.BlockSpec(memory_space=pl.ANY)] * count,
        out_specs=tuple([pl.BlockSpec(memory_space=pl.ANY)] * count),
        scratch_shapes=room(n) + room(n) + room(2 * line) + room(line) + room(2, line)
        + [dma((count, n)), dma((count, n)), dma((count, n)), dma((count, 2 * line)), dma((count, 2 * line)),
           dma((count, line)), dma((count, line)), dma((count, 2, line)), dma((count, 2, line)), dma((count,)), dma((count,))],
        compiler_params=pltpu.CompilerParams(collective_id=number, has_side_effects=True, vmem_limit_bytes=60 * 2**20),
    )(*parts)


def exchange_kernel(offsets, rows, count, x_ref, o_ref, send, recv):
    core = lax.axis_index("dp")
    place = lax.axis_index("fsdp")
    pieces = []
    for k, offset in enumerate(offsets):
        first, cut = offset // rows, offset % rows
        for part, (gap, low, high, to) in enumerate(
            ((first, cut, rows, 0), (first + 1, 0, cut, rows - cut))
        ):
            if high > low:
                pieces.append((k, part, gap, low, high - low, to))
    gaps = sorted({abs(p[2]) for p in pieces} - {0})
    gaps = [-g for g in gaps] + gaps
    barrier = pltpu.get_barrier_semaphore()

    def present(gap):
        return jnp.logical_and(place + gap >= 0, place + gap < count)

    met = jnp.int32(0)
    for gap in gaps:
        met = met + jnp.where(present(gap), 1, 0)

        @pl.when(present(gap))
        def _():
            pl.semaphore_signal(
                barrier, inc=1, device_id=(core, place + gap), device_id_type=MESH
            )

    pl.semaphore_wait(barrier, met)

    def piece(k, part, gap, low, size, to):
        return pltpu.make_async_remote_copy(
            src_ref=x_ref.at[k, pl.ds(low, size)],
            dst_ref=o_ref.at[k, pl.ds(to, size)],
            send_sem=send.at[k, part],
            recv_sem=recv.at[k, part],
            device_id=(core, place - gap),
            device_id_type=MESH,
        )

    for p in pieces:
        k, part, gap, low, size, to = p
        if gap == 0:
            o_ref[k, to : to + size] = x_ref[k, low : low + size]
        else:
            pl.when(present(-gap))(lambda p=p: piece(*p).start())
    for p in pieces:
        if p[2]:
            pl.when(present(p[2]))(lambda p=p: piece(*p).wait_recv())
    for p in pieces:
        if p[2]:
            pl.when(present(-p[2]))(lambda p=p: piece(*p).wait_send())


def exchange(x, offsets, number):
    entries, rows = x.shape[:2]
    return pl.pallas_call(
        functools.partial(exchange_kernel, offsets, rows, lax.axis_size("fsdp")),
        out_shape=jax.ShapeDtypeStruct(x.shape, x.dtype),
        in_specs=[pl.BlockSpec(memory_space=pltpu.VMEM)],
        out_specs=pl.BlockSpec(memory_space=pltpu.VMEM),
        scratch_shapes=[
            pltpu.SemaphoreType.DMA((entries, 2)),
            pltpu.SemaphoreType.DMA((entries, 2)),
        ],
        compiler_params=pltpu.CompilerParams(
            collective_id=number, has_side_effects=True, vmem_limit_bytes=32 * 2**20
        ),
    )(x)


def gather_all(shards, number):
    if lax.axis_size("fsdp") == 16:
        return gather(shards, number)
    return tuple(lax.all_gather(s, "fsdp", axis=0) for s in shards)


def reduce_all(parts, number):
    if lax.axis_size("fsdp") == 16:
        return reduce_shards(parts, number)
    out = []
    for part in parts:
        lead, count, rows, cols = part.shape
        shard = lax.psum_scatter(part, "fsdp", scatter_dimension=1, tiled=True)
        out.append(lax.psum(shard, "dp").reshape(lead, rows, cols))
    return tuple(out)


def silu_slope(values):
    sigmoid_value = jax.nn.sigmoid(values)
    return sigmoid_value * (1.0 + values * (1.0 - sigmoid_value))


def shift_along(values, offset, axis_number):
    if offset == 0:
        return values
    length = values.shape[axis_number]
    pad_shape = list(values.shape)
    pad_shape[axis_number] = abs(offset)
    zero_block = jnp.zeros(pad_shape, values.dtype)
    if offset > 0:
        return jnp.concatenate(
            [lax.slice_in_dim(values, offset, length, axis=axis_number), zero_block], axis_number
        )
    return jnp.concatenate(
        [zero_block, lax.slice_in_dim(values, 0, length + offset, axis=axis_number)], axis_number
    )


def inside_rows(layout, offset):
    row_ids, row_top, row_bottom, row_side = layout
    return (row_ids + offset >= row_top) & (row_ids + offset < row_bottom)


def inside_cols(layout, offset, col_count):
    row_ids, row_top, row_bottom, row_side = layout
    columns = jnp.arange(col_count, dtype=jnp.int32)
    return (columns[None, :] + offset >= 0) & (columns[None, :] + offset < row_side[:, None])


def column_sums(inputs, weight, rate, layout):
    col_count = inputs.shape[1]
    products = jnp.einsum("rwc,kco->krwo", inputs, weight, preferred_element_type=jnp.float32)
    sums = []
    for row_step in range(3):
        summed = 0.0
        for col_step in range(3):
            across = (col_step - 1) * rate
            summed = summed + jnp.where(
                inside_cols(layout, across, col_count)[:, :, None],
                shift_along(products[3 * row_step + col_step], across, 1),
                0.0,
            )
        sums.append(summed)
    return sums


def dilated_forward(inputs, weights, rates, layout, number):
    outer, centers = [], []
    for weight, rate in zip(weights, rates):
        low, center, high = column_sums(inputs, weight, rate, layout)
        outer += [low.astype(jnp.bfloat16), high.astype(jnp.bfloat16)]
        centers.append(center)
    offsets = tuple(o for rate in rates for o in (-rate, rate))
    pulled = exchange(jnp.stack(outer), offsets, number)
    results = []
    for k, (center, rate) in enumerate(zip(centers, rates)):
        for j, down in ((2 * k, -rate), (2 * k + 1, rate)):
            center = center + jnp.where(
                inside_rows(layout, down)[:, None, None], pulled[j].astype(jnp.float32), 0.0
            )
        results.append(center)
    return results


def spread_taps(grads, rates, layout, number):
    row_ids = layout[0]
    row_count, col_count = grads[0].shape[:2]
    total_rows = row_count * lax.axis_size("fsdp")
    outer = []
    for grad, rate in zip(grads, rates):
        for down in (-rate, rate):
            outer.append(
                jnp.where(inside_rows(layout, down)[:, None, None], grad, jnp.bfloat16(0.0))
            )
    offsets = tuple(o for rate in rates for o in (rate, -rate))
    pulled = exchange(jnp.stack(outer), offsets, number)
    results = []
    for k, (grad, rate) in enumerate(zip(grads, rates)):
        taps = []
        for row_step in range(3):
            down = (row_step - 1) * rate
            if row_step == 1:
                arrived = grad
            else:
                there = (row_ids - down >= 0) & (row_ids - down < total_rows)
                arrived = jnp.where(
                    there[:, None, None], pulled[2 * k + row_step // 2], jnp.bfloat16(0.0)
                )
            for col_step in range(3):
                across = (col_step - 1) * rate
                kept = jnp.where(
                    inside_cols(layout, across, col_count)[:, :, None], arrived, jnp.bfloat16(0.0)
                )
                taps.append(shift_along(kept, -across, 1))
        results.append(taps)
    return results


def spread(stat):
    return stat.reshape(stat.shape[:-1] + (1, 1) + stat.shape[-1:])


def totals_of(one, two, number):
    local_sums = jnp.stack([jnp.sum(one, axis=(-3, -2)), jnp.sum(two, axis=(-3, -2))])
    flat = all_sum(local_sums.reshape(2, -1), number)
    return flat.reshape(local_sums.shape)


def moments(values, valid_mask, number):
    weighted = values * valid_mask[..., None]
    return totals_of(weighted, weighted * values, number)


def normalize(values, sums, valid_count, gain_row, bias_row):
    mean_value = sums[0] / valid_count
    variance = sums[1] / valid_count - mean_value * mean_value
    inverse = lax.rsqrt(variance + norm_epsilon)
    scaled = (values - spread(mean_value)) * spread(inverse)
    return (scaled, inverse, scaled * spread(gain_row) + spread(bias_row))


def norm_backward(grad_norm, scaled, inverse, gain_row, valid_mask, valid_count, number):
    masked = grad_norm * valid_mask[..., None]
    sums = totals_of(masked, masked * scaled, number)
    grad_values = (
        valid_mask[..., None]
        * spread(inverse * gain_row)
        * (masked - spread(sums[0] / valid_count) - scaled * spread(sums[1] / valid_count))
    )
    return (grad_values, sums)


def update(param, moment, grad):
    moment_new = momentum_decay * moment + grad
    return (param - step_rate * moment_new, moment_new)


def local(
    features,
    cotangent,
    crop_heights,
    task_scale,
    w_reduce,
    w_dilated,
    w_expand,
    w_heads,
    norm_params,
    m_reduce,
    m_dilated,
    m_expand,
    m_heads,
    norm_moment,
):
    row_count = features.shape[1]
    col_count = features.shape[2]
    channels = features.shape[3]
    middle = w_reduce.shape[1]
    head_width = w_heads.shape[2]
    head_total = w_heads.shape[0]
    group_index = lax.axis_index("dp")
    place_index = lax.axis_index("fsdp")
    group_heights = lax.dynamic_index_in_dim(crop_heights, group_index, 0, keepdims=False)
    crop_order = jnp.arange(group_heights.shape[0], dtype=jnp.int32)
    crop_ends = jnp.sum(
        jnp.where(crop_order[None, :] <= crop_order[:, None], group_heights[None, :], 0),
        axis=1,
        dtype=jnp.int32,
    )
    crop_starts = crop_ends - group_heights
    row_ids = place_index * row_count + jnp.arange(row_count, dtype=jnp.int32)
    member = (row_ids[:, None] >= crop_starts[None, :]) & (row_ids[:, None] < crop_ends[None, :])
    row_top = jnp.sum(jnp.where(member, crop_starts[None, :], 0), axis=1, dtype=jnp.int32)
    row_bottom = jnp.sum(jnp.where(member, crop_ends[None, :], 0), axis=1, dtype=jnp.int32)
    row_side = jnp.sum(jnp.where(member, group_heights[None, :], 0), axis=1, dtype=jnp.int32)
    layout = (row_ids, row_top, row_bottom, row_side)
    valid_mask = (jnp.arange(col_count, dtype=jnp.int32)[None, :] < row_side[:, None]).astype(
        jnp.float32
    )
    valid_count = jnp.sum(crop_heights * crop_heights).astype(jnp.float32)
    gain_values = norm_params[0]
    bias_values = norm_params[1]
    trunk_end = 2 * middle + channels
    inputs = features[0]
    inputs_float = inputs.astype(jnp.float32)
    place_count = lax.axis_size("fsdp")
    half_rows = w_heads.shape[1] // 2
    heads_half = lax.dynamic_slice_in_dim(w_heads, group_index * half_rows, half_rows, 1)
    heads_low = lax.all_gather(
        heads_half.astype(jnp.bfloat16), ("fsdp", "dp"), axis=1, tiled=True
    ).reshape(head_total * 9, channels, head_width)
    reduce_low, dilated_low, expand_low = gather_all(
        (
            w_reduce.astype(jnp.bfloat16),
            w_dilated.astype(jnp.bfloat16),
            w_expand.astype(jnp.bfloat16),
        ),
        0,
    )
    reduce_low = reduce_low.reshape(channels, middle)
    dilated_low = dilated_low.reshape(9, middle, middle)
    first = jnp.einsum("rwc,cm->rwm", inputs, reduce_low, preferred_element_type=jnp.float32)
    scaled_one, inverse_one, normed_one = normalize(
        first, moments(first, valid_mask, 1), valid_count, gain_values[:middle], bias_values[:middle]
    )
    hidden_one = jax.nn.silu(normed_one).astype(jnp.bfloat16)
    (second,) = dilated_forward(hidden_one, (dilated_low,), (trunk_rate,), layout, 2)
    scaled_two, inverse_two, normed_two = normalize(
        second,
        moments(second, valid_mask, 3),
        valid_count,
        gain_values[middle : 2 * middle],
        bias_values[middle : 2 * middle],
    )
    hidden_two = jax.nn.silu(normed_two).astype(jnp.bfloat16)
    third = jnp.einsum(
        "rwm,kmc->rwkc", hidden_two, expand_low, preferred_element_type=jnp.float32
    ).reshape(row_count, col_count, channels)
    scaled_three, inverse_three, normed_three = normalize(
        third,
        moments(third, valid_mask, 4),
        valid_count,
        gain_values[2 * middle : trunk_end],
        bias_values[2 * middle : trunk_end],
    )
    pre_act = inputs_float + normed_three
    trunk_out = jax.nn.silu(pre_act).astype(jnp.bfloat16)
    responses = jnp.stack(
        dilated_forward(
            trunk_out,
            [heads_low[9 * k : 9 * k + 9] for k in range(head_total)],
            head_rates,
            layout,
            5,
        )
    )
    head_gain = gain_values[trunk_end:].reshape(head_total, head_width)
    head_bias = bias_values[trunk_end:].reshape(head_total, head_width)
    head_scaled, head_inverse, head_normed = normalize(
        responses, moments(responses, valid_mask, 6), valid_count, head_gain, head_bias
    )
    grad_normed = cotangent[:, 0].astype(jnp.float32) * silu_slope(head_normed)
    grad_responses, head_sums = norm_backward(
        grad_normed, head_scaled, head_inverse, head_gain, valid_mask, valid_count, 7
    )
    grad_responses = grad_responses.astype(jnp.bfloat16)
    taps = spread_taps(
        [grad_responses[k] for k in range(head_total)], head_rates, layout, 8
    )
    head_taps = [jnp.stack(t) for t in taps]
    head_grads = [
        jnp.einsum(
            "krwo,kco->rwc",
            head_taps[k],
            heads_low[9 * k : 9 * k + 9],
            preferred_element_type=jnp.float32,
        )
        for k in range(head_total)
    ]
    squares = jnp.stack([jnp.sum(g * g) for g in head_grads])
    squares = all_sum(jnp.broadcast_to(squares[:, None], (head_total, 128)), 9)[:, 0]
    task_rms = jnp.sqrt(squares / (valid_count * channels) + task_epsilon)
    task_weight = task_scale / task_rms
    grad_trunk = task_weight[0] * head_grads[0]
    for k in range(1, head_total):
        grad_trunk = grad_trunk + task_weight[k] * head_grads[k]
    grad_heads = jnp.einsum(
        "rwc,krwo->kco",
        trunk_out,
        jnp.concatenate(head_taps),
        preferred_element_type=jnp.float32,
    ).astype(jnp.bfloat16)
    (heads_total,) = reduce_all(
        (grad_heads.reshape(head_total, place_count, -1, head_width),), 10
    )
    grad_pre = grad_trunk * silu_slope(pre_act)
    grad_third, sums_three = norm_backward(
        grad_pre,
        scaled_three,
        inverse_three,
        gain_values[2 * middle : trunk_end],
        valid_mask,
        valid_count,
        11,
    )
    grad_third = grad_third.astype(jnp.bfloat16).reshape(row_count, col_count, place_count, -1)
    grad_expand = jnp.einsum(
        "rwm,rwkc->kmc", hidden_two, grad_third, preferred_element_type=jnp.float32
    )
    grad_hidden_two = jnp.einsum(
        "rwkc,kmc->rwm", grad_third, expand_low, preferred_element_type=jnp.float32
    )
    grad_second, sums_two = norm_backward(
        grad_hidden_two * silu_slope(normed_two),
        scaled_two,
        inverse_two,
        gain_values[middle : 2 * middle],
        valid_mask,
        valid_count,
        12,
    )
    (taps,) = spread_taps([grad_second.astype(jnp.bfloat16)], (trunk_rate,), layout, 13)
    taps = jnp.stack(taps)
    grad_hidden_one = jnp.einsum(
        "krwo,kco->rwc", taps, dilated_low, preferred_element_type=jnp.float32
    )
    grad_dilated = jnp.einsum(
        "rwc,krwo->kco", hidden_one, taps, preferred_element_type=jnp.float32
    )
    grad_first, sums_one = norm_backward(
        grad_hidden_one * silu_slope(normed_one),
        scaled_one,
        inverse_one,
        gain_values[:middle],
        valid_mask,
        valid_count,
        14,
    )
    grad_first = grad_first.astype(jnp.bfloat16)
    grad_reduce = jnp.einsum("rwc,rwm->cm", inputs, grad_first, preferred_element_type=jnp.float32)
    features_grad = (
        jnp.einsum("rwm,cm->rwc", grad_first, reduce_low, preferred_element_type=jnp.float32)
        + grad_pre
    )
    trunk_totals = reduce_all(
        (
            grad_reduce.astype(jnp.bfloat16).reshape(1, place_count, -1, middle),
            grad_dilated.astype(jnp.bfloat16).reshape(1, place_count, -1, middle),
            grad_expand.astype(jnp.bfloat16)[None],
        ),
        15,
    )
    totals = tuple(t[0].astype(jnp.float32) for t in trunk_totals) + (
        task_weight[:, None, None] * heads_total.astype(jnp.float32),
    )
    gain_grad = jnp.concatenate(
        [sums_one[1], sums_two[1], sums_three[1], (task_weight[:, None] * head_sums[1]).reshape(-1)]
    )
    bias_grad = jnp.concatenate(
        [sums_one[0], sums_two[0], sums_three[0], (task_weight[:, None] * head_sums[0]).reshape(-1)]
    )
    norm_grad = jnp.stack([gain_grad, bias_grad])
    w_reduce_new, m_reduce_new = update(w_reduce, m_reduce, totals[0])
    w_dilated_new, m_dilated_new = update(w_dilated, m_dilated, totals[1])
    w_expand_new, m_expand_new = update(w_expand, m_expand, totals[2])
    w_heads_new, m_heads_new = update(w_heads, m_heads, totals[3])
    norm_params_new, norm_moment_new = update(norm_params, norm_moment, norm_grad)
    return (
        features_grad[None],
        w_reduce_new,
        m_reduce_new,
        w_dilated_new,
        m_dilated_new,
        w_expand_new,
        m_expand_new,
        w_heads_new,
        m_heads_new,
        norm_params_new,
        norm_moment_new,
    )


def solution(mesh):
    placed = (
        P("dp", "fsdp", None, None),
        P(None, "dp", "fsdp", None, None),
        P(),
        P(),
        P("fsdp", None),
        P("fsdp", None),
        P(None, "fsdp"),
        P(None, "fsdp", None),
        P(),
        P("fsdp", None),
        P("fsdp", None),
        P(None, "fsdp"),
        P(None, "fsdp", None),
        P(),
    )
    return jax.shard_map(
        local,
        mesh=mesh,
        in_specs=placed,
        out_specs=(
            P("dp", "fsdp", None, None),
            P("fsdp", None),
            P("fsdp", None),
            P("fsdp", None),
            P("fsdp", None),
            P(None, "fsdp"),
            P(None, "fsdp"),
            P(None, "fsdp", None),
            P(None, "fsdp", None),
            P(),
            P(),
        ),
        check_vma=False,
    )
```

```python
import functools

import jax
import jax.numpy as jnp
from jax import lax
from jax.experimental import pallas as pl
from jax.experimental.pallas import tpu as pltpu
from jax.sharding import PartitionSpec as P

MESH = pl.DeviceIdType.MESH
norm_epsilon = 1e-05
task_epsilon = 1e-06
momentum_decay = 0.9
step_rate = 0.01
trunk_rate = 4
head_rates = (12, 24, 36)

class Tree:
    def __init__(self):
        self.core = lax.axis_index("dp")
        self.place = lax.axis_index("fsdp")
        self.count = lax.axis_size("fsdp")
        self.line = self.count // 4
        self.z = self.place // 4
        self.low = self.place % 4
        self.step_a = 1 + self.core
        self.step_b = 2 - self.core
        self.move_a = self.step_a * (1 - 2 * ((self.low // self.step_a) % 2))
        self.move_b = self.step_b * (1 - 2 * ((self.low // self.step_b) % 2))

    def at(self, place):
        return (self.core, place)

    @property
    def partner(self):
        return (1 - self.core, self.place)

    @property
    def a(self):
        return self.at(self.place + self.move_a)

    @property
    def b(self):
        return self.at(self.place + self.move_b)

    @property
    def down(self):
        return self.at(self.place - 4)

    @property
    def up(self):
        return self.at(self.place + 4)

    def greet(self):
        barrier = pltpu.get_barrier_semaphore()
        for peer in (self.partner, self.a, self.b):
            pl.semaphore_signal(barrier, inc=1, device_id=peer, device_id_type=MESH)

        @pl.when(self.z > 0)
        def _():
            pl.semaphore_signal(barrier, inc=1, device_id=self.down, device_id_type=MESH)

        @pl.when(self.z < self.line - 1)
        def _():
            pl.semaphore_signal(barrier, inc=1, device_id=self.up, device_id_type=MESH)

        pl.semaphore_wait(
            barrier,
            3
            + jnp.where(self.z > 0, 1, 0)
            + jnp.where(self.z < self.line - 1, 1, 0),
        )


def gather_kernel(count, *refs):
    shards, outs = refs[:count], refs[count : 2 * count]
    own_sem, sends, arrives, shares = refs[2 * count :]
    t = Tree()
    t.greet()
    line = t.line

    def half(ref, core):
        rows = ref.shape[-2] // 2
        return pl.ds(pl.multiple_of(core * rows, 8), rows)

    def copy(k, kind, block, peer, own=False, shared=False):
        dst = outs[k].at[block, half(outs[k], t.core)]
        src = shards[k].at[half(shards[k], t.core)] if own else dst
        return pltpu.make_async_remote_copy(
            src_ref=src,
            dst_ref=dst,
            send_sem=sends.at[k, kind, block],
            recv_sem=(shares if shared else arrives).at[k, block],
            device_id=peer,
            device_id_type=MESH,
        )

    def arrive(k, block):
        copy(k, 0, block, t.partner).wait_recv()

    def fan(k, block, own, go_down, go_up, to_a, to_b, finish):
        def act(c):
            c.wait_send() if finish else c.start()

        if go_down:
            pl.when(t.z > 0)(lambda: act(copy(k, 0, block, t.down, own)))
        if go_up:
            pl.when(t.z < line - 1)(lambda: act(copy(k, 1, block, t.up, own)))
        if to_a:
            act(copy(k, 2, block, t.a, own))
        if to_b:
            act(copy(k, 3, block, t.b, own))
        act(copy(k, 4, block, t.partner, own, shared=True))

    def walk(finish):
        def own():
            for k in range(count):
                here = outs[k].at[t.place]
                c = pltpu.make_async_copy(
                    shards[k].at[half(shards[k], t.core)],
                    outs[k].at[t.place, half(outs[k], t.core)],
                    own_sem.at[k],
                )
                c.wait() if finish else c.start()
                fan(k, t.place, True, True, True, True, True, finish)

        def along(s):
            for k in range(count):
                @pl.when(t.z - s >= 0)
                def _():
                    block = t.place - 4 * s
                    if not finish:
                        arrive(k, block)
                    fan(k, block, False, False, True, True, True, finish)

                @pl.when(t.z + s < line)
                def _():
                    block = t.place + 4 * s
                    if not finish:
                        arrive(k, block)
                    fan(k, block, False, True, False, True, True, finish)

        def side(s, move, to_b):
            for k in range(count):
                @pl.when(t.z - s >= 0)
                def _():
                    block = t.place - 4 * s + move
                    if not finish:
                        arrive(k, block)
                    fan(k, block, False, False, False, False, to_b, finish)

                if s:
                    @pl.when(t.z + s < line)
                    def _():
                        block = t.place + 4 * s + move
                        if not finish:
                            arrive(k, block)
                        fan(k, block, False, False, False, False, to_b, finish)

        own()
        for s in range(line):
            if s:
                along(s)
            if s >= 1:
                side(s - 1, t.move_a, True)
        side(line - 1, t.move_a, True)
        for s in range(line):
            side(s, t.move_b, False)
            side(s, t.move_a + t.move_b, False)

    walk(False)

    @pl.loop(0, t.count)
    def _(block):
        for k in range(count):
            other = outs[k].at[block, half(outs[k], 1 - t.core)]
            pltpu.make_async_remote_copy(
                src_ref=other,
                dst_ref=other,
                send_sem=sends.at[k, 4, block],
                recv_sem=shares.at[k, block],
                device_id=t.partner,
                device_id_type=MESH,
            ).wait_recv()

    walk(True)


def gather(shards, number):
    n = lax.axis_size("fsdp")
    count = len(shards)
    return pl.pallas_call(
        functools.partial(gather_kernel, count),
        out_shape=tuple(jax.ShapeDtypeStruct((n,) + s.shape, s.dtype) for s in shards),
        in_specs=[pl.BlockSpec(memory_space=pl.ANY)] * count,
        out_specs=tuple([pl.BlockSpec(memory_space=pl.ANY)] * count),
        scratch_shapes=[
            pltpu.SemaphoreType.DMA((count,)),
            pltpu.SemaphoreType.DMA((count, 5, n)),
            pltpu.SemaphoreType.DMA((count, n)),
            pltpu.SemaphoreType.DMA((count, n)),
        ],
        compiler_params=pltpu.CompilerParams(collective_id=number, has_side_effects=True),
    )(*shards)


def plane_sum_kernel(line, x_ref, o_ref, near, part, far, n_send, n_recv, f_send, f_recv):
    core = lax.axis_index("dp")
    place = lax.axis_index("fsdp")
    z, low = place // 4, place % 4
    me = low * 2 + core

    def beside(s):
        other = (me + s) % 8
        return (other % 2, z * 4 + other // 2)

    def away(s):
        return (core, ((z + s) % line) * 4 + low)

    barrier = pltpu.get_barrier_semaphore()
    for s in range(1, 8):
        pl.semaphore_signal(barrier, inc=1, device_id=beside(s), device_id_type=MESH)

    @pl.loop(1, line)
    def _(s):
        pl.semaphore_signal(barrier, inc=1, device_id=away(s), device_id_type=MESH)

    near[me] = x_ref[...]
    pl.semaphore_wait(barrier, 7 + line - 1)

    def to_beside(s):
        return pltpu.make_async_remote_copy(src_ref=x_ref, dst_ref=near.at[me], send_sem=n_send.at[s], recv_sem=n_recv, device_id=beside(s), device_id_type=MESH)

    def to_away(s):
        return pltpu.make_async_remote_copy(src_ref=part, dst_ref=far.at[z], send_sem=f_send.at[s], recv_sem=f_recv, device_id=away(s), device_id_type=MESH)

    for s in range(1, 8):
        to_beside(s).start()
    seven = near.at[pl.ds(0, 7)]
    pltpu.make_async_copy(seven, seven, n_recv).wait()
    total = jnp.sum(near[...], axis=0)
    part[...] = total
    pl.loop(1, line)(lambda s: to_away(s).start())
    far[z] = total
    rest = far.at[pl.ds(0, line - 1)]
    pltpu.make_async_copy(rest, rest, f_recv).wait()
    o_ref[...] = jnp.sum(far[...], axis=0)
    for s in range(1, 8):
        to_beside(s).wait_send()
    pl.loop(1, line)(lambda s: to_away(s).wait_send())


def all_sum(x, number):
    line = lax.axis_size("fsdp") // 4
    dma = pltpu.SemaphoreType.DMA
    return pl.pallas_call(
        functools.partial(plane_sum_kernel, line),
        out_shape=jax.ShapeDtypeStruct(x.shape, x.dtype),
        in_specs=[pl.BlockSpec(memory_space=pltpu.VMEM)],
        out_specs=pl.BlockSpec(memory_space=pltpu.VMEM),
        scratch_shapes=[
            pltpu.VMEM((8,) + x.shape, x.dtype), pltpu.VMEM(x.shape, x.dtype), pltpu.VMEM((line,) + x.shape, x.dtype),
            dma((8,)), dma, dma((line,)), dma,
        ],
        compiler_params=pltpu.CompilerParams(collective_id=number, has_side_effects=True),
    )(x)


def reduce_kernel(kinds, *refs):
    count = len(kinds)
    parts, outs = refs[:count], refs[count : 2 * count]
    scratch = refs[2 * count :]
    accs, prx, brx, arx, zrx = (scratch[k * count : (k + 1) * count] for k in range(5))
    load_sem, p_send, p_recv, b_send, b_recv, a_send, a_recv, z_send, z_recv, s_send, s_recv = scratch[5 * count :]
    t = Tree()
    t.greet()
    line, z, low = t.line, t.z, t.low

    def rows_of(k, core):
        rows = kinds[k][1] // 2
        return pl.ds(pl.multiple_of(core * rows, 16), rows)

    def remote(src, dst, send, recv, peer):
        return pltpu.make_async_remote_copy(src_ref=src, dst_ref=dst, send_sem=send, recv_sem=recv, device_id=peer, device_id_type=MESH)

    def load(k, block):
        return pltpu.make_async_copy(parts[k].at[:, block, rows_of(k, t.core)], accs[k].at[block], load_sem.at[k, block])

    def to_partner(k, block):
        return remote(parts[k].at[:, block, rows_of(k, 1 - t.core)], prx[k].at[block], p_send.at[k, block], p_recv.at[k, block], t.partner)

    upper = z >= line // 2
    own_spot = jnp.where(upper, z, line - 1 - z)

    def spot(j):
        q = j + jnp.where(j >= own_spot, 1, 0)
        other = jnp.where(upper, q, line - 1 - q)
        return jnp.where(j == line - 1, z, other)

    lows = (low + t.move_b, low + t.move_a + t.move_b, low + t.move_a, low)

    def to_b(k, zz, which):
        return remote(accs[k].at[zz * 4 + lows[which]], brx[k].at[zz * 2 + which], b_send.at[k, zz * 2 + which], b_recv.at[k, zz * 2 + which], t.b)

    def to_a(k, zz):
        return remote(accs[k].at[zz * 4 + lows[2]], arx[k].at[zz], a_send.at[k, zz], a_recv.at[k, zz], t.a)

    def along(k, zz, up):
        w = 1 if up else 0
        return remote(accs[k].at[zz * 4 + low], zrx[k].at[w, zz], z_send.at[k, w, zz], z_recv.at[k, w, zz], t.up if up else t.down)

    def add(k, block, ref):
        lead = kinds[k][0]

        @pl.loop(0, lead)
        def _(h):
            accs[k][block, h] = accs[k][block, h] + ref[h]

    def begin(j):
        zz = spot(j)
        for w in range(4):
            for k in range(count):
                to_partner(k, zz * 4 + lows[w]).start()
                load(k, zz * 4 + lows[w]).start()

    def stage_b(j):
        zz = spot(j)
        for w in range(4):
            for k in range(count):
                block = zz * 4 + lows[w]
                load(k, block).wait()
                to_partner(k, block).wait_recv()
                add(k, block, prx[k].at[block])
                if w < 2:
                    to_b(k, zz, w).start()

    def stage_a(j):
        zz = spot(j)
        for w in (1, 0):
            for k in range(count):
                to_b(k, zz, w).wait_recv()
                add(k, zz * 4 + lows[3 - w if w == 0 else 2], brx[k].at[zz * 2 + w])
                if w == 1:
                    to_a(k, zz).start()

    def stage_z(j):
        zz = spot(j)
        for k in range(count):
            to_a(k, zz).wait_recv()
            add(k, zz * 4 + low, arx[k].at[zz])

            @pl.when(jnp.logical_and(zz >= z, z > 0))
            def _():
                along(k, zz, True).wait_recv()
                add(k, zz * 4 + low, zrx[k].at[1, zz])

            @pl.when(jnp.logical_and(zz <= z, z < line - 1))
            def _():
                along(k, zz, False).wait_recv()
                add(k, zz * 4 + low, zrx[k].at[0, zz])

            @pl.when(zz > z)
            def _():
                along(k, zz, True).start()

            @pl.when(zz < z)
            def _():
                along(k, zz, False).start()

    pl.loop(0, line)(begin)

    @pl.loop(0, line + 2)
    def _(j):
        pl.when(j < line)(lambda: stage_b(j))
        pl.when(jnp.logical_and(j >= 1, j < line + 1))(lambda: stage_a(j - 1))
        pl.when(j >= 2)(lambda: stage_z(j - 2))

    def share(k):
        return remote(accs[k].at[t.place], outs[k].at[:, rows_of(k, t.core)], s_send.at[k], s_recv.at[k], t.partner)

    def keep(k):
        return pltpu.make_async_copy(accs[k].at[t.place], outs[k].at[:, rows_of(k, t.core)], load_sem.at[k, 0])

    for k in range(count):
        share(k).start()
        keep(k).start()

    @pl.loop(0, line)
    def _(j):
        zz = spot(j)
        for k in range(count):
            for w in range(4):
                to_partner(k, zz * 4 + lows[w]).wait_send()
            to_b(k, zz, 0).wait_send()
            to_b(k, zz, 1).wait_send()
            to_a(k, zz).wait_send()
            pl.when(zz > z)(lambda: along(k, zz, True).wait_send())
            pl.when(zz < z)(lambda: along(k, zz, False).wait_send())

    for k in range(count):
        keep(k).wait()
        other = outs[k].at[:, rows_of(k, 1 - t.core)]
        remote(other, other, s_send.at[k], s_recv.at[k], t.partner).wait_recv()
        share(k).wait_send()


def reduce_shards(parts, number):
    n = lax.axis_size("fsdp")
    line = n // 4
    kinds = [(p.shape[0], p.shape[2], p.shape[3]) for p in parts]
    bf = jnp.bfloat16
    count = len(parts)
    dma = pltpu.SemaphoreType.DMA

    def room(*lead):
        return [pltpu.VMEM(tuple(lead) + (l, r // 2, c), bf) for l, r, c in kinds]

    return pl.pallas_call(
        functools.partial(reduce_kernel, kinds),
        out_shape=tuple(jax.ShapeDtypeStruct((l, r, c), bf) for l, r, c in kinds),
        in_specs=[pl.BlockSpec(memory_space=pl.ANY)] * count,
        out_specs=tuple([pl.BlockSpec(memory_space=pl.ANY)] * count),
        scratch_shapes=room(n) + room(n) + room(2 * line) + room(line) + room(2, line)
        + [dma((count, n)), dma((count, n)), dma((count, n)), dma((count, 2 * line)), dma((count, 2 * line)),
           dma((count, line)), dma((count, line)), dma((count, 2, line)), dma((count, 2, line)), dma((count,)), dma((count,))],
        compiler_params=pltpu.CompilerParams(collective_id=number, has_side_effects=True, vmem_limit_bytes=60 * 2**20),
    )(*parts)


def exchange_kernel(offsets, rows, count, x_ref, o_ref, send, recv):
    core = lax.axis_index("dp")
    place = lax.axis_index("fsdp")
    pieces = []
    for k, offset in enumerate(offsets):
        first, cut = offset // rows, offset % rows
        for part, (gap, low, high, to) in enumerate(
            ((first, cut, rows, 0), (first + 1, 0, cut, rows - cut))
        ):
            if high > low:
                pieces.append((k, part, gap, low, high - low, to))
    gaps = sorted({abs(p[2]) for p in pieces} - {0})
    gaps = [-g for g in gaps] + gaps
    barrier = pltpu.get_barrier_semaphore()

    def present(gap):
        return jnp.logical_and(place + gap >= 0, place + gap < count)

    met = jnp.int32(0)
    for gap in gaps:
        met = met + jnp.where(present(gap), 1, 0)

        @pl.when(present(gap))
        def _():
            pl.semaphore_signal(
                barrier, inc=1, device_id=(core, place + gap), device_id_type=MESH
            )

    pl.semaphore_wait(barrier, met)

    def piece(k, part, gap, low, size, to):
        return pltpu.make_async_remote_copy(
            src_ref=x_ref.at[k, pl.ds(low, size)],
            dst_ref=o_ref.at[k, pl.ds(to, size)],
            send_sem=send.at[k, part],
            recv_sem=recv.at[k, part],
            device_id=(core, place - gap),
            device_id_type=MESH,
        )

    for p in pieces:
        k, part, gap, low, size, to = p
        if gap == 0:
            o_ref[k, to : to + size] = x_ref[k, low : low + size]
        else:
            pl.when(present(-gap))(lambda p=p: piece(*p).start())
    for p in pieces:
        if p[2]:
            pl.when(present(p[2]))(lambda p=p: piece(*p).wait_recv())
    for p in pieces:
        if p[2]:
            pl.when(present(-p[2]))(lambda p=p: piece(*p).wait_send())


def exchange(x, offsets, number):
    entries, rows = x.shape[:2]
    return pl.pallas_call(
        functools.partial(exchange_kernel, offsets, rows, lax.axis_size("fsdp")),
        out_shape=jax.ShapeDtypeStruct(x.shape, x.dtype),
        in_specs=[pl.BlockSpec(memory_space=pltpu.VMEM)],
        out_specs=pl.BlockSpec(memory_space=pltpu.VMEM),
        scratch_shapes=[
            pltpu.SemaphoreType.DMA((entries, 2)),
            pltpu.SemaphoreType.DMA((entries, 2)),
        ],
        compiler_params=pltpu.CompilerParams(
            collective_id=number, has_side_effects=True, vmem_limit_bytes=32 * 2**20
        ),
    )(x)


def plane_signal(line, core, z, low):
    barrier = pltpu.get_barrier_semaphore()
    me = low * 2 + core
    for s in range(1, 8):
        other = (me + s) % 8
        pl.semaphore_signal(
            barrier, inc=1, device_id=(other % 2, z * 4 + other // 2), device_id_type=MESH
        )

    @pl.loop(1, line)
    def _(s):
        pl.semaphore_signal(
            barrier, inc=1, device_id=(core, ((z + s) % line) * 4 + low), device_id_type=MESH
        )


def plane_scratch(line, shape):
    dma = pltpu.SemaphoreType.DMA
    return [
        pltpu.VMEM((8,) + shape, jnp.float32),
        pltpu.VMEM(shape, jnp.float32),
        pltpu.VMEM((line,) + shape, jnp.float32),
        dma((8,)),
        dma,
        dma((line,)),
        dma,
    ]


def plane_sum(line, fill, room):
    near, part, far, n_send, n_recv, f_send, f_recv = room
    core = lax.axis_index("dp")
    place = lax.axis_index("fsdp")
    z, low = place // 4, place % 4
    me = low * 2 + core

    def to_beside(s):
        other = (me + s) % 8
        return pltpu.make_async_remote_copy(
            src_ref=near.at[me],
            dst_ref=near.at[me],
            send_sem=n_send.at[s],
            recv_sem=n_recv,
            device_id=(other % 2, z * 4 + other // 2),
            device_id_type=MESH,
        )

    def to_away(s):
        return pltpu.make_async_remote_copy(
            src_ref=part,
            dst_ref=far.at[z],
            send_sem=f_send.at[s],
            recv_sem=f_recv,
            device_id=(core, ((z + s) % line) * 4 + low),
            device_id_type=MESH,
        )

    fill(near.at[me])
    for s in range(1, 8):
        to_beside(s).start()
    seven = near.at[pl.ds(0, 7)]
    pltpu.make_async_copy(seven, seven, n_recv).wait()
    total = jnp.sum(near[...], axis=0)
    part[...] = total
    pl.loop(1, line)(lambda s: to_away(s).start())
    far[z] = total
    rest = far.at[pl.ds(0, line - 1)]
    pltpu.make_async_copy(rest, rest, f_recv).wait()
    result = jnp.sum(far[...], axis=0)
    for s in range(1, 8):
        to_beside(s).wait_send()
    pl.loop(1, line)(lambda s: to_away(s).wait_send())
    return result


def row_pieces(offset, rows):
    first, cut = offset // rows, offset % rows
    pieces = [(first, cut, rows - cut, 0)]
    if cut:
        pieces.append((first + 1, 0, cut, rows - cut))
    return pieces


def row_gaps(offsets, rows):
    gaps = {abs(p[0]) for o in offsets for p in row_pieces(o, rows)} - {0}
    return sorted(-g for g in gaps) + sorted(gaps)


def greet_rows(gaps, count):
    barrier = pltpu.get_barrier_semaphore()
    core = lax.axis_index("dp")
    place = lax.axis_index("fsdp")
    met = jnp.int32(0)
    for gap in gaps:
        here = jnp.logical_and(place + gap >= 0, place + gap < count)
        met = met + jnp.where(here, 1, 0)

        @pl.when(here)
        def _():
            pl.semaphore_signal(
                barrier, inc=1, device_id=(core, place + gap), device_id_type=MESH
            )

    return met


class Rows:
    def __init__(self, offsets, rows, cols, count, x_ref, o_ref, send, recv):
        self.core = lax.axis_index("dp")
        self.place = lax.axis_index("fsdp")
        self.rows, self.cols, self.count = rows, cols, count
        self.offsets, self.x_ref, self.o_ref = offsets, x_ref, o_ref
        self.send, self.recv = send, recv

    def present(self, gap):
        return jnp.logical_and(self.place + gap >= 0, self.place + gap < self.count)

    def copies(self, k):
        for part, (gap, low, size, to) in enumerate(row_pieces(self.offsets[k], self.rows)):
            yield gap, low, size, to, pltpu.make_async_remote_copy(
                src_ref=self.x_ref.at[k, pl.ds(low * self.cols, size * self.cols)],
                dst_ref=self.o_ref.at[k, pl.ds(to * self.cols, size * self.cols)],
                send_sem=self.send.at[k, part],
                recv_sem=self.recv.at[k, part],
                device_id=(self.core, self.place - gap),
                device_id_type=MESH,
            )

    def start(self, k):
        for gap, low, size, to, copy in self.copies(k):
            if gap == 0:
                cols = self.cols
                self.o_ref[k, to * cols : (to + size) * cols] = self.x_ref[
                    k, low * cols : (low + size) * cols
                ]
            else:
                pl.when(self.present(-gap))(copy.start)

    def wait_recv(self, k):
        for gap, _, _, _, copy in self.copies(k):
            if gap:
                pl.when(self.present(gap))(copy.wait_recv)

    def wait_send(self, k):
        for gap, _, _, _, copy in self.copies(k):
            if gap:
                pl.when(self.present(-gap))(copy.wait_send)


def heads_kernel(
    rates, rows, cols, count,
    x_ref, xt_ref, w_ref, cot_ref, par_ref, mask_ref,
    g_ref, dw_ref, sums_ref, sq_ref,
    wv, out_rows, in_rows, resp, dn, taps, g_room, dw_room,
    w_sem, f_send, f_recv, e_send, e_recv, g_sem, dw_sem, *rooms,
):
    px = rows * cols
    heads = len(rates)
    width = par_ref.shape[1]
    line = count // 4
    core = lax.axis_index("dp")
    place = lax.axis_index("fsdp")
    z, low = place // 4, place % 4
    one, two, three = rooms[:7], rooms[7:14], rooms[14:]

    def w_copy(k):
        return pltpu.make_async_copy(
            w_ref.at[k], wv.at[k // 9, :, pl.ds(pl.multiple_of((k % 9) * width, width), width)], w_sem.at[k]
        )

    pl.loop(0, 9 * heads)(lambda k: w_copy(k).start())
    fwd = Rows([o for r in rates for o in (-r, r)], rows, cols, count, out_rows, in_rows, f_send, f_recv)
    bwd = Rows([o for r in rates for o in (r, -r)], rows, cols, count, out_rows, in_rows, e_send, e_recv)
    plane_signal(line, core, z, low)
    met = greet_rows(row_gaps(fwd.offsets, rows), count)
    barrier = pltpu.get_barrier_semaphore()

    def mask(t, k):
        return mask_ref[t, :, k : k + 1]

    @pl.loop(0, heads)
    def _(t):
        rate = 12 * (t + 1)
        for j in range(3):
            summed = None
            for c in range(3):
                k = 3 * j + c
                w_copy(t * 9 + k).wait()
                prod = jnp.dot(
                    x_ref[...], wv[t, :, k * width : (k + 1) * width], preferred_element_type=jnp.float32
                )
                if c == 0:
                    summed = jnp.where(mask(t, 1) > 0, pltpu.roll(prod, rate, 0), 0.0)
                elif c == 1:
                    summed = summed + jnp.where(mask(t, 0) > 0, prod, 0.0)
                else:
                    summed = summed + jnp.where(mask(t, 2) > 0, pltpu.roll(prod, px - rate, 0), 0.0)
            if j == 1:
                resp[t] = summed
            else:
                out_rows[t * 2 + j // 2] = summed.astype(jnp.bfloat16)

        @pl.when(t == 0)
        def _():
            pl.semaphore_wait(barrier, 7 + line - 1 + met)

        for h in range(heads):
            @pl.when(t == h)
            def _():
                fwd.start(2 * h)
                fwd.start(2 * h + 1)

    def stats(ref):
        for h in range(heads):
            total = resp[h]
            for j in (0, 1):
                fwd.wait_recv(2 * h + j)
                total = total + jnp.where(
                    mask(h, 3 + j) > 0, in_rows[2 * h + j].astype(jnp.float32), 0.0
                )
            resp[h] = total
            kept = total * mask(h, 0)
            ref[2 * h : 2 * h + 1] = jnp.sum(kept, axis=0, keepdims=True)
            ref[2 * h + 1 : 2 * h + 2] = jnp.sum(kept * total, axis=0, keepdims=True)

    sums = plane_sum(line, stats, one)
    pixels = par_ref[2 * heads : 2 * heads + 1]
    inverses = []

    def grads(ref):
        for h in range(heads):
            mean = sums[2 * h : 2 * h + 1] / pixels
            var = sums[2 * h + 1 : 2 * h + 2] / pixels - mean * mean
            inverse = lax.rsqrt(var + norm_epsilon)
            inverses.append(inverse)
            scaled = (resp[h] - mean) * inverse
            normed = scaled * par_ref[2 * h : 2 * h + 1] + par_ref[2 * h + 1 : 2 * h + 2]
            s = jax.nn.sigmoid(normed)
            d = cot_ref[h].astype(jnp.float32) * (s * (1.0 + normed * (1.0 - s))) * mask(h, 0)
            resp[h] = scaled
            dn[h] = d
            ref[2 * h : 2 * h + 1] = jnp.sum(d, axis=0, keepdims=True)
            ref[2 * h + 1 : 2 * h + 2] = jnp.sum(d * scaled, axis=0, keepdims=True)

    back = plane_sum(line, grads, two)
    sums_ref[...] = back
    for h in range(heads):
        fwd.wait_send(2 * h)
        fwd.wait_send(2 * h + 1)
        e = (
            mask(h, 0)
            * (inverses[h] * par_ref[2 * h : 2 * h + 1])
            * (dn[h] - back[2 * h : 2 * h + 1] / pixels - resp[h] * (back[2 * h + 1 : 2 * h + 2] / pixels))
        )
        dn[h] = e
        out_rows[2 * h] = jnp.where(mask(h, 3) > 0, e, 0.0).astype(jnp.bfloat16)
        out_rows[2 * h + 1] = jnp.where(mask(h, 4) > 0, e, 0.0).astype(jnp.bfloat16)
        bwd.start(2 * h)
        bwd.start(2 * h + 1)

    def g_copy(t):
        return pltpu.make_async_copy(g_room, g_ref.at[t], g_sem)

    def dw_copy(k):
        return pltpu.make_async_copy(dw_room.at[k % 2], dw_ref.at[k], dw_sem.at[k % 2])

    def spread(t, j, arrived):
        rate = 12 * (t + 1)
        for c in range(3):
            if c == 0:
                tap = pltpu.roll(jnp.where(mask(t, 1) > 0, arrived, 0.0), px - rate, 0)
            elif c == 1:
                tap = jnp.where(mask(t, 0) > 0, arrived, 0.0)
            else:
                tap = pltpu.roll(jnp.where(mask(t, 2) > 0, arrived, 0.0), rate, 0)
            k = 3 * j + c
            taps[:, k * width : (k + 1) * width] = tap.astype(jnp.bfloat16)

    tiles = wv.shape[1] // width
    sq_ref[...] = jnp.zeros_like(sq_ref)

    @pl.loop(0, heads)
    def _(t):
        for h in range(heads):
            @pl.when(t == h)
            def _():
                bwd.wait_recv(2 * h)
                bwd.wait_recv(2 * h + 1)

        spread(t, 1, dn[t].astype(jnp.bfloat16).astype(jnp.float32))
        spread(t, 0, jnp.where(mask(t, 5) > 0, in_rows[2 * t].astype(jnp.float32), 0.0))
        spread(t, 2, jnp.where(mask(t, 6) > 0, in_rows[2 * t + 1].astype(jnp.float32), 0.0))

        @pl.loop(0, 9)
        def _(k):
            at = t * 9 + k

            @pl.when(at >= 2)
            def _():
                dw_copy(at - 2).wait()

            dw_room[at % 2] = jnp.dot(
                xt_ref[...],
                taps[:, pl.ds(pl.multiple_of(k * width, width), width)],
                preferred_element_type=jnp.float32,
            ).astype(jnp.bfloat16)
            dw_copy(at).start()

        pl.when(t > 0)(lambda: g_copy(t - 1).wait())
        def tile(n, square):
            cut = pl.ds(pl.multiple_of(n * width, width), width)
            g = lax.dot_general(
                taps[...], wv[t, cut, :], (((1,), (1,)), ((), ())), preferred_element_type=jnp.float32
            )
            g_room[:, cut] = g
            return square + jnp.sum(g * g, axis=0, keepdims=True)

        square = lax.fori_loop(0, tiles, tile, jnp.zeros((1, width), jnp.float32))
        sq_ref[pl.ds(t, 1)] = square
        g_copy(t).start()

    g_copy(heads - 1).wait()
    dw_copy(9 * heads - 2).wait()
    dw_copy(9 * heads - 1).wait()

    def fill(ref):
        ref[...] = sq_ref[...]

    sq_ref[...] = plane_sum(line, fill, three)
    for k in range(2 * heads):
        bwd.wait_send(k)


def heads_step(trunk_out, weights, cotangent, params, masks, rates, rows, cols, number):
    px, channels = trunk_out.shape
    heads, width = len(rates), weights.shape[-1]
    count = lax.axis_size("fsdp")
    line = count // 4
    bf, f32 = jnp.bfloat16, jnp.float32
    dma = pltpu.SemaphoreType.DMA
    vmem = pl.BlockSpec(memory_space=pltpu.VMEM)
    hbm = pl.BlockSpec(memory_space=pl.ANY)
    return pl.pallas_call(
        functools.partial(heads_kernel, rates, rows, cols, count),
        out_shape=(
            jax.ShapeDtypeStruct((heads, px, channels), f32),
            jax.ShapeDtypeStruct((9 * heads, channels, width), bf),
            jax.ShapeDtypeStruct((2 * heads, width), f32),
            jax.ShapeDtypeStruct((8, width), f32),
        ),
        in_specs=[vmem, vmem, hbm, vmem, vmem, vmem],
        out_specs=(hbm, hbm, vmem, vmem),
        scratch_shapes=[
            pltpu.VMEM((heads, channels, 9 * width), bf),
            pltpu.VMEM((2 * heads, px, width), bf),
            pltpu.VMEM((2 * heads, px, width), bf),
            pltpu.VMEM((heads, px, width), f32),
            pltpu.VMEM((heads, px, width), f32),
            pltpu.VMEM((px, 9 * width), bf),
            pltpu.VMEM((px, channels), f32),
            pltpu.VMEM((2, channels, width), bf),
            dma((9 * heads,)),
            dma((2 * heads, 2)),
            dma((2 * heads, 2)),
            dma((2 * heads, 2)),
            dma((2 * heads, 2)),
            dma,
            dma((2,)),
        ]
        + plane_scratch(line, (2 * heads, width))
        + plane_scratch(line, (2 * heads, width))
        + plane_scratch(line, (8, width)),
        compiler_params=pltpu.CompilerParams(
            collective_id=number, has_side_effects=True, vmem_limit_bytes=62 * 2**20
        ),
    )(trunk_out, trunk_out.T, weights, cotangent, params, masks)


def gather_all(shards, number):
    if lax.axis_size("fsdp") == 16:
        return gather(shards, number)
    return tuple(lax.all_gather(s, "fsdp", axis=0) for s in shards)


def reduce_all(parts, number):
    if lax.axis_size("fsdp") == 16:
        return reduce_shards(parts, number)
    out = []
    for part in parts:
        lead, count, rows, cols = part.shape
        shard = lax.psum_scatter(part, "fsdp", scatter_dimension=1, tiled=True)
        out.append(lax.psum(shard, "dp").reshape(lead, rows, cols))
    return tuple(out)


def silu_slope(values):
    sigmoid_value = jax.nn.sigmoid(values)
    return sigmoid_value * (1.0 + values * (1.0 - sigmoid_value))


def shift_along(values, offset, axis_number):
    if offset == 0:
        return values
    length = values.shape[axis_number]
    pad_shape = list(values.shape)
    pad_shape[axis_number] = abs(offset)
    zero_block = jnp.zeros(pad_shape, values.dtype)
    if offset > 0:
        return jnp.concatenate(
            [lax.slice_in_dim(values, offset, length, axis=axis_number), zero_block], axis_number
        )
    return jnp.concatenate(
        [zero_block, lax.slice_in_dim(values, 0, length + offset, axis=axis_number)], axis_number
    )


def inside_rows(layout, offset):
    row_ids, row_top, row_bottom, row_side = layout
    return (row_ids + offset >= row_top) & (row_ids + offset < row_bottom)


def inside_cols(layout, offset, col_count):
    row_ids, row_top, row_bottom, row_side = layout
    columns = jnp.arange(col_count, dtype=jnp.int32)
    return (columns[None, :] + offset >= 0) & (columns[None, :] + offset < row_side[:, None])


def column_sums(inputs, weight, rate, layout):
    col_count = inputs.shape[1]
    products = jnp.einsum("rwc,kco->krwo", inputs, weight, preferred_element_type=jnp.float32)
    sums = []
    for row_step in range(3):
        summed = 0.0
        for col_step in range(3):
            across = (col_step - 1) * rate
            summed = summed + jnp.where(
                inside_cols(layout, across, col_count)[:, :, None],
                shift_along(products[3 * row_step + col_step], across, 1),
                0.0,
            )
        sums.append(summed)
    return sums


def dilated_forward(inputs, weights, rates, layout, number):
    outer, centers = [], []
    for weight, rate in zip(weights, rates):
        low, center, high = column_sums(inputs, weight, rate, layout)
        outer += [low.astype(jnp.bfloat16), high.astype(jnp.bfloat16)]
        centers.append(center)
    offsets = tuple(o for rate in rates for o in (-rate, rate))
    pulled = exchange(jnp.stack(outer), offsets, number)
    results = []
    for k, (center, rate) in enumerate(zip(centers, rates)):
        for j, down in ((2 * k, -rate), (2 * k + 1, rate)):
            center = center + jnp.where(
                inside_rows(layout, down)[:, None, None], pulled[j].astype(jnp.float32), 0.0
            )
        results.append(center)
    return results


def spread_taps(grads, rates, layout, number):
    row_ids = layout[0]
    row_count, col_count = grads[0].shape[:2]
    total_rows = row_count * lax.axis_size("fsdp")
    outer = []
    for grad, rate in zip(grads, rates):
        for down in (-rate, rate):
            outer.append(
                jnp.where(inside_rows(layout, down)[:, None, None], grad, jnp.bfloat16(0.0))
            )
    offsets = tuple(o for rate in rates for o in (rate, -rate))
    pulled = exchange(jnp.stack(outer), offsets, number)
    results = []
    for k, (grad, rate) in enumerate(zip(grads, rates)):
        taps = []
        for row_step in range(3):
            down = (row_step - 1) * rate
            if row_step == 1:
                arrived = grad
            else:
                there = (row_ids - down >= 0) & (row_ids - down < total_rows)
                arrived = jnp.where(
                    there[:, None, None], pulled[2 * k + row_step // 2], jnp.bfloat16(0.0)
                )
            for col_step in range(3):
                across = (col_step - 1) * rate
                kept = jnp.where(
                    inside_cols(layout, across, col_count)[:, :, None], arrived, jnp.bfloat16(0.0)
                )
                taps.append(shift_along(kept, -across, 1))
        results.append(taps)
    return results


def spread(stat):
    return stat.reshape(stat.shape[:-1] + (1, 1) + stat.shape[-1:])


def totals_of(one, two, number):
    local_sums = jnp.stack([jnp.sum(one, axis=(-3, -2)), jnp.sum(two, axis=(-3, -2))])
    flat = all_sum(local_sums.reshape(2, -1), number)
    return flat.reshape(local_sums.shape)


def moments(values, valid_mask, number):
    weighted = values * valid_mask[..., None]
    return totals_of(weighted, weighted * values, number)


def normalize(values, sums, valid_count, gain_row, bias_row):
    mean_value = sums[0] / valid_count
    variance = sums[1] / valid_count - mean_value * mean_value
    inverse = lax.rsqrt(variance + norm_epsilon)
    scaled = (values - spread(mean_value)) * spread(inverse)
    return (scaled, inverse, scaled * spread(gain_row) + spread(bias_row))


def norm_backward(grad_norm, scaled, inverse, gain_row, valid_mask, valid_count, number):
    masked = grad_norm * valid_mask[..., None]
    sums = totals_of(masked, masked * scaled, number)
    grad_values = (
        valid_mask[..., None]
        * spread(inverse * gain_row)
        * (masked - spread(sums[0] / valid_count) - scaled * spread(sums[1] / valid_count))
    )
    return (grad_values, sums)


def update(param, moment, grad):
    moment_new = momentum_decay * moment + grad
    return (param - step_rate * moment_new, moment_new)


def local(
    features,
    cotangent,
    crop_heights,
    task_scale,
    w_reduce,
    w_dilated,
    w_expand,
    w_heads,
    norm_params,
    m_reduce,
    m_dilated,
    m_expand,
    m_heads,
    norm_moment,
):
    row_count = features.shape[1]
    col_count = features.shape[2]
    channels = features.shape[3]
    middle = w_reduce.shape[1]
    head_width = w_heads.shape[2]
    head_total = w_heads.shape[0]
    group_index = lax.axis_index("dp")
    place_index = lax.axis_index("fsdp")
    group_heights = lax.dynamic_index_in_dim(crop_heights, group_index, 0, keepdims=False)
    crop_order = jnp.arange(group_heights.shape[0], dtype=jnp.int32)
    crop_ends = jnp.sum(
        jnp.where(crop_order[None, :] <= crop_order[:, None], group_heights[None, :], 0),
        axis=1,
        dtype=jnp.int32,
    )
    crop_starts = crop_ends - group_heights
    row_ids = place_index * row_count + jnp.arange(row_count, dtype=jnp.int32)
    member = (row_ids[:, None] >= crop_starts[None, :]) & (row_ids[:, None] < crop_ends[None, :])
    row_top = jnp.sum(jnp.where(member, crop_starts[None, :], 0), axis=1, dtype=jnp.int32)
    row_bottom = jnp.sum(jnp.where(member, crop_ends[None, :], 0), axis=1, dtype=jnp.int32)
    row_side = jnp.sum(jnp.where(member, group_heights[None, :], 0), axis=1, dtype=jnp.int32)
    layout = (row_ids, row_top, row_bottom, row_side)
    valid_mask = (jnp.arange(col_count, dtype=jnp.int32)[None, :] < row_side[:, None]).astype(
        jnp.float32
    )
    valid_count = jnp.sum(crop_heights * crop_heights).astype(jnp.float32)
    gain_values = norm_params[0]
    bias_values = norm_params[1]
    trunk_end = 2 * middle + channels
    inputs = features[0]
    inputs_float = inputs.astype(jnp.float32)
    place_count = lax.axis_size("fsdp")
    half_rows = w_heads.shape[1] // 2
    heads_half = lax.dynamic_slice_in_dim(w_heads, group_index * half_rows, half_rows, 1)
    heads_low = lax.all_gather(
        heads_half.astype(jnp.bfloat16), ("fsdp", "dp"), axis=1, tiled=True
    ).reshape(head_total * 9, channels, head_width)
    reduce_low, dilated_low, expand_low = gather_all(
        (
            w_reduce.astype(jnp.bfloat16),
            w_dilated.astype(jnp.bfloat16),
            w_expand.astype(jnp.bfloat16),
        ),
        0,
    )
    reduce_low = reduce_low.reshape(channels, middle)
    dilated_low = dilated_low.reshape(9, middle, middle)
    first = jnp.einsum("rwc,cm->rwm", inputs, reduce_low, preferred_element_type=jnp.float32)
    scaled_one, inverse_one, normed_one = normalize(
        first, moments(first, valid_mask, 1), valid_count, gain_values[:middle], bias_values[:middle]
    )
    hidden_one = jax.nn.silu(normed_one).astype(jnp.bfloat16)
    (second,) = dilated_forward(hidden_one, (dilated_low,), (trunk_rate,), layout, 2)
    scaled_two, inverse_two, normed_two = normalize(
        second,
        moments(second, valid_mask, 3),
        valid_count,
        gain_values[middle : 2 * middle],
        bias_values[middle : 2 * middle],
    )
    hidden_two = jax.nn.silu(normed_two).astype(jnp.bfloat16)
    third = jnp.einsum(
        "rwm,kmc->rwkc", hidden_two, expand_low, preferred_element_type=jnp.float32
    ).reshape(row_count, col_count, channels)
    scaled_three, inverse_three, normed_three = normalize(
        third,
        moments(third, valid_mask, 4),
        valid_count,
        gain_values[2 * middle : trunk_end],
        bias_values[2 * middle : trunk_end],
    )
    pre_act = inputs_float + normed_three
    trunk_out = jax.nn.silu(pre_act).astype(jnp.bfloat16)
    pixels = row_count * col_count
    head_gain = gain_values[trunk_end:].reshape(head_total, head_width)
    head_bias = bias_values[trunk_end:].reshape(head_total, head_width)
    head_params = jnp.concatenate(
        [
            jnp.stack([head_gain, head_bias], 1).reshape(2 * head_total, head_width),
            jnp.broadcast_to(valid_count, (2, head_width)),
        ]
    )
    total_rows = row_count * place_count
    masks = []
    for rate in head_rates:
        flags = [
            inside_cols(layout, 0, col_count),
            inside_cols(layout, -rate, col_count),
            inside_cols(layout, rate, col_count),
        ] + [
            jnp.broadcast_to(flag[:, None], (row_count, col_count))
            for flag in (
                inside_rows(layout, -rate),
                inside_rows(layout, rate),
                row_ids + rate < total_rows,
                row_ids - rate >= 0,
            )
        ]
        flags = jnp.stack([f.reshape(pixels) for f in flags], 1).astype(jnp.float32)
        masks.append(jnp.pad(flags, ((0, 0), (0, 128 - flags.shape[1]))))
    head_grads, grad_heads, head_sums, squares = heads_step(
        trunk_out.reshape(pixels, channels),
        heads_low,
        cotangent.reshape(head_total, pixels, head_width),
        head_params,
        jnp.stack(masks),
        head_rates,
        row_count,
        col_count,
        5,
    )
    head_sums = head_sums.reshape(head_total, 2, head_width).transpose(1, 0, 2)
    squares = jnp.sum(squares[:head_total], axis=1)
    task_rms = jnp.sqrt(squares / (valid_count * channels) + task_epsilon)
    task_weight = task_scale / task_rms
    grad_trunk = task_weight[0] * head_grads[0]
    for k in range(1, head_total):
        grad_trunk = grad_trunk + task_weight[k] * head_grads[k]
    grad_trunk = grad_trunk.reshape(row_count, col_count, channels)
    (heads_total,) = reduce_all(
        (grad_heads.reshape(head_total, place_count, -1, head_width),), 10
    )
    grad_pre = grad_trunk * silu_slope(pre_act)
    grad_third, sums_three = norm_backward(
        grad_pre,
        scaled_three,
        inverse_three,
        gain_values[2 * middle : trunk_end],
        valid_mask,
        valid_count,
        11,
    )
    grad_third = grad_third.astype(jnp.bfloat16).reshape(row_count, col_count, place_count, -1)
    grad_expand = jnp.einsum(
        "rwm,rwkc->kmc", hidden_two, grad_third, preferred_element_type=jnp.float32
    )
    grad_hidden_two = jnp.einsum(
        "rwkc,kmc->rwm", grad_third, expand_low, preferred_element_type=jnp.float32
    )
    grad_second, sums_two = norm_backward(
        grad_hidden_two * silu_slope(normed_two),
        scaled_two,
        inverse_two,
        gain_values[middle : 2 * middle],
        valid_mask,
        valid_count,
        12,
    )
    (taps,) = spread_taps([grad_second.astype(jnp.bfloat16)], (trunk_rate,), layout, 13)
    taps = jnp.stack(taps)
    grad_hidden_one = jnp.einsum(
        "krwo,kco->rwc", taps, dilated_low, preferred_element_type=jnp.float32
    )
    grad_dilated = jnp.einsum(
        "rwc,krwo->kco", hidden_one, taps, preferred_element_type=jnp.float32
    )
    grad_first, sums_one = norm_backward(
        grad_hidden_one * silu_slope(normed_one),
        scaled_one,
        inverse_one,
        gain_values[:middle],
        valid_mask,
        valid_count,
        14,
    )
    grad_first = grad_first.astype(jnp.bfloat16)
    grad_reduce = jnp.einsum("rwc,rwm->cm", inputs, grad_first, preferred_element_type=jnp.float32)
    features_grad = (
        jnp.einsum("rwm,cm->rwc", grad_first, reduce_low, preferred_element_type=jnp.float32)
        + grad_pre
    )
    trunk_totals = reduce_all(
        (
            grad_reduce.astype(jnp.bfloat16).reshape(1, place_count, -1, middle),
            grad_dilated.astype(jnp.bfloat16).reshape(1, place_count, -1, middle),
            grad_expand.astype(jnp.bfloat16)[None],
        ),
        15,
    )
    totals = tuple(t[0].astype(jnp.float32) for t in trunk_totals) + (
        task_weight[:, None, None] * heads_total.astype(jnp.float32),
    )
    gain_grad = jnp.concatenate(
        [sums_one[1], sums_two[1], sums_three[1], (task_weight[:, None] * head_sums[1]).reshape(-1)]
    )
    bias_grad = jnp.concatenate(
        [sums_one[0], sums_two[0], sums_three[0], (task_weight[:, None] * head_sums[0]).reshape(-1)]
    )
    norm_grad = jnp.stack([gain_grad, bias_grad])
    w_reduce_new, m_reduce_new = update(w_reduce, m_reduce, totals[0])
    w_dilated_new, m_dilated_new = update(w_dilated, m_dilated, totals[1])
    w_expand_new, m_expand_new = update(w_expand, m_expand, totals[2])
    w_heads_new, m_heads_new = update(w_heads, m_heads, totals[3])
    norm_params_new, norm_moment_new = update(norm_params, norm_moment, norm_grad)
    return (
        features_grad[None],
        w_reduce_new,
        m_reduce_new,
        w_dilated_new,
        m_dilated_new,
        w_expand_new,
        m_expand_new,
        w_heads_new,
        m_heads_new,
        norm_params_new,
        norm_moment_new,
    )


def solution(mesh):
    placed = (
        P("dp", "fsdp", None, None),
        P(None, "dp", "fsdp", None, None),
        P(),
        P(),
        P("fsdp", None),
        P("fsdp", None),
        P(None, "fsdp"),
        P(None, "fsdp", None),
        P(),
        P("fsdp", None),
        P("fsdp", None),
        P(None, "fsdp"),
        P(None, "fsdp", None),
        P(),
    )
    return jax.shard_map(
        local,
        mesh=mesh,
        in_specs=placed,
        out_specs=(
            P("dp", "fsdp", None, None),
            P("fsdp", None),
            P("fsdp", None),
            P("fsdp", None),
            P("fsdp", None),
            P(None, "fsdp"),
            P(None, "fsdp"),
            P(None, "fsdp", None),
            P(None, "fsdp", None),
            P(),
            P(),
        ),
        check_vma=False,
    )
```

```python
import functools

import jax
import jax.numpy as jnp
from jax import lax
from jax.experimental import pallas as pl
from jax.experimental.pallas import tpu as pltpu
from jax.sharding import PartitionSpec as P

MESH = pl.DeviceIdType.MESH
norm_epsilon = 1e-05
task_epsilon = 1e-06
momentum_decay = 0.9
step_rate = 0.01
trunk_rate = 4
head_rates = (12, 24, 36)

class Tree:
    def __init__(self):
        self.core = lax.axis_index("dp")
        self.place = lax.axis_index("fsdp")
        self.count = lax.axis_size("fsdp")
        self.line = self.count // 4
        self.z = self.place // 4
        self.low = self.place % 4
        self.step_a = 1 + self.core
        self.step_b = 2 - self.core
        self.move_a = self.step_a * (1 - 2 * ((self.low // self.step_a) % 2))
        self.move_b = self.step_b * (1 - 2 * ((self.low // self.step_b) % 2))

    def at(self, place):
        return (self.core, place)

    @property
    def partner(self):
        return (1 - self.core, self.place)

    @property
    def a(self):
        return self.at(self.place + self.move_a)

    @property
    def b(self):
        return self.at(self.place + self.move_b)

    @property
    def down(self):
        return self.at(self.place - 4)

    @property
    def up(self):
        return self.at(self.place + 4)

    def greet(self):
        barrier = pltpu.get_barrier_semaphore()
        for peer in (self.partner, self.a, self.b):
            pl.semaphore_signal(barrier, inc=1, device_id=peer, device_id_type=MESH)

        @pl.when(self.z > 0)
        def _():
            pl.semaphore_signal(barrier, inc=1, device_id=self.down, device_id_type=MESH)

        @pl.when(self.z < self.line - 1)
        def _():
            pl.semaphore_signal(barrier, inc=1, device_id=self.up, device_id_type=MESH)

        pl.semaphore_wait(
            barrier,
            3
            + jnp.where(self.z > 0, 1, 0)
            + jnp.where(self.z < self.line - 1, 1, 0),
        )


def plane_sum_kernel(line, x_ref, o_ref, near, part, far, n_send, n_recv, f_send, f_recv):
    core = lax.axis_index("dp")
    place = lax.axis_index("fsdp")
    z, low = place // 4, place % 4
    me = low * 2 + core

    def beside(s):
        other = (me + s) % 8
        return (other % 2, z * 4 + other // 2)

    def away(s):
        return (core, ((z + s) % line) * 4 + low)

    barrier = pltpu.get_barrier_semaphore()
    for s in range(1, 8):
        pl.semaphore_signal(barrier, inc=1, device_id=beside(s), device_id_type=MESH)

    @pl.loop(1, line)
    def _(s):
        pl.semaphore_signal(barrier, inc=1, device_id=away(s), device_id_type=MESH)

    near[me] = x_ref[...]
    pl.semaphore_wait(barrier, 7 + line - 1)

    def to_beside(s):
        return pltpu.make_async_remote_copy(src_ref=x_ref, dst_ref=near.at[me], send_sem=n_send.at[s], recv_sem=n_recv, device_id=beside(s), device_id_type=MESH)

    def to_away(s):
        return pltpu.make_async_remote_copy(src_ref=part, dst_ref=far.at[z], send_sem=f_send.at[s], recv_sem=f_recv, device_id=away(s), device_id_type=MESH)

    for s in range(1, 8):
        to_beside(s).start()
    seven = near.at[pl.ds(0, 7)]
    pltpu.make_async_copy(seven, seven, n_recv).wait()
    total = jnp.sum(near[...], axis=0)
    part[...] = total
    pl.loop(1, line)(lambda s: to_away(s).start())
    far[z] = total
    rest = far.at[pl.ds(0, line - 1)]
    pltpu.make_async_copy(rest, rest, f_recv).wait()
    o_ref[...] = jnp.sum(far[...], axis=0)
    for s in range(1, 8):
        to_beside(s).wait_send()
    pl.loop(1, line)(lambda s: to_away(s).wait_send())


def all_sum(x, number):
    line = lax.axis_size("fsdp") // 4
    dma = pltpu.SemaphoreType.DMA
    return pl.pallas_call(
        functools.partial(plane_sum_kernel, line),
        out_shape=jax.ShapeDtypeStruct(x.shape, x.dtype),
        in_specs=[pl.BlockSpec(memory_space=pltpu.VMEM)],
        out_specs=pl.BlockSpec(memory_space=pltpu.VMEM),
        scratch_shapes=[
            pltpu.VMEM((8,) + x.shape, x.dtype), pltpu.VMEM(x.shape, x.dtype), pltpu.VMEM((line,) + x.shape, x.dtype),
            dma((8,)), dma, dma((line,)), dma,
        ],
        compiler_params=pltpu.CompilerParams(collective_id=number, has_side_effects=True),
    )(x)


def reduce_kernel(kinds, whole, *refs):
    count = len(kinds)
    parts, outs = refs[:count], refs[count : 2 * count]
    scratch = refs[2 * count :]
    accs, arx, zrx = (scratch[k * count : (k + 1) * count] for k in range(3))
    prx, brx = (scratch[3 * count + k * whole : 3 * count + (k + 1) * whole] for k in range(2))
    (
        load_sem, p_send, p_recv, b_send, b_recv, a_send, a_recv, z_send, z_recv, s_send, s_recv,
    ) = scratch[3 * count + 2 * whole :]
    t = Tree()
    t.greet()
    line, z, low = t.line, t.z, t.low

    def rows_of(k, core):
        rows = kinds[k][1] // 2
        return pl.ds(pl.multiple_of(core * rows, 16), rows)

    def remote(src, dst, send, recv, peer):
        return pltpu.make_async_remote_copy(src_ref=src, dst_ref=dst, send_sem=send, recv_sem=recv, device_id=peer, device_id_type=MESH)

    def load(k, block):
        return pltpu.make_async_copy(
            parts[k].at[:, block, rows_of(k, t.core)], accs[k].at[block], load_sem.at[k, block]
        )

    def load_late(k, at):
        return pltpu.make_async_copy(parts[k].at[at], accs[k].at[at], load_sem.at[k, at])

    def spot_of(k, zz, w):
        if k < whole:
            return zz * 4 + lows[w]
        return zz * 2 + (3 - w)

    def to_partner(k, block):
        return remote(parts[k].at[:, block, rows_of(k, 1 - t.core)], prx[k].at[block], p_send.at[k, block], p_recv.at[k, block], t.partner)

    upper = z >= line // 2
    own_spot = jnp.where(upper, z, line - 1 - z)

    def spot(j):
        q = j + jnp.where(j >= own_spot, 1, 0)
        other = jnp.where(upper, q, line - 1 - q)
        return jnp.where(j == line - 1, z, other)

    lows = (low + t.move_b, low + t.move_a + t.move_b, low + t.move_a, low)

    def to_b(k, zz, which):
        return remote(accs[k].at[zz * 4 + lows[which]], brx[k].at[zz * 2 + which], b_send.at[k, zz * 2 + which], b_recv.at[k, zz * 2 + which], t.b)

    def to_a(k, zz):
        return remote(accs[k].at[spot_of(k, zz, 2)], arx[k].at[zz], a_send.at[k, zz], a_recv.at[k, zz], t.a)

    def along(k, zz, up):
        w = 1 if up else 0
        return remote(accs[k].at[spot_of(k, zz, 3)], zrx[k].at[w, zz], z_send.at[k, w, zz], z_recv.at[k, w, zz], t.up if up else t.down)

    def add(k, block, ref):
        lead = kinds[k][0]

        @pl.loop(0, lead)
        def _(h):
            accs[k][block, h] = accs[k][block, h] + ref[h]

    def begin(j):
        zz = spot(j)
        for k in range(whole, count):
            load_late(k, zz * 2).start()
            load_late(k, zz * 2 + 1).start()
        for w in range(4):
            for k in range(whole):
                to_partner(k, zz * 4 + lows[w]).start()
                load(k, zz * 4 + lows[w]).start()

    first, last = range(whole), range(whole, count)

    def send_late(j):
        zz = spot(j)
        for k in last:
            load_late(k, zz * 2 + 1).wait()
            to_a(k, zz).start()

    def stage_b(j):
        zz = spot(j)
        for w in range(4):
            for k in first:
                block = zz * 4 + lows[w]
                load(k, block).wait()
                to_partner(k, block).wait_recv()
                add(k, block, prx[k].at[block])
                if w < 2:
                    to_b(k, zz, w).start()

    def stage_a(j):
        zz = spot(j)
        for w in (1, 0):
            for k in first:
                to_b(k, zz, w).wait_recv()
                add(k, zz * 4 + lows[3 if w == 0 else 2], brx[k].at[zz * 2 + w])
                if w == 1:
                    to_a(k, zz).start()

    def stage_z(j, ks):
        zz = spot(j)
        for k in ks:
            if k >= whole:
                load_late(k, zz * 2).wait()
            to_a(k, zz).wait_recv()
            here = spot_of(k, zz, 3)
            add(k, here, arx[k].at[zz])

            @pl.when(jnp.logical_and(zz >= z, z > 0))
            def _():
                along(k, zz, True).wait_recv()
                add(k, here, zrx[k].at[1, zz])

            @pl.when(jnp.logical_and(zz <= z, z < line - 1))
            def _():
                along(k, zz, False).wait_recv()
                add(k, here, zrx[k].at[0, zz])

            @pl.when(zz > z)
            def _():
                along(k, zz, True).start()

            @pl.when(zz < z)
            def _():
                along(k, zz, False).start()

    pl.loop(0, line)(begin)
    pl.loop(0, line)(send_late)
    pl.loop(0, line)(stage_b)

    @pl.loop(0, line + 1)
    def _(j):
        pl.when(j < line)(lambda: stage_z(j, last))
        pl.when(j >= 1)(lambda: stage_a(j - 1))

    pl.loop(0, line)(lambda j: stage_z(j, first))

    def half(k, core):
        if k < whole:
            return outs[k].at[:, rows_of(k, core)]
        cols = kinds[k][2]
        return outs[k].at[:, :, pl.ds(pl.multiple_of(core * cols, cols), cols)]

    def share(k):
        return remote(accs[k].at[spot_of(k, z, 3)], half(k, t.core), s_send.at[k], s_recv.at[k], t.partner)

    def keep(k):
        return pltpu.make_async_copy(accs[k].at[spot_of(k, z, 3)], half(k, t.core), load_sem.at[k, 0])

    for k in range(count):
        share(k).start()
        keep(k).start()

    @pl.loop(0, line)
    def _(j):
        zz = spot(j)
        for k in range(count):
            if k < whole:
                for w in range(4):
                    to_partner(k, zz * 4 + lows[w]).wait_send()
                to_b(k, zz, 0).wait_send()
                to_b(k, zz, 1).wait_send()
            to_a(k, zz).wait_send()
            pl.when(zz > z)(lambda: along(k, zz, True).wait_send())
            pl.when(zz < z)(lambda: along(k, zz, False).wait_send())

    for k in range(count):
        keep(k).wait()
        other = half(k, 1 - t.core)
        remote(other, other, s_send.at[k], s_recv.at[k], t.partner).wait_recv()
        share(k).wait_send()


def reduce_shards(parts, late, number):
    n = lax.axis_size("fsdp")
    line = n // 4
    whole = len(parts)
    kinds = [(p.shape[0], p.shape[2], p.shape[3]) for p in parts] + [p.shape[1:] for p in late]
    sizes = [(l, r // 2, c) for l, r, c in kinds[:whole]] + kinds[whole:]
    results = kinds[:whole] + [(l, r, 2 * c) for l, r, c in kinds[whole:]]
    bf = jnp.bfloat16
    count = len(kinds)
    dma = pltpu.SemaphoreType.DMA

    def room(some, *lead):
        return [pltpu.VMEM(tuple(lead) + tuple(s), bf) for s in some]

    accs = [
        pltpu.VMEM((n if k < whole else 2 * line,) + tuple(s), bf) for k, s in enumerate(sizes)
    ]
    return pl.pallas_call(
        functools.partial(reduce_kernel, kinds, whole),
        out_shape=tuple(jax.ShapeDtypeStruct(r, bf) for r in results),
        in_specs=[pl.BlockSpec(memory_space=pl.ANY)] * count,
        out_specs=tuple([pl.BlockSpec(memory_space=pl.ANY)] * count),
        scratch_shapes=accs
        + room(sizes, line)
        + room(sizes, 2, line)
        + room(sizes[:whole], n)
        + room(sizes[:whole], 2 * line)
        + [
            dma((count, n)),
            dma((count, n)),
            dma((count, n)),
            dma((count, 2 * line)),
            dma((count, 2 * line)),
            dma((count, line)),
            dma((count, line)),
            dma((count, 2, line)),
            dma((count, 2, line)),
            dma((count,)),
            dma((count,)),
        ],
        compiler_params=pltpu.CompilerParams(
            collective_id=number, has_side_effects=True, vmem_limit_bytes=60 * 2**20
        ),
    )(*parts, *late)


def exchange_kernel(offsets, rows, count, x_ref, o_ref, send, recv):
    core = lax.axis_index("dp")
    place = lax.axis_index("fsdp")
    pieces = []
    for k, offset in enumerate(offsets):
        first, cut = offset // rows, offset % rows
        for part, (gap, low, high, to) in enumerate(
            ((first, cut, rows, 0), (first + 1, 0, cut, rows - cut))
        ):
            if high > low:
                pieces.append((k, part, gap, low, high - low, to))
    gaps = sorted({abs(p[2]) for p in pieces} - {0})
    gaps = [-g for g in gaps] + gaps
    barrier = pltpu.get_barrier_semaphore()

    def present(gap):
        return jnp.logical_and(place + gap >= 0, place + gap < count)

    met = jnp.int32(0)
    for gap in gaps:
        met = met + jnp.where(present(gap), 1, 0)

        @pl.when(present(gap))
        def _():
            pl.semaphore_signal(
                barrier, inc=1, device_id=(core, place + gap), device_id_type=MESH
            )

    pl.semaphore_wait(barrier, met)

    def piece(k, part, gap, low, size, to):
        return pltpu.make_async_remote_copy(
            src_ref=x_ref.at[k, pl.ds(low, size)],
            dst_ref=o_ref.at[k, pl.ds(to, size)],
            send_sem=send.at[k, part],
            recv_sem=recv.at[k, part],
            device_id=(core, place - gap),
            device_id_type=MESH,
        )

    for p in pieces:
        k, part, gap, low, size, to = p
        if gap == 0:
            o_ref[k, to : to + size] = x_ref[k, low : low + size]
        else:
            pl.when(present(-gap))(lambda p=p: piece(*p).start())
    for p in pieces:
        if p[2]:
            pl.when(present(p[2]))(lambda p=p: piece(*p).wait_recv())
    for p in pieces:
        if p[2]:
            pl.when(present(-p[2]))(lambda p=p: piece(*p).wait_send())


def exchange(x, offsets, number):
    entries, rows = x.shape[:2]
    return pl.pallas_call(
        functools.partial(exchange_kernel, offsets, rows, lax.axis_size("fsdp")),
        out_shape=jax.ShapeDtypeStruct(x.shape, x.dtype),
        in_specs=[pl.BlockSpec(memory_space=pltpu.VMEM)],
        out_specs=pl.BlockSpec(memory_space=pltpu.VMEM),
        scratch_shapes=[
            pltpu.SemaphoreType.DMA((entries, 2)),
            pltpu.SemaphoreType.DMA((entries, 2)),
        ],
        compiler_params=pltpu.CompilerParams(
            collective_id=number, has_side_effects=True, vmem_limit_bytes=32 * 2**20
        ),
    )(x)


def plane_signal(line, core, z, low):
    barrier = pltpu.get_barrier_semaphore()
    me = low * 2 + core
    for s in range(1, 8):
        other = (me + s) % 8
        pl.semaphore_signal(
            barrier, inc=1, device_id=(other % 2, z * 4 + other // 2), device_id_type=MESH
        )

    @pl.loop(1, line)
    def _(s):
        pl.semaphore_signal(
            barrier, inc=1, device_id=(core, ((z + s) % line) * 4 + low), device_id_type=MESH
        )


def plane_scratch(line, shape):
    dma = pltpu.SemaphoreType.DMA
    return [
        pltpu.VMEM((8,) + shape, jnp.float32),
        pltpu.VMEM(shape, jnp.float32),
        pltpu.VMEM((line,) + shape, jnp.float32),
        dma((8,)),
        dma,
        dma((line,)),
        dma,
    ]


def plane_sum(line, fill, room, meanwhile=None, later=None):
    near, part, far, n_send, n_recv, f_send, f_recv = room
    core = lax.axis_index("dp")
    place = lax.axis_index("fsdp")
    z, low = place // 4, place % 4
    me = low * 2 + core

    def to_beside(s):
        other = (me + s) % 8
        return pltpu.make_async_remote_copy(
            src_ref=near.at[me],
            dst_ref=near.at[me],
            send_sem=n_send.at[s],
            recv_sem=n_recv,
            device_id=(other % 2, z * 4 + other // 2),
            device_id_type=MESH,
        )

    def to_away(s):
        return pltpu.make_async_remote_copy(
            src_ref=part,
            dst_ref=far.at[z],
            send_sem=f_send.at[s],
            recv_sem=f_recv,
            device_id=(core, ((z + s) % line) * 4 + low),
            device_id_type=MESH,
        )

    fill(near.at[me])
    for s in range(1, 8):
        to_beside(s).start()
    if meanwhile is not None:
        meanwhile()
    seven = near.at[pl.ds(0, 7)]
    pltpu.make_async_copy(seven, seven, n_recv).wait()
    total = jnp.sum(near[...], axis=0)
    part[...] = total
    pl.loop(1, line)(lambda s: to_away(s).start())
    far[z] = total
    if later is not None:
        later()
    rest = far.at[pl.ds(0, line - 1)]
    pltpu.make_async_copy(rest, rest, f_recv).wait()
    result = jnp.sum(far[...], axis=0)
    for s in range(1, 8):
        to_beside(s).wait_send()
    pl.loop(1, line)(lambda s: to_away(s).wait_send())
    return result


def row_pieces(offset, rows):
    first, cut = offset // rows, offset % rows
    pieces = [(first, cut, rows - cut, 0)]
    if cut:
        pieces.append((first + 1, 0, cut, rows - cut))
    return pieces


def row_gaps(offsets, rows):
    gaps = {abs(p[0]) for o in offsets for p in row_pieces(o, rows)} - {0}
    return sorted(-g for g in gaps) + sorted(gaps)


def greet_rows(gaps, count):
    barrier = pltpu.get_barrier_semaphore()
    core = lax.axis_index("dp")
    place = lax.axis_index("fsdp")
    met = jnp.int32(0)
    for gap in gaps:
        here = jnp.logical_and(place + gap >= 0, place + gap < count)
        met = met + jnp.where(here, 1, 0)

        @pl.when(here)
        def _():
            pl.semaphore_signal(
                barrier, inc=1, device_id=(core, place + gap), device_id_type=MESH
            )

    return met


class Rows:
    def __init__(self, offsets, rows, cols, count, x_ref, o_ref, send, recv):
        self.core = lax.axis_index("dp")
        self.place = lax.axis_index("fsdp")
        self.rows, self.cols, self.count = rows, cols, count
        self.offsets, self.x_ref, self.o_ref = offsets, x_ref, o_ref
        self.send, self.recv = send, recv

    def present(self, gap):
        return jnp.logical_and(self.place + gap >= 0, self.place + gap < self.count)

    def copies(self, k):
        for part, (gap, low, size, to) in enumerate(row_pieces(self.offsets[k], self.rows)):
            yield gap, low, size, to, pltpu.make_async_remote_copy(
                src_ref=self.x_ref.at[k, pl.ds(low * self.cols, size * self.cols)],
                dst_ref=self.o_ref.at[k, pl.ds(to * self.cols, size * self.cols)],
                send_sem=self.send.at[k, part],
                recv_sem=self.recv.at[k, part],
                device_id=(self.core, self.place - gap),
                device_id_type=MESH,
            )

    def start(self, k):
        for gap, low, size, to, copy in self.copies(k):
            if gap == 0:
                cols = self.cols
                self.o_ref[k, to * cols : (to + size) * cols] = self.x_ref[
                    k, low * cols : (low + size) * cols
                ]
            else:
                pl.when(self.present(-gap))(copy.start)

    def wait_recv(self, k):
        for gap, _, _, _, copy in self.copies(k):
            if gap:
                pl.when(self.present(gap))(copy.wait_recv)

    def wait_send(self, k):
        for gap, _, _, _, copy in self.copies(k):
            if gap:
                pl.when(self.present(-gap))(copy.wait_send)


def heads_kernel(
    rates, rows, cols, count,
    x_ref, xt_ref, wa_ref, wb_ref, cot_ref, par_ref, mask_ref,
    g_ref, own_ref, got_ref, sums_ref, sq_ref,
    wv, out_rows, in_rows, resp, dn, taps, g_room, dw_room,
    w_sem, f_send, f_recv, e_send, e_recv, g_sem, dw_sem, hand_sem, got_sem, *rooms,
):
    px = rows * cols
    heads = len(rates)
    width = par_ref.shape[1]
    line = count // 4
    core = lax.axis_index("dp")
    place = lax.axis_index("fsdp")
    z, low = place // 4, place % 4
    one, two, three = rooms[:7], rooms[7:14], rooms[14:]

    def w_copy(t, k):
        early = wa_ref.shape[0] // 9
        src = wa_ref.at[t * 9 + k] if t < early else wb_ref.at[(t - early) * 9 + k]
        return pltpu.make_async_copy(
            src, wv.at[t, :, k * width : (k + 1) * width], w_sem.at[t * 9 + k]
        )

    for t in reversed(range(heads)):
        for k in range(9):
            w_copy(t, k).start()
    fwd = Rows([o for r in rates for o in (-r, r)], rows, cols, count, out_rows, in_rows, f_send, f_recv)
    bwd = Rows([o for r in rates for o in (r, -r)], rows, cols, count, out_rows, in_rows, e_send, e_recv)
    plane_signal(line, core, z, low)
    met = greet_rows(row_gaps(fwd.offsets, rows), count)
    barrier = pltpu.get_barrier_semaphore()

    def mask(t, k):
        return mask_ref[t, :, k : k + 1]

    @pl.loop(0, heads)
    def _(step):
        t = heads - 1 - step
        rate = 12 * (t + 1)
        for j in range(3):
            summed = None
            for c in range(3):
                k = 3 * j + c
                pltpu.make_async_copy(
                    wa_ref.at[k], wv.at[t, :, k * width : (k + 1) * width], w_sem.at[t * 9 + k]
                ).wait()
                prod = jnp.dot(
                    x_ref[...], wv[t, :, k * width : (k + 1) * width], preferred_element_type=jnp.float32
                )
                if c == 0:
                    summed = jnp.where(mask(t, 1) > 0, pltpu.roll(prod, rate, 0), 0.0)
                elif c == 1:
                    summed = summed + jnp.where(mask(t, 0) > 0, prod, 0.0)
                else:
                    summed = summed + jnp.where(mask(t, 2) > 0, pltpu.roll(prod, px - rate, 0), 0.0)
            if j == 1:
                resp[t] = summed
            else:
                out_rows[t * 2 + j // 2] = summed.astype(jnp.bfloat16)

        @pl.when(step == 0)
        def _():
            pl.semaphore_wait(barrier, 7 + line - 1 + met)

        for h in range(heads):
            @pl.when(t == h)
            def _():
                fwd.start(2 * h)
                fwd.start(2 * h + 1)

    def stats(ref):
        for h in range(heads):
            total = resp[h]
            for j in (0, 1):
                fwd.wait_recv(2 * h + j)
                total = total + jnp.where(
                    mask(h, 3 + j) > 0, in_rows[2 * h + j].astype(jnp.float32), 0.0
                )
            resp[h] = total
            kept = total * mask(h, 0)
            ref[2 * h : 2 * h + 1] = jnp.sum(kept, axis=0, keepdims=True)
            ref[2 * h + 1 : 2 * h + 2] = jnp.sum(kept * total, axis=0, keepdims=True)

    sums = plane_sum(line, stats, one)
    pixels = par_ref[2 * heads : 2 * heads + 1]
    inverses = []

    def grads(ref):
        for h in range(heads):
            mean = sums[2 * h : 2 * h + 1] / pixels
            var = sums[2 * h + 1 : 2 * h + 2] / pixels - mean * mean
            inverse = lax.rsqrt(var + norm_epsilon)
            inverses.append(inverse)
            scaled = (resp[h] - mean) * inverse
            normed = scaled * par_ref[2 * h : 2 * h + 1] + par_ref[2 * h + 1 : 2 * h + 2]
            s = jax.nn.sigmoid(normed)
            d = cot_ref[h].astype(jnp.float32) * (s * (1.0 + normed * (1.0 - s))) * mask(h, 0)
            resp[h] = scaled
            dn[h] = d
            ref[2 * h : 2 * h + 1] = jnp.sum(d, axis=0, keepdims=True)
            ref[2 * h + 1 : 2 * h + 2] = jnp.sum(d * scaled, axis=0, keepdims=True)

    back = plane_sum(line, grads, two)
    sums_ref[...] = back
    for h in range(heads):
        fwd.wait_send(2 * h)
        fwd.wait_send(2 * h + 1)
        e = (
            mask(h, 0)
            * (inverses[h] * par_ref[2 * h : 2 * h + 1])
            * (dn[h] - back[2 * h : 2 * h + 1] / pixels - resp[h] * (back[2 * h + 1 : 2 * h + 2] / pixels))
        )
        dn[h] = e
        out_rows[2 * h] = jnp.where(mask(h, 3) > 0, e, 0.0).astype(jnp.bfloat16)
        out_rows[2 * h + 1] = jnp.where(mask(h, 4) > 0, e, 0.0).astype(jnp.bfloat16)
        bwd.start(2 * h)
        bwd.start(2 * h + 1)

    def g_copy(t):
        return pltpu.make_async_copy(g_room, g_ref.at[t], g_sem)

    half = width // 2

    def lanes(owner):
        return pl.ds(pl.multiple_of(owner * half, half), half)

    def keep(slot, at):
        return pltpu.make_async_copy(
            dw_room.at[slot, :, lanes(core)], own_ref.at[at], dw_sem.at[slot]
        )

    def hand(slot, at):
        return pltpu.make_async_remote_copy(
            src_ref=dw_room.at[slot, :, lanes(1 - core)],
            dst_ref=got_ref.at[at],
            send_sem=hand_sem.at[slot],
            recv_sem=got_sem,
            device_id=(1 - core, place),
            device_id_type=MESH,
        )

    def dw_wait(slot):
        keep(slot, 0).wait()
        hand(slot, 0).wait_send()

    def weigh(t, k, number):
        slot = lax.rem(number, 2)
        pl.when(number >= 2)(lambda: dw_wait(slot))
        dw_room[slot] = jnp.dot(
            xt_ref[...],
            taps[:, pl.ds(pl.multiple_of(k * width, width), width)],
            preferred_element_type=jnp.float32,
        ).astype(jnp.bfloat16)
        keep(slot, t * 9 + k).start()
        hand(slot, t * 9 + k).start()

    def spread(t, j, arrived):
        rate = 12 * (t + 1)
        for c in range(3):
            if c == 0:
                tap = pltpu.roll(jnp.where(mask(t, 1) > 0, arrived, 0.0), px - rate, 0)
            elif c == 1:
                tap = jnp.where(mask(t, 0) > 0, arrived, 0.0)
            else:
                tap = pltpu.roll(jnp.where(mask(t, 2) > 0, arrived, 0.0), rate, 0)
            k = 3 * j + c
            taps[:, k * width : (k + 1) * width] = tap.astype(jnp.bfloat16)

    tiles = wv.shape[1] // width
    sq_ref[...] = jnp.zeros_like(sq_ref)

    def center(t):
        spread(t, 1, dn[t].astype(jnp.bfloat16).astype(jnp.float32))

    @pl.loop(0, heads)
    def _(t):
        center(t)
        pl.loop(0, 3)(lambda k: weigh(t, 3 + k, t * 3 + k))

    @pl.loop(0, heads)
    def _(t):
        center(t)
        for h in range(heads):
            @pl.when(t == h)
            def _():
                bwd.wait_recv(2 * h)
                bwd.wait_recv(2 * h + 1)

        spread(t, 0, jnp.where(mask(t, 5) > 0, in_rows[2 * t].astype(jnp.float32), 0.0))
        spread(t, 2, jnp.where(mask(t, 6) > 0, in_rows[2 * t + 1].astype(jnp.float32), 0.0))

        pl.loop(0, 6)(
            lambda k: weigh(t, k + jnp.where(k >= 3, 3, 0), 3 * heads + t * 6 + k)
        )
        pl.when(t > 0)(lambda: g_copy(t - 1).wait())
        def tile(n, square):
            cut = pl.ds(pl.multiple_of(n * width, width), width)
            g = lax.dot_general(
                taps[...], wv[t, cut, :], (((1,), (1,)), ((), ())), preferred_element_type=jnp.float32
            )
            g_room[:, cut] = g
            return square + jnp.sum(g * g, axis=0, keepdims=True)

        square = lax.fori_loop(0, tiles, tile, jnp.zeros((1, width), jnp.float32))
        sq_ref[pl.ds(t, 1)] = square
        g_copy(t).start()

    g_copy(heads - 1).wait()
    dw_wait(0)
    dw_wait(1)
    pltpu.make_async_copy(got_ref, got_ref, got_sem).wait()

    def fill(ref):
        ref[...] = sq_ref[...]

    sq_ref[...] = plane_sum(line, fill, three)
    for k in range(2 * heads):
        bwd.wait_send(k)


def heads_step(trunk_out, early, late, cotangent, params, masks, rates, rows, cols, number):
    px, channels = trunk_out.shape
    heads, width = len(rates), early.shape[-1]
    count = lax.axis_size("fsdp")
    line = count // 4
    bf, f32 = jnp.bfloat16, jnp.float32
    dma = pltpu.SemaphoreType.DMA
    vmem = pl.BlockSpec(memory_space=pltpu.VMEM)
    hbm = pl.BlockSpec(memory_space=pl.ANY)
    return pl.pallas_call(
        functools.partial(heads_kernel, rates, rows, cols, count),
        out_shape=(
            jax.ShapeDtypeStruct((heads, px, channels), f32),
            jax.ShapeDtypeStruct((9 * heads, channels, width // 2), bf),
            jax.ShapeDtypeStruct((9 * heads, channels, width // 2), bf),
            jax.ShapeDtypeStruct((2 * heads, width), f32),
            jax.ShapeDtypeStruct((8, width), f32),
        ),
        in_specs=[vmem, vmem, hbm, hbm, vmem, vmem, vmem],
        out_specs=(hbm, hbm, hbm, vmem, vmem),
        scratch_shapes=[
            pltpu.VMEM((heads, channels, 9 * width), bf),
            pltpu.VMEM((2 * heads, px, width), bf),
            pltpu.VMEM((2 * heads, px, width), bf),
            pltpu.VMEM((heads, px, width), f32),
            pltpu.VMEM((heads, px, width), f32),
            pltpu.VMEM((px, 9 * width), bf),
            pltpu.VMEM((px, channels), f32),
            pltpu.VMEM((2, channels, width), bf),
            dma((9 * heads,)),
            dma((2 * heads, 2)),
            dma((2 * heads, 2)),
            dma((2 * heads, 2)),
            dma((2 * heads, 2)),
            dma,
            dma((2,)),
            dma((2,)),
            dma,
        ]
        + plane_scratch(line, (2 * heads, width))
        + plane_scratch(line, (2 * heads, width))
        + plane_scratch(line, (8, width)),
        compiler_params=pltpu.CompilerParams(
            collective_id=number, has_side_effects=True, vmem_limit_bytes=62 * 2**20
        ),
    )(trunk_out, trunk_out.T, early, late, cotangent, params, masks)


class Fan:
    def __init__(self, t, arrays, sends, arrives, shares, own_sem):
        self.t, self.arrays = t, arrays
        self.sends, self.arrives, self.shares, self.own_sem = sends, arrives, shares, own_sem

    def copy(self, k, kind, block, peer, own=False):
        src, place = self.arrays[k]
        dst = place(block, self.t.core)
        return pltpu.make_async_remote_copy(
            src_ref=src if own else dst,
            dst_ref=dst,
            send_sem=self.sends.at[k, kind, block],
            recv_sem=(self.shares if kind == 4 else self.arrives).at[k, block],
            device_id=peer,
            device_id_type=MESH,
        )

    def fan(self, k, block, own, down, up, a, b, finish):
        t = self.t

        def act(kind, peer):
            c = self.copy(k, kind, block, peer, own)
            c.wait_send() if finish else c.start()

        if down:
            pl.when(t.z > 0)(lambda: act(0, t.down))
        if up:
            pl.when(t.z < t.line - 1)(lambda: act(1, t.up))
        if a:
            act(2, t.a)
        if b:
            act(3, t.b)
        act(4, t.partner)

    def stay(self, k):
        src, place = self.arrays[k]
        return pltpu.make_async_copy(src, place(self.t.place, self.t.core), self.own_sem.at[k])

    def own(self, ks, finish=False):
        for k in ks:
            if not finish:
                self.stay(k).start()
            self.fan(k, self.t.place, True, True, True, True, True, finish)

    def step(self, ks, s, move, down, up, a, b, finish):
        t = self.t
        for k in ks:
            def one(block, down, up):
                if not finish:
                    self.copy(k, 0, block, t.partner).wait_recv()
                self.fan(k, block, False, down, up, a, b, finish)

            pl.when(t.z - s >= 0)(lambda: one(t.place - 4 * s + move, down, False))
            if s:
                pl.when(t.z + s < t.line)(lambda: one(t.place + 4 * s + move, False, up))

    def steps(self, ks, finish=False):
        t = self.t
        result = []
        for s in range(1, t.line):
            result.append(lambda s=s: self.along(ks, s, finish))
            result.append(lambda s=s: self.step(ks, s - 1, t.move_a, False, False, False, True, finish))
        result.append(lambda: self.step(ks, t.line - 1, t.move_a, False, False, False, True, finish))
        tail = []
        for s in range(t.line):
            tail.append(lambda s=s: self.step(ks, s, t.move_b, False, False, False, False, finish))
            tail.append(
                lambda s=s: self.step(ks, s, t.move_a + t.move_b, False, False, False, False, finish)
            )
        return result, tail

    def along(self, ks, s, finish):
        t = self.t
        for k in ks:
            def one(block, down, up):
                if not finish:
                    self.copy(k, 0, block, t.partner).wait_recv()
                self.fan(k, block, False, down, up, True, True, finish)

            pl.when(t.z - s >= 0)(lambda: one(t.place - 4 * s, False, True))
            pl.when(t.z + s < t.line)(lambda: one(t.place + 4 * s, True, False))

    def wait_shares(self, ks):
        t = self.t
        for k in ks:
            self.stay(k).wait()

        @pl.loop(0, t.count)
        def _(block):
            for k in ks:
                other = self.arrays[k][1](block, 1 - t.core)
                pltpu.make_async_remote_copy(
                    src_ref=other,
                    dst_ref=other,
                    send_sem=self.sends.at[k, 4, block],
                    recv_sem=self.shares.at[k, block],
                    device_id=t.partner,
                    device_id_type=MESH,
                ).wait_recv()

    def finish(self, ks):
        self.own(ks, True)
        first, tail = self.steps(ks, True)
        for f in first + tail:
            f()


def silu(v):
    return v * jax.nn.sigmoid(v)


def scale_rows(sums, pixels):
    mean = sums[0:1] / pixels
    var = sums[1:2] / pixels - mean * mean
    return mean, lax.rsqrt(var + norm_epsilon)


def trunk_kernel(
    rate, rows, cols, count,
    x_ref, wr_s, wd_s, we_s, wh_s, par_ref, par3_ref, mask_ref,
    wr_o, wd_o, we_o, wh_o, out_ref, sc1_ref, sc2_ref, sc3_ref, s1_ref, s2_ref, s3_ref,
    wr_v, wd_v, we_v, ext, taps,
    sends, arrives, shares, own_sem, save_sem, h_send, h_recv, *rooms,
):
    px = rows * cols
    line = count // 4
    middle = par_ref.shape[1]
    channels = out_ref.shape[1]
    t = Tree()
    one, two, three = rooms[:7], rooms[7:14], rooms[14:]
    halo = rate * cols

    def cut(start, size, step=8):
        return pl.ds(pl.multiple_of(start, step), size)

    def rows_array(shard, full):
        size = shard.shape[0]
        return (
            shard.at[cut(t.core * (size // 2), size // 2, 16)],
            lambda block, core: full.at[cut(block * size + core * (size // 2), size // 2, 16)],
        )

    half_e = we_s.shape[0] // 2
    half_h = wh_s.shape[1] // 2
    fan = Fan(
        t,
        [
            rows_array(wr_s, wr_v),
            rows_array(wd_s, wd_v),
            (
                we_s.at[cut(t.core * half_e, half_e, 16)],
                lambda block, core: we_v.at[
                    cut(core * half_e, half_e, 16), cut(block * we_s.shape[1], we_s.shape[1], 128)
                ],
            ),
            (
                wh_s.at[:, cut(t.core * half_h, half_h, 16)],
                lambda block, core: wh_o.at[:, block, cut(core * half_h, half_h, 16)],
            ),
        ],
        sends, arrives, shares, own_sem,
    )
    plane_signal(line, t.core, t.z, t.low)
    met = greet_rows((-1, 1), count)
    pl.semaphore_wait(pltpu.get_barrier_semaphore(), 7 + line - 1 + met)
    small, heads = (0, 1, 2), (3,)
    fan.own(small)
    first_steps, first_tail = fan.steps(small)
    for f in first_steps:
        f()
    fan.own(heads)
    for f in first_tail:
        f()
    head_steps, head_tail = fan.steps(heads)
    queue = head_steps + head_tail

    def forward(number):
        for _ in range(number):
            if queue:
                queue.pop(0)()

    pixels = par_ref[4:5]

    def mask(k):
        return mask_ref[:, k : k + 1]

    def moments_of(v, ref, at):
        kept = v * mask(0)
        ref[at : at + 1] = jnp.sum(kept, axis=0, keepdims=True)
        ref[at + 1 : at + 2] = jnp.sum(kept * v, axis=0, keepdims=True)

    fan.wait_shares((0,))
    sc1_ref[...] = jnp.dot(x_ref[...], wr_v[...], preferred_element_type=jnp.float32)
    forward(1)
    s1_ref[...] = plane_sum(line, lambda ref: moments_of(sc1_ref[...], ref, 0), one)
    mean, inverse = scale_rows(s1_ref, pixels)
    scaled = (sc1_ref[...] - mean) * inverse
    sc1_ref[...] = scaled
    ext[halo : halo + px] = silu(scaled * par_ref[0:1] + par_ref[1:2]).astype(jnp.bfloat16)

    def edge(up):
        src = ext.at[pl.ds(halo if not up else halo + px - halo, halo)]
        dst = ext.at[pl.ds(halo + px if not up else 0, halo)]
        return pltpu.make_async_remote_copy(
            src_ref=src,
            dst_ref=dst,
            send_sem=h_send.at[int(up)],
            recv_sem=h_recv.at[int(up)],
            device_id=t.at(t.place + (1 if up else -1)),
            device_id_type=MESH,
        )

    has_next, has_last = t.place < count - 1, t.place > 0
    pl.when(has_last)(lambda: edge(False).start())
    pl.when(has_next)(lambda: edge(True).start())
    fan.wait_shares((1, 2))
    forward(2)
    saves = [
        pltpu.make_async_copy(wr_v, wr_o, save_sem.at[0]),
        pltpu.make_async_copy(wd_v, wd_o, save_sem.at[1]),
        pltpu.make_async_copy(we_v, we_o, save_sem.at[2]),
    ]
    for save in saves:
        save.start()
    pl.when(has_next)(lambda: edge(False).wait_recv())
    pl.when(has_last)(lambda: edge(True).wait_recv())
    for j in range(3):
        v = ext[j * halo : j * halo + px].astype(jnp.float32)
        kept_row = 1.0 if j == 1 else mask(3 + j // 2)
        for c in range(3):
            moved = v if c == 1 else pltpu.roll(v, rate if c == 0 else px - rate, 0)
            kept = mask((1, 0, 2)[c]) * kept_row
            k = 3 * j + c
            taps[:, k * middle : (k + 1) * middle] = jnp.where(kept > 0, moved, 0.0).astype(jnp.bfloat16)
    sc2_ref[...] = jnp.dot(taps[...], wd_v[...], preferred_element_type=jnp.float32)
    forward(2)
    s2_ref[...] = plane_sum(line, lambda ref: moments_of(sc2_ref[...], ref, 0), two)
    mean, inverse = scale_rows(s2_ref, pixels)
    scaled = (sc2_ref[...] - mean) * inverse
    sc2_ref[...] = scaled
    hidden = silu(scaled * par_ref[2:3] + par_ref[3:4]).astype(jnp.bfloat16)
    forward(2)
    parts = channels // middle

    def wide(ref):
        for q in range(parts):
            third = jnp.dot(
                hidden, we_v[:, q * middle : (q + 1) * middle], preferred_element_type=jnp.float32
            )
            sc3_ref[:, q * middle : (q + 1) * middle] = third
            moments_of(third, ref, 2 * q)

    s3_ref[...] = plane_sum(line, wide, three)
    forward(1)
    for q in range(parts):
        at = slice(q * middle, (q + 1) * middle)
        mean, inverse = scale_rows(s3_ref[2 * q : 2 * q + 2], pixels)
        scaled = (sc3_ref[:, at] - mean) * inverse
        sc3_ref[:, at] = scaled
        pre = x_ref[:, at].astype(jnp.float32) + (
            scaled * par3_ref[2 * q : 2 * q + 1] + par3_ref[2 * q + 1 : 2 * q + 2]
        )
        out_ref[:, at] = silu(pre).astype(jnp.bfloat16)
    forward(len(queue))
    fan.wait_shares(heads)
    for save in saves:
        save.wait()
    pl.when(has_last)(lambda: edge(False).wait_send())
    pl.when(has_next)(lambda: edge(True).wait_send())
    fan.finish(small + heads)


def trunk_step(x, shards, params, params3, masks, rate, rows, cols, number):
    px, channels = x.shape
    count = lax.axis_size("fsdp")
    line = count // 4
    middle = params.shape[1]
    bf, f32 = jnp.bfloat16, jnp.float32
    dma = pltpu.SemaphoreType.DMA
    vmem = pl.BlockSpec(memory_space=pltpu.VMEM)
    hbm = pl.BlockSpec(memory_space=pl.ANY)
    parts = channels // middle
    heads, head_rows, width = shards[3].shape
    S = jax.ShapeDtypeStruct
    return pl.pallas_call(
        functools.partial(trunk_kernel, rate, rows, cols, count),
        out_shape=(
            S((channels, middle), bf),
            S((9 * middle, middle), bf),
            S((middle, channels), bf),
            S((heads, count, head_rows, width), bf),
            S((px, channels), bf),
            S((px, middle), f32),
            S((px, middle), f32),
            S((px, channels), f32),
            S((2, middle), f32),
            S((2, middle), f32),
            S((2 * parts, middle), f32),
        ),
        in_specs=[vmem] + [hbm] * 4 + [vmem] * 3,
        out_specs=(hbm,) * 4 + (vmem,) * 7,
        scratch_shapes=[
            pltpu.VMEM((channels, middle), bf),
            pltpu.VMEM((9 * middle, middle), bf),
            pltpu.VMEM((middle, channels), bf),
            pltpu.VMEM((px + 2 * rate * cols, middle), bf),
            pltpu.VMEM((px, 9 * middle), bf),
            dma((4, 5, count)),
            dma((4, count)),
            dma((4, count)),
            dma((4,)),
            dma((3,)),
            dma((2,)),
            dma((2,)),
        ]
        + plane_scratch(line, (2, middle))
        + plane_scratch(line, (2, middle))
        + plane_scratch(line, (2 * parts, middle)),
        compiler_params=pltpu.CompilerParams(
            collective_id=number, has_side_effects=True, vmem_limit_bytes=56 * 2**20
        ),
    )(x, *shards, params, params3, masks)


FEED = {'join': 2, 'pass': 1, 'keep': 1, 'third': 1, 'd2': 2, 'ge': 2, 'edge': 3, 'd1': 1, 'gd': 1, 'later3': 4, 'later2': 4, 'later1': 8}


def nt(a, b):
    return lax.dot_general(a, b, (((1,), (1,)), ((), ())), preferred_element_type=jnp.float32)


def tn(a, b):
    return lax.dot_general(a, b, (((0,), (0,)), ((), ())), preferred_element_type=jnp.float32)


def slope(v):
    s = jax.nn.sigmoid(v)
    return s * (1.0 + v * (1.0 - s))


def back_kernel(
    rate, rows, cols, count, heads,
    x_ref, tw_ref, sc1_ref, sc2_ref, par_ref, par3_ref, s1_ref, s2_ref, s3_ref, mask_ref,
    g_ref, sc3_ref, wr_ref, wd_ref, we_ref, own_ref, got_ref,
    bs1_ref, bs2_ref, bs3_ref, fg_ref, gr_ref, gd_ref, ge_ref, sum_ref,
    b_send, acc, b_room, extra, g_room, s_room, dpre, dthird, wr_v, wd_v, we_v, ext, taps, out_room, grad_room,
    load_sem, extra_sem, bs_sem, br_sem, g_sem, s_sem, w_sem, h_send, h_recv, out_sem, grad_sem, sum_sem, *rooms,
):
    px = rows * cols
    line = count // 4
    middle = par_ref.shape[1]
    channels = x_ref.shape[1]
    parts = channels // middle
    wide = g_room.shape[-1]
    chunks = channels // wide
    halo = rate * cols
    t = Tree()
    one, two, three = rooms[:7], rooms[7:14], rooms[14:]
    bf, f32 = jnp.bfloat16, jnp.float32

    weights = [
        pltpu.make_async_copy(we_ref, we_v, w_sem.at[0]),
        pltpu.make_async_copy(wd_ref, wd_v, w_sem.at[1]),
        pltpu.make_async_copy(wr_ref, wr_v, w_sem.at[2]),
    ]

    def lanes(c):
        return pl.ds(c * wide, wide)

    def g_load(c):
        return pltpu.make_async_copy(g_ref.at[:, :, lanes(c)], g_room.at[c % 2], g_sem.at[c % 2])

    def s_load(c):
        return pltpu.make_async_copy(sc3_ref.at[:, lanes(c)], s_room.at[c % 2], s_sem.at[c % 2])

    moves = (t.move_b, t.move_a + t.move_b, 0, t.move_a)

    def pair(n, w):
        block = n * 4 + t.low + moves[w]
        room = (b_send if w < 2 else acc).at[n * 2 + w % 2]
        slot = w % 2
        return (
            pltpu.make_async_copy(own_ref.at[:, block], room, load_sem.at[slot]),
            pltpu.make_async_copy(got_ref.at[:, block], extra.at[slot], extra_sem.at[slot]),
        )

    def join(n, w):
        for c in pair(n, w):
            c.wait()
        room = b_send if w < 2 else acc
        at = n * 2 + w % 2

        @pl.loop(0, heads)
        def _(h):
            room[at, h] = room[at, h] + extra[w % 2, h]

    def to_b(n, w, piece=None):
        at = (n * 2 + w,)
        if piece is not None:
            at = at + (piece[0], pl.ds(piece[1], piece[2]))
        return pltpu.make_async_remote_copy(
            src_ref=b_send.at[at],
            dst_ref=b_room.at[at],
            send_sem=bs_sem.at[n * 2 + w],
            recv_sem=br_sem.at[n * 2 + w],
            device_id=t.b,
            device_id_type=MESH,
        )

    head_rows = b_send.shape[2]
    size = head_rows // 4
    pieces = [
        to_b(n, w, (h, r, size))
        for n in range(line)
        for w in (1, 0)
        for h in range(heads)
        for r in range(0, head_rows, size)
    ]

    def feed(number):
        for _ in range(min(number, len(pieces))):
            pieces.pop(0).start()

    plane_signal(line, t.core, t.z, t.low)
    met = greet_rows((-1, 1), count)
    for w in (1, 0):
        for c in pair(0, w):
            c.start()
    for c in weights:
        c.start()
    for c in (0, 1):
        g_load(c).start()
        s_load(c).start()
    pl.semaphore_wait(pltpu.get_barrier_semaphore(), 7 + line - 1 + met)

    for n in range(line):
        for w in (1, 0):
            join(n, w)
            feed(FEED["join"])
            if n < line - 1:
                for c in pair(n + 1, w):
                    c.start()

    for w in (3, 2):
        for c in pair(0, w):
            c.start()

    def mask(k):
        return mask_ref[:, k : k + 1]

    pixels = par_ref[4:5]
    pixels_wide = pixels[:, :wide]

    def third_params(c):
        q, at = (c * wide) // middle, (c * wide) % middle
        at = slice(at, at + wide)
        return 2 * q, at

    def moved_sums(ref, row, at, d, scaled):
        ref[row : row + 1, at] = jnp.sum(d, axis=0, keepdims=True)
        ref[row + 1 : row + 2, at] = jnp.sum(d * scaled, axis=0, keepdims=True)

    def first_pass(ref):
        for c in range(chunks):
            g_load(c).wait()
            s_load(c).wait()
            row, at = third_params(c)
            total = tw_ref[0:1, 0:1] * g_room[c % 2, 0]
            for h in range(1, heads):
                total = total + tw_ref[h : h + 1, 0:1] * g_room[c % 2, h]
            scaled = s_room[c % 2]
            here = slice(c * wide, (c + 1) * wide)
            pre = x_ref[:, here].astype(f32) + (
                scaled * par3_ref[row : row + 1, at] + par3_ref[row + 1 : row + 2, at]
            )
            d = total * slope(pre)
            dpre[:, here] = d
            d = d * mask(0)
            moved_sums(ref, row, at, d, scaled)
            feed(FEED["pass"])
            if c + 2 < chunks:
                g_load(c + 2).start()
                s_load(c + 2).start()
        for c in (0, 1):
            s_load(c).start()

    def keep_rest():
        for n in range(line):
            for w in (3, 2):
                feed(FEED["keep"])
                join(n, w)
                if n < line - 1:
                    for c in pair(n + 1, w):
                        c.start()

    back3 = plane_sum(line, first_pass, three, keep_rest, lambda: feed(FEED["later3"]))
    bs3_ref[...] = back3
    for c in range(chunks):
        s_load(c).wait()
        row, at = third_params(c)
        mean = s3_ref[row : row + 1, at] / pixels_wide
        var = s3_ref[row + 1 : row + 2, at] / pixels_wide - mean * mean
        inverse = lax.rsqrt(var + norm_epsilon)
        here = slice(c * wide, (c + 1) * wide)
        v = (
            mask(0)
            * (inverse * par3_ref[row : row + 1, at])
            * (
                dpre[:, here] * mask(0)
                - back3[row : row + 1, at] / pixels_wide
                - s_room[c % 2] * (back3[row + 1 : row + 2, at] / pixels_wide)
            )
        )
        dthird[:, here] = v.astype(bf)
        feed(FEED["third"])
        if c + 2 < chunks:
            s_load(c + 2).start()
    weights[0].wait()
    scaled2 = sc2_ref[...]
    normed2 = scaled2 * par_ref[2:3] + par_ref[3:4]
    feed(FEED["d2"])
    d2 = nt(dthird[...], we_v[...]) * slope(normed2) * mask(0)

    def grad_out(n, ref):
        return pltpu.make_async_copy(grad_room.at[n % 2], ref, grad_sem.at[n % 2])

    state = []

    def put(value, ref):
        n = len(state)
        if n >= 2:
            state[n - 2].wait()
        grad_room[n % 2] = value.astype(bf)
        c = grad_out(n, ref)
        c.start()
        state.append(c)

    hidden2 = silu(normed2).astype(bf)

    def expand_grads():
        for q in range(parts):
            feed(FEED["ge"])
            put(tn(hidden2, dthird[:, q * middle : (q + 1) * middle]), ge_ref.at[q])

    back2 = plane_sum(
        line, lambda ref: moved_sums(ref, 0, slice(None), d2, scaled2), two, expand_grads,
        lambda: feed(FEED["later2"]),
    )
    bs2_ref[...] = back2

    def through(d, scaled, sums, back, gain):
        _, inverse = scale_rows(sums, pixels)
        return mask(0) * (inverse * gain) * (d - back[0:1] / pixels - scaled * (back[1:2] / pixels))

    ext[halo : halo + px] = through(d2, scaled2, s2_ref, back2, par_ref[2:3]).astype(bf)

    def edge(up):
        src = ext.at[pl.ds(px if up else halo, halo)]
        dst = ext.at[pl.ds(0 if up else halo + px, halo)]
        return pltpu.make_async_remote_copy(
            src_ref=src,
            dst_ref=dst,
            send_sem=h_send.at[int(up)],
            recv_sem=h_recv.at[int(up)],
            device_id=t.at(t.place + (1 if up else -1)),
            device_id_type=MESH,
        )

    has_next, has_last = t.place < count - 1, t.place > 0
    pl.when(has_last)(lambda: edge(False).start())
    pl.when(has_next)(lambda: edge(True).start())
    weights[1].wait()
    scaled1 = sc1_ref[...]
    normed1 = scaled1 * par_ref[0:1] + par_ref[1:2]
    hidden1 = silu(normed1).astype(bf)

    def spread(j):
        v = ext[(2 - j) * halo : (2 - j) * halo + px].astype(f32)
        kept_row = 1.0 if j == 1 else mask(4 if j == 0 else 3)
        for c in range(3):
            if c == 0:
                moved, kept = pltpu.roll(v, px - rate, 0), mask(2)
            elif c == 1:
                moved, kept = v, mask(0)
            else:
                moved, kept = pltpu.roll(v, rate, 0), mask(1) * mask(0)
            k = 3 * j + c
            taps[:, k * middle : (k + 1) * middle] = jnp.where(kept * kept_row > 0, moved, 0.0).astype(bf)

    def tap(k):
        return taps[:, k * middle : (k + 1) * middle]

    feed(FEED["edge"])
    spread(1)
    d1 = None
    for j in (1, 0, 2):
        if j == 0:
            pl.when(has_next)(lambda: edge(False).wait_recv())
            pl.when(has_last)(lambda: edge(True).wait_recv())
            spread(0)
            spread(2)
        for c in range(3):
            k = 3 * j + c
            feed(FEED["d1"])
            part = nt(tap(k), wd_v[k * middle : (k + 1) * middle])
            d1 = part if d1 is None else d1 + part
    d1 = d1 * slope(normed1) * mask(0)

    def dilated_grads():
        for k in range(9):
            feed(FEED["gd"])
            put(tn(hidden1, tap(k)), gd_ref.at[k])

    back1 = plane_sum(
        line, lambda ref: moved_sums(ref, 0, slice(None), d1, scaled1), one, dilated_grads,
        lambda: feed(FEED["later1"]),
    )
    bs1_ref[...] = back1
    dfirst = through(d1, scaled1, s1_ref, back1, par_ref[0:1]).astype(bf)
    feed(len(pieces))
    weights[2].wait()
    outs = []
    for q in range(parts):
        here = slice(q * middle, (q + 1) * middle)
        if q >= 2:
            outs[q - 2].wait()
        out_room[q % 2] = nt(dfirst, wr_v[here]) + dpre[:, here]
        outs.append(
            pltpu.make_async_copy(
                out_room.at[q % 2], fg_ref.at[:, pl.ds(q * middle, middle)], out_sem.at[q % 2]
            )
        )
        outs[q].start()
    for q in range(parts):
        here = slice(q * middle, (q + 1) * middle)
        put(tn(x_ref[:, here], dfirst), gr_ref.at[pl.ds(q * middle, middle)])

    def stays(n):
        return pltpu.make_async_copy(acc.at[n], sum_ref.at[n], sum_sem.at[n])

    @pl.loop(0, line)
    def _(n):
        for w in (1, 0):
            to_b(n, w).wait_recv()
            at = n * 2 + w

            @pl.loop(0, heads)
            def _(h):
                acc[at, h] = acc[at, h] + b_room[at, h]

            stays(at).start()

    for c in state[-2:] + outs[-2:]:
        c.wait()

    @pl.loop(0, line)
    def _(n):
        for w in (1, 0):
            to_b(n, w).wait_send()
            stays(n * 2 + w).wait()

    pl.when(has_last)(lambda: edge(False).wait_send())
    pl.when(has_next)(lambda: edge(True).wait_send())


def back_step(x, task_weights, scaled1, scaled2, scaled3, params, params3, sums1, sums2, sums3, masks, grads,
              wr, wd, we, own, got, rate, rows, cols, number):
    px, channels = x.shape
    count = lax.axis_size("fsdp")
    line = count // 4
    middle = params.shape[1]
    parts = channels // middle
    wide = middle // 2
    heads, _, head_rows, half = own.shape
    bf, f32 = jnp.bfloat16, jnp.float32
    dma = pltpu.SemaphoreType.DMA
    vmem = pl.BlockSpec(memory_space=pltpu.VMEM)
    hbm = pl.BlockSpec(memory_space=pl.ANY)
    S = jax.ShapeDtypeStruct
    V = pltpu.VMEM
    return pl.pallas_call(
        functools.partial(back_kernel, rate, rows, cols, count, heads),
        out_shape=(
            S((2, middle), f32),
            S((2, middle), f32),
            S((2 * parts, middle), f32),
            S((px, channels), f32),
            S((channels, middle), bf),
            S((9, middle, middle), bf),
            S((parts, middle, middle), bf),
            S((2 * line, heads, head_rows, half), bf),
        ),
        in_specs=[vmem] * 10 + [hbm] * 7,
        out_specs=(vmem,) * 3 + (hbm,) * 5,
        scratch_shapes=[
            V((2 * line, heads, head_rows, half), bf),
            V((2 * line, heads, head_rows, half), bf),
            V((2 * line, heads, head_rows, half), bf),
            V((2, heads, head_rows, half), bf),
            V((2, heads, px, wide), f32),
            V((2, px, wide), f32),
            V((px, channels), f32),
            V((px, channels), bf),
            V((channels, middle), bf),
            V((9 * middle, middle), bf),
            V((middle, channels), bf),
            V((px + 2 * rate * cols, middle), bf),
            V((px, 9 * middle), bf),
            V((2, px, middle), f32),
            V((2, middle, middle), bf),
            dma((2,)),
            dma((2,)),
            dma((2 * line,)),
            dma((2 * line,)),
            dma((2,)),
            dma((2,)),
            dma((3,)),
            dma((2,)),
            dma((2,)),
            dma((2,)),
            dma((2,)),
            dma((2 * line,)),
        ]
        + plane_scratch(line, (2, middle))
        + plane_scratch(line, (2, middle))
        + plane_scratch(line, (2 * parts, middle)),
        compiler_params=pltpu.CompilerParams(
            collective_id=number, has_side_effects=True, vmem_limit_bytes=63 * 2**20
        ),
    )(x, task_weights, scaled1, scaled2, params, params3, sums1, sums2, sums3, masks,
      grads, scaled3, wr, wd, we, own, got)


def silu_slope(values):
    sigmoid_value = jax.nn.sigmoid(values)
    return sigmoid_value * (1.0 + values * (1.0 - sigmoid_value))


def shift_along(values, offset, axis_number):
    if offset == 0:
        return values
    length = values.shape[axis_number]
    pad_shape = list(values.shape)
    pad_shape[axis_number] = abs(offset)
    zero_block = jnp.zeros(pad_shape, values.dtype)
    if offset > 0:
        return jnp.concatenate(
            [lax.slice_in_dim(values, offset, length, axis=axis_number), zero_block], axis_number
        )
    return jnp.concatenate(
        [zero_block, lax.slice_in_dim(values, 0, length + offset, axis=axis_number)], axis_number
    )


def inside_rows(layout, offset):
    row_ids, row_top, row_bottom, row_side = layout
    return (row_ids + offset >= row_top) & (row_ids + offset < row_bottom)


def inside_cols(layout, offset, col_count):
    row_ids, row_top, row_bottom, row_side = layout
    columns = jnp.arange(col_count, dtype=jnp.int32)
    return (columns[None, :] + offset >= 0) & (columns[None, :] + offset < row_side[:, None])


def column_sums(inputs, weight, rate, layout):
    col_count = inputs.shape[1]
    products = jnp.einsum("rwc,kco->krwo", inputs, weight, preferred_element_type=jnp.float32)
    sums = []
    for row_step in range(3):
        summed = 0.0
        for col_step in range(3):
            across = (col_step - 1) * rate
            summed = summed + jnp.where(
                inside_cols(layout, across, col_count)[:, :, None],
                shift_along(products[3 * row_step + col_step], across, 1),
                0.0,
            )
        sums.append(summed)
    return sums


def dilated_forward(inputs, weights, rates, layout, number):
    outer, centers = [], []
    for weight, rate in zip(weights, rates):
        low, center, high = column_sums(inputs, weight, rate, layout)
        outer += [low.astype(jnp.bfloat16), high.astype(jnp.bfloat16)]
        centers.append(center)
    offsets = tuple(o for rate in rates for o in (-rate, rate))
    pulled = exchange(jnp.stack(outer), offsets, number)
    results = []
    for k, (center, rate) in enumerate(zip(centers, rates)):
        for j, down in ((2 * k, -rate), (2 * k + 1, rate)):
            center = center + jnp.where(
                inside_rows(layout, down)[:, None, None], pulled[j].astype(jnp.float32), 0.0
            )
        results.append(center)
    return results


def spread_taps(grads, rates, layout, number):
    row_ids = layout[0]
    row_count, col_count = grads[0].shape[:2]
    total_rows = row_count * lax.axis_size("fsdp")
    outer = []
    for grad, rate in zip(grads, rates):
        for down in (-rate, rate):
            outer.append(
                jnp.where(inside_rows(layout, down)[:, None, None], grad, jnp.bfloat16(0.0))
            )
    offsets = tuple(o for rate in rates for o in (rate, -rate))
    pulled = exchange(jnp.stack(outer), offsets, number)
    results = []
    for k, (grad, rate) in enumerate(zip(grads, rates)):
        taps = []
        for row_step in range(3):
            down = (row_step - 1) * rate
            if row_step == 1:
                arrived = grad
            else:
                there = (row_ids - down >= 0) & (row_ids - down < total_rows)
                arrived = jnp.where(
                    there[:, None, None], pulled[2 * k + row_step // 2], jnp.bfloat16(0.0)
                )
            for col_step in range(3):
                across = (col_step - 1) * rate
                kept = jnp.where(
                    inside_cols(layout, across, col_count)[:, :, None], arrived, jnp.bfloat16(0.0)
                )
                taps.append(shift_along(kept, -across, 1))
        results.append(taps)
    return results


def spread(stat):
    return stat.reshape(stat.shape[:-1] + (1, 1) + stat.shape[-1:])


def totals_of(one, two, number):
    local_sums = jnp.stack([jnp.sum(one, axis=(-3, -2)), jnp.sum(two, axis=(-3, -2))])
    flat = all_sum(local_sums.reshape(2, -1), number)
    return flat.reshape(local_sums.shape)


def moments(values, valid_mask, number):
    weighted = values * valid_mask[..., None]
    return totals_of(weighted, weighted * values, number)


def normalize(values, sums, valid_count, gain_row, bias_row):
    mean_value = sums[0] / valid_count
    variance = sums[1] / valid_count - mean_value * mean_value
    inverse = lax.rsqrt(variance + norm_epsilon)
    scaled = (values - spread(mean_value)) * spread(inverse)
    return (scaled, inverse, scaled * spread(gain_row) + spread(bias_row))


def norm_backward(grad_norm, scaled, inverse, gain_row, valid_mask, valid_count, number):
    masked = grad_norm * valid_mask[..., None]
    sums = totals_of(masked, masked * scaled, number)
    grad_values = (
        valid_mask[..., None]
        * spread(inverse * gain_row)
        * (masked - spread(sums[0] / valid_count) - scaled * spread(sums[1] / valid_count))
    )
    return (grad_values, sums)


def update(param, moment, grad):
    moment_new = momentum_decay * moment + grad
    return (param - step_rate * moment_new, moment_new)


def local(
    features,
    cotangent,
    crop_heights,
    task_scale,
    w_reduce,
    w_dilated,
    w_expand,
    w_heads,
    norm_params,
    m_reduce,
    m_dilated,
    m_expand,
    m_heads,
    norm_moment,
):
    row_count = features.shape[1]
    col_count = features.shape[2]
    channels = features.shape[3]
    middle = w_reduce.shape[1]
    head_width = w_heads.shape[2]
    head_total = w_heads.shape[0]
    group_index = lax.axis_index("dp")
    place_index = lax.axis_index("fsdp")
    group_heights = lax.dynamic_index_in_dim(crop_heights, group_index, 0, keepdims=False)
    crop_order = jnp.arange(group_heights.shape[0], dtype=jnp.int32)
    crop_ends = jnp.sum(
        jnp.where(crop_order[None, :] <= crop_order[:, None], group_heights[None, :], 0),
        axis=1,
        dtype=jnp.int32,
    )
    crop_starts = crop_ends - group_heights
    row_ids = place_index * row_count + jnp.arange(row_count, dtype=jnp.int32)
    member = (row_ids[:, None] >= crop_starts[None, :]) & (row_ids[:, None] < crop_ends[None, :])
    row_top = jnp.sum(jnp.where(member, crop_starts[None, :], 0), axis=1, dtype=jnp.int32)
    row_bottom = jnp.sum(jnp.where(member, crop_ends[None, :], 0), axis=1, dtype=jnp.int32)
    row_side = jnp.sum(jnp.where(member, group_heights[None, :], 0), axis=1, dtype=jnp.int32)
    layout = (row_ids, row_top, row_bottom, row_side)
    valid_mask = (jnp.arange(col_count, dtype=jnp.int32)[None, :] < row_side[:, None]).astype(
        jnp.float32
    )
    valid_count = jnp.sum(crop_heights * crop_heights).astype(jnp.float32)
    gain_values = norm_params[0]
    bias_values = norm_params[1]
    trunk_end = 2 * middle + channels
    inputs = features[0]
    inputs_float = inputs.astype(jnp.float32)
    place_count = lax.axis_size("fsdp")
    pixels = row_count * col_count
    head_gain = gain_values[trunk_end:].reshape(head_total, head_width)
    head_bias = bias_values[trunk_end:].reshape(head_total, head_width)
    head_params = jnp.concatenate(
        [
            jnp.stack([head_gain, head_bias], 1).reshape(2 * head_total, head_width),
            jnp.broadcast_to(valid_count, (2, head_width)),
        ]
    )
    total_rows = row_count * place_count
    masks = []
    for rate in head_rates + (trunk_rate,):
        flags = [
            inside_cols(layout, 0, col_count),
            inside_cols(layout, -rate, col_count),
            inside_cols(layout, rate, col_count),
        ] + [
            jnp.broadcast_to(flag[:, None], (row_count, col_count))
            for flag in (
                inside_rows(layout, -rate),
                inside_rows(layout, rate),
                row_ids + rate < total_rows,
                row_ids - rate >= 0,
            )
        ]
        flags = jnp.stack([f.reshape(pixels) for f in flags], 1).astype(jnp.float32)
        masks.append(jnp.pad(flags, ((0, 0), (0, 128 - flags.shape[1]))))
    half_rows = w_heads.shape[1] // 2
    heads_half = lax.dynamic_slice_in_dim(w_heads, group_index * half_rows, half_rows, 1)

    def beside(part):
        return lax.all_gather(
            part.astype(jnp.bfloat16), ("fsdp", "dp"), axis=1, tiled=True
        ).reshape(-1, channels, head_width)

    heads_late = beside(heads_half[1:])
    if place_count == 16:
        flat_params = jnp.concatenate(
            [
                jnp.stack([gain_values[:middle], bias_values[:middle]]),
                jnp.stack([gain_values[middle : 2 * middle], bias_values[middle : 2 * middle]]),
                jnp.broadcast_to(valid_count, (4, middle)),
            ]
        )
        wide_params = jnp.stack(
            [
                gain_values[2 * middle : trunk_end].reshape(-1, middle),
                bias_values[2 * middle : trunk_end].reshape(-1, middle),
            ],
            1,
        ).reshape(-1, middle)
        (
            reduce_low, dilated_low, expand_low, heads_early, trunk_out,
            scaled_one, scaled_two, scaled_three, sums_in_one, sums_in_two, sums_in_three,
        ) = trunk_step(
            inputs.reshape(pixels, channels),
            (
                w_reduce.astype(jnp.bfloat16),
                w_dilated.astype(jnp.bfloat16),
                w_expand.astype(jnp.bfloat16),
                w_heads[:1].astype(jnp.bfloat16),
            ),
            flat_params,
            wide_params,
            masks[-1],
            trunk_rate,
            row_count,
            col_count,
            0,
        )
        heads_early = heads_early.reshape(-1, channels, head_width)
    else:
        heads_early = beside(heads_half[:1])
        reduce_low, dilated_low, expand_low = (
            lax.all_gather(w.astype(jnp.bfloat16), "fsdp", axis=0)
            for w in (w_reduce, w_dilated, w_expand)
        )
        reduce_low = reduce_low.reshape(channels, middle)
        dilated_low = dilated_low.reshape(9, middle, middle)
        first = jnp.einsum("rwc,cm->rwm", inputs, reduce_low, preferred_element_type=jnp.float32)
        scaled_one, inverse_one, normed_one = normalize(
            first, moments(first, valid_mask, 1), valid_count, gain_values[:middle], bias_values[:middle]
        )
        hidden_one = jax.nn.silu(normed_one).astype(jnp.bfloat16)
        (second,) = dilated_forward(hidden_one, (dilated_low,), (trunk_rate,), layout, 2)
        scaled_two, inverse_two, normed_two = normalize(
            second,
            moments(second, valid_mask, 3),
            valid_count,
            gain_values[middle : 2 * middle],
            bias_values[middle : 2 * middle],
        )
        hidden_two = jax.nn.silu(normed_two).astype(jnp.bfloat16)
        expand_low = expand_low.transpose(1, 0, 2).reshape(middle, channels)
        third = jnp.einsum("rwm,mc->rwc", hidden_two, expand_low, preferred_element_type=jnp.float32)
        scaled_three, inverse_three, normed_three = normalize(
            third,
            moments(third, valid_mask, 4),
            valid_count,
            gain_values[2 * middle : trunk_end],
            bias_values[2 * middle : trunk_end],
        )
        pre_act = inputs_float + normed_three
        trunk_out = jax.nn.silu(pre_act).astype(jnp.bfloat16)
    head_grads, grads_own, grads_got, head_sums, squares = heads_step(
        trunk_out.reshape(pixels, channels),
        heads_early,
        heads_late,
        cotangent.reshape(head_total, pixels, head_width),
        head_params,
        jnp.stack(masks[:-1]),
        head_rates,
        row_count,
        col_count,
        5,
    )
    head_sums = head_sums.reshape(head_total, 2, head_width).transpose(1, 0, 2)
    squares = jnp.sum(squares[:head_total], axis=1)
    task_rms = jnp.sqrt(squares / (valid_count * channels) + task_epsilon)
    task_weight = task_scale / task_rms
    if place_count == 16:
        (
            back_one, back_two, back_three, features_grad, grad_reduce, grad_dilated, grad_expand, late,
        ) = back_step(
            inputs.reshape(pixels, channels),
            jnp.broadcast_to(jnp.pad(task_weight, (0, 8 - head_total))[:, None], (8, 128)),
            scaled_one,
            scaled_two,
            scaled_three,
            flat_params,
            wide_params,
            sums_in_one,
            sums_in_two,
            sums_in_three,
            masks[-1],
            head_grads,
            reduce_low,
            dilated_low,
            expand_low,
            grads_own.reshape(head_total, place_count, -1, head_width // 2),
            grads_got.reshape(head_total, place_count, -1, head_width // 2),
            trunk_rate,
            row_count,
            col_count,
            1,
        )
        features_grad = features_grad.reshape(row_count, col_count, channels)
        *trunk_totals, heads_total = reduce_shards(
            (
                grad_reduce.reshape(1, place_count, -1, middle),
                grad_dilated.reshape(1, place_count, -1, middle),
                grad_expand.transpose(1, 0, 2)
                .reshape(middle, place_count, -1)
                .transpose(1, 0, 2)[None],
            ),
            (late,),
            2,
        )
        trunk_totals = [t[0] for t in trunk_totals]
        sums_one, sums_two = back_one, back_two
        sums_three = back_three.reshape(-1, 2, middle).transpose(1, 0, 2).reshape(2, channels)
    else:
        grad_trunk = task_weight[0] * head_grads[0]
        for k in range(1, head_total):
            grad_trunk = grad_trunk + task_weight[k] * head_grads[k]
        grad_trunk = grad_trunk.reshape(row_count, col_count, channels)
        grad_pre = grad_trunk * silu_slope(pre_act)
        grad_third, sums_three = norm_backward(
            grad_pre,
            scaled_three,
            inverse_three,
            gain_values[2 * middle : trunk_end],
            valid_mask,
            valid_count,
            11,
        )
        grad_third = grad_third.astype(jnp.bfloat16)
        grad_expand = jnp.einsum(
            "rwm,rwc->mc", hidden_two, grad_third, preferred_element_type=jnp.float32
        ).astype(jnp.bfloat16)
        grad_hidden_two = jnp.einsum(
            "rwc,mc->rwm", grad_third, expand_low, preferred_element_type=jnp.float32
        )
        grad_second, sums_two = norm_backward(
            grad_hidden_two * silu_slope(normed_two),
            scaled_two,
            inverse_two,
            gain_values[middle : 2 * middle],
            valid_mask,
            valid_count,
            12,
        )
        (taps,) = spread_taps([grad_second.astype(jnp.bfloat16)], (trunk_rate,), layout, 13)
        taps = jnp.stack(taps)
        grad_hidden_one = jnp.einsum(
            "krwo,kco->rwc", taps, dilated_low, preferred_element_type=jnp.float32
        )
        grad_dilated = jnp.einsum(
            "rwc,krwo->kco", hidden_one, taps, preferred_element_type=jnp.float32
        )
        grad_first, sums_one = norm_backward(
            grad_hidden_one * silu_slope(normed_one),
            scaled_one,
            inverse_one,
            gain_values[:middle],
            valid_mask,
            valid_count,
            14,
        )
        grad_first = grad_first.astype(jnp.bfloat16)
        grad_reduce = jnp.einsum("rwc,rwm->cm", inputs, grad_first, preferred_element_type=jnp.float32)
        features_grad = (
            jnp.einsum("rwm,cm->rwc", grad_first, reduce_low, preferred_element_type=jnp.float32)
            + grad_pre
        )
        trunk_totals = []
        for grad, axis in ((grad_reduce, 0), (grad_dilated.reshape(-1, middle), 0), (grad_expand, 1)):
            shard = lax.psum_scatter(
                grad.astype(jnp.bfloat16), "fsdp", scatter_dimension=axis, tiled=True
            )
            trunk_totals.append(lax.psum(shard, "dp"))
        shared = lax.psum_scatter(
            (grads_own + grads_got).reshape(head_total, -1, head_width // 2),
            "fsdp",
            scatter_dimension=1,
            tiled=True,
        )
        heads_total = lax.all_gather(shared, "dp", axis=2, tiled=True)
    totals = tuple(t.astype(jnp.float32) for t in trunk_totals) + (
        task_weight[:, None, None] * heads_total.astype(jnp.float32),
    )
    gain_grad = jnp.concatenate(
        [sums_one[1], sums_two[1], sums_three[1], (task_weight[:, None] * head_sums[1]).reshape(-1)]
    )
    bias_grad = jnp.concatenate(
        [sums_one[0], sums_two[0], sums_three[0], (task_weight[:, None] * head_sums[0]).reshape(-1)]
    )
    norm_grad = jnp.stack([gain_grad, bias_grad])
    w_reduce_new, m_reduce_new = update(w_reduce, m_reduce, totals[0])
    w_dilated_new, m_dilated_new = update(w_dilated, m_dilated, totals[1])
    w_expand_new, m_expand_new = update(w_expand, m_expand, totals[2])
    w_heads_new, m_heads_new = update(w_heads, m_heads, totals[3])
    norm_params_new, norm_moment_new = update(norm_params, norm_moment, norm_grad)
    return (
        features_grad[None],
        w_reduce_new,
        m_reduce_new,
        w_dilated_new,
        m_dilated_new,
        w_expand_new,
        m_expand_new,
        w_heads_new,
        m_heads_new,
        norm_params_new,
        norm_moment_new,
    )


def solution(mesh):
    placed = (
        P("dp", "fsdp", None, None),
        P(None, "dp", "fsdp", None, None),
        P(),
        P(),
        P("fsdp", None),
        P("fsdp", None),
        P(None, "fsdp"),
        P(None, "fsdp", None),
        P(),
        P("fsdp", None),
        P("fsdp", None),
        P(None, "fsdp"),
        P(None, "fsdp", None),
        P(),
    )
    return jax.shard_map(
        local,
        mesh=mesh,
        in_specs=placed,
        out_specs=(
            P("dp", "fsdp", None, None),
            P("fsdp", None),
            P("fsdp", None),
            P("fsdp", None),
            P("fsdp", None),
            P(None, "fsdp"),
            P(None, "fsdp"),
            P(None, "fsdp", None),
            P(None, "fsdp", None),
            P(),
            P(),
        ),
        check_vma=False,
    )
```

```python
import functools

import jax
import jax.numpy as jnp
from jax import lax
from jax.experimental import pallas as pl
from jax.experimental.pallas import tpu as pltpu
from jax.sharding import PartitionSpec as P

MESH = pl.DeviceIdType.MESH
norm_epsilon = 1e-05
task_epsilon = 1e-06
momentum_decay = 0.9
step_rate = 0.01
trunk_rate = 4
head_rates = (12, 24, 36)

class Tree:
    def __init__(self):
        self.core = lax.axis_index("dp")
        self.place = lax.axis_index("fsdp")
        self.count = lax.axis_size("fsdp")
        self.line = self.count // 4
        self.z = self.place // 4
        self.low = self.place % 4
        self.step_a = 1 + self.core
        self.step_b = 2 - self.core
        self.move_a = self.step_a * (1 - 2 * ((self.low // self.step_a) % 2))
        self.move_b = self.step_b * (1 - 2 * ((self.low // self.step_b) % 2))

    def at(self, place):
        return (self.core, place)

    @property
    def partner(self):
        return (1 - self.core, self.place)

    @property
    def a(self):
        return self.at(self.place + self.move_a)

    @property
    def b(self):
        return self.at(self.place + self.move_b)

    @property
    def down(self):
        return self.at(self.place - 4)

    @property
    def up(self):
        return self.at(self.place + 4)

    def greet(self):
        barrier = pltpu.get_barrier_semaphore()
        for peer in (self.partner, self.a, self.b):
            pl.semaphore_signal(barrier, inc=1, device_id=peer, device_id_type=MESH)

        @pl.when(self.z > 0)
        def _():
            pl.semaphore_signal(barrier, inc=1, device_id=self.down, device_id_type=MESH)

        @pl.when(self.z < self.line - 1)
        def _():
            pl.semaphore_signal(barrier, inc=1, device_id=self.up, device_id_type=MESH)

        pl.semaphore_wait(
            barrier,
            3
            + jnp.where(self.z > 0, 1, 0)
            + jnp.where(self.z < self.line - 1, 1, 0),
        )


def plane_sum_kernel(line, x_ref, o_ref, near, part, far, n_send, n_recv, f_send, f_recv):
    core = lax.axis_index("dp")
    place = lax.axis_index("fsdp")
    z, low = place // 4, place % 4
    me = low * 2 + core

    def beside(s):
        other = (me + s) % 8
        return (other % 2, z * 4 + other // 2)

    def away(s):
        return (core, ((z + s) % line) * 4 + low)

    barrier = pltpu.get_barrier_semaphore()
    for s in range(1, 8):
        pl.semaphore_signal(barrier, inc=1, device_id=beside(s), device_id_type=MESH)

    @pl.loop(1, line)
    def _(s):
        pl.semaphore_signal(barrier, inc=1, device_id=away(s), device_id_type=MESH)

    near[me] = x_ref[...]
    pl.semaphore_wait(barrier, 7 + line - 1)

    def to_beside(s):
        return pltpu.make_async_remote_copy(src_ref=x_ref, dst_ref=near.at[me], send_sem=n_send.at[s], recv_sem=n_recv, device_id=beside(s), device_id_type=MESH)

    def to_away(s):
        return pltpu.make_async_remote_copy(src_ref=part, dst_ref=far.at[z], send_sem=f_send.at[s], recv_sem=f_recv, device_id=away(s), device_id_type=MESH)

    for s in range(1, 8):
        to_beside(s).start()
    seven = near.at[pl.ds(0, 7)]
    pltpu.make_async_copy(seven, seven, n_recv).wait()
    total = jnp.sum(near[...], axis=0)
    part[...] = total
    pl.loop(1, line)(lambda s: to_away(s).start())
    far[z] = total
    rest = far.at[pl.ds(0, line - 1)]
    pltpu.make_async_copy(rest, rest, f_recv).wait()
    o_ref[...] = jnp.sum(far[...], axis=0)
    for s in range(1, 8):
        to_beside(s).wait_send()
    pl.loop(1, line)(lambda s: to_away(s).wait_send())


def all_sum(x, number):
    line = lax.axis_size("fsdp") // 4
    dma = pltpu.SemaphoreType.DMA
    return pl.pallas_call(
        functools.partial(plane_sum_kernel, line),
        out_shape=jax.ShapeDtypeStruct(x.shape, x.dtype),
        in_specs=[pl.BlockSpec(memory_space=pltpu.VMEM)],
        out_specs=pl.BlockSpec(memory_space=pltpu.VMEM),
        scratch_shapes=[
            pltpu.VMEM((8,) + x.shape, x.dtype), pltpu.VMEM(x.shape, x.dtype), pltpu.VMEM((line,) + x.shape, x.dtype),
            dma((8,)), dma, dma((line,)), dma,
        ],
        compiler_params=pltpu.CompilerParams(collective_id=number, has_side_effects=True),
    )(x)


def reduce_kernel(kinds, whole, *refs):
    count = len(kinds)
    parts, outs = refs[:count], refs[count : 2 * count]
    scratch = refs[2 * count :]
    accs, arx, zrx = (scratch[k * count : (k + 1) * count] for k in range(3))
    prx, brx = (scratch[3 * count + k * whole : 3 * count + (k + 1) * whole] for k in range(2))
    (
        load_sem, p_send, p_recv, b_send, b_recv, a_send, a_recv, z_send, z_recv, s_send, s_recv,
    ) = scratch[3 * count + 2 * whole :]
    t = Tree()
    t.greet()
    line, z, low = t.line, t.z, t.low

    def rows_of(k, core):
        rows = kinds[k][1] // 2
        return pl.ds(pl.multiple_of(core * rows, 16), rows)

    def remote(src, dst, send, recv, peer):
        return pltpu.make_async_remote_copy(src_ref=src, dst_ref=dst, send_sem=send, recv_sem=recv, device_id=peer, device_id_type=MESH)

    def load(k, block):
        return pltpu.make_async_copy(
            parts[k].at[:, block, rows_of(k, t.core)], accs[k].at[block], load_sem.at[k, block]
        )

    def load_late(k, at):
        return pltpu.make_async_copy(parts[k].at[at], accs[k].at[at], load_sem.at[k, at])

    def spot_of(k, zz, w):
        if k < whole:
            return zz * 4 + lows[w]
        return zz * 2 + (3 - w)

    def to_partner(k, block):
        return remote(parts[k].at[:, block, rows_of(k, 1 - t.core)], prx[k].at[block], p_send.at[k, block], p_recv.at[k, block], t.partner)

    upper = z >= line // 2
    own_spot = jnp.where(upper, z, line - 1 - z)

    def spot(j):
        q = j + jnp.where(j >= own_spot, 1, 0)
        other = jnp.where(upper, q, line - 1 - q)
        return jnp.where(j == line - 1, z, other)

    lows = (low + t.move_b, low + t.move_a + t.move_b, low + t.move_a, low)

    def to_b(k, zz, which):
        return remote(accs[k].at[zz * 4 + lows[which]], brx[k].at[zz * 2 + which], b_send.at[k, zz * 2 + which], b_recv.at[k, zz * 2 + which], t.b)

    def to_a(k, zz):
        return remote(accs[k].at[spot_of(k, zz, 2)], arx[k].at[zz], a_send.at[k, zz], a_recv.at[k, zz], t.a)

    def along(k, zz, up):
        w = 1 if up else 0
        return remote(accs[k].at[spot_of(k, zz, 3)], zrx[k].at[w, zz], z_send.at[k, w, zz], z_recv.at[k, w, zz], t.up if up else t.down)

    def add(k, block, ref):
        lead = kinds[k][0]

        @pl.loop(0, lead)
        def _(h):
            accs[k][block, h] = accs[k][block, h] + ref[h]

    def begin(j):
        zz = spot(j)
        for k in range(whole, count):
            load_late(k, zz * 2).start()
            load_late(k, zz * 2 + 1).start()
        for w in range(4):
            for k in range(whole):
                to_partner(k, zz * 4 + lows[w]).start()
                load(k, zz * 4 + lows[w]).start()

    first, last = range(whole), range(whole, count)

    def send_late(j):
        zz = spot(j)
        for k in last:
            load_late(k, zz * 2 + 1).wait()
            to_a(k, zz).start()

    def stage_b(j):
        zz = spot(j)
        for w in range(4):
            for k in first:
                block = zz * 4 + lows[w]
                load(k, block).wait()
                to_partner(k, block).wait_recv()
                add(k, block, prx[k].at[block])
                if w < 2:
                    to_b(k, zz, w).start()

    def stage_a(j):
        zz = spot(j)
        for w in (1, 0):
            for k in first:
                to_b(k, zz, w).wait_recv()
                add(k, zz * 4 + lows[3 if w == 0 else 2], brx[k].at[zz * 2 + w])
                if w == 1:
                    to_a(k, zz).start()

    def stage_z(j, ks):
        zz = spot(j)
        for k in ks:
            if k >= whole:
                load_late(k, zz * 2).wait()
            to_a(k, zz).wait_recv()
            here = spot_of(k, zz, 3)
            add(k, here, arx[k].at[zz])

            @pl.when(jnp.logical_and(zz >= z, z > 0))
            def _():
                along(k, zz, True).wait_recv()
                add(k, here, zrx[k].at[1, zz])

            @pl.when(jnp.logical_and(zz <= z, z < line - 1))
            def _():
                along(k, zz, False).wait_recv()
                add(k, here, zrx[k].at[0, zz])

            @pl.when(zz > z)
            def _():
                along(k, zz, True).start()

            @pl.when(zz < z)
            def _():
                along(k, zz, False).start()

    pl.loop(0, line)(begin)
    pl.loop(0, line)(send_late)
    pl.loop(0, line)(stage_b)

    @pl.loop(0, line + 1)
    def _(j):
        pl.when(j < line)(lambda: stage_z(j, last))
        pl.when(j >= 1)(lambda: stage_a(j - 1))

    pl.loop(0, line)(lambda j: stage_z(j, first))

    def half(k, core):
        if k < whole:
            return outs[k].at[:, rows_of(k, core)]
        cols = kinds[k][2]
        return outs[k].at[:, :, pl.ds(pl.multiple_of(core * cols, cols), cols)]

    def share(k):
        return remote(accs[k].at[spot_of(k, z, 3)], half(k, t.core), s_send.at[k], s_recv.at[k], t.partner)

    def keep(k):
        return pltpu.make_async_copy(accs[k].at[spot_of(k, z, 3)], half(k, t.core), load_sem.at[k, 0])

    for k in range(count):
        share(k).start()
        keep(k).start()

    @pl.loop(0, line)
    def _(j):
        zz = spot(j)
        for k in range(count):
            if k < whole:
                for w in range(4):
                    to_partner(k, zz * 4 + lows[w]).wait_send()
                to_b(k, zz, 0).wait_send()
                to_b(k, zz, 1).wait_send()
            to_a(k, zz).wait_send()
            pl.when(zz > z)(lambda: along(k, zz, True).wait_send())
            pl.when(zz < z)(lambda: along(k, zz, False).wait_send())

    for k in range(count):
        keep(k).wait()
        other = half(k, 1 - t.core)
        remote(other, other, s_send.at[k], s_recv.at[k], t.partner).wait_recv()
        share(k).wait_send()


def reduce_shards(parts, late, number):
    n = lax.axis_size("fsdp")
    line = n // 4
    whole = len(parts)
    kinds = [(p.shape[0], p.shape[2], p.shape[3]) for p in parts] + [p.shape[1:] for p in late]
    sizes = [(l, r // 2, c) for l, r, c in kinds[:whole]] + kinds[whole:]
    results = kinds[:whole] + [(l, r, 2 * c) for l, r, c in kinds[whole:]]
    bf = jnp.bfloat16
    count = len(kinds)
    dma = pltpu.SemaphoreType.DMA

    def room(some, *lead):
        return [pltpu.VMEM(tuple(lead) + tuple(s), bf) for s in some]

    accs = [
        pltpu.VMEM((n if k < whole else 2 * line,) + tuple(s), bf) for k, s in enumerate(sizes)
    ]
    return pl.pallas_call(
        functools.partial(reduce_kernel, kinds, whole),
        out_shape=tuple(jax.ShapeDtypeStruct(r, bf) for r in results),
        in_specs=[pl.BlockSpec(memory_space=pl.ANY)] * count,
        out_specs=tuple([pl.BlockSpec(memory_space=pl.ANY)] * count),
        scratch_shapes=accs
        + room(sizes, line)
        + room(sizes, 2, line)
        + room(sizes[:whole], n)
        + room(sizes[:whole], 2 * line)
        + [
            dma((count, n)),
            dma((count, n)),
            dma((count, n)),
            dma((count, 2 * line)),
            dma((count, 2 * line)),
            dma((count, line)),
            dma((count, line)),
            dma((count, 2, line)),
            dma((count, 2, line)),
            dma((count,)),
            dma((count,)),
        ],
        compiler_params=pltpu.CompilerParams(
            collective_id=number, has_side_effects=True, vmem_limit_bytes=60 * 2**20
        ),
    )(*parts, *late)


def exchange_kernel(offsets, rows, count, x_ref, o_ref, send, recv):
    core = lax.axis_index("dp")
    place = lax.axis_index("fsdp")
    pieces = []
    for k, offset in enumerate(offsets):
        first, cut = offset // rows, offset % rows
        for part, (gap, low, high, to) in enumerate(
            ((first, cut, rows, 0), (first + 1, 0, cut, rows - cut))
        ):
            if high > low:
                pieces.append((k, part, gap, low, high - low, to))
    gaps = sorted({abs(p[2]) for p in pieces} - {0})
    gaps = [-g for g in gaps] + gaps
    barrier = pltpu.get_barrier_semaphore()

    def present(gap):
        return jnp.logical_and(place + gap >= 0, place + gap < count)

    met = jnp.int32(0)
    for gap in gaps:
        met = met + jnp.where(present(gap), 1, 0)

        @pl.when(present(gap))
        def _():
            pl.semaphore_signal(
                barrier, inc=1, device_id=(core, place + gap), device_id_type=MESH
            )

    pl.semaphore_wait(barrier, met)

    def piece(k, part, gap, low, size, to):
        return pltpu.make_async_remote_copy(
            src_ref=x_ref.at[k, pl.ds(low, size)],
            dst_ref=o_ref.at[k, pl.ds(to, size)],
            send_sem=send.at[k, part],
            recv_sem=recv.at[k, part],
            device_id=(core, place - gap),
            device_id_type=MESH,
        )

    for p in pieces:
        k, part, gap, low, size, to = p
        if gap == 0:
            o_ref[k, to : to + size] = x_ref[k, low : low + size]
        else:
            pl.when(present(-gap))(lambda p=p: piece(*p).start())
    for p in pieces:
        if p[2]:
            pl.when(present(p[2]))(lambda p=p: piece(*p).wait_recv())
    for p in pieces:
        if p[2]:
            pl.when(present(-p[2]))(lambda p=p: piece(*p).wait_send())


def exchange(x, offsets, number):
    entries, rows = x.shape[:2]
    return pl.pallas_call(
        functools.partial(exchange_kernel, offsets, rows, lax.axis_size("fsdp")),
        out_shape=jax.ShapeDtypeStruct(x.shape, x.dtype),
        in_specs=[pl.BlockSpec(memory_space=pltpu.VMEM)],
        out_specs=pl.BlockSpec(memory_space=pltpu.VMEM),
        scratch_shapes=[
            pltpu.SemaphoreType.DMA((entries, 2)),
            pltpu.SemaphoreType.DMA((entries, 2)),
        ],
        compiler_params=pltpu.CompilerParams(
            collective_id=number, has_side_effects=True, vmem_limit_bytes=32 * 2**20
        ),
    )(x)


def plane_signal(line, core, z, low):
    barrier = pltpu.get_barrier_semaphore()
    me = low * 2 + core
    for s in range(1, 8):
        other = (me + s) % 8
        pl.semaphore_signal(
            barrier, inc=1, device_id=(other % 2, z * 4 + other // 2), device_id_type=MESH
        )

    @pl.loop(1, line)
    def _(s):
        pl.semaphore_signal(
            barrier, inc=1, device_id=(core, ((z + s) % line) * 4 + low), device_id_type=MESH
        )


def plane_scratch(line, shape):
    dma = pltpu.SemaphoreType.DMA
    return [
        pltpu.VMEM((8,) + shape, jnp.float32),
        pltpu.VMEM(shape, jnp.float32),
        pltpu.VMEM((line,) + shape, jnp.float32),
        dma((8,)),
        dma,
        dma((line,)),
        dma,
    ]


def plane_sum(line, fill, room, meanwhile=None, later=None):
    near, part, far, n_send, n_recv, f_send, f_recv = room
    core = lax.axis_index("dp")
    place = lax.axis_index("fsdp")
    z, low = place // 4, place % 4
    me = low * 2 + core

    def to_beside(s):
        other = (me + s) % 8
        return pltpu.make_async_remote_copy(
            src_ref=near.at[me],
            dst_ref=near.at[me],
            send_sem=n_send.at[s],
            recv_sem=n_recv,
            device_id=(other % 2, z * 4 + other // 2),
            device_id_type=MESH,
        )

    def to_away(s):
        return pltpu.make_async_remote_copy(
            src_ref=part,
            dst_ref=far.at[z],
            send_sem=f_send.at[s],
            recv_sem=f_recv,
            device_id=(core, ((z + s) % line) * 4 + low),
            device_id_type=MESH,
        )

    fill(near.at[me])
    for s in range(1, 8):
        to_beside(s).start()
    if meanwhile is not None:
        meanwhile()
    seven = near.at[pl.ds(0, 7)]
    pltpu.make_async_copy(seven, seven, n_recv).wait()
    total = jnp.sum(near[...], axis=0)
    part[...] = total
    pl.loop(1, line)(lambda s: to_away(s).start())
    far[z] = total
    if later is not None:
        later()
    rest = far.at[pl.ds(0, line - 1)]
    pltpu.make_async_copy(rest, rest, f_recv).wait()
    result = jnp.sum(far[...], axis=0)
    for s in range(1, 8):
        to_beside(s).wait_send()
    pl.loop(1, line)(lambda s: to_away(s).wait_send())
    return result


def row_pieces(offset, rows):
    first, cut = offset // rows, offset % rows
    pieces = [(first, cut, rows - cut, 0)]
    if cut:
        pieces.append((first + 1, 0, cut, rows - cut))
    return pieces


def row_gaps(offsets, rows):
    gaps = {abs(p[0]) for o in offsets for p in row_pieces(o, rows)} - {0}
    return sorted(-g for g in gaps) + sorted(gaps)


def greet_rows(gaps, count):
    barrier = pltpu.get_barrier_semaphore()
    core = lax.axis_index("dp")
    place = lax.axis_index("fsdp")
    met = jnp.int32(0)
    for gap in gaps:
        here = jnp.logical_and(place + gap >= 0, place + gap < count)
        met = met + jnp.where(here, 1, 0)

        @pl.when(here)
        def _():
            pl.semaphore_signal(
                barrier, inc=1, device_id=(core, place + gap), device_id_type=MESH
            )

    return met


class Rows:
    def __init__(self, offsets, rows, cols, count, x_ref, o_ref, send, recv):
        self.core = lax.axis_index("dp")
        self.place = lax.axis_index("fsdp")
        self.rows, self.cols, self.count = rows, cols, count
        self.offsets, self.x_ref, self.o_ref = offsets, x_ref, o_ref
        self.send, self.recv = send, recv

    def present(self, gap):
        return jnp.logical_and(self.place + gap >= 0, self.place + gap < self.count)

    def copies(self, k):
        for part, (gap, low, size, to) in enumerate(row_pieces(self.offsets[k], self.rows)):
            yield gap, low, size, to, pltpu.make_async_remote_copy(
                src_ref=self.x_ref.at[k, pl.ds(low * self.cols, size * self.cols)],
                dst_ref=self.o_ref.at[k, pl.ds(to * self.cols, size * self.cols)],
                send_sem=self.send.at[k, part],
                recv_sem=self.recv.at[k, part],
                device_id=(self.core, self.place - gap),
                device_id_type=MESH,
            )

    def start(self, k):
        for gap, low, size, to, copy in self.copies(k):
            if gap == 0:
                cols = self.cols
                self.o_ref[k, to * cols : (to + size) * cols] = self.x_ref[
                    k, low * cols : (low + size) * cols
                ]
            else:
                pl.when(self.present(-gap))(copy.start)

    def wait_recv(self, k):
        for gap, _, _, _, copy in self.copies(k):
            if gap:
                pl.when(self.present(gap))(copy.wait_recv)

    def wait_send(self, k):
        for gap, _, _, _, copy in self.copies(k):
            if gap:
                pl.when(self.present(-gap))(copy.wait_send)


def heads_kernel(
    rates, rows, cols, count,
    x_ref, xt_ref, wa_ref, wb_ref, cot_ref, par_ref, mask_ref,
    g_ref, own_ref, got_ref, late_ref, sums_ref, sq_ref,
    wv, out_rows, in_rows, resp, dn, taps, g_room, dw_room,
    w_sem, f_send, f_recv, e_send, e_recv, g_sem, dw_sem, hand_sem, got_sem, *rooms,
):
    px = rows * cols
    heads = len(rates)
    width = par_ref.shape[1]
    line = count // 4
    core = lax.axis_index("dp")
    place = lax.axis_index("fsdp")
    z, low = place // 4, place % 4
    one, two, three = rooms[:7], rooms[7:14], rooms[14:]

    def w_copy(t, k):
        early = wa_ref.shape[0] // 9
        src = wa_ref.at[t * 9 + k] if t < early else wb_ref.at[(t - early) * 9 + k]
        return pltpu.make_async_copy(
            src, wv.at[t, :, k * width : (k + 1) * width], w_sem.at[t * 9 + k]
        )

    for t in reversed(range(heads)):
        for k in range(9):
            w_copy(t, k).start()
    fwd = Rows([o for r in rates for o in (-r, r)], rows, cols, count, out_rows, in_rows, f_send, f_recv)
    bwd = Rows([o for r in rates for o in (r, -r)], rows, cols, count, out_rows, in_rows, e_send, e_recv)
    plane_signal(line, core, z, low)
    met = greet_rows(row_gaps(fwd.offsets, rows), count)
    barrier = pltpu.get_barrier_semaphore()

    def mask(t, k):
        return mask_ref[t, :, k : k + 1]

    @pl.loop(0, heads)
    def _(step):
        t = heads - 1 - step
        rate = 12 * (t + 1)
        for j in (0, 2, 1):
            summed = None
            for c in range(3):
                k = 3 * j + c
                pltpu.make_async_copy(
                    wa_ref.at[k], wv.at[t, :, k * width : (k + 1) * width], w_sem.at[t * 9 + k]
                ).wait()
                prod = jnp.dot(
                    x_ref[...], wv[t, :, k * width : (k + 1) * width], preferred_element_type=jnp.float32
                )
                if c == 0:
                    summed = jnp.where(mask(t, 1) > 0, pltpu.roll(prod, rate, 0), 0.0)
                elif c == 1:
                    summed = summed + jnp.where(mask(t, 0) > 0, prod, 0.0)
                else:
                    summed = summed + jnp.where(mask(t, 2) > 0, pltpu.roll(prod, px - rate, 0), 0.0)
            if j == 1:
                resp[t] = summed
                continue
            out_rows[t * 2 + j // 2] = summed.astype(jnp.bfloat16)
            if j == 0:

                @pl.when(step == 0)
                def _():
                    pl.semaphore_wait(barrier, 7 + line - 1 + met)

            for h in range(heads):
                pl.when(t == h)(lambda: fwd.start(2 * h + j // 2))

    def stats(ref):
        for h in range(heads):
            total = resp[h]
            for j in (0, 1):
                fwd.wait_recv(2 * h + j)
                total = total + jnp.where(
                    mask(h, 3 + j) > 0, in_rows[2 * h + j].astype(jnp.float32), 0.0
                )
            resp[h] = total
            kept = total * mask(h, 0)
            ref[2 * h : 2 * h + 1] = jnp.sum(kept, axis=0, keepdims=True)
            ref[2 * h + 1 : 2 * h + 2] = jnp.sum(kept * total, axis=0, keepdims=True)

    sums = plane_sum(line, stats, one)
    pixels = par_ref[2 * heads : 2 * heads + 1]
    inverses = []

    def grads(ref):
        for h in range(heads):
            mean = sums[2 * h : 2 * h + 1] / pixels
            var = sums[2 * h + 1 : 2 * h + 2] / pixels - mean * mean
            inverse = lax.rsqrt(var + norm_epsilon)
            inverses.append(inverse)
            scaled = (resp[h] - mean) * inverse
            normed = scaled * par_ref[2 * h : 2 * h + 1] + par_ref[2 * h + 1 : 2 * h + 2]
            s = jax.nn.sigmoid(normed)
            d = cot_ref[h].astype(jnp.float32) * (s * (1.0 + normed * (1.0 - s))) * mask(h, 0)
            resp[h] = scaled
            dn[h] = d
            ref[2 * h : 2 * h + 1] = jnp.sum(d, axis=0, keepdims=True)
            ref[2 * h + 1 : 2 * h + 2] = jnp.sum(d * scaled, axis=0, keepdims=True)

    back = plane_sum(line, grads, two)
    sums_ref[...] = back
    for h in range(heads):
        fwd.wait_send(2 * h)
        fwd.wait_send(2 * h + 1)
        e = (
            mask(h, 0)
            * (inverses[h] * par_ref[2 * h : 2 * h + 1])
            * (dn[h] - back[2 * h : 2 * h + 1] / pixels - resp[h] * (back[2 * h + 1 : 2 * h + 2] / pixels))
        )
        dn[h] = e
        out_rows[2 * h] = jnp.where(mask(h, 3) > 0, e, 0.0).astype(jnp.bfloat16)
        out_rows[2 * h + 1] = jnp.where(mask(h, 4) > 0, e, 0.0).astype(jnp.bfloat16)
        bwd.start(2 * h)
        bwd.start(2 * h + 1)

    def g_copy(t):
        return pltpu.make_async_copy(g_room, g_ref.at[t], g_sem)

    half = width // 2

    def lanes(owner):
        return pl.ds(pl.multiple_of(owner * half, half), half)

    def keep(slot, at):
        return pltpu.make_async_copy(
            dw_room.at[slot, :, lanes(core)], own_ref.at[at], dw_sem.at[slot]
        )

    def hand(slot, at):
        return pltpu.make_async_remote_copy(
            src_ref=dw_room.at[slot, :, lanes(1 - core)],
            dst_ref=got_ref.at[at],
            send_sem=hand_sem.at[slot],
            recv_sem=got_sem,
            device_id=(1 - core, place),
            device_id_type=MESH,
        )

    def put(slot, at):
        return pltpu.make_async_copy(
            dw_room.at[slot], late_ref.at[at - own_ref.shape[0]], dw_sem.at[slot]
        )

    def handed(t):
        return (t + 1) * 9 <= own_ref.shape[0]

    def dw_start(slot, t, k):
        at = t * 9 + k

        @pl.when(handed(t))
        def _():
            keep(slot, at).start()
            hand(slot, at).start()

        pl.when(jnp.logical_not(handed(t)))(lambda: put(slot, at).start())

    def dw_wait(slot, t):
        @pl.when(handed(t))
        def _():
            keep(slot, 0).wait()
            hand(slot, 0).wait_send()

        pl.when(jnp.logical_not(handed(t)))(lambda: put(slot, own_ref.shape[0]).wait())

    def weigh(t, k, number, before):
        slot = lax.rem(number, 2)
        pl.when(number >= 2)(lambda: dw_wait(slot, before))
        dw_room[slot] = jnp.dot(
            xt_ref[...],
            taps[:, pl.ds(pl.multiple_of(k * width, width), width)],
            preferred_element_type=jnp.float32,
        ).astype(jnp.bfloat16)
        dw_start(slot, t, k)

    def spread(t, j, arrived):
        rate = 12 * (t + 1)
        for c in range(3):
            if c == 0:
                tap = pltpu.roll(jnp.where(mask(t, 1) > 0, arrived, 0.0), px - rate, 0)
            elif c == 1:
                tap = jnp.where(mask(t, 0) > 0, arrived, 0.0)
            else:
                tap = pltpu.roll(jnp.where(mask(t, 2) > 0, arrived, 0.0), rate, 0)
            k = 3 * j + c
            taps[:, k * width : (k + 1) * width] = tap.astype(jnp.bfloat16)

    tiles = wv.shape[1] // width
    sq_ref[...] = jnp.zeros_like(sq_ref)

    def center(t):
        spread(t, 1, dn[t].astype(jnp.bfloat16).astype(jnp.float32))

    @pl.loop(0, heads)
    def _(t):
        center(t)
        pl.loop(0, 3)(lambda k: weigh(t, 3 + k, t * 3 + k, t - jnp.where(k < 2, 1, 0)))

    @pl.loop(0, heads)
    def _(t):
        center(t)
        for h in range(heads):
            @pl.when(t == h)
            def _():
                bwd.wait_recv(2 * h)
                bwd.wait_recv(2 * h + 1)

        spread(t, 0, jnp.where(mask(t, 5) > 0, in_rows[2 * t].astype(jnp.float32), 0.0))
        spread(t, 2, jnp.where(mask(t, 6) > 0, in_rows[2 * t + 1].astype(jnp.float32), 0.0))

        pl.loop(0, 6)(
            lambda k: weigh(
                t,
                k + jnp.where(k >= 3, 3, 0),
                3 * heads + t * 6 + k,
                jnp.where(k < 2, jnp.where(t > 0, t - 1, heads - 1), t),
            )
        )
        pl.when(t > 0)(lambda: g_copy(t - 1).wait())
        def tile(n, square):
            cut = pl.ds(pl.multiple_of(n * width, width), width)
            g = lax.dot_general(
                taps[...], wv[t, cut, :], (((1,), (1,)), ((), ())), preferred_element_type=jnp.float32
            )
            g_room[:, cut] = g
            return square + jnp.sum(g * g, axis=0, keepdims=True)

        square = lax.fori_loop(0, tiles, tile, jnp.zeros((1, width), jnp.float32))
        sq_ref[pl.ds(t, 1)] = square
        g_copy(t).start()

    g_copy(heads - 1).wait()
    dw_wait(0, heads - 1)
    dw_wait(1, heads - 1)
    pltpu.make_async_copy(got_ref, got_ref, got_sem).wait()

    def fill(ref):
        ref[...] = sq_ref[...]

    sq_ref[...] = plane_sum(line, fill, three)
    for k in range(2 * heads):
        bwd.wait_send(k)


def heads_step(trunk_out, early, late, cotangent, params, masks, rates, rows, cols, handed, number):
    px, channels = trunk_out.shape
    heads, width = len(rates), early.shape[-1]
    count = lax.axis_size("fsdp")
    line = count // 4
    bf, f32 = jnp.bfloat16, jnp.float32
    dma = pltpu.SemaphoreType.DMA
    vmem = pl.BlockSpec(memory_space=pltpu.VMEM)
    hbm = pl.BlockSpec(memory_space=pl.ANY)
    return pl.pallas_call(
        functools.partial(heads_kernel, rates, rows, cols, count),
        out_shape=(
            jax.ShapeDtypeStruct((heads, px, channels), f32),
            jax.ShapeDtypeStruct((9 * handed, channels, width // 2), bf),
            jax.ShapeDtypeStruct((9 * handed, channels, width // 2), bf),
            jax.ShapeDtypeStruct((9 * (heads - handed), channels, width), bf),
            jax.ShapeDtypeStruct((2 * heads, width), f32),
            jax.ShapeDtypeStruct((8, width), f32),
        ),
        in_specs=[vmem, vmem, hbm, hbm, vmem, vmem, vmem],
        out_specs=(hbm, hbm, hbm, hbm, vmem, vmem),
        scratch_shapes=[
            pltpu.VMEM((heads, channels, 9 * width), bf),
            pltpu.VMEM((2 * heads, px, width), bf),
            pltpu.VMEM((2 * heads, px, width), bf),
            pltpu.VMEM((heads, px, width), f32),
            pltpu.VMEM((heads, px, width), f32),
            pltpu.VMEM((px, 9 * width), bf),
            pltpu.VMEM((px, channels), f32),
            pltpu.VMEM((2, channels, width), bf),
            dma((9 * heads,)),
            dma((2 * heads, 2)),
            dma((2 * heads, 2)),
            dma((2 * heads, 2)),
            dma((2 * heads, 2)),
            dma,
            dma((2,)),
            dma((2,)),
            dma,
        ]
        + plane_scratch(line, (2 * heads, width))
        + plane_scratch(line, (2 * heads, width))
        + plane_scratch(line, (8, width)),
        compiler_params=pltpu.CompilerParams(
            collective_id=number, has_side_effects=True, vmem_limit_bytes=62 * 2**20
        ),
    )(trunk_out, trunk_out.T, early, late, cotangent, params, masks)


class Fan:
    def __init__(self, t, arrays, sends, arrives, shares, own_sem):
        self.t, self.arrays = t, arrays
        self.sends, self.arrives, self.shares, self.own_sem = sends, arrives, shares, own_sem

    def copy(self, k, kind, block, peer, own=False):
        src, place = self.arrays[k]
        dst = place(block, self.t.core)
        return pltpu.make_async_remote_copy(
            src_ref=src if own else dst,
            dst_ref=dst,
            send_sem=self.sends.at[k, kind, block],
            recv_sem=(self.shares if kind == 4 else self.arrives).at[k, block],
            device_id=peer,
            device_id_type=MESH,
        )

    def fan(self, k, block, own, down, up, a, b, finish):
        t = self.t

        def act(kind, peer):
            c = self.copy(k, kind, block, peer, own)
            c.wait_send() if finish else c.start()

        if down:
            pl.when(t.z > 0)(lambda: act(0, t.down))
        if up:
            pl.when(t.z < t.line - 1)(lambda: act(1, t.up))
        if a:
            act(2, t.a)
        if b:
            act(3, t.b)
        act(4, t.partner)

    def stay(self, k):
        src, place = self.arrays[k]
        return pltpu.make_async_copy(src, place(self.t.place, self.t.core), self.own_sem.at[k])

    def own(self, ks, finish=False):
        for k in ks:
            if not finish:
                self.stay(k).start()
            self.fan(k, self.t.place, True, True, True, True, True, finish)

    def step(self, ks, s, move, down, up, a, b, finish):
        t = self.t
        for k in ks:
            def one(block, down, up):
                if not finish:
                    self.copy(k, 0, block, t.partner).wait_recv()
                self.fan(k, block, False, down, up, a, b, finish)

            pl.when(t.z - s >= 0)(lambda: one(t.place - 4 * s + move, down, False))
            if s:
                pl.when(t.z + s < t.line)(lambda: one(t.place + 4 * s + move, False, up))

    def steps(self, ks, finish=False):
        t = self.t
        result = []
        for s in range(1, t.line):
            result.append(lambda s=s: self.along(ks, s, finish))
            result.append(lambda s=s: self.step(ks, s - 1, t.move_a, False, False, False, True, finish))
        result.append(lambda: self.step(ks, t.line - 1, t.move_a, False, False, False, True, finish))
        tail = []
        for s in range(t.line):
            tail.append(lambda s=s: self.step(ks, s, t.move_b, False, False, False, False, finish))
            tail.append(
                lambda s=s: self.step(ks, s, t.move_a + t.move_b, False, False, False, False, finish)
            )
        return result, tail

    def along(self, ks, s, finish):
        t = self.t
        for k in ks:
            def one(block, down, up):
                if not finish:
                    self.copy(k, 0, block, t.partner).wait_recv()
                self.fan(k, block, False, down, up, True, True, finish)

            pl.when(t.z - s >= 0)(lambda: one(t.place - 4 * s, False, True))
            pl.when(t.z + s < t.line)(lambda: one(t.place + 4 * s, True, False))

    def wait_shares(self, ks):
        t = self.t
        for k in ks:
            self.stay(k).wait()

        @pl.loop(0, t.count)
        def _(block):
            for k in ks:
                other = self.arrays[k][1](block, 1 - t.core)
                pltpu.make_async_remote_copy(
                    src_ref=other,
                    dst_ref=other,
                    send_sem=self.sends.at[k, 4, block],
                    recv_sem=self.shares.at[k, block],
                    device_id=t.partner,
                    device_id_type=MESH,
                ).wait_recv()

    def finish(self, ks):
        self.own(ks, True)
        first, tail = self.steps(ks, True)
        for f in first + tail:
            f()


def silu(v):
    return v * jax.nn.sigmoid(v)


def scale_rows(sums, pixels):
    mean = sums[0:1] / pixels
    var = sums[1:2] / pixels - mean * mean
    return mean, lax.rsqrt(var + norm_epsilon)


def trunk_kernel(
    rate, rows, cols, count,
    x_ref, wr_s, wd_s, we_s, wh_s, par_ref, par3_ref, mask_ref,
    wr_o, wd_o, we_o, wh_o, out_ref, sc1_ref, sc2_ref, sc3_ref, s1_ref, s2_ref, s3_ref,
    wr_v, wd_v, we_v, ext, taps,
    sends, arrives, shares, own_sem, save_sem, h_send, h_recv, *rooms,
):
    px = rows * cols
    line = count // 4
    middle = par_ref.shape[1]
    channels = out_ref.shape[1]
    t = Tree()
    one, two, three = rooms[:7], rooms[7:14], rooms[14:]
    halo = rate * cols

    def cut(start, size, step=8):
        return pl.ds(pl.multiple_of(start, step), size)

    def rows_array(shard, full):
        size = shard.shape[0]
        return (
            shard.at[cut(t.core * (size // 2), size // 2, 16)],
            lambda block, core: full.at[cut(block * size + core * (size // 2), size // 2, 16)],
        )

    half_e = we_s.shape[0] // 2
    half_h = wh_s.shape[1] // 2
    fan = Fan(
        t,
        [
            rows_array(wr_s, wr_v),
            rows_array(wd_s, wd_v),
            (
                we_s.at[cut(t.core * half_e, half_e, 16)],
                lambda block, core: we_v.at[
                    cut(core * half_e, half_e, 16), cut(block * we_s.shape[1], we_s.shape[1], 128)
                ],
            ),
            (
                wh_s.at[:, cut(t.core * half_h, half_h, 16)],
                lambda block, core: wh_o.at[:, block, cut(core * half_h, half_h, 16)],
            ),
        ],
        sends, arrives, shares, own_sem,
    )
    plane_signal(line, t.core, t.z, t.low)
    met = greet_rows((-1, 1), count)
    pl.semaphore_wait(pltpu.get_barrier_semaphore(), 7 + line - 1 + met)
    small, heads = (0, 1, 2), (3,)
    fan.own(small)
    first_steps, first_tail = fan.steps(small)
    for f in first_steps:
        f()
    fan.own(heads)
    for f in first_tail:
        f()
    head_steps, head_tail = fan.steps(heads)
    queue = head_steps + head_tail

    def forward(number):
        for _ in range(number):
            if queue:
                queue.pop(0)()

    pixels = par_ref[4:5]

    def mask(k):
        return mask_ref[:, k : k + 1]

    def moments_of(v, ref, at):
        kept = v * mask(0)
        ref[at : at + 1] = jnp.sum(kept, axis=0, keepdims=True)
        ref[at + 1 : at + 2] = jnp.sum(kept * v, axis=0, keepdims=True)

    fan.wait_shares((0,))
    sc1_ref[...] = jnp.dot(x_ref[...], wr_v[...], preferred_element_type=jnp.float32)
    forward(1)
    s1_ref[...] = plane_sum(line, lambda ref: moments_of(sc1_ref[...], ref, 0), one)
    mean, inverse = scale_rows(s1_ref, pixels)
    scaled = (sc1_ref[...] - mean) * inverse
    sc1_ref[...] = scaled
    ext[halo : halo + px] = silu(scaled * par_ref[0:1] + par_ref[1:2]).astype(jnp.bfloat16)

    def edge(up):
        src = ext.at[pl.ds(halo if not up else halo + px - halo, halo)]
        dst = ext.at[pl.ds(halo + px if not up else 0, halo)]
        return pltpu.make_async_remote_copy(
            src_ref=src,
            dst_ref=dst,
            send_sem=h_send.at[int(up)],
            recv_sem=h_recv.at[int(up)],
            device_id=t.at(t.place + (1 if up else -1)),
            device_id_type=MESH,
        )

    has_next, has_last = t.place < count - 1, t.place > 0
    pl.when(has_last)(lambda: edge(False).start())
    pl.when(has_next)(lambda: edge(True).start())
    fan.wait_shares((1, 2))
    forward(2)
    saves = [
        pltpu.make_async_copy(wr_v, wr_o, save_sem.at[0]),
        pltpu.make_async_copy(wd_v, wd_o, save_sem.at[1]),
        pltpu.make_async_copy(we_v, we_o, save_sem.at[2]),
    ]
    for save in saves:
        save.start()
    pl.when(has_next)(lambda: edge(False).wait_recv())
    pl.when(has_last)(lambda: edge(True).wait_recv())
    for j in range(3):
        v = ext[j * halo : j * halo + px].astype(jnp.float32)
        kept_row = 1.0 if j == 1 else mask(3 + j // 2)
        for c in range(3):
            moved = v if c == 1 else pltpu.roll(v, rate if c == 0 else px - rate, 0)
            kept = mask((1, 0, 2)[c]) * kept_row
            k = 3 * j + c
            taps[:, k * middle : (k + 1) * middle] = jnp.where(kept > 0, moved, 0.0).astype(jnp.bfloat16)
    sc2_ref[...] = jnp.dot(taps[...], wd_v[...], preferred_element_type=jnp.float32)
    forward(2)
    s2_ref[...] = plane_sum(line, lambda ref: moments_of(sc2_ref[...], ref, 0), two)
    mean, inverse = scale_rows(s2_ref, pixels)
    scaled = (sc2_ref[...] - mean) * inverse
    sc2_ref[...] = scaled
    hidden = silu(scaled * par_ref[2:3] + par_ref[3:4]).astype(jnp.bfloat16)
    forward(2)
    parts = channels // middle

    def wide(ref):
        for q in range(parts):
            third = jnp.dot(
                hidden, we_v[:, q * middle : (q + 1) * middle], preferred_element_type=jnp.float32
            )
            sc3_ref[:, q * middle : (q + 1) * middle] = third
            moments_of(third, ref, 2 * q)

    s3_ref[...] = plane_sum(line, wide, three)
    forward(1)
    for q in range(parts):
        at = slice(q * middle, (q + 1) * middle)
        mean, inverse = scale_rows(s3_ref[2 * q : 2 * q + 2], pixels)
        scaled = (sc3_ref[:, at] - mean) * inverse
        sc3_ref[:, at] = scaled
        pre = x_ref[:, at].astype(jnp.float32) + (
            scaled * par3_ref[2 * q : 2 * q + 1] + par3_ref[2 * q + 1 : 2 * q + 2]
        )
        out_ref[:, at] = silu(pre).astype(jnp.bfloat16)
    forward(len(queue))
    fan.wait_shares(heads)
    for save in saves:
        save.wait()
    pl.when(has_last)(lambda: edge(False).wait_send())
    pl.when(has_next)(lambda: edge(True).wait_send())
    fan.finish(small + heads)


def trunk_step(x, shards, params, params3, masks, rate, rows, cols, number):
    px, channels = x.shape
    count = lax.axis_size("fsdp")
    line = count // 4
    middle = params.shape[1]
    bf, f32 = jnp.bfloat16, jnp.float32
    dma = pltpu.SemaphoreType.DMA
    vmem = pl.BlockSpec(memory_space=pltpu.VMEM)
    hbm = pl.BlockSpec(memory_space=pl.ANY)
    parts = channels // middle
    heads, head_rows, width = shards[3].shape
    S = jax.ShapeDtypeStruct
    return pl.pallas_call(
        functools.partial(trunk_kernel, rate, rows, cols, count),
        out_shape=(
            S((channels, middle), bf),
            S((9 * middle, middle), bf),
            S((middle, channels), bf),
            S((heads, count, head_rows, width), bf),
            S((px, channels), bf),
            S((px, middle), f32),
            S((px, middle), f32),
            S((px, channels), f32),
            S((2, middle), f32),
            S((2, middle), f32),
            S((2 * parts, middle), f32),
        ),
        in_specs=[vmem] + [hbm] * 4 + [vmem] * 3,
        out_specs=(hbm,) * 4 + (vmem,) * 7,
        scratch_shapes=[
            pltpu.VMEM((channels, middle), bf),
            pltpu.VMEM((9 * middle, middle), bf),
            pltpu.VMEM((middle, channels), bf),
            pltpu.VMEM((px + 2 * rate * cols, middle), bf),
            pltpu.VMEM((px, 9 * middle), bf),
            dma((4, 5, count)),
            dma((4, count)),
            dma((4, count)),
            dma((4,)),
            dma((3,)),
            dma((2,)),
            dma((2,)),
        ]
        + plane_scratch(line, (2, middle))
        + plane_scratch(line, (2, middle))
        + plane_scratch(line, (2 * parts, middle)),
        compiler_params=pltpu.CompilerParams(
            collective_id=number, has_side_effects=True, vmem_limit_bytes=56 * 2**20
        ),
    )(x, *shards, params, params3, masks)


FEED = {'join': 2, 'pass': 1, 'keep': 1, 'third': 1, 'd2': 2, 'ge': 2, 'edge': 3, 'd1': 1, 'gd': 1, 'later3': 4, 'later2': 4, 'later1': 8}


def nt(a, b):
    return lax.dot_general(a, b, (((1,), (1,)), ((), ())), preferred_element_type=jnp.float32)


def tn(a, b):
    return lax.dot_general(a, b, (((0,), (0,)), ((), ())), preferred_element_type=jnp.float32)


def slope(v):
    s = jax.nn.sigmoid(v)
    return s * (1.0 + v * (1.0 - s))


def back_kernel(
    rate, rows, cols, count, heads,
    x_ref, tw_ref, sc1_ref, sc2_ref, par_ref, par3_ref, s1_ref, s2_ref, s3_ref, mask_ref,
    g_ref, sc3_ref, wr_ref, wd_ref, we_ref, own_ref, got_ref,
    bs1_ref, bs2_ref, bs3_ref, fg_ref, gr_ref, gd_ref, ge_ref, sum_ref,
    b_send, acc, b_room, extra, g_room, s_room, dpre, dthird, wr_v, wd_v, we_v, ext, taps, out_room, grad_room,
    load_sem, extra_sem, bs_sem, br_sem, g_sem, s_sem, w_sem, h_send, h_recv, out_sem, grad_sem, sum_sem, *rooms,
):
    px = rows * cols
    line = count // 4
    middle = par_ref.shape[1]
    channels = x_ref.shape[1]
    parts = channels // middle
    wide = g_room.shape[-1]
    chunks = channels // wide
    halo = rate * cols
    t = Tree()
    one, two, three = rooms[:7], rooms[7:14], rooms[14:]
    bf, f32 = jnp.bfloat16, jnp.float32

    weights = [
        pltpu.make_async_copy(we_ref, we_v, w_sem.at[0]),
        pltpu.make_async_copy(wd_ref, wd_v, w_sem.at[1]),
        pltpu.make_async_copy(wr_ref, wr_v, w_sem.at[2]),
    ]

    def lanes(c):
        return pl.ds(c * wide, wide)

    def g_load(c):
        return pltpu.make_async_copy(g_ref.at[:, :, lanes(c)], g_room.at[c % 2], g_sem.at[c % 2])

    def s_load(c):
        return pltpu.make_async_copy(sc3_ref.at[:, lanes(c)], s_room.at[c % 2], s_sem.at[c % 2])

    moves = (t.move_b, t.move_a + t.move_b, 0, t.move_a)

    def pair(n, w):
        block = n * 4 + t.low + moves[w]
        room = (b_send if w < 2 else acc).at[n * 2 + w % 2]
        slot = w % 2
        return (
            pltpu.make_async_copy(own_ref.at[:, block], room, load_sem.at[slot]),
            pltpu.make_async_copy(got_ref.at[:, block], extra.at[slot], extra_sem.at[slot]),
        )

    def join(n, w):
        for c in pair(n, w):
            c.wait()
        room = b_send if w < 2 else acc
        at = n * 2 + w % 2

        @pl.loop(0, heads)
        def _(h):
            room[at, h] = room[at, h] + extra[w % 2, h]

    def to_b(n, w, piece=None):
        at = (n * 2 + w,)
        if piece is not None:
            at = at + (piece[0], pl.ds(piece[1], piece[2]))
        return pltpu.make_async_remote_copy(
            src_ref=b_send.at[at],
            dst_ref=b_room.at[at],
            send_sem=bs_sem.at[n * 2 + w],
            recv_sem=br_sem.at[n * 2 + w],
            device_id=t.b,
            device_id_type=MESH,
        )

    head_rows = b_send.shape[2]
    size = head_rows // 4
    pieces = [
        to_b(n, w, (h, r, size))
        for n in range(line)
        for w in (1, 0)
        for h in range(heads)
        for r in range(0, head_rows, size)
    ]

    def feed(number):
        for _ in range(min(number, len(pieces))):
            pieces.pop(0).start()

    plane_signal(line, t.core, t.z, t.low)
    met = greet_rows((-1, 1), count)
    for w in (1, 0):
        for c in pair(0, w):
            c.start()
    for c in weights:
        c.start()
    for c in (0, 1):
        g_load(c).start()
        s_load(c).start()
    pl.semaphore_wait(pltpu.get_barrier_semaphore(), 7 + line - 1 + met)

    for n in range(line):
        for w in (1, 0):
            join(n, w)
            feed(FEED["join"])
            if n < line - 1:
                for c in pair(n + 1, w):
                    c.start()

    for w in (3, 2):
        for c in pair(0, w):
            c.start()

    def mask(k):
        return mask_ref[:, k : k + 1]

    pixels = par_ref[4:5]
    pixels_wide = pixels[:, :wide]

    def third_params(c):
        q, at = (c * wide) // middle, (c * wide) % middle
        at = slice(at, at + wide)
        return 2 * q, at

    def moved_sums(ref, row, at, d, scaled):
        ref[row : row + 1, at] = jnp.sum(d, axis=0, keepdims=True)
        ref[row + 1 : row + 2, at] = jnp.sum(d * scaled, axis=0, keepdims=True)

    def first_pass(ref):
        for c in range(chunks):
            g_load(c).wait()
            s_load(c).wait()
            row, at = third_params(c)
            total = tw_ref[0:1, 0:1] * g_room[c % 2, 0]
            for h in range(1, g_ref.shape[0]):
                total = total + tw_ref[h : h + 1, 0:1] * g_room[c % 2, h]
            scaled = s_room[c % 2]
            here = slice(c * wide, (c + 1) * wide)
            pre = x_ref[:, here].astype(f32) + (
                scaled * par3_ref[row : row + 1, at] + par3_ref[row + 1 : row + 2, at]
            )
            d = total * slope(pre)
            dpre[:, here] = d
            d = d * mask(0)
            moved_sums(ref, row, at, d, scaled)
            feed(FEED["pass"])
            if c + 2 < chunks:
                g_load(c + 2).start()
                s_load(c + 2).start()
        for c in (0, 1):
            s_load(c).start()

    def keep_rest():
        for n in range(line):
            for w in (3, 2):
                feed(FEED["keep"])
                join(n, w)
                if n < line - 1:
                    for c in pair(n + 1, w):
                        c.start()

    back3 = plane_sum(line, first_pass, three, keep_rest, lambda: feed(FEED["later3"]))
    bs3_ref[...] = back3
    for c in range(chunks):
        s_load(c).wait()
        row, at = third_params(c)
        mean = s3_ref[row : row + 1, at] / pixels_wide
        var = s3_ref[row + 1 : row + 2, at] / pixels_wide - mean * mean
        inverse = lax.rsqrt(var + norm_epsilon)
        here = slice(c * wide, (c + 1) * wide)
        v = (
            mask(0)
            * (inverse * par3_ref[row : row + 1, at])
            * (
                dpre[:, here] * mask(0)
                - back3[row : row + 1, at] / pixels_wide
                - s_room[c % 2] * (back3[row + 1 : row + 2, at] / pixels_wide)
            )
        )
        dthird[:, here] = v.astype(bf)
        feed(FEED["third"])
        if c + 2 < chunks:
            s_load(c + 2).start()
    weights[0].wait()
    scaled2 = sc2_ref[...]
    normed2 = scaled2 * par_ref[2:3] + par_ref[3:4]
    feed(FEED["d2"])
    d2 = nt(dthird[...], we_v[...]) * slope(normed2) * mask(0)

    state = []

    def put(value, *targets):
        n = len(state)
        if n >= 2:
            for c in state[n - 2]:
                c.wait()
        grad_room[n % 2] = value.astype(bf)
        cols = middle // len(targets)
        state.append(
            [
                pltpu.make_async_copy(
                    grad_room.at[n % 2, :, pl.ds(i * cols, cols)], ref, grad_sem.at[n % 2, i]
                )
                for i, ref in enumerate(targets)
            ]
        )
        for c in state[n]:
            c.start()

    hidden2 = silu(normed2).astype(bf)

    def expand_grads():
        for q in range(parts):
            feed(FEED["ge"])
            per = count // parts
            put(
                tn(hidden2, dthird[:, q * middle : (q + 1) * middle]),
                *(ge_ref.at[q * per + i] for i in range(per)),
            )

    back2 = plane_sum(
        line, lambda ref: moved_sums(ref, 0, slice(None), d2, scaled2), two, expand_grads,
        lambda: feed(FEED["later2"]),
    )
    bs2_ref[...] = back2

    def through(d, scaled, sums, back, gain):
        _, inverse = scale_rows(sums, pixels)
        return mask(0) * (inverse * gain) * (d - back[0:1] / pixels - scaled * (back[1:2] / pixels))

    ext[halo : halo + px] = through(d2, scaled2, s2_ref, back2, par_ref[2:3]).astype(bf)

    def edge(up):
        src = ext.at[pl.ds(px if up else halo, halo)]
        dst = ext.at[pl.ds(0 if up else halo + px, halo)]
        return pltpu.make_async_remote_copy(
            src_ref=src,
            dst_ref=dst,
            send_sem=h_send.at[int(up)],
            recv_sem=h_recv.at[int(up)],
            device_id=t.at(t.place + (1 if up else -1)),
            device_id_type=MESH,
        )

    has_next, has_last = t.place < count - 1, t.place > 0
    pl.when(has_last)(lambda: edge(False).start())
    pl.when(has_next)(lambda: edge(True).start())
    weights[1].wait()
    scaled1 = sc1_ref[...]
    normed1 = scaled1 * par_ref[0:1] + par_ref[1:2]
    hidden1 = silu(normed1).astype(bf)

    def spread(j):
        v = ext[(2 - j) * halo : (2 - j) * halo + px].astype(f32)
        kept_row = 1.0 if j == 1 else mask(4 if j == 0 else 3)
        for c in range(3):
            if c == 0:
                moved, kept = pltpu.roll(v, px - rate, 0), mask(2)
            elif c == 1:
                moved, kept = v, mask(0)
            else:
                moved, kept = pltpu.roll(v, rate, 0), mask(1) * mask(0)
            k = 3 * j + c
            taps[:, k * middle : (k + 1) * middle] = jnp.where(kept * kept_row > 0, moved, 0.0).astype(bf)

    def tap(k):
        return taps[:, k * middle : (k + 1) * middle]

    feed(FEED["edge"])
    spread(1)
    d1 = None
    for j in (1, 0, 2):
        if j == 0:
            pl.when(has_next)(lambda: edge(False).wait_recv())
            pl.when(has_last)(lambda: edge(True).wait_recv())
            spread(0)
            spread(2)
        for c in range(3):
            k = 3 * j + c
            feed(FEED["d1"])
            part = nt(tap(k), wd_v[k * middle : (k + 1) * middle])
            d1 = part if d1 is None else d1 + part
    d1 = d1 * slope(normed1) * mask(0)

    def dilated_grads():
        for k in range(9):
            feed(FEED["gd"])
            put(tn(hidden1, tap(k)), gd_ref.at[k])

    back1 = plane_sum(
        line, lambda ref: moved_sums(ref, 0, slice(None), d1, scaled1), one, dilated_grads,
        lambda: feed(FEED["later1"]),
    )
    bs1_ref[...] = back1
    dfirst = through(d1, scaled1, s1_ref, back1, par_ref[0:1]).astype(bf)
    feed(len(pieces))
    weights[2].wait()
    outs = []
    for q in range(parts):
        here = slice(q * middle, (q + 1) * middle)
        if q >= 2:
            outs[q - 2].wait()
        out_room[q % 2] = nt(dfirst, wr_v[here]) + dpre[:, here]
        outs.append(
            pltpu.make_async_copy(
                out_room.at[q % 2], fg_ref.at[:, pl.ds(q * middle, middle)], out_sem.at[q % 2]
            )
        )
        outs[q].start()
    for q in range(parts):
        here = slice(q * middle, (q + 1) * middle)
        put(tn(x_ref[:, here], dfirst), gr_ref.at[pl.ds(q * middle, middle)])

    def stays(n):
        return pltpu.make_async_copy(acc.at[n], sum_ref.at[n], sum_sem.at[n])

    @pl.loop(0, line)
    def _(n):
        for w in (1, 0):
            to_b(n, w).wait_recv()
            at = n * 2 + w

            @pl.loop(0, heads)
            def _(h):
                acc[at, h] = acc[at, h] + b_room[at, h]

            stays(at).start()

    for c in state[-2] + state[-1] + outs[-2:]:
        c.wait()

    @pl.loop(0, line)
    def _(n):
        for w in (1, 0):
            to_b(n, w).wait_send()
            stays(n * 2 + w).wait()

    pl.when(has_last)(lambda: edge(False).wait_send())
    pl.when(has_next)(lambda: edge(True).wait_send())


def back_step(x, task_weights, scaled1, scaled2, scaled3, params, params3, sums1, sums2, sums3, masks, grads,
              wr, wd, we, own, got, rate, rows, cols, number):
    px, channels = x.shape
    count = lax.axis_size("fsdp")
    line = count // 4
    middle = params.shape[1]
    parts = channels // middle
    wide = middle // 2
    heads, _, head_rows, half = own.shape
    bf, f32 = jnp.bfloat16, jnp.float32
    dma = pltpu.SemaphoreType.DMA
    vmem = pl.BlockSpec(memory_space=pltpu.VMEM)
    hbm = pl.BlockSpec(memory_space=pl.ANY)
    S = jax.ShapeDtypeStruct
    V = pltpu.VMEM
    return pl.pallas_call(
        functools.partial(back_kernel, rate, rows, cols, count, heads),
        out_shape=(
            S((2, middle), f32),
            S((2, middle), f32),
            S((2 * parts, middle), f32),
            S((px, channels), f32),
            S((channels, middle), bf),
            S((9, middle, middle), bf),
            S((count, middle, channels // count), bf),
            S((2 * line, heads, head_rows, half), bf),
        ),
        in_specs=[vmem] * 10 + [hbm] * 7,
        out_specs=(vmem,) * 3 + (hbm,) * 5,
        scratch_shapes=[
            V((2 * line, heads, head_rows, half), bf),
            V((2 * line, heads, head_rows, half), bf),
            V((2 * line, heads, head_rows, half), bf),
            V((2, heads, head_rows, half), bf),
            V((2, grads.shape[0], px, wide), f32),
            V((2, px, wide), f32),
            V((px, channels), f32),
            V((px, channels), bf),
            V((channels, middle), bf),
            V((9 * middle, middle), bf),
            V((middle, channels), bf),
            V((px + 2 * rate * cols, middle), bf),
            V((px, 9 * middle), bf),
            V((2, px, middle), f32),
            V((2, middle, middle), bf),
            dma((2,)),
            dma((2,)),
            dma((2 * line,)),
            dma((2 * line,)),
            dma((2,)),
            dma((2,)),
            dma((3,)),
            dma((2,)),
            dma((2,)),
            dma((2,)),
            dma((2, count // parts)),
            dma((2 * line,)),
        ]
        + plane_scratch(line, (2, middle))
        + plane_scratch(line, (2, middle))
        + plane_scratch(line, (2 * parts, middle)),
        compiler_params=pltpu.CompilerParams(
            collective_id=number, has_side_effects=True, vmem_limit_bytes=63 * 2**20
        ),
    )(x, task_weights, scaled1, scaled2, params, params3, sums1, sums2, sums3, masks,
      grads, scaled3, wr, wd, we, own, got)


def silu_slope(values):
    sigmoid_value = jax.nn.sigmoid(values)
    return sigmoid_value * (1.0 + values * (1.0 - sigmoid_value))


def shift_along(values, offset, axis_number):
    if offset == 0:
        return values
    length = values.shape[axis_number]
    pad_shape = list(values.shape)
    pad_shape[axis_number] = abs(offset)
    zero_block = jnp.zeros(pad_shape, values.dtype)
    if offset > 0:
        return jnp.concatenate(
            [lax.slice_in_dim(values, offset, length, axis=axis_number), zero_block], axis_number
        )
    return jnp.concatenate(
        [zero_block, lax.slice_in_dim(values, 0, length + offset, axis=axis_number)], axis_number
    )


def inside_rows(layout, offset):
    row_ids, row_top, row_bottom, row_side = layout
    return (row_ids + offset >= row_top) & (row_ids + offset < row_bottom)


def inside_cols(layout, offset, col_count):
    row_ids, row_top, row_bottom, row_side = layout
    columns = jnp.arange(col_count, dtype=jnp.int32)
    return (columns[None, :] + offset >= 0) & (columns[None, :] + offset < row_side[:, None])


def column_sums(inputs, weight, rate, layout):
    col_count = inputs.shape[1]
    products = jnp.einsum("rwc,kco->krwo", inputs, weight, preferred_element_type=jnp.float32)
    sums = []
    for row_step in range(3):
        summed = 0.0
        for col_step in range(3):
            across = (col_step - 1) * rate
            summed = summed + jnp.where(
                inside_cols(layout, across, col_count)[:, :, None],
                shift_along(products[3 * row_step + col_step], across, 1),
                0.0,
            )
        sums.append(summed)
    return sums


def dilated_forward(inputs, weights, rates, layout, number):
    outer, centers = [], []
    for weight, rate in zip(weights, rates):
        low, center, high = column_sums(inputs, weight, rate, layout)
        outer += [low.astype(jnp.bfloat16), high.astype(jnp.bfloat16)]
        centers.append(center)
    offsets = tuple(o for rate in rates for o in (-rate, rate))
    pulled = exchange(jnp.stack(outer), offsets, number)
    results = []
    for k, (center, rate) in enumerate(zip(centers, rates)):
        for j, down in ((2 * k, -rate), (2 * k + 1, rate)):
            center = center + jnp.where(
                inside_rows(layout, down)[:, None, None], pulled[j].astype(jnp.float32), 0.0
            )
        results.append(center)
    return results


def spread_taps(grads, rates, layout, number):
    row_ids = layout[0]
    row_count, col_count = grads[0].shape[:2]
    total_rows = row_count * lax.axis_size("fsdp")
    outer = []
    for grad, rate in zip(grads, rates):
        for down in (-rate, rate):
            outer.append(
                jnp.where(inside_rows(layout, down)[:, None, None], grad, jnp.bfloat16(0.0))
            )
    offsets = tuple(o for rate in rates for o in (rate, -rate))
    pulled = exchange(jnp.stack(outer), offsets, number)
    results = []
    for k, (grad, rate) in enumerate(zip(grads, rates)):
        taps = []
        for row_step in range(3):
            down = (row_step - 1) * rate
            if row_step == 1:
                arrived = grad
            else:
                there = (row_ids - down >= 0) & (row_ids - down < total_rows)
                arrived = jnp.where(
                    there[:, None, None], pulled[2 * k + row_step // 2], jnp.bfloat16(0.0)
                )
            for col_step in range(3):
                across = (col_step - 1) * rate
                kept = jnp.where(
                    inside_cols(layout, across, col_count)[:, :, None], arrived, jnp.bfloat16(0.0)
                )
                taps.append(shift_along(kept, -across, 1))
        results.append(taps)
    return results


def spread(stat):
    return stat.reshape(stat.shape[:-1] + (1, 1) + stat.shape[-1:])


def totals_of(one, two, number):
    local_sums = jnp.stack([jnp.sum(one, axis=(-3, -2)), jnp.sum(two, axis=(-3, -2))])
    flat = all_sum(local_sums.reshape(2, -1), number)
    return flat.reshape(local_sums.shape)


def moments(values, valid_mask, number):
    weighted = values * valid_mask[..., None]
    return totals_of(weighted, weighted * values, number)


def normalize(values, sums, valid_count, gain_row, bias_row):
    mean_value = sums[0] / valid_count
    variance = sums[1] / valid_count - mean_value * mean_value
    inverse = lax.rsqrt(variance + norm_epsilon)
    scaled = (values - spread(mean_value)) * spread(inverse)
    return (scaled, inverse, scaled * spread(gain_row) + spread(bias_row))


def norm_backward(grad_norm, scaled, inverse, gain_row, valid_mask, valid_count, number):
    masked = grad_norm * valid_mask[..., None]
    sums = totals_of(masked, masked * scaled, number)
    grad_values = (
        valid_mask[..., None]
        * spread(inverse * gain_row)
        * (masked - spread(sums[0] / valid_count) - scaled * spread(sums[1] / valid_count))
    )
    return (grad_values, sums)


def update(param, moment, grad):
    moment_new = momentum_decay * moment + grad
    return (param - step_rate * moment_new, moment_new)


def local(
    features,
    cotangent,
    crop_heights,
    task_scale,
    w_reduce,
    w_dilated,
    w_expand,
    w_heads,
    norm_params,
    m_reduce,
    m_dilated,
    m_expand,
    m_heads,
    norm_moment,
):
    row_count = features.shape[1]
    col_count = features.shape[2]
    channels = features.shape[3]
    middle = w_reduce.shape[1]
    head_width = w_heads.shape[2]
    head_total = w_heads.shape[0]
    group_index = lax.axis_index("dp")
    place_index = lax.axis_index("fsdp")
    group_heights = lax.dynamic_index_in_dim(crop_heights, group_index, 0, keepdims=False)
    crop_order = jnp.arange(group_heights.shape[0], dtype=jnp.int32)
    crop_ends = jnp.sum(
        jnp.where(crop_order[None, :] <= crop_order[:, None], group_heights[None, :], 0),
        axis=1,
        dtype=jnp.int32,
    )
    crop_starts = crop_ends - group_heights
    row_ids = place_index * row_count + jnp.arange(row_count, dtype=jnp.int32)
    member = (row_ids[:, None] >= crop_starts[None, :]) & (row_ids[:, None] < crop_ends[None, :])
    row_top = jnp.sum(jnp.where(member, crop_starts[None, :], 0), axis=1, dtype=jnp.int32)
    row_bottom = jnp.sum(jnp.where(member, crop_ends[None, :], 0), axis=1, dtype=jnp.int32)
    row_side = jnp.sum(jnp.where(member, group_heights[None, :], 0), axis=1, dtype=jnp.int32)
    layout = (row_ids, row_top, row_bottom, row_side)
    valid_mask = (jnp.arange(col_count, dtype=jnp.int32)[None, :] < row_side[:, None]).astype(
        jnp.float32
    )
    valid_count = jnp.sum(crop_heights * crop_heights).astype(jnp.float32)
    gain_values = norm_params[0]
    bias_values = norm_params[1]
    trunk_end = 2 * middle + channels
    inputs = features[0]
    inputs_float = inputs.astype(jnp.float32)
    place_count = lax.axis_size("fsdp")
    pixels = row_count * col_count
    head_gain = gain_values[trunk_end:].reshape(head_total, head_width)
    head_bias = bias_values[trunk_end:].reshape(head_total, head_width)
    head_params = jnp.concatenate(
        [
            jnp.stack([head_gain, head_bias], 1).reshape(2 * head_total, head_width),
            jnp.broadcast_to(valid_count, (2, head_width)),
        ]
    )
    total_rows = row_count * place_count
    masks = []
    for rate in head_rates + (trunk_rate,):
        flags = [
            inside_cols(layout, 0, col_count),
            inside_cols(layout, -rate, col_count),
            inside_cols(layout, rate, col_count),
        ] + [
            jnp.broadcast_to(flag[:, None], (row_count, col_count))
            for flag in (
                inside_rows(layout, -rate),
                inside_rows(layout, rate),
                row_ids + rate < total_rows,
                row_ids - rate >= 0,
            )
        ]
        flags = jnp.stack([f.reshape(pixels) for f in flags], 1).astype(jnp.float32)
        masks.append(jnp.pad(flags, ((0, 0), (0, 128 - flags.shape[1]))))
    half_rows = w_heads.shape[1] // 2
    heads_half = lax.dynamic_slice_in_dim(w_heads, group_index * half_rows, half_rows, 1)

    def beside(part):
        return lax.all_gather(
            part.astype(jnp.bfloat16), ("fsdp", "dp"), axis=1, tiled=True
        ).reshape(-1, channels, head_width)

    heads_late = beside(heads_half[1:])
    if place_count == 16:
        flat_params = jnp.concatenate(
            [
                jnp.stack([gain_values[:middle], bias_values[:middle]]),
                jnp.stack([gain_values[middle : 2 * middle], bias_values[middle : 2 * middle]]),
                jnp.broadcast_to(valid_count, (4, middle)),
            ]
        )
        wide_params = jnp.stack(
            [
                gain_values[2 * middle : trunk_end].reshape(-1, middle),
                bias_values[2 * middle : trunk_end].reshape(-1, middle),
            ],
            1,
        ).reshape(-1, middle)
        (
            reduce_low, dilated_low, expand_low, heads_early, trunk_out,
            scaled_one, scaled_two, scaled_three, sums_in_one, sums_in_two, sums_in_three,
        ) = trunk_step(
            inputs.reshape(pixels, channels),
            (
                w_reduce.astype(jnp.bfloat16),
                w_dilated.astype(jnp.bfloat16),
                w_expand.astype(jnp.bfloat16),
                w_heads[:1].astype(jnp.bfloat16),
            ),
            flat_params,
            wide_params,
            masks[-1],
            trunk_rate,
            row_count,
            col_count,
            0,
        )
        heads_early = heads_early.reshape(-1, channels, head_width)
    else:
        heads_early = beside(heads_half[:1])
        reduce_low, dilated_low, expand_low = (
            lax.all_gather(w.astype(jnp.bfloat16), "fsdp", axis=0)
            for w in (w_reduce, w_dilated, w_expand)
        )
        reduce_low = reduce_low.reshape(channels, middle)
        dilated_low = dilated_low.reshape(9, middle, middle)
        first = jnp.einsum("rwc,cm->rwm", inputs, reduce_low, preferred_element_type=jnp.float32)
        scaled_one, inverse_one, normed_one = normalize(
            first, moments(first, valid_mask, 1), valid_count, gain_values[:middle], bias_values[:middle]
        )
        hidden_one = jax.nn.silu(normed_one).astype(jnp.bfloat16)
        (second,) = dilated_forward(hidden_one, (dilated_low,), (trunk_rate,), layout, 2)
        scaled_two, inverse_two, normed_two = normalize(
            second,
            moments(second, valid_mask, 3),
            valid_count,
            gain_values[middle : 2 * middle],
            bias_values[middle : 2 * middle],
        )
        hidden_two = jax.nn.silu(normed_two).astype(jnp.bfloat16)
        expand_low = expand_low.transpose(1, 0, 2).reshape(middle, channels)
        third = jnp.einsum("rwm,mc->rwc", hidden_two, expand_low, preferred_element_type=jnp.float32)
        scaled_three, inverse_three, normed_three = normalize(
            third,
            moments(third, valid_mask, 4),
            valid_count,
            gain_values[2 * middle : trunk_end],
            bias_values[2 * middle : trunk_end],
        )
        pre_act = inputs_float + normed_three
        trunk_out = jax.nn.silu(pre_act).astype(jnp.bfloat16)
    handed = head_total - 1
    head_grads, grads_own, grads_got, grads_late, head_sums, squares = heads_step(
        trunk_out.reshape(pixels, channels),
        heads_early,
        heads_late,
        cotangent.reshape(head_total, pixels, head_width),
        head_params,
        jnp.stack(masks[:-1]),
        head_rates,
        row_count,
        col_count,
        handed,
        5,
    )
    head_sums = head_sums.reshape(head_total, 2, head_width).transpose(1, 0, 2)
    squares = jnp.sum(squares[:head_total], axis=1)
    task_rms = jnp.sqrt(squares / (valid_count * channels) + task_epsilon)
    task_weight = task_scale / task_rms
    shared = lax.psum_scatter(
        grads_late.reshape(-1, head_width), ("fsdp", "dp"), scatter_dimension=0, tiled=True
    )
    late_total = lax.all_gather(shared, "dp", axis=0, tiled=True)[None]
    if place_count == 16:
        (
            back_one, back_two, back_three, features_grad, grad_reduce, grad_dilated, grad_expand, late,
        ) = back_step(
            inputs.reshape(pixels, channels),
            jnp.broadcast_to(jnp.pad(task_weight, (0, 8 - head_total))[:, None], (8, 128)),
            scaled_one,
            scaled_two,
            scaled_three,
            flat_params,
            wide_params,
            sums_in_one,
            sums_in_two,
            sums_in_three,
            masks[-1],
            head_grads,
            reduce_low,
            dilated_low,
            expand_low,
            grads_own.reshape(handed, place_count, -1, head_width // 2),
            grads_got.reshape(handed, place_count, -1, head_width // 2),
            trunk_rate,
            row_count,
            col_count,
            1,
        )
        features_grad = features_grad.reshape(row_count, col_count, channels)
        *trunk_totals, heads_total = reduce_shards(
            (
                grad_reduce.reshape(1, place_count, -1, middle),
                grad_dilated.reshape(1, place_count, -1, middle),
                grad_expand[None],
            ),
            (late,),
            2,
        )
        trunk_totals = [t[0] for t in trunk_totals]
        sums_one, sums_two = back_one, back_two
        sums_three = back_three.reshape(-1, 2, middle).transpose(1, 0, 2).reshape(2, channels)
    else:
        grad_trunk = task_weight[0] * head_grads[0]
        for k in range(1, head_total):
            grad_trunk = grad_trunk + task_weight[k] * head_grads[k]
        grad_trunk = grad_trunk.reshape(row_count, col_count, channels)
        grad_pre = grad_trunk * silu_slope(pre_act)
        grad_third, sums_three = norm_backward(
            grad_pre,
            scaled_three,
            inverse_three,
            gain_values[2 * middle : trunk_end],
            valid_mask,
            valid_count,
            11,
        )
        grad_third = grad_third.astype(jnp.bfloat16)
        grad_expand = jnp.einsum(
            "rwm,rwc->mc", hidden_two, grad_third, preferred_element_type=jnp.float32
        ).astype(jnp.bfloat16)
        grad_hidden_two = jnp.einsum(
            "rwc,mc->rwm", grad_third, expand_low, preferred_element_type=jnp.float32
        )
        grad_second, sums_two = norm_backward(
            grad_hidden_two * silu_slope(normed_two),
            scaled_two,
            inverse_two,
            gain_values[middle : 2 * middle],
            valid_mask,
            valid_count,
            12,
        )
        (taps,) = spread_taps([grad_second.astype(jnp.bfloat16)], (trunk_rate,), layout, 13)
        taps = jnp.stack(taps)
        grad_hidden_one = jnp.einsum(
            "krwo,kco->rwc", taps, dilated_low, preferred_element_type=jnp.float32
        )
        grad_dilated = jnp.einsum(
            "rwc,krwo->kco", hidden_one, taps, preferred_element_type=jnp.float32
        )
        grad_first, sums_one = norm_backward(
            grad_hidden_one * silu_slope(normed_one),
            scaled_one,
            inverse_one,
            gain_values[:middle],
            valid_mask,
            valid_count,
            14,
        )
        grad_first = grad_first.astype(jnp.bfloat16)
        grad_reduce = jnp.einsum("rwc,rwm->cm", inputs, grad_first, preferred_element_type=jnp.float32)
        features_grad = (
            jnp.einsum("rwm,cm->rwc", grad_first, reduce_low, preferred_element_type=jnp.float32)
            + grad_pre
        )
        trunk_totals = []
        for grad, axis in ((grad_reduce, 0), (grad_dilated.reshape(-1, middle), 0), (grad_expand, 1)):
            shard = lax.psum_scatter(
                grad.astype(jnp.bfloat16), "fsdp", scatter_dimension=axis, tiled=True
            )
            trunk_totals.append(lax.psum(shard, "dp"))
        shared = lax.psum_scatter(
            (grads_own + grads_got).reshape(handed, -1, head_width // 2),
            "fsdp",
            scatter_dimension=1,
            tiled=True,
        )
        heads_total = lax.all_gather(shared, "dp", axis=2, tiled=True)
    totals = tuple(t.astype(jnp.float32) for t in trunk_totals) + (
        task_weight[:, None, None]
        * jnp.concatenate([heads_total, late_total]).astype(jnp.float32),
    )
    gain_grad = jnp.concatenate(
        [sums_one[1], sums_two[1], sums_three[1], (task_weight[:, None] * head_sums[1]).reshape(-1)]
    )
    bias_grad = jnp.concatenate(
        [sums_one[0], sums_two[0], sums_three[0], (task_weight[:, None] * head_sums[0]).reshape(-1)]
    )
    norm_grad = jnp.stack([gain_grad, bias_grad])
    w_reduce_new, m_reduce_new = update(w_reduce, m_reduce, totals[0])
    w_dilated_new, m_dilated_new = update(w_dilated, m_dilated, totals[1])
    w_expand_new, m_expand_new = update(w_expand, m_expand, totals[2])
    w_heads_new, m_heads_new = update(w_heads, m_heads, totals[3])
    norm_params_new, norm_moment_new = update(norm_params, norm_moment, norm_grad)
    return (
        features_grad[None],
        w_reduce_new,
        m_reduce_new,
        w_dilated_new,
        m_dilated_new,
        w_expand_new,
        m_expand_new,
        w_heads_new,
        m_heads_new,
        norm_params_new,
        norm_moment_new,
    )


def solution(mesh):
    placed = (
        P("dp", "fsdp", None, None),
        P(None, "dp", "fsdp", None, None),
        P(),
        P(),
        P("fsdp", None),
        P("fsdp", None),
        P(None, "fsdp"),
        P(None, "fsdp", None),
        P(),
        P("fsdp", None),
        P("fsdp", None),
        P(None, "fsdp"),
        P(None, "fsdp", None),
        P(),
    )
    return jax.shard_map(
        local,
        mesh=mesh,
        in_specs=placed,
        out_specs=(
            P("dp", "fsdp", None, None),
            P("fsdp", None),
            P("fsdp", None),
            P("fsdp", None),
            P("fsdp", None),
            P(None, "fsdp"),
            P(None, "fsdp"),
            P(None, "fsdp", None),
            P(None, "fsdp", None),
            P(),
            P(),
        ),
        check_vma=False,
    )
```

```python
import functools

import jax
import jax.numpy as jnp
from jax import lax
from jax.experimental import pallas as pl
from jax.experimental.pallas import tpu as pltpu
from jax.sharding import PartitionSpec as P

MESH = pl.DeviceIdType.MESH
norm_epsilon = 1e-05
task_epsilon = 1e-06
momentum_decay = 0.9
step_rate = 0.01
trunk_rate = 4
head_rates = (12, 24, 36)

class Tree:
    def __init__(self):
        self.core = lax.axis_index("dp")
        self.place = lax.axis_index("fsdp")
        self.count = lax.axis_size("fsdp")
        self.line = self.count // 4
        self.z = self.place // 4
        self.low = self.place % 4
        self.step_a = 1 + self.core
        self.step_b = 2 - self.core
        self.move_a = self.step_a * (1 - 2 * ((self.low // self.step_a) % 2))
        self.move_b = self.step_b * (1 - 2 * ((self.low // self.step_b) % 2))

    def at(self, place):
        return (self.core, place)

    @property
    def partner(self):
        return (1 - self.core, self.place)

    @property
    def a(self):
        return self.at(self.place + self.move_a)

    @property
    def b(self):
        return self.at(self.place + self.move_b)

    @property
    def down(self):
        return self.at(self.place - 4)

    @property
    def up(self):
        return self.at(self.place + 4)

    def greet(self):
        barrier = pltpu.get_barrier_semaphore()
        for peer in (self.partner, self.a, self.b):
            pl.semaphore_signal(barrier, inc=1, device_id=peer, device_id_type=MESH)

        @pl.when(self.z > 0)
        def _():
            pl.semaphore_signal(barrier, inc=1, device_id=self.down, device_id_type=MESH)

        @pl.when(self.z < self.line - 1)
        def _():
            pl.semaphore_signal(barrier, inc=1, device_id=self.up, device_id_type=MESH)

        pl.semaphore_wait(
            barrier,
            3
            + jnp.where(self.z > 0, 1, 0)
            + jnp.where(self.z < self.line - 1, 1, 0),
        )


def plane_sum_kernel(line, x_ref, o_ref, near, part, far, n_send, n_recv, f_send, f_recv):
    core = lax.axis_index("dp")
    place = lax.axis_index("fsdp")
    z, low = place // 4, place % 4
    me = low * 2 + core

    def beside(s):
        other = (me + s) % 8
        return (other % 2, z * 4 + other // 2)

    def away(s):
        return (core, ((z + s) % line) * 4 + low)

    barrier = pltpu.get_barrier_semaphore()
    for s in range(1, 8):
        pl.semaphore_signal(barrier, inc=1, device_id=beside(s), device_id_type=MESH)

    @pl.loop(1, line)
    def _(s):
        pl.semaphore_signal(barrier, inc=1, device_id=away(s), device_id_type=MESH)

    near[me] = x_ref[...]
    pl.semaphore_wait(barrier, 7 + line - 1)

    def to_beside(s):
        return pltpu.make_async_remote_copy(src_ref=x_ref, dst_ref=near.at[me], send_sem=n_send.at[s], recv_sem=n_recv, device_id=beside(s), device_id_type=MESH)

    def to_away(s):
        return pltpu.make_async_remote_copy(src_ref=part, dst_ref=far.at[z], send_sem=f_send.at[s], recv_sem=f_recv, device_id=away(s), device_id_type=MESH)

    for s in range(1, 8):
        to_beside(s).start()
    seven = near.at[pl.ds(0, 7)]
    pltpu.make_async_copy(seven, seven, n_recv).wait()
    total = jnp.sum(near[...], axis=0)
    part[...] = total
    pl.loop(1, line)(lambda s: to_away(s).start())
    far[z] = total
    rest = far.at[pl.ds(0, line - 1)]
    pltpu.make_async_copy(rest, rest, f_recv).wait()
    o_ref[...] = jnp.sum(far[...], axis=0)
    for s in range(1, 8):
        to_beside(s).wait_send()
    pl.loop(1, line)(lambda s: to_away(s).wait_send())


def all_sum(x, number):
    line = lax.axis_size("fsdp") // 4
    dma = pltpu.SemaphoreType.DMA
    return pl.pallas_call(
        functools.partial(plane_sum_kernel, line),
        out_shape=jax.ShapeDtypeStruct(x.shape, x.dtype),
        in_specs=[pl.BlockSpec(memory_space=pltpu.VMEM)],
        out_specs=pl.BlockSpec(memory_space=pltpu.VMEM),
        scratch_shapes=[
            pltpu.VMEM((8,) + x.shape, x.dtype), pltpu.VMEM(x.shape, x.dtype), pltpu.VMEM((line,) + x.shape, x.dtype),
            dma((8,)), dma, dma((line,)), dma,
        ],
        compiler_params=pltpu.CompilerParams(collective_id=number, has_side_effects=True),
    )(x)


def reduce_kernel(kinds, whole, *refs):
    count = len(kinds)
    parts, outs = refs[:count], refs[count : 2 * count]
    scratch = refs[2 * count :]
    accs, arx, zrx = (scratch[k * count : (k + 1) * count] for k in range(3))
    prx, brx = (scratch[3 * count + k * whole : 3 * count + (k + 1) * whole] for k in range(2))
    (
        load_sem, p_send, p_recv, b_send, b_recv, a_send, a_recv, z_send, z_recv, s_send, s_recv,
    ) = scratch[3 * count + 2 * whole :]
    t = Tree()
    t.greet()
    line, z, low = t.line, t.z, t.low

    def rows_of(k, core):
        rows = kinds[k][1] // 2
        return pl.ds(pl.multiple_of(core * rows, 16), rows)

    def remote(src, dst, send, recv, peer):
        return pltpu.make_async_remote_copy(src_ref=src, dst_ref=dst, send_sem=send, recv_sem=recv, device_id=peer, device_id_type=MESH)

    def load(k, block):
        return pltpu.make_async_copy(
            parts[k].at[:, block, rows_of(k, t.core)], accs[k].at[block], load_sem.at[k, block]
        )

    def load_late(k, at):
        return pltpu.make_async_copy(parts[k].at[at], accs[k].at[at], load_sem.at[k, at])

    def spot_of(k, zz, w):
        if k < whole:
            return zz * 4 + lows[w]
        return zz * 2 + (3 - w)

    def to_partner(k, block):
        return remote(parts[k].at[:, block, rows_of(k, 1 - t.core)], prx[k].at[block], p_send.at[k, block], p_recv.at[k, block], t.partner)

    upper = z >= line // 2
    own_spot = jnp.where(upper, z, line - 1 - z)

    def spot(j):
        q = j + jnp.where(j >= own_spot, 1, 0)
        other = jnp.where(upper, q, line - 1 - q)
        return jnp.where(j == line - 1, z, other)

    lows = (low + t.move_b, low + t.move_a + t.move_b, low + t.move_a, low)

    def to_b(k, zz, which):
        return remote(accs[k].at[zz * 4 + lows[which]], brx[k].at[zz * 2 + which], b_send.at[k, zz * 2 + which], b_recv.at[k, zz * 2 + which], t.b)

    def to_a(k, zz):
        return remote(accs[k].at[spot_of(k, zz, 2)], arx[k].at[zz], a_send.at[k, zz], a_recv.at[k, zz], t.a)

    def along(k, zz, up):
        w = 1 if up else 0
        return remote(accs[k].at[spot_of(k, zz, 3)], zrx[k].at[w, zz], z_send.at[k, w, zz], z_recv.at[k, w, zz], t.up if up else t.down)

    def add(k, block, ref):
        lead = kinds[k][0]

        @pl.loop(0, lead)
        def _(h):
            accs[k][block, h] = accs[k][block, h] + ref[h]

    def begin(j):
        zz = spot(j)
        for k in range(whole, count):
            load_late(k, zz * 2).start()
            load_late(k, zz * 2 + 1).start()
        for w in range(4):
            for k in range(whole):
                to_partner(k, zz * 4 + lows[w]).start()
                load(k, zz * 4 + lows[w]).start()

    first, last = range(whole), range(whole, count)

    def send_late(j):
        zz = spot(j)
        for k in last:
            load_late(k, zz * 2 + 1).wait()
            to_a(k, zz).start()

    def stage_b(j):
        zz = spot(j)
        for w in range(4):
            for k in first:
                block = zz * 4 + lows[w]
                load(k, block).wait()
                to_partner(k, block).wait_recv()
                add(k, block, prx[k].at[block])
                if w < 2:
                    to_b(k, zz, w).start()

    def stage_a(j):
        zz = spot(j)
        for w in (1, 0):
            for k in first:
                to_b(k, zz, w).wait_recv()
                add(k, zz * 4 + lows[3 if w == 0 else 2], brx[k].at[zz * 2 + w])
                if w == 1:
                    to_a(k, zz).start()

    def stage_z(j, ks):
        zz = spot(j)
        for k in ks:
            if k >= whole:
                load_late(k, zz * 2).wait()
            to_a(k, zz).wait_recv()
            here = spot_of(k, zz, 3)
            add(k, here, arx[k].at[zz])

            @pl.when(jnp.logical_and(zz >= z, z > 0))
            def _():
                along(k, zz, True).wait_recv()
                add(k, here, zrx[k].at[1, zz])

            @pl.when(jnp.logical_and(zz <= z, z < line - 1))
            def _():
                along(k, zz, False).wait_recv()
                add(k, here, zrx[k].at[0, zz])

            @pl.when(zz > z)
            def _():
                along(k, zz, True).start()

            @pl.when(zz < z)
            def _():
                along(k, zz, False).start()

    pl.loop(0, line)(begin)
    pl.loop(0, line)(send_late)
    pl.loop(0, line)(stage_b)

    @pl.loop(0, line + 1)
    def _(j):
        pl.when(j < line)(lambda: stage_z(j, last))
        pl.when(j >= 1)(lambda: stage_a(j - 1))

    pl.loop(0, line)(lambda j: stage_z(j, first))

    def half(k, core):
        if k < whole:
            return outs[k].at[:, rows_of(k, core)]
        cols = kinds[k][2]
        return outs[k].at[:, :, pl.ds(pl.multiple_of(core * cols, cols), cols)]

    def share(k):
        return remote(accs[k].at[spot_of(k, z, 3)], half(k, t.core), s_send.at[k], s_recv.at[k], t.partner)

    def keep(k):
        return pltpu.make_async_copy(accs[k].at[spot_of(k, z, 3)], half(k, t.core), load_sem.at[k, 0])

    for k in range(count):
        share(k).start()
        keep(k).start()

    @pl.loop(0, line)
    def _(j):
        zz = spot(j)
        for k in range(count):
            if k < whole:
                for w in range(4):
                    to_partner(k, zz * 4 + lows[w]).wait_send()
                to_b(k, zz, 0).wait_send()
                to_b(k, zz, 1).wait_send()
            to_a(k, zz).wait_send()
            pl.when(zz > z)(lambda: along(k, zz, True).wait_send())
            pl.when(zz < z)(lambda: along(k, zz, False).wait_send())

    for k in range(count):
        keep(k).wait()
        other = half(k, 1 - t.core)
        remote(other, other, s_send.at[k], s_recv.at[k], t.partner).wait_recv()
        share(k).wait_send()


def reduce_shards(parts, late, number):
    n = lax.axis_size("fsdp")
    line = n // 4
    whole = len(parts)
    kinds = [(p.shape[0], p.shape[2], p.shape[3]) for p in parts] + [p.shape[1:] for p in late]
    sizes = [(l, r // 2, c) for l, r, c in kinds[:whole]] + kinds[whole:]
    results = kinds[:whole] + [(l, r, 2 * c) for l, r, c in kinds[whole:]]
    bf = jnp.bfloat16
    count = len(kinds)
    dma = pltpu.SemaphoreType.DMA

    def room(some, *lead):
        return [pltpu.VMEM(tuple(lead) + tuple(s), bf) for s in some]

    accs = [
        pltpu.VMEM((n if k < whole else 2 * line,) + tuple(s), bf) for k, s in enumerate(sizes)
    ]
    return pl.pallas_call(
        functools.partial(reduce_kernel, kinds, whole),
        out_shape=tuple(jax.ShapeDtypeStruct(r, bf) for r in results),
        in_specs=[pl.BlockSpec(memory_space=pl.ANY)] * count,
        out_specs=tuple([pl.BlockSpec(memory_space=pl.ANY)] * count),
        scratch_shapes=accs
        + room(sizes, line)
        + room(sizes, 2, line)
        + room(sizes[:whole], n)
        + room(sizes[:whole], 2 * line)
        + [
            dma((count, n)),
            dma((count, n)),
            dma((count, n)),
            dma((count, 2 * line)),
            dma((count, 2 * line)),
            dma((count, line)),
            dma((count, line)),
            dma((count, 2, line)),
            dma((count, 2, line)),
            dma((count,)),
            dma((count,)),
        ],
        compiler_params=pltpu.CompilerParams(
            collective_id=number, has_side_effects=True, vmem_limit_bytes=60 * 2**20
        ),
    )(*parts, *late)


def exchange_kernel(offsets, rows, count, x_ref, o_ref, send, recv):
    core = lax.axis_index("dp")
    place = lax.axis_index("fsdp")
    pieces = []
    for k, offset in enumerate(offsets):
        first, cut = offset // rows, offset % rows
        for part, (gap, low, high, to) in enumerate(
            ((first, cut, rows, 0), (first + 1, 0, cut, rows - cut))
        ):
            if high > low:
                pieces.append((k, part, gap, low, high - low, to))
    gaps = sorted({abs(p[2]) for p in pieces} - {0})
    gaps = [-g for g in gaps] + gaps
    barrier = pltpu.get_barrier_semaphore()

    def present(gap):
        return jnp.logical_and(place + gap >= 0, place + gap < count)

    met = jnp.int32(0)
    for gap in gaps:
        met = met + jnp.where(present(gap), 1, 0)

        @pl.when(present(gap))
        def _():
            pl.semaphore_signal(
                barrier, inc=1, device_id=(core, place + gap), device_id_type=MESH
            )

    pl.semaphore_wait(barrier, met)

    def piece(k, part, gap, low, size, to):
        return pltpu.make_async_remote_copy(
            src_ref=x_ref.at[k, pl.ds(low, size)],
            dst_ref=o_ref.at[k, pl.ds(to, size)],
            send_sem=send.at[k, part],
            recv_sem=recv.at[k, part],
            device_id=(core, place - gap),
            device_id_type=MESH,
        )

    for p in pieces:
        k, part, gap, low, size, to = p
        if gap == 0:
            o_ref[k, to : to + size] = x_ref[k, low : low + size]
        else:
            pl.when(present(-gap))(lambda p=p: piece(*p).start())
    for p in pieces:
        if p[2]:
            pl.when(present(p[2]))(lambda p=p: piece(*p).wait_recv())
    for p in pieces:
        if p[2]:
            pl.when(present(-p[2]))(lambda p=p: piece(*p).wait_send())


def exchange(x, offsets, number):
    entries, rows = x.shape[:2]
    return pl.pallas_call(
        functools.partial(exchange_kernel, offsets, rows, lax.axis_size("fsdp")),
        out_shape=jax.ShapeDtypeStruct(x.shape, x.dtype),
        in_specs=[pl.BlockSpec(memory_space=pltpu.VMEM)],
        out_specs=pl.BlockSpec(memory_space=pltpu.VMEM),
        scratch_shapes=[
            pltpu.SemaphoreType.DMA((entries, 2)),
            pltpu.SemaphoreType.DMA((entries, 2)),
        ],
        compiler_params=pltpu.CompilerParams(
            collective_id=number, has_side_effects=True, vmem_limit_bytes=32 * 2**20
        ),
    )(x)


def plane_signal(line, core, z, low):
    barrier = pltpu.get_barrier_semaphore()
    me = low * 2 + core
    for s in range(1, 8):
        other = (me + s) % 8
        pl.semaphore_signal(
            barrier, inc=1, device_id=(other % 2, z * 4 + other // 2), device_id_type=MESH
        )

    @pl.loop(1, line)
    def _(s):
        pl.semaphore_signal(
            barrier, inc=1, device_id=(core, ((z + s) % line) * 4 + low), device_id_type=MESH
        )


def plane_scratch(line, shape):
    dma = pltpu.SemaphoreType.DMA
    return [
        pltpu.VMEM((8,) + shape, jnp.float32),
        pltpu.VMEM(shape, jnp.float32),
        pltpu.VMEM((line,) + shape, jnp.float32),
        dma((8,)),
        dma,
        dma((line,)),
        dma,
    ]


def plane_sum(line, fill, room, meanwhile=None, later=None):
    near, part, far, n_send, n_recv, f_send, f_recv = room
    core = lax.axis_index("dp")
    place = lax.axis_index("fsdp")
    z, low = place // 4, place % 4
    me = low * 2 + core

    def to_beside(s):
        other = (me + s) % 8
        return pltpu.make_async_remote_copy(
            src_ref=near.at[me],
            dst_ref=near.at[me],
            send_sem=n_send.at[s],
            recv_sem=n_recv,
            device_id=(other % 2, z * 4 + other // 2),
            device_id_type=MESH,
        )

    def to_away(s):
        return pltpu.make_async_remote_copy(
            src_ref=part,
            dst_ref=far.at[z],
            send_sem=f_send.at[s],
            recv_sem=f_recv,
            device_id=(core, ((z + s) % line) * 4 + low),
            device_id_type=MESH,
        )

    fill(near.at[me])
    for s in range(1, 8):
        to_beside(s).start()
    if meanwhile is not None:
        meanwhile()
    seven = near.at[pl.ds(0, 7)]
    pltpu.make_async_copy(seven, seven, n_recv).wait()
    total = jnp.sum(near[...], axis=0)
    part[...] = total
    pl.loop(1, line)(lambda s: to_away(s).start())
    far[z] = total
    if later is not None:
        later()
    rest = far.at[pl.ds(0, line - 1)]
    pltpu.make_async_copy(rest, rest, f_recv).wait()
    result = jnp.sum(far[...], axis=0)
    for s in range(1, 8):
        to_beside(s).wait_send()
    pl.loop(1, line)(lambda s: to_away(s).wait_send())
    return result


def row_pieces(offset, rows):
    first, cut = offset // rows, offset % rows
    pieces = [(first, cut, rows - cut, 0)]
    if cut:
        pieces.append((first + 1, 0, cut, rows - cut))
    return pieces


def row_gaps(offsets, rows):
    gaps = {abs(p[0]) for o in offsets for p in row_pieces(o, rows)} - {0}
    return sorted(-g for g in gaps) + sorted(gaps)


def greet_rows(gaps, count):
    barrier = pltpu.get_barrier_semaphore()
    core = lax.axis_index("dp")
    place = lax.axis_index("fsdp")
    met = jnp.int32(0)
    for gap in gaps:
        here = jnp.logical_and(place + gap >= 0, place + gap < count)
        met = met + jnp.where(here, 1, 0)

        @pl.when(here)
        def _():
            pl.semaphore_signal(
                barrier, inc=1, device_id=(core, place + gap), device_id_type=MESH
            )

    return met


class Rows:
    def __init__(self, offsets, rows, cols, count, x_ref, o_ref, send, recv):
        self.core = lax.axis_index("dp")
        self.place = lax.axis_index("fsdp")
        self.rows, self.cols, self.count = rows, cols, count
        self.offsets, self.x_ref, self.o_ref = offsets, x_ref, o_ref
        self.send, self.recv = send, recv

    def present(self, gap):
        return jnp.logical_and(self.place + gap >= 0, self.place + gap < self.count)

    def copies(self, k):
        for part, (gap, low, size, to) in enumerate(row_pieces(self.offsets[k], self.rows)):
            yield gap, low, size, to, pltpu.make_async_remote_copy(
                src_ref=self.x_ref.at[k, pl.ds(low * self.cols, size * self.cols)],
                dst_ref=self.o_ref.at[k, pl.ds(to * self.cols, size * self.cols)],
                send_sem=self.send.at[k, part],
                recv_sem=self.recv.at[k, part],
                device_id=(self.core, self.place - gap),
                device_id_type=MESH,
            )

    def start(self, k):
        for gap, low, size, to, copy in self.copies(k):
            if gap == 0:
                cols = self.cols
                self.o_ref[k, to * cols : (to + size) * cols] = self.x_ref[
                    k, low * cols : (low + size) * cols
                ]
            else:
                pl.when(self.present(-gap))(copy.start)

    def wait_recv(self, k):
        for gap, _, _, _, copy in self.copies(k):
            if gap:
                pl.when(self.present(gap))(copy.wait_recv)

    def wait_send(self, k):
        for gap, _, _, _, copy in self.copies(k):
            if gap:
                pl.when(self.present(-gap))(copy.wait_send)


def heads_kernel(
    rates, rows, cols, count,
    x_ref, xt_ref, wa_ref, wb_ref, cot_ref, par_ref, mask_ref,
    g_ref, own_ref, got_ref, late_ref, sums_ref, sq_ref,
    wv, out_rows, in_rows, resp, dn, taps, g_room, dw_room,
    w_sem, f_send, f_recv, e_send, e_recv, g_sem, dw_sem, hand_sem, got_sem, *rooms,
):
    px = rows * cols
    heads = len(rates)
    width = par_ref.shape[1]
    line = count // 4
    core = lax.axis_index("dp")
    place = lax.axis_index("fsdp")
    z, low = place // 4, place % 4
    one, two = rooms[:7], rooms[7:]

    def w_copy(t, k):
        early = wa_ref.shape[0] // 9
        src = wa_ref.at[t * 9 + k] if t < early else wb_ref.at[(t - early) * 9 + k]
        return pltpu.make_async_copy(
            src, wv.at[t, :, k * width : (k + 1) * width], w_sem.at[t * 9 + k]
        )

    for t in reversed(range(heads)):
        for k in range(9):
            w_copy(t, k).start()
    fwd = Rows([o for r in rates for o in (-r, r)], rows, cols, count, out_rows, in_rows, f_send, f_recv)
    bwd = Rows([o for r in rates for o in (r, -r)], rows, cols, count, out_rows, in_rows, e_send, e_recv)
    plane_signal(line, core, z, low)
    met = greet_rows(row_gaps(fwd.offsets, rows), count)
    barrier = pltpu.get_barrier_semaphore()

    def mask(t, k):
        return mask_ref[t, :, k : k + 1]

    @pl.loop(0, heads)
    def _(step):
        t = heads - 1 - step
        rate = 12 * (t + 1)
        for j in (0, 2, 1):
            summed = None
            for c in range(3):
                k = 3 * j + c
                pltpu.make_async_copy(
                    wa_ref.at[k], wv.at[t, :, k * width : (k + 1) * width], w_sem.at[t * 9 + k]
                ).wait()
                prod = jnp.dot(
                    x_ref[...], wv[t, :, k * width : (k + 1) * width], preferred_element_type=jnp.float32
                )
                if c == 0:
                    summed = jnp.where(mask(t, 1) > 0, pltpu.roll(prod, rate, 0), 0.0)
                elif c == 1:
                    summed = summed + jnp.where(mask(t, 0) > 0, prod, 0.0)
                else:
                    summed = summed + jnp.where(mask(t, 2) > 0, pltpu.roll(prod, px - rate, 0), 0.0)
            if j == 1:
                resp[t] = summed
                continue
            out_rows[t * 2 + j // 2] = summed.astype(jnp.bfloat16)
            if j == 0:

                @pl.when(step == 0)
                def _():
                    pl.semaphore_wait(barrier, 7 + line - 1 + met)

            for h in range(heads):
                pl.when(t == h)(lambda: fwd.start(2 * h + j // 2))

    def stats(ref):
        for h in range(heads):
            total = resp[h]
            for j in (0, 1):
                fwd.wait_recv(2 * h + j)
                total = total + jnp.where(
                    mask(h, 3 + j) > 0, in_rows[2 * h + j].astype(jnp.float32), 0.0
                )
            resp[h] = total
            kept = total * mask(h, 0)
            ref[2 * h : 2 * h + 1] = jnp.sum(kept, axis=0, keepdims=True)
            ref[2 * h + 1 : 2 * h + 2] = jnp.sum(kept * total, axis=0, keepdims=True)

    sums = plane_sum(line, stats, one)
    pixels = par_ref[2 * heads : 2 * heads + 1]
    inverses = []

    def grads(ref):
        for h in range(heads):
            mean = sums[2 * h : 2 * h + 1] / pixels
            var = sums[2 * h + 1 : 2 * h + 2] / pixels - mean * mean
            inverse = lax.rsqrt(var + norm_epsilon)
            inverses.append(inverse)
            scaled = (resp[h] - mean) * inverse
            normed = scaled * par_ref[2 * h : 2 * h + 1] + par_ref[2 * h + 1 : 2 * h + 2]
            s = jax.nn.sigmoid(normed)
            d = cot_ref[h].astype(jnp.float32) * (s * (1.0 + normed * (1.0 - s))) * mask(h, 0)
            resp[h] = scaled
            dn[h] = d
            ref[2 * h : 2 * h + 1] = jnp.sum(d, axis=0, keepdims=True)
            ref[2 * h + 1 : 2 * h + 2] = jnp.sum(d * scaled, axis=0, keepdims=True)

    back = plane_sum(line, grads, two)
    sums_ref[...] = back
    for h in range(heads):
        fwd.wait_send(2 * h)
        fwd.wait_send(2 * h + 1)
        e = (
            mask(h, 0)
            * (inverses[h] * par_ref[2 * h : 2 * h + 1])
            * (dn[h] - back[2 * h : 2 * h + 1] / pixels - resp[h] * (back[2 * h + 1 : 2 * h + 2] / pixels))
        )
        dn[h] = e
        out_rows[2 * h] = jnp.where(mask(h, 3) > 0, e, 0.0).astype(jnp.bfloat16)
        out_rows[2 * h + 1] = jnp.where(mask(h, 4) > 0, e, 0.0).astype(jnp.bfloat16)
        bwd.start(2 * h)
        bwd.start(2 * h + 1)

    def g_copy(t):
        return pltpu.make_async_copy(g_room, g_ref.at[t], g_sem)

    half = width // 2

    def lanes(owner):
        return pl.ds(pl.multiple_of(owner * half, half), half)

    def keep(slot, at):
        return pltpu.make_async_copy(
            dw_room.at[slot, :, lanes(core)], own_ref.at[at], dw_sem.at[slot]
        )

    def hand(slot, at):
        return pltpu.make_async_remote_copy(
            src_ref=dw_room.at[slot, :, lanes(1 - core)],
            dst_ref=got_ref.at[at],
            send_sem=hand_sem.at[slot],
            recv_sem=got_sem,
            device_id=(1 - core, place),
            device_id_type=MESH,
        )

    def put(slot, at):
        return pltpu.make_async_copy(
            dw_room.at[slot], late_ref.at[at - own_ref.shape[0]], dw_sem.at[slot]
        )

    def handed(t):
        return (t + 1) * 9 <= own_ref.shape[0]

    def dw_start(slot, t, k):
        at = t * 9 + k

        @pl.when(handed(t))
        def _():
            keep(slot, at).start()
            hand(slot, at).start()

        pl.when(jnp.logical_not(handed(t)))(lambda: put(slot, at).start())

    def dw_wait(slot, t):
        @pl.when(handed(t))
        def _():
            keep(slot, 0).wait()
            hand(slot, 0).wait_send()

        pl.when(jnp.logical_not(handed(t)))(lambda: put(slot, own_ref.shape[0]).wait())

    def weigh(t, k, number, before):
        slot = lax.rem(number, 2)
        pl.when(number >= 2)(lambda: dw_wait(slot, before))
        dw_room[slot] = jnp.dot(
            xt_ref[...],
            taps[:, pl.ds(pl.multiple_of(k * width, width), width)],
            preferred_element_type=jnp.float32,
        ).astype(jnp.bfloat16)
        dw_start(slot, t, k)

    def spread(t, j, arrived):
        rate = 12 * (t + 1)
        for c in range(3):
            if c == 0:
                tap = pltpu.roll(jnp.where(mask(t, 1) > 0, arrived, 0.0), px - rate, 0)
            elif c == 1:
                tap = jnp.where(mask(t, 0) > 0, arrived, 0.0)
            else:
                tap = pltpu.roll(jnp.where(mask(t, 2) > 0, arrived, 0.0), rate, 0)
            k = 3 * j + c
            taps[:, k * width : (k + 1) * width] = tap.astype(jnp.bfloat16)

    tiles = wv.shape[1] // width
    sq_ref[...] = jnp.zeros_like(sq_ref)

    def center(t):
        spread(t, 1, dn[t].astype(jnp.bfloat16).astype(jnp.float32))

    @pl.loop(0, heads)
    def _(t):
        center(t)
        pl.loop(0, 3)(lambda k: weigh(t, 3 + k, t * 3 + k, t - jnp.where(k < 2, 1, 0)))

    @pl.loop(0, heads)
    def _(t):
        center(t)
        for h in range(heads):
            @pl.when(t == h)
            def _():
                bwd.wait_recv(2 * h)
                bwd.wait_recv(2 * h + 1)

        spread(t, 0, jnp.where(mask(t, 5) > 0, in_rows[2 * t].astype(jnp.float32), 0.0))
        spread(t, 2, jnp.where(mask(t, 6) > 0, in_rows[2 * t + 1].astype(jnp.float32), 0.0))

        pl.loop(0, 6)(
            lambda k: weigh(
                t,
                k + jnp.where(k >= 3, 3, 0),
                3 * heads + t * 6 + k,
                jnp.where(k < 2, jnp.where(t > 0, t - 1, heads - 1), t),
            )
        )
        pl.when(t > 0)(lambda: g_copy(t - 1).wait())
        def tile(n, square):
            cut = pl.ds(pl.multiple_of(n * width, width), width)
            g = lax.dot_general(
                taps[...], wv[t, cut, :], (((1,), (1,)), ((), ())), preferred_element_type=jnp.float32
            )
            g_room[:, cut] = g
            return square + jnp.sum(g * g, axis=0, keepdims=True)

        square = lax.fori_loop(0, tiles, tile, jnp.zeros((1, width), jnp.float32))
        sq_ref[pl.ds(t, 1)] = square
        g_copy(t).start()

    g_copy(heads - 1).wait()
    dw_wait(0, heads - 1)
    dw_wait(1, heads - 1)
    pltpu.make_async_copy(got_ref, got_ref, got_sem).wait()

    for k in range(2 * heads):
        bwd.wait_send(k)


def heads_step(trunk_out, turned, early, late, cotangent, params, masks, rates, rows, cols, handed, number):
    px, channels = trunk_out.shape
    heads, width = len(rates), early.shape[-1]
    count = lax.axis_size("fsdp")
    line = count // 4
    bf, f32 = jnp.bfloat16, jnp.float32
    dma = pltpu.SemaphoreType.DMA
    vmem = pl.BlockSpec(memory_space=pltpu.VMEM)
    hbm = pl.BlockSpec(memory_space=pl.ANY)
    return pl.pallas_call(
        functools.partial(heads_kernel, rates, rows, cols, count),
        out_shape=(
            jax.ShapeDtypeStruct((heads, px, channels), f32),
            jax.ShapeDtypeStruct((9 * handed, channels, width // 2), bf),
            jax.ShapeDtypeStruct((9 * handed, channels, width // 2), bf),
            jax.ShapeDtypeStruct((9 * (heads - handed), channels, width), bf),
            jax.ShapeDtypeStruct((2 * heads, width), f32),
            jax.ShapeDtypeStruct((8, width), f32),
        ),
        in_specs=[vmem, vmem, hbm, hbm, vmem, vmem, vmem],
        out_specs=(hbm, hbm, hbm, hbm, vmem, vmem),
        scratch_shapes=[
            pltpu.VMEM((heads, channels, 9 * width), bf),
            pltpu.VMEM((2 * heads, px, width), bf),
            pltpu.VMEM((2 * heads, px, width), bf),
            pltpu.VMEM((heads, px, width), f32),
            pltpu.VMEM((heads, px, width), f32),
            pltpu.VMEM((px, 9 * width), bf),
            pltpu.VMEM((px, channels), f32),
            pltpu.VMEM((2, channels, width), bf),
            dma((9 * heads,)),
            dma((2 * heads, 2)),
            dma((2 * heads, 2)),
            dma((2 * heads, 2)),
            dma((2 * heads, 2)),
            dma,
            dma((2,)),
            dma((2,)),
            dma,
        ]
        + plane_scratch(line, (2 * heads, width))
        + plane_scratch(line, (2 * heads, width)),
        compiler_params=pltpu.CompilerParams(
            collective_id=number, has_side_effects=True, vmem_limit_bytes=62 * 2**20
        ),
    )(trunk_out, turned, early, late, cotangent, params, masks)


class Fan:
    def __init__(self, t, arrays, sends, arrives, shares, own_sem):
        self.t, self.arrays = t, arrays
        self.sends, self.arrives, self.shares, self.own_sem = sends, arrives, shares, own_sem

    def copy(self, k, kind, block, peer, own=False):
        src, place = self.arrays[k]
        dst = place(block, self.t.core)
        return pltpu.make_async_remote_copy(
            src_ref=src if own else dst,
            dst_ref=dst,
            send_sem=self.sends.at[k, kind, block],
            recv_sem=(self.shares if kind == 4 else self.arrives).at[k, block],
            device_id=peer,
            device_id_type=MESH,
        )

    def fan(self, k, block, own, down, up, a, b, finish):
        t = self.t

        def act(kind, peer):
            c = self.copy(k, kind, block, peer, own)
            c.wait_send() if finish else c.start()

        if down:
            pl.when(t.z > 0)(lambda: act(0, t.down))
        if up:
            pl.when(t.z < t.line - 1)(lambda: act(1, t.up))
        if a:
            act(2, t.a)
        if b:
            act(3, t.b)
        act(4, t.partner)

    def stay(self, k):
        src, place = self.arrays[k]
        return pltpu.make_async_copy(src, place(self.t.place, self.t.core), self.own_sem.at[k])

    def own(self, ks, finish=False):
        for k in ks:
            if not finish:
                self.stay(k).start()
            self.fan(k, self.t.place, True, True, True, True, True, finish)

    def step(self, ks, s, move, down, up, a, b, finish):
        t = self.t
        for k in ks:
            def one(block, down, up):
                if not finish:
                    self.copy(k, 0, block, t.partner).wait_recv()
                self.fan(k, block, False, down, up, a, b, finish)

            pl.when(t.z - s >= 0)(lambda: one(t.place - 4 * s + move, down, False))
            if s:
                pl.when(t.z + s < t.line)(lambda: one(t.place + 4 * s + move, False, up))

    def steps(self, ks, finish=False):
        t = self.t
        result = []
        for s in range(1, t.line):
            result.append(lambda s=s: self.along(ks, s, finish))
            result.append(lambda s=s: self.step(ks, s - 1, t.move_a, False, False, False, True, finish))
        result.append(lambda: self.step(ks, t.line - 1, t.move_a, False, False, False, True, finish))
        tail = []
        for s in range(t.line):
            tail.append(lambda s=s: self.step(ks, s, t.move_b, False, False, False, False, finish))
            tail.append(
                lambda s=s: self.step(ks, s, t.move_a + t.move_b, False, False, False, False, finish)
            )
        return result, tail

    def along(self, ks, s, finish):
        t = self.t
        for k in ks:
            def one(block, down, up):
                if not finish:
                    self.copy(k, 0, block, t.partner).wait_recv()
                self.fan(k, block, False, down, up, True, True, finish)

            pl.when(t.z - s >= 0)(lambda: one(t.place - 4 * s, False, True))
            pl.when(t.z + s < t.line)(lambda: one(t.place + 4 * s, True, False))

    def wait_shares(self, ks):
        t = self.t
        for k in ks:
            self.stay(k).wait()

        @pl.loop(0, t.count)
        def _(block):
            for k in ks:
                other = self.arrays[k][1](block, 1 - t.core)
                pltpu.make_async_remote_copy(
                    src_ref=other,
                    dst_ref=other,
                    send_sem=self.sends.at[k, 4, block],
                    recv_sem=self.shares.at[k, block],
                    device_id=t.partner,
                    device_id_type=MESH,
                ).wait_recv()

    def finish(self, ks):
        self.own(ks, True)
        first, tail = self.steps(ks, True)
        for f in first + tail:
            f()


def silu(v):
    return v * jax.nn.sigmoid(v)


def scale_rows(sums, pixels):
    mean = sums[0:1] / pixels
    var = sums[1:2] / pixels - mean * mean
    return mean, lax.rsqrt(var + norm_epsilon)


def read_params(norm_ref, crop_ref, par_ref, par3_ref, heads_ref):
    middle, width = par_ref.shape[1], heads_ref.shape[1]
    total = jnp.int32(0)
    for g in range(crop_ref.shape[0]):
        for c in range(crop_ref.shape[1]):
            total = total + crop_ref[g, c] * crop_ref[g, c]
    total = total.astype(jnp.float32)
    for k in range(2):
        for row in range(2):
            par_ref[2 * k + row : 2 * k + row + 1] = norm_ref[row : row + 1, k * middle : (k + 1) * middle]
    par_ref[4:] = jnp.full((par_ref.shape[0] - 4, middle), total)
    parts = par3_ref.shape[0] // 2
    for k in range(parts):
        at = (2 + k) * middle
        for row in range(2):
            par3_ref[2 * k + row : 2 * k + row + 1] = norm_ref[row : row + 1, at : at + middle]
    heads = heads_ref.shape[0] // 2 - 1
    for k in range(heads):
        at = (2 + parts) * middle + k * width
        for row in range(2):
            heads_ref[2 * k + row : 2 * k + row + 1] = norm_ref[row : row + 1, at : at + width]
    heads_ref[2 * heads :] = jnp.full((2, width), total)


def read_layout(crop_ref, group, row_start, total_rows, cols, rates, masks_ref, at):
    shape = masks_ref.shape[1:]
    pixel = lax.broadcasted_iota(jnp.int32, shape, 0)
    lane = lax.broadcasted_iota(jnp.int32, shape, 1)
    row = row_start + lax.div(pixel, jnp.full(shape, cols, jnp.int32))
    col = lax.rem(pixel, jnp.full(shape, cols, jnp.int32))
    top = bottom = side = jnp.zeros(shape, jnp.int32)
    start = jnp.int32(0)
    for c in range(crop_ref.shape[1]):
        height = crop_ref[group, c]
        member = jnp.logical_and(row >= start, row < start + height)
        top = jnp.where(member, start, top)
        bottom = jnp.where(member, start + height, bottom)
        side = jnp.where(member, height, side)
        start = start + height
    for k, rate in enumerate(rates):
        flags = (
            col < side,
            jnp.logical_and(col >= rate, col - rate < side),
            col + rate < side,
            jnp.logical_and(row - rate >= top, row - rate < bottom),
            jnp.logical_and(row + rate >= top, row + rate < bottom),
            row + rate < total_rows,
            row >= rate,
        )
        value = jnp.zeros(shape, jnp.float32)
        for n, flag in enumerate(flags):
            value = jnp.where(jnp.logical_and(lane == n, flag), 1.0, value)
        masks_ref[at + k] = value


def trunk_kernel(
    rates, rows, cols, count,
    x_ref, wr_s, wd_s, we_s, wh_s, norm_ref, crop_ref,
    wr_o, wd_o, we_o, wh_o, out_ref, sc1_ref, sc2_ref, sc3_ref, s1_ref, s2_ref, s3_ref,
    par_ref, par3_ref, heads_ref, masks_ref, turned_ref,
    wr_v, wd_v, we_v, ext, taps,
    sends, arrives, shares, own_sem, save_sem, h_send, h_recv, *rooms,
):
    rate = rates[-1]
    px = rows * cols
    line = count // 4
    middle = par_ref.shape[1]
    channels = out_ref.shape[1]
    t = Tree()
    one, two, three = rooms[:7], rooms[7:14], rooms[14:]
    halo = rate * cols

    def cut(start, size, step=8):
        return pl.ds(pl.multiple_of(start, step), size)

    def rows_array(shard, full):
        size = shard.shape[0]
        return (
            shard.at[cut(t.core * (size // 2), size // 2, 16)],
            lambda block, core: full.at[cut(block * size + core * (size // 2), size // 2, 16)],
        )

    half_e = we_s.shape[0] // 2
    half_h = wh_s.shape[1] // 2
    fan = Fan(
        t,
        [
            rows_array(wr_s, wr_v),
            rows_array(wd_s, wd_v),
            (
                we_s.at[cut(t.core * half_e, half_e, 16)],
                lambda block, core: we_v.at[
                    cut(core * half_e, half_e, 16), cut(block * we_s.shape[1], we_s.shape[1], 128)
                ],
            ),
            (
                wh_s.at[:, cut(t.core * half_h, half_h, 16)],
                lambda block, core: wh_o.at[:, block, cut(core * half_h, half_h, 16)],
            ),
        ],
        sends, arrives, shares, own_sem,
    )
    plane_signal(line, t.core, t.z, t.low)
    met = greet_rows((-1, 1), count)
    read_params(norm_ref, crop_ref, par_ref, par3_ref, heads_ref)
    mask_ref = masks_ref.at[len(rates) - 1]
    read_layout(crop_ref, t.core, t.place * rows, rows * count, cols, rates[-1:], masks_ref, len(rates) - 1)
    pl.semaphore_wait(pltpu.get_barrier_semaphore(), 7 + line - 1 + met)
    small, heads = (0, 1, 2), (3,)
    fan.own(small)
    first_steps, first_tail = fan.steps(small)
    for f in first_steps:
        f()
    fan.own(heads)
    read_layout(crop_ref, t.core, t.place * rows, rows * count, cols, rates[:-1], masks_ref, 0)
    for f in first_tail:
        f()
    head_steps, head_tail = fan.steps(heads)
    queue = head_steps + head_tail

    def forward(number):
        for _ in range(number):
            if queue:
                queue.pop(0)()

    pixels = par_ref[4:5]

    def mask(k):
        return mask_ref[:, k : k + 1]

    def moments_of(v, ref, at):
        kept = v * mask(0)
        ref[at : at + 1] = jnp.sum(kept, axis=0, keepdims=True)
        ref[at + 1 : at + 2] = jnp.sum(kept * v, axis=0, keepdims=True)

    fan.wait_shares((0,))
    sc1_ref[...] = jnp.dot(x_ref[...], wr_v[...], preferred_element_type=jnp.float32)
    forward(1)
    s1_ref[...] = plane_sum(line, lambda ref: moments_of(sc1_ref[...], ref, 0), one)
    mean, inverse = scale_rows(s1_ref, pixels)
    scaled = (sc1_ref[...] - mean) * inverse
    sc1_ref[...] = scaled
    ext[halo : halo + px] = silu(scaled * par_ref[0:1] + par_ref[1:2]).astype(jnp.bfloat16)

    def edge(up):
        src = ext.at[pl.ds(halo if not up else halo + px - halo, halo)]
        dst = ext.at[pl.ds(halo + px if not up else 0, halo)]
        return pltpu.make_async_remote_copy(
            src_ref=src,
            dst_ref=dst,
            send_sem=h_send.at[int(up)],
            recv_sem=h_recv.at[int(up)],
            device_id=t.at(t.place + (1 if up else -1)),
            device_id_type=MESH,
        )

    has_next, has_last = t.place < count - 1, t.place > 0
    pl.when(has_last)(lambda: edge(False).start())
    pl.when(has_next)(lambda: edge(True).start())
    fan.wait_shares((1, 2))
    forward(2)
    saves = [
        pltpu.make_async_copy(wr_v, wr_o, save_sem.at[0]),
        pltpu.make_async_copy(wd_v, wd_o, save_sem.at[1]),
        pltpu.make_async_copy(we_v, we_o, save_sem.at[2]),
    ]
    for save in saves:
        save.start()
    pl.when(has_next)(lambda: edge(False).wait_recv())
    pl.when(has_last)(lambda: edge(True).wait_recv())
    for j in range(3):
        v = ext[j * halo : j * halo + px].astype(jnp.float32)
        kept_row = 1.0 if j == 1 else mask(3 + j // 2)
        for c in range(3):
            moved = v if c == 1 else pltpu.roll(v, rate if c == 0 else px - rate, 0)
            kept = mask((1, 0, 2)[c]) * kept_row
            k = 3 * j + c
            taps[:, k * middle : (k + 1) * middle] = jnp.where(kept > 0, moved, 0.0).astype(jnp.bfloat16)
    sc2_ref[...] = jnp.dot(taps[...], wd_v[...], preferred_element_type=jnp.float32)
    forward(2)
    s2_ref[...] = plane_sum(line, lambda ref: moments_of(sc2_ref[...], ref, 0), two)
    mean, inverse = scale_rows(s2_ref, pixels)
    scaled = (sc2_ref[...] - mean) * inverse
    sc2_ref[...] = scaled
    hidden = silu(scaled * par_ref[2:3] + par_ref[3:4]).astype(jnp.bfloat16)
    forward(2)
    parts = channels // middle

    def wide(ref):
        for q in range(parts):
            third = jnp.dot(
                hidden, we_v[:, q * middle : (q + 1) * middle], preferred_element_type=jnp.float32
            )
            sc3_ref[:, q * middle : (q + 1) * middle] = third
            moments_of(third, ref, 2 * q)

    s3_ref[...] = plane_sum(line, wide, three)
    forward(1)
    for q in range(parts):
        at = slice(q * middle, (q + 1) * middle)
        mean, inverse = scale_rows(s3_ref[2 * q : 2 * q + 2], pixels)
        scaled = (sc3_ref[:, at] - mean) * inverse
        sc3_ref[:, at] = scaled
        pre = x_ref[:, at].astype(jnp.float32) + (
            scaled * par3_ref[2 * q : 2 * q + 1] + par3_ref[2 * q + 1 : 2 * q + 2]
        )
        active = silu(pre)
        out_ref[:, at] = active.astype(jnp.bfloat16)
        turned_ref[at] = active.T.astype(jnp.bfloat16)
    forward(len(queue))
    fan.wait_shares(heads)
    for save in saves:
        save.wait()
    pl.when(has_last)(lambda: edge(False).wait_send())
    pl.when(has_next)(lambda: edge(True).wait_send())
    fan.finish(small + heads)


def trunk_step(x, shards, norm_params, crop_heights, rates, rows, cols, middle, number):
    px, channels = x.shape
    count = lax.axis_size("fsdp")
    line = count // 4
    rate = rates[-1]
    bf, f32 = jnp.bfloat16, jnp.float32
    dma = pltpu.SemaphoreType.DMA
    vmem = pl.BlockSpec(memory_space=pltpu.VMEM)
    hbm = pl.BlockSpec(memory_space=pl.ANY)
    parts = channels // middle
    heads, head_rows, width = shards[3].shape
    S = jax.ShapeDtypeStruct
    return pl.pallas_call(
        functools.partial(trunk_kernel, rates, rows, cols, count),
        out_shape=(
            S((channels, middle), bf),
            S((9 * middle, middle), bf),
            S((middle, channels), bf),
            S((heads, count, head_rows, width), bf),
            S((px, channels), bf),
            S((px, middle), f32),
            S((px, middle), f32),
            S((px, channels), f32),
            S((2, middle), f32),
            S((2, middle), f32),
            S((2 * parts, middle), f32),
            S((8, middle), f32),
            S((2 * parts, middle), f32),
            S((2 * len(rates), width), f32),
            S((len(rates), px, 128), f32),
            S((channels, px), bf),
        ),
        in_specs=[vmem] + [hbm] * 4 + [vmem, pl.BlockSpec(memory_space=pltpu.SMEM)],
        out_specs=(hbm,) * 4 + (vmem,) * 12,
        scratch_shapes=[
            pltpu.VMEM((channels, middle), bf),
            pltpu.VMEM((9 * middle, middle), bf),
            pltpu.VMEM((middle, channels), bf),
            pltpu.VMEM((px + 2 * rate * cols, middle), bf),
            pltpu.VMEM((px, 9 * middle), bf),
            dma((4, 5, count)),
            dma((4, count)),
            dma((4, count)),
            dma((4,)),
            dma((3,)),
            dma((2,)),
            dma((2,)),
        ]
        + plane_scratch(line, (2, middle))
        + plane_scratch(line, (2, middle))
        + plane_scratch(line, (2 * parts, middle)),
        compiler_params=pltpu.CompilerParams(
            collective_id=number, has_side_effects=True, vmem_limit_bytes=56 * 2**20
        ),
    )(x, *shards, norm_params, crop_heights)


FEED = {"join": 1, "pass": 1, "keep": 1, "third": 1, "d2": 1, "ge": 1, "edge": 2, "d1": 1, "gd": 1, "later3": 4, "later2": 4, "later1": 4}


def nt(a, b):
    return lax.dot_general(a, b, (((1,), (1,)), ((), ())), preferred_element_type=jnp.float32)


def tn(a, b):
    return lax.dot_general(a, b, (((0,), (0,)), ((), ())), preferred_element_type=jnp.float32)


def slope(v):
    s = jax.nn.sigmoid(v)
    return s * (1.0 + v * (1.0 - s))


def back_kernel(
    rate, rows, cols, count, heads,
    x_ref, scale_ref, sq_ref, sc1_ref, sc2_ref, par_ref, par3_ref, s1_ref, s2_ref, s3_ref, mask_ref,
    g_ref, sc3_ref, wr_ref, wd_ref, we_ref, own_ref, got_ref,
    tw_ref, bs1_ref, bs2_ref, bs3_ref, fg_ref, gr_ref, gd_ref, ge_ref, sum_ref,
    b_send, acc, b_room, extra, g_room, s_room, dpre, dthird, wr_v, wd_v, we_v, ext, taps, out_room, grad_room,
    load_sem, extra_sem, bs_sem, br_sem, g_sem, s_sem, w_sem, h_send, h_recv, out_sem, grad_sem, sum_sem, *rooms,
):
    px = rows * cols
    line = count // 4
    middle = par_ref.shape[1]
    channels = x_ref.shape[1]
    parts = channels // middle
    wide = g_room.shape[-1]
    chunks = channels // wide
    halo = rate * cols
    t = Tree()
    one, two, three, four = rooms[:7], rooms[7:14], rooms[14:21], rooms[21:]
    bf, f32 = jnp.bfloat16, jnp.float32

    weights = [
        pltpu.make_async_copy(we_ref, we_v, w_sem.at[0]),
        pltpu.make_async_copy(wd_ref, wd_v, w_sem.at[1]),
        pltpu.make_async_copy(wr_ref, wr_v, w_sem.at[2]),
    ]

    def lanes(c):
        return pl.ds(c * wide, wide)

    def g_load(c):
        return pltpu.make_async_copy(g_ref.at[:, :, lanes(c)], g_room.at[c % 2], g_sem.at[c % 2])

    def s_load(c):
        return pltpu.make_async_copy(sc3_ref.at[:, lanes(c)], s_room.at[c % 2], s_sem.at[c % 2])

    moves = (t.move_b, t.move_a + t.move_b, 0, t.move_a)

    def pair(n, w):
        block = n * 4 + t.low + moves[w]
        room = (b_send if w < 2 else acc).at[n * 2 + w % 2]
        slot = w % 2
        return (
            pltpu.make_async_copy(own_ref.at[:, block], room, load_sem.at[slot]),
            pltpu.make_async_copy(got_ref.at[:, block], extra.at[slot], extra_sem.at[slot]),
        )

    def join(n, w):
        for c in pair(n, w):
            c.wait()
        room = b_send if w < 2 else acc
        at = n * 2 + w % 2

        @pl.loop(0, heads)
        def _(h):
            room[at, h] = room[at, h] + extra[w % 2, h]

    def to_b(n, w, piece=None):
        at = (n * 2 + w,)
        if piece is not None:
            at = at + (piece[0], pl.ds(piece[1], piece[2]))
        return pltpu.make_async_remote_copy(
            src_ref=b_send.at[at],
            dst_ref=b_room.at[at],
            send_sem=bs_sem.at[n * 2 + w],
            recv_sem=br_sem.at[n * 2 + w],
            device_id=t.b,
            device_id_type=MESH,
        )

    head_rows = b_send.shape[2]
    size = head_rows // 4
    pieces = [
        to_b(n, w, (h, r, size))
        for n in range(line)
        for w in (1, 0)
        for h in range(heads)
        for r in range(0, head_rows, size)
    ]

    def feed(number):
        for _ in range(min(number, len(pieces))):
            pieces.pop(0).start()

    plane_signal(line, t.core, t.z, t.low)
    met = greet_rows((-1, 1), count)
    for w in (1, 0):
        for c in pair(0, w):
            c.start()
    for c in weights:
        c.start()
    for c in (0, 1):
        g_load(c).start()
        s_load(c).start()
    pl.semaphore_wait(pltpu.get_barrier_semaphore(), 7 + line - 1 + met)

    def squares(ref):
        ref[...] = sq_ref[...]

    def send_side():
        for n in range(line):
            for w in (1, 0):
                join(n, w)
                feed(FEED["join"])
                if n < line - 1:
                    for c in pair(n + 1, w):
                        c.start()

    square_sums = jnp.sum(plane_sum(line, squares, four, send_side), axis=1, keepdims=True)
    tw_ref[...] = scale_ref[...] / jnp.sqrt(
        square_sums / (par_ref[4:5, 0:1] * channels) + task_epsilon
    )

    for w in (3, 2):
        for c in pair(0, w):
            c.start()

    def mask(k):
        return mask_ref[mask_ref.shape[0] - 1, :, k : k + 1]

    pixels = par_ref[4:5]
    pixels_wide = pixels[:, :wide]

    def third_params(c):
        q, at = (c * wide) // middle, (c * wide) % middle
        at = slice(at, at + wide)
        return 2 * q, at

    def moved_sums(ref, row, at, d, scaled):
        ref[row : row + 1, at] = jnp.sum(d, axis=0, keepdims=True)
        ref[row + 1 : row + 2, at] = jnp.sum(d * scaled, axis=0, keepdims=True)

    def first_pass(ref):
        for c in range(chunks):
            g_load(c).wait()
            s_load(c).wait()
            row, at = third_params(c)
            total = tw_ref[0:1, 0:1] * g_room[c % 2, 0]
            for h in range(1, g_ref.shape[0]):
                total = total + tw_ref[h : h + 1, 0:1] * g_room[c % 2, h]
            scaled = s_room[c % 2]
            here = slice(c * wide, (c + 1) * wide)
            pre = x_ref[:, here].astype(f32) + (
                scaled * par3_ref[row : row + 1, at] + par3_ref[row + 1 : row + 2, at]
            )
            d = total * slope(pre)
            dpre[:, here] = d
            d = d * mask(0)
            moved_sums(ref, row, at, d, scaled)
            feed(FEED["pass"])
            if c + 2 < chunks:
                g_load(c + 2).start()
                s_load(c + 2).start()
        for c in (0, 1):
            s_load(c).start()

    def keep_rest():
        for n in range(line):
            for w in (3, 2):
                feed(FEED["keep"])
                join(n, w)
                if n < line - 1:
                    for c in pair(n + 1, w):
                        c.start()

    back3 = plane_sum(line, first_pass, three, keep_rest, lambda: feed(FEED["later3"]))
    bs3_ref[...] = back3
    for c in range(chunks):
        s_load(c).wait()
        row, at = third_params(c)
        mean = s3_ref[row : row + 1, at] / pixels_wide
        var = s3_ref[row + 1 : row + 2, at] / pixels_wide - mean * mean
        inverse = lax.rsqrt(var + norm_epsilon)
        here = slice(c * wide, (c + 1) * wide)
        v = (
            mask(0)
            * (inverse * par3_ref[row : row + 1, at])
            * (
                dpre[:, here] * mask(0)
                - back3[row : row + 1, at] / pixels_wide
                - s_room[c % 2] * (back3[row + 1 : row + 2, at] / pixels_wide)
            )
        )
        dthird[:, here] = v.astype(bf)
        feed(FEED["third"])
        if c + 2 < chunks:
            s_load(c + 2).start()
    weights[0].wait()
    scaled2 = sc2_ref[...]
    normed2 = scaled2 * par_ref[2:3] + par_ref[3:4]
    feed(FEED["d2"])
    d2 = nt(dthird[...], we_v[...]) * slope(normed2) * mask(0)

    state = []

    def put(value, *targets):
        n = len(state)
        if n >= 2:
            for c in state[n - 2]:
                c.wait()
        grad_room[n % 2] = value.astype(bf)
        cols = middle // len(targets)
        state.append(
            [
                pltpu.make_async_copy(
                    grad_room.at[n % 2, :, pl.ds(i * cols, cols)], ref, grad_sem.at[n % 2, i]
                )
                for i, ref in enumerate(targets)
            ]
        )
        for c in state[n]:
            c.start()

    hidden2 = silu(normed2).astype(bf)

    def expand_grads():
        for q in range(parts):
            feed(FEED["ge"])
            per = count // parts
            put(
                tn(hidden2, dthird[:, q * middle : (q + 1) * middle]),
                *(ge_ref.at[q * per + i] for i in range(per)),
            )

    back2 = plane_sum(
        line, lambda ref: moved_sums(ref, 0, slice(None), d2, scaled2), two, expand_grads,
        lambda: feed(FEED["later2"]),
    )
    bs2_ref[...] = back2

    def through(d, scaled, sums, back, gain):
        _, inverse = scale_rows(sums, pixels)
        return mask(0) * (inverse * gain) * (d - back[0:1] / pixels - scaled * (back[1:2] / pixels))

    ext[halo : halo + px] = through(d2, scaled2, s2_ref, back2, par_ref[2:3]).astype(bf)

    def edge(up):
        src = ext.at[pl.ds(px if up else halo, halo)]
        dst = ext.at[pl.ds(0 if up else halo + px, halo)]
        return pltpu.make_async_remote_copy(
            src_ref=src,
            dst_ref=dst,
            send_sem=h_send.at[int(up)],
            recv_sem=h_recv.at[int(up)],
            device_id=t.at(t.place + (1 if up else -1)),
            device_id_type=MESH,
        )

    has_next, has_last = t.place < count - 1, t.place > 0
    pl.when(has_last)(lambda: edge(False).start())
    pl.when(has_next)(lambda: edge(True).start())
    weights[1].wait()
    scaled1 = sc1_ref[...]
    normed1 = scaled1 * par_ref[0:1] + par_ref[1:2]
    hidden1 = silu(normed1).astype(bf)

    def spread(j):
        v = ext[(2 - j) * halo : (2 - j) * halo + px].astype(f32)
        kept_row = 1.0 if j == 1 else mask(4 if j == 0 else 3)
        for c in range(3):
            if c == 0:
                moved, kept = pltpu.roll(v, px - rate, 0), mask(2)
            elif c == 1:
                moved, kept = v, mask(0)
            else:
                moved, kept = pltpu.roll(v, rate, 0), mask(1) * mask(0)
            k = 3 * j + c
            taps[:, k * middle : (k + 1) * middle] = jnp.where(kept * kept_row > 0, moved, 0.0).astype(bf)

    def tap(k):
        return taps[:, k * middle : (k + 1) * middle]

    feed(FEED["edge"])
    spread(1)
    d1 = None
    for j in (1, 0, 2):
        if j == 0:
            pl.when(has_next)(lambda: edge(False).wait_recv())
            pl.when(has_last)(lambda: edge(True).wait_recv())
            spread(0)
            spread(2)
        for c in range(3):
            k = 3 * j + c
            feed(FEED["d1"])
            part = nt(tap(k), wd_v[k * middle : (k + 1) * middle])
            d1 = part if d1 is None else d1 + part
    d1 = d1 * slope(normed1) * mask(0)

    def dilated_grads():
        for k in range(9):
            feed(FEED["gd"])
            put(tn(hidden1, tap(k)), gd_ref.at[k])

    back1 = plane_sum(
        line, lambda ref: moved_sums(ref, 0, slice(None), d1, scaled1), one, dilated_grads,
        lambda: feed(FEED["later1"]),
    )
    bs1_ref[...] = back1
    dfirst = through(d1, scaled1, s1_ref, back1, par_ref[0:1]).astype(bf)
    feed(len(pieces))
    weights[2].wait()
    outs = []
    for q in range(parts):
        here = slice(q * middle, (q + 1) * middle)
        if q >= 2:
            outs[q - 2].wait()
        out_room[q % 2] = nt(dfirst, wr_v[here]) + dpre[:, here]
        outs.append(
            pltpu.make_async_copy(
                out_room.at[q % 2], fg_ref.at[:, pl.ds(q * middle, middle)], out_sem.at[q % 2]
            )
        )
        outs[q].start()
    for q in range(parts):
        here = slice(q * middle, (q + 1) * middle)
        put(tn(x_ref[:, here], dfirst), gr_ref.at[pl.ds(q * middle, middle)])

    def stays(n):
        return pltpu.make_async_copy(acc.at[n], sum_ref.at[n], sum_sem.at[n])

    @pl.loop(0, line)
    def _(n):
        for w in (1, 0):
            to_b(n, w).wait_recv()
            at = n * 2 + w

            @pl.loop(0, heads)
            def _(h):
                acc[at, h] = acc[at, h] + b_room[at, h]

            stays(at).start()

    for c in state[-2] + state[-1] + outs[-2:]:
        c.wait()

    @pl.loop(0, line)
    def _(n):
        for w in (1, 0):
            to_b(n, w).wait_send()
            stays(n * 2 + w).wait()

    pl.when(has_last)(lambda: edge(False).wait_send())
    pl.when(has_next)(lambda: edge(True).wait_send())


def back_step(x, task_scale, squares, scaled1, scaled2, scaled3, params, params3, sums1, sums2, sums3, masks, grads,
              wr, wd, we, own, got, rate, rows, cols, number):
    px, channels = x.shape
    count = lax.axis_size("fsdp")
    line = count // 4
    middle = params.shape[1]
    parts = channels // middle
    wide = middle // 2
    heads, _, head_rows, half = own.shape
    bf, f32 = jnp.bfloat16, jnp.float32
    dma = pltpu.SemaphoreType.DMA
    vmem = pl.BlockSpec(memory_space=pltpu.VMEM)
    hbm = pl.BlockSpec(memory_space=pl.ANY)
    S = jax.ShapeDtypeStruct
    V = pltpu.VMEM
    return pl.pallas_call(
        functools.partial(back_kernel, rate, rows, cols, count, heads),
        out_shape=(
            S(task_scale.shape, f32),
            S((2, middle), f32),
            S((2, middle), f32),
            S((2 * parts, middle), f32),
            S((px, channels), f32),
            S((channels, middle), bf),
            S((9, middle, middle), bf),
            S((count, middle, channels // count), bf),
            S((2 * line, heads, head_rows, half), bf),
        ),
        in_specs=[vmem] * 11 + [hbm] * 7,
        out_specs=(vmem,) * 4 + (hbm,) * 5,
        scratch_shapes=[
            V((2 * line, heads, head_rows, half), bf),
            V((2 * line, heads, head_rows, half), bf),
            V((2 * line, heads, head_rows, half), bf),
            V((2, heads, head_rows, half), bf),
            V((2, grads.shape[0], px, wide), f32),
            V((2, px, wide), f32),
            V((px, channels), f32),
            V((px, channels), bf),
            V((channels, middle), bf),
            V((9 * middle, middle), bf),
            V((middle, channels), bf),
            V((px + 2 * rate * cols, middle), bf),
            V((px, 9 * middle), bf),
            V((2, px, middle), f32),
            V((2, middle, middle), bf),
            dma((2,)),
            dma((2,)),
            dma((2 * line,)),
            dma((2 * line,)),
            dma((2,)),
            dma((2,)),
            dma((3,)),
            dma((2,)),
            dma((2,)),
            dma((2,)),
            dma((2, count // parts)),
            dma((2 * line,)),
        ]
        + plane_scratch(line, (2, middle))
        + plane_scratch(line, (2, middle))
        + plane_scratch(line, (2 * parts, middle))
        + plane_scratch(line, squares.shape),
        compiler_params=pltpu.CompilerParams(
            collective_id=number, has_side_effects=True, vmem_limit_bytes=63 * 2**20
        ),
    )(x, task_scale, squares, scaled1, scaled2, params, params3, sums1, sums2, sums3, masks,
      grads, scaled3, wr, wd, we, own, got)


def silu_slope(values):
    sigmoid_value = jax.nn.sigmoid(values)
    return sigmoid_value * (1.0 + values * (1.0 - sigmoid_value))


def shift_along(values, offset, axis_number):
    if offset == 0:
        return values
    length = values.shape[axis_number]
    pad_shape = list(values.shape)
    pad_shape[axis_number] = abs(offset)
    zero_block = jnp.zeros(pad_shape, values.dtype)
    if offset > 0:
        return jnp.concatenate(
            [lax.slice_in_dim(values, offset, length, axis=axis_number), zero_block], axis_number
        )
    return jnp.concatenate(
        [zero_block, lax.slice_in_dim(values, 0, length + offset, axis=axis_number)], axis_number
    )


def inside_rows(layout, offset):
    row_ids, row_top, row_bottom, row_side = layout
    return (row_ids + offset >= row_top) & (row_ids + offset < row_bottom)


def inside_cols(layout, offset, col_count):
    row_ids, row_top, row_bottom, row_side = layout
    columns = jnp.arange(col_count, dtype=jnp.int32)
    return (columns[None, :] + offset >= 0) & (columns[None, :] + offset < row_side[:, None])


def column_sums(inputs, weight, rate, layout):
    col_count = inputs.shape[1]
    products = jnp.einsum("rwc,kco->krwo", inputs, weight, preferred_element_type=jnp.float32)
    sums = []
    for row_step in range(3):
        summed = 0.0
        for col_step in range(3):
            across = (col_step - 1) * rate
            summed = summed + jnp.where(
                inside_cols(layout, across, col_count)[:, :, None],
                shift_along(products[3 * row_step + col_step], across, 1),
                0.0,
            )
        sums.append(summed)
    return sums


def dilated_forward(inputs, weights, rates, layout, number):
    outer, centers = [], []
    for weight, rate in zip(weights, rates):
        low, center, high = column_sums(inputs, weight, rate, layout)
        outer += [low.astype(jnp.bfloat16), high.astype(jnp.bfloat16)]
        centers.append(center)
    offsets = tuple(o for rate in rates for o in (-rate, rate))
    pulled = exchange(jnp.stack(outer), offsets, number)
    results = []
    for k, (center, rate) in enumerate(zip(centers, rates)):
        for j, down in ((2 * k, -rate), (2 * k + 1, rate)):
            center = center + jnp.where(
                inside_rows(layout, down)[:, None, None], pulled[j].astype(jnp.float32), 0.0
            )
        results.append(center)
    return results


def spread_taps(grads, rates, layout, number):
    row_ids = layout[0]
    row_count, col_count = grads[0].shape[:2]
    total_rows = row_count * lax.axis_size("fsdp")
    outer = []
    for grad, rate in zip(grads, rates):
        for down in (-rate, rate):
            outer.append(
                jnp.where(inside_rows(layout, down)[:, None, None], grad, jnp.bfloat16(0.0))
            )
    offsets = tuple(o for rate in rates for o in (rate, -rate))
    pulled = exchange(jnp.stack(outer), offsets, number)
    results = []
    for k, (grad, rate) in enumerate(zip(grads, rates)):
        taps = []
        for row_step in range(3):
            down = (row_step - 1) * rate
            if row_step == 1:
                arrived = grad
            else:
                there = (row_ids - down >= 0) & (row_ids - down < total_rows)
                arrived = jnp.where(
                    there[:, None, None], pulled[2 * k + row_step // 2], jnp.bfloat16(0.0)
                )
            for col_step in range(3):
                across = (col_step - 1) * rate
                kept = jnp.where(
                    inside_cols(layout, across, col_count)[:, :, None], arrived, jnp.bfloat16(0.0)
                )
                taps.append(shift_along(kept, -across, 1))
        results.append(taps)
    return results


def spread(stat):
    return stat.reshape(stat.shape[:-1] + (1, 1) + stat.shape[-1:])


def totals_of(one, two, number):
    local_sums = jnp.stack([jnp.sum(one, axis=(-3, -2)), jnp.sum(two, axis=(-3, -2))])
    flat = all_sum(local_sums.reshape(2, -1), number)
    return flat.reshape(local_sums.shape)


def moments(values, valid_mask, number):
    weighted = values * valid_mask[..., None]
    return totals_of(weighted, weighted * values, number)


def normalize(values, sums, valid_count, gain_row, bias_row):
    mean_value = sums[0] / valid_count
    variance = sums[1] / valid_count - mean_value * mean_value
    inverse = lax.rsqrt(variance + norm_epsilon)
    scaled = (values - spread(mean_value)) * spread(inverse)
    return (scaled, inverse, scaled * spread(gain_row) + spread(bias_row))


def norm_backward(grad_norm, scaled, inverse, gain_row, valid_mask, valid_count, number):
    masked = grad_norm * valid_mask[..., None]
    sums = totals_of(masked, masked * scaled, number)
    grad_values = (
        valid_mask[..., None]
        * spread(inverse * gain_row)
        * (masked - spread(sums[0] / valid_count) - scaled * spread(sums[1] / valid_count))
    )
    return (grad_values, sums)


def update(param, moment, grad):
    moment_new = momentum_decay * moment + grad
    return (param - step_rate * moment_new, moment_new)


def local(
    features,
    cotangent,
    crop_heights,
    task_scale,
    w_reduce,
    w_dilated,
    w_expand,
    w_heads,
    norm_params,
    m_reduce,
    m_dilated,
    m_expand,
    m_heads,
    norm_moment,
):
    row_count = features.shape[1]
    col_count = features.shape[2]
    channels = features.shape[3]
    middle = w_reduce.shape[1]
    head_width = w_heads.shape[2]
    head_total = w_heads.shape[0]
    group_index = lax.axis_index("dp")
    place_index = lax.axis_index("fsdp")
    group_heights = lax.dynamic_index_in_dim(crop_heights, group_index, 0, keepdims=False)
    crop_order = jnp.arange(group_heights.shape[0], dtype=jnp.int32)
    crop_ends = jnp.sum(
        jnp.where(crop_order[None, :] <= crop_order[:, None], group_heights[None, :], 0),
        axis=1,
        dtype=jnp.int32,
    )
    crop_starts = crop_ends - group_heights
    row_ids = place_index * row_count + jnp.arange(row_count, dtype=jnp.int32)
    member = (row_ids[:, None] >= crop_starts[None, :]) & (row_ids[:, None] < crop_ends[None, :])
    row_top = jnp.sum(jnp.where(member, crop_starts[None, :], 0), axis=1, dtype=jnp.int32)
    row_bottom = jnp.sum(jnp.where(member, crop_ends[None, :], 0), axis=1, dtype=jnp.int32)
    row_side = jnp.sum(jnp.where(member, group_heights[None, :], 0), axis=1, dtype=jnp.int32)
    layout = (row_ids, row_top, row_bottom, row_side)
    valid_mask = (jnp.arange(col_count, dtype=jnp.int32)[None, :] < row_side[:, None]).astype(
        jnp.float32
    )
    valid_count = jnp.sum(crop_heights * crop_heights).astype(jnp.float32)
    gain_values = norm_params[0]
    bias_values = norm_params[1]
    trunk_end = 2 * middle + channels
    inputs = features[0]
    inputs_float = inputs.astype(jnp.float32)
    place_count = lax.axis_size("fsdp")
    pixels = row_count * col_count
    half_rows = w_heads.shape[1] // 2
    heads_half = lax.dynamic_slice_in_dim(w_heads, group_index * half_rows, half_rows, 1)

    def beside(part):
        return lax.all_gather(
            part.astype(jnp.bfloat16), ("fsdp", "dp"), axis=1, tiled=True
        ).reshape(-1, channels, head_width)

    heads_late = beside(heads_half[1:])
    if place_count == 16:
        (
            reduce_low, dilated_low, expand_low, heads_early, trunk_out,
            scaled_one, scaled_two, scaled_three, sums_in_one, sums_in_two, sums_in_three,
            flat_params, wide_params, head_params, masks, turned,
        ) = trunk_step(
            inputs.reshape(pixels, channels),
            (
                w_reduce.astype(jnp.bfloat16),
                w_dilated.astype(jnp.bfloat16),
                w_expand.astype(jnp.bfloat16),
                w_heads[:1].astype(jnp.bfloat16),
            ),
            norm_params,
            crop_heights,
            head_rates + (trunk_rate,),
            row_count,
            col_count,
            middle,
            0,
        )
        heads_early = heads_early.reshape(-1, channels, head_width)
    else:
        head_gain = gain_values[trunk_end:].reshape(head_total, head_width)
        head_bias = bias_values[trunk_end:].reshape(head_total, head_width)
        head_params = jnp.concatenate(
            [
                jnp.stack([head_gain, head_bias], 1).reshape(2 * head_total, head_width),
                jnp.broadcast_to(valid_count, (2, head_width)),
            ]
        )
        total_rows = row_count * place_count
        masks = []
        for rate in head_rates + (trunk_rate,):
            flags = [
                inside_cols(layout, 0, col_count),
                inside_cols(layout, -rate, col_count),
                inside_cols(layout, rate, col_count),
            ] + [
                jnp.broadcast_to(flag[:, None], (row_count, col_count))
                for flag in (
                    inside_rows(layout, -rate),
                    inside_rows(layout, rate),
                    row_ids + rate < total_rows,
                    row_ids - rate >= 0,
                )
            ]
            flags = jnp.stack([f.reshape(pixels) for f in flags], 1).astype(jnp.float32)
            masks.append(jnp.pad(flags, ((0, 0), (0, 128 - flags.shape[1]))))
        masks = jnp.stack(masks)
        heads_early = beside(heads_half[:1])
        reduce_low, dilated_low, expand_low = (
            lax.all_gather(w.astype(jnp.bfloat16), "fsdp", axis=0)
            for w in (w_reduce, w_dilated, w_expand)
        )
        reduce_low = reduce_low.reshape(channels, middle)
        dilated_low = dilated_low.reshape(9, middle, middle)
        first = jnp.einsum("rwc,cm->rwm", inputs, reduce_low, preferred_element_type=jnp.float32)
        scaled_one, inverse_one, normed_one = normalize(
            first, moments(first, valid_mask, 1), valid_count, gain_values[:middle], bias_values[:middle]
        )
        hidden_one = jax.nn.silu(normed_one).astype(jnp.bfloat16)
        (second,) = dilated_forward(hidden_one, (dilated_low,), (trunk_rate,), layout, 2)
        scaled_two, inverse_two, normed_two = normalize(
            second,
            moments(second, valid_mask, 3),
            valid_count,
            gain_values[middle : 2 * middle],
            bias_values[middle : 2 * middle],
        )
        hidden_two = jax.nn.silu(normed_two).astype(jnp.bfloat16)
        expand_low = expand_low.transpose(1, 0, 2).reshape(middle, channels)
        third = jnp.einsum("rwm,mc->rwc", hidden_two, expand_low, preferred_element_type=jnp.float32)
        scaled_three, inverse_three, normed_three = normalize(
            third,
            moments(third, valid_mask, 4),
            valid_count,
            gain_values[2 * middle : trunk_end],
            bias_values[2 * middle : trunk_end],
        )
        pre_act = inputs_float + normed_three
        trunk_out = jax.nn.silu(pre_act).astype(jnp.bfloat16).reshape(pixels, channels)
        turned = trunk_out.T
    handed = head_total - 1
    head_grads, grads_own, grads_got, grads_late, head_sums, squares = heads_step(
        trunk_out,
        turned,
        heads_early,
        heads_late,
        cotangent.reshape(head_total, pixels, head_width),
        head_params,
        masks,
        head_rates,
        row_count,
        col_count,
        handed,
        5,
    )
    head_sums = head_sums.reshape(head_total, 2, head_width).transpose(1, 0, 2)
    shared = lax.psum_scatter(
        grads_late.reshape(-1, head_width), ("fsdp", "dp"), scatter_dimension=0, tiled=True
    )
    late_total = lax.all_gather(shared, "dp", axis=0, tiled=True)[None]
    if place_count == 16:
        (
            task_weight, back_one, back_two, back_three, features_grad, grad_reduce, grad_dilated, grad_expand, late,
        ) = back_step(
            inputs.reshape(pixels, channels),
            jnp.broadcast_to(jnp.pad(task_scale, (0, 8 - head_total))[:, None], (8, 128)),
            squares,
            scaled_one,
            scaled_two,
            scaled_three,
            flat_params,
            wide_params,
            sums_in_one,
            sums_in_two,
            sums_in_three,
            masks,
            head_grads,
            reduce_low,
            dilated_low,
            expand_low,
            grads_own.reshape(handed, place_count, -1, head_width // 2),
            grads_got.reshape(handed, place_count, -1, head_width // 2),
            trunk_rate,
            row_count,
            col_count,
            1,
        )
        task_weight = task_weight[:head_total, 0]
        features_grad = features_grad.reshape(row_count, col_count, channels)
        *trunk_totals, heads_total = reduce_shards(
            (
                grad_reduce.reshape(1, place_count, -1, middle),
                grad_dilated.reshape(1, place_count, -1, middle),
                grad_expand[None],
            ),
            (late,),
            2,
        )
        trunk_totals = [t[0] for t in trunk_totals]
        sums_one, sums_two = back_one, back_two
        sums_three = back_three.reshape(-1, 2, middle).transpose(1, 0, 2).reshape(2, channels)
    else:
        squares = jnp.sum(all_sum(squares, 9)[:head_total], axis=1)
        task_rms = jnp.sqrt(squares / (valid_count * channels) + task_epsilon)
        task_weight = task_scale / task_rms
        grad_trunk = task_weight[0] * head_grads[0]
        for k in range(1, head_total):
            grad_trunk = grad_trunk + task_weight[k] * head_grads[k]
        grad_trunk = grad_trunk.reshape(row_count, col_count, channels)
        grad_pre = grad_trunk * silu_slope(pre_act)
        grad_third, sums_three = norm_backward(
            grad_pre,
            scaled_three,
            inverse_three,
            gain_values[2 * middle : trunk_end],
            valid_mask,
            valid_count,
            11,
        )
        grad_third = grad_third.astype(jnp.bfloat16)
        grad_expand = jnp.einsum(
            "rwm,rwc->mc", hidden_two, grad_third, preferred_element_type=jnp.float32
        ).astype(jnp.bfloat16)
        grad_hidden_two = jnp.einsum(
            "rwc,mc->rwm", grad_third, expand_low, preferred_element_type=jnp.float32
        )
        grad_second, sums_two = norm_backward(
            grad_hidden_two * silu_slope(normed_two),
            scaled_two,
            inverse_two,
            gain_values[middle : 2 * middle],
            valid_mask,
            valid_count,
            12,
        )
        (taps,) = spread_taps([grad_second.astype(jnp.bfloat16)], (trunk_rate,), layout, 13)
        taps = jnp.stack(taps)
        grad_hidden_one = jnp.einsum(
            "krwo,kco->rwc", taps, dilated_low, preferred_element_type=jnp.float32
        )
        grad_dilated = jnp.einsum(
            "rwc,krwo->kco", hidden_one, taps, preferred_element_type=jnp.float32
        )
        grad_first, sums_one = norm_backward(
            grad_hidden_one * silu_slope(normed_one),
            scaled_one,
            inverse_one,
            gain_values[:middle],
            valid_mask,
            valid_count,
            14,
        )
        grad_first = grad_first.astype(jnp.bfloat16)
        grad_reduce = jnp.einsum("rwc,rwm->cm", inputs, grad_first, preferred_element_type=jnp.float32)
        features_grad = (
            jnp.einsum("rwm,cm->rwc", grad_first, reduce_low, preferred_element_type=jnp.float32)
            + grad_pre
        )
        trunk_totals = []
        for grad, axis in ((grad_reduce, 0), (grad_dilated.reshape(-1, middle), 0), (grad_expand, 1)):
            shard = lax.psum_scatter(
                grad.astype(jnp.bfloat16), "fsdp", scatter_dimension=axis, tiled=True
            )
            trunk_totals.append(lax.psum(shard, "dp"))
        shared = lax.psum_scatter(
            (grads_own + grads_got).reshape(handed, -1, head_width // 2),
            "fsdp",
            scatter_dimension=1,
            tiled=True,
        )
        heads_total = lax.all_gather(shared, "dp", axis=2, tiled=True)
    totals = tuple(t.astype(jnp.float32) for t in trunk_totals) + (
        task_weight[:, None, None]
        * jnp.concatenate([heads_total, late_total]).astype(jnp.float32),
    )
    gain_grad = jnp.concatenate(
        [sums_one[1], sums_two[1], sums_three[1], (task_weight[:, None] * head_sums[1]).reshape(-1)]
    )
    bias_grad = jnp.concatenate(
        [sums_one[0], sums_two[0], sums_three[0], (task_weight[:, None] * head_sums[0]).reshape(-1)]
    )
    norm_grad = jnp.stack([gain_grad, bias_grad])
    w_reduce_new, m_reduce_new = update(w_reduce, m_reduce, totals[0])
    w_dilated_new, m_dilated_new = update(w_dilated, m_dilated, totals[1])
    w_expand_new, m_expand_new = update(w_expand, m_expand, totals[2])
    w_heads_new, m_heads_new = update(w_heads, m_heads, totals[3])
    norm_params_new, norm_moment_new = update(norm_params, norm_moment, norm_grad)
    return (
        features_grad[None],
        w_reduce_new,
        m_reduce_new,
        w_dilated_new,
        m_dilated_new,
        w_expand_new,
        m_expand_new,
        w_heads_new,
        m_heads_new,
        norm_params_new,
        norm_moment_new,
    )


def solution(mesh):
    placed = (
        P("dp", "fsdp", None, None),
        P(None, "dp", "fsdp", None, None),
        P(),
        P(),
        P("fsdp", None),
        P("fsdp", None),
        P(None, "fsdp"),
        P(None, "fsdp", None),
        P(),
        P("fsdp", None),
        P("fsdp", None),
        P(None, "fsdp"),
        P(None, "fsdp", None),
        P(),
    )
    return jax.shard_map(
        local,
        mesh=mesh,
        in_specs=placed,
        out_specs=(
            P("dp", "fsdp", None, None),
            P("fsdp", None),
            P("fsdp", None),
            P("fsdp", None),
            P("fsdp", None),
            P(None, "fsdp"),
            P(None, "fsdp"),
            P(None, "fsdp", None),
            P(None, "fsdp", None),
            P(),
            P(),
        ),
        check_vma=False,
    )
```

```python
import functools

import jax
import jax.numpy as jnp
from jax import lax
from jax.experimental import pallas as pl
from jax.experimental.pallas import tpu as pltpu
from jax.sharding import PartitionSpec as P

MESH = pl.DeviceIdType.MESH
norm_epsilon = 1e-05
task_epsilon = 1e-06
momentum_decay = 0.9
step_rate = 0.01
trunk_rate = 4
head_rates = (12, 24, 36)

class Tree:
    def __init__(self):
        self.core = lax.axis_index("dp")
        self.place = lax.axis_index("fsdp")
        self.count = lax.axis_size("fsdp")
        self.line = self.count // 4
        self.z = self.place // 4
        self.low = self.place % 4
        self.step_a = 1 + self.core
        self.step_b = 2 - self.core
        self.move_a = self.step_a * (1 - 2 * ((self.low // self.step_a) % 2))
        self.move_b = self.step_b * (1 - 2 * ((self.low // self.step_b) % 2))

    def at(self, place):
        return (self.core, place)

    @property
    def partner(self):
        return (1 - self.core, self.place)

    @property
    def a(self):
        return self.at(self.place + self.move_a)

    @property
    def b(self):
        return self.at(self.place + self.move_b)

    @property
    def down(self):
        return self.at(self.place - 4)

    @property
    def up(self):
        return self.at(self.place + 4)

    def greet(self):
        barrier = pltpu.get_barrier_semaphore()
        for peer in (self.partner, self.a, self.b):
            pl.semaphore_signal(barrier, inc=1, device_id=peer, device_id_type=MESH)

        @pl.when(self.z > 0)
        def _():
            pl.semaphore_signal(barrier, inc=1, device_id=self.down, device_id_type=MESH)

        @pl.when(self.z < self.line - 1)
        def _():
            pl.semaphore_signal(barrier, inc=1, device_id=self.up, device_id_type=MESH)

        pl.semaphore_wait(
            barrier,
            3
            + jnp.where(self.z > 0, 1, 0)
            + jnp.where(self.z < self.line - 1, 1, 0),
        )


def plane_sum_kernel(line, x_ref, o_ref, near, part, far, n_send, n_recv, f_send, f_recv):
    core = lax.axis_index("dp")
    place = lax.axis_index("fsdp")
    z, low = place // 4, place % 4
    me = low * 2 + core

    def beside(s):
        other = (me + s) % 8
        return (other % 2, z * 4 + other // 2)

    def away(s):
        return (core, ((z + s) % line) * 4 + low)

    barrier = pltpu.get_barrier_semaphore()
    for s in range(1, 8):
        pl.semaphore_signal(barrier, inc=1, device_id=beside(s), device_id_type=MESH)

    @pl.loop(1, line)
    def _(s):
        pl.semaphore_signal(barrier, inc=1, device_id=away(s), device_id_type=MESH)

    near[me] = x_ref[...]
    pl.semaphore_wait(barrier, 7 + line - 1)

    def to_beside(s):
        return pltpu.make_async_remote_copy(src_ref=x_ref, dst_ref=near.at[me], send_sem=n_send.at[s], recv_sem=n_recv, device_id=beside(s), device_id_type=MESH)

    def to_away(s):
        return pltpu.make_async_remote_copy(src_ref=part, dst_ref=far.at[z], send_sem=f_send.at[s], recv_sem=f_recv, device_id=away(s), device_id_type=MESH)

    for s in range(1, 8):
        to_beside(s).start()
    seven = near.at[pl.ds(0, 7)]
    pltpu.make_async_copy(seven, seven, n_recv).wait()
    total = jnp.sum(near[...], axis=0)
    part[...] = total
    pl.loop(1, line)(lambda s: to_away(s).start())
    far[z] = total
    rest = far.at[pl.ds(0, line - 1)]
    pltpu.make_async_copy(rest, rest, f_recv).wait()
    o_ref[...] = jnp.sum(far[...], axis=0)
    for s in range(1, 8):
        to_beside(s).wait_send()
    pl.loop(1, line)(lambda s: to_away(s).wait_send())


def all_sum(x, number):
    line = lax.axis_size("fsdp") // 4
    dma = pltpu.SemaphoreType.DMA
    return pl.pallas_call(
        functools.partial(plane_sum_kernel, line),
        out_shape=jax.ShapeDtypeStruct(x.shape, x.dtype),
        in_specs=[pl.BlockSpec(memory_space=pltpu.VMEM)],
        out_specs=pl.BlockSpec(memory_space=pltpu.VMEM),
        scratch_shapes=[
            pltpu.VMEM((8,) + x.shape, x.dtype), pltpu.VMEM(x.shape, x.dtype), pltpu.VMEM((line,) + x.shape, x.dtype),
            dma((8,)), dma, dma((line,)), dma,
        ],
        compiler_params=pltpu.CompilerParams(collective_id=number, has_side_effects=True),
    )(x)


def reduce_kernel(kinds, whole, *refs):
    count = len(kinds)
    parts, outs = refs[:count], refs[count : 2 * count]
    scratch = refs[2 * count :]
    accs, arx, zrx = (scratch[k * count : (k + 1) * count] for k in range(3))
    prx, brx = (scratch[3 * count + k * whole : 3 * count + (k + 1) * whole] for k in range(2))
    (
        load_sem, p_send, p_recv, b_send, b_recv, a_send, a_recv, z_send, z_recv, s_send, s_recv,
    ) = scratch[3 * count + 2 * whole :]
    t = Tree()
    t.greet()
    line, z, low = t.line, t.z, t.low

    def rows_of(k, core):
        rows = kinds[k][1] // 2
        return pl.ds(pl.multiple_of(core * rows, 16), rows)

    def remote(src, dst, send, recv, peer):
        return pltpu.make_async_remote_copy(src_ref=src, dst_ref=dst, send_sem=send, recv_sem=recv, device_id=peer, device_id_type=MESH)

    def load(k, block):
        return pltpu.make_async_copy(
            parts[k].at[:, block, rows_of(k, t.core)], accs[k].at[block], load_sem.at[k, block]
        )

    def load_late(k, at):
        return pltpu.make_async_copy(parts[k].at[at], accs[k].at[at], load_sem.at[k, at])

    def spot_of(k, zz, w):
        if k < whole:
            return zz * 4 + lows[w]
        return zz * 2 + (3 - w)

    def to_partner(k, block):
        return remote(parts[k].at[:, block, rows_of(k, 1 - t.core)], prx[k].at[block], p_send.at[k, block], p_recv.at[k, block], t.partner)

    upper = z >= line // 2
    own_spot = jnp.where(upper, z, line - 1 - z)

    def spot(j):
        q = j + jnp.where(j >= own_spot, 1, 0)
        other = jnp.where(upper, q, line - 1 - q)
        return jnp.where(j == line - 1, z, other)

    lows = (low + t.move_b, low + t.move_a + t.move_b, low + t.move_a, low)

    def to_b(k, zz, which):
        return remote(accs[k].at[zz * 4 + lows[which]], brx[k].at[zz * 2 + which], b_send.at[k, zz * 2 + which], b_recv.at[k, zz * 2 + which], t.b)

    def to_a(k, zz):
        return remote(accs[k].at[spot_of(k, zz, 2)], arx[k].at[zz], a_send.at[k, zz], a_recv.at[k, zz], t.a)

    def along(k, zz, up):
        w = 1 if up else 0
        return remote(accs[k].at[spot_of(k, zz, 3)], zrx[k].at[w, zz], z_send.at[k, w, zz], z_recv.at[k, w, zz], t.up if up else t.down)

    def add(k, block, ref):
        lead = kinds[k][0]

        @pl.loop(0, lead)
        def _(h):
            accs[k][block, h] = accs[k][block, h] + ref[h]

    def begin(j):
        zz = spot(j)
        for k in range(whole, count):
            load_late(k, zz * 2).start()
            load_late(k, zz * 2 + 1).start()
        for w in range(4):
            for k in range(whole):
                to_partner(k, zz * 4 + lows[w]).start()
                load(k, zz * 4 + lows[w]).start()

    first, last = range(whole), range(whole, count)

    def send_late(j):
        zz = spot(j)
        for k in last:
            load_late(k, zz * 2 + 1).wait()
            to_a(k, zz).start()

    def stage_b(j):
        zz = spot(j)
        for w in range(4):
            for k in first:
                block = zz * 4 + lows[w]
                load(k, block).wait()
                to_partner(k, block).wait_recv()
                add(k, block, prx[k].at[block])
                if w < 2:
                    to_b(k, zz, w).start()

    def stage_a(j):
        zz = spot(j)
        for w in (1, 0):
            for k in first:
                to_b(k, zz, w).wait_recv()
                add(k, zz * 4 + lows[3 if w == 0 else 2], brx[k].at[zz * 2 + w])
                if w == 1:
                    to_a(k, zz).start()

    def stage_z(j, ks):
        zz = spot(j)
        for k in ks:
            if k >= whole:
                load_late(k, zz * 2).wait()
            to_a(k, zz).wait_recv()
            here = spot_of(k, zz, 3)
            add(k, here, arx[k].at[zz])

            @pl.when(jnp.logical_and(zz >= z, z > 0))
            def _():
                along(k, zz, True).wait_recv()
                add(k, here, zrx[k].at[1, zz])

            @pl.when(jnp.logical_and(zz <= z, z < line - 1))
            def _():
                along(k, zz, False).wait_recv()
                add(k, here, zrx[k].at[0, zz])

            @pl.when(zz > z)
            def _():
                along(k, zz, True).start()

            @pl.when(zz < z)
            def _():
                along(k, zz, False).start()

    pl.loop(0, line)(begin)
    pl.loop(0, line)(send_late)
    pl.loop(0, line)(stage_b)

    @pl.loop(0, line + 1)
    def _(j):
        pl.when(j < line)(lambda: stage_z(j, last))
        pl.when(j >= 1)(lambda: stage_a(j - 1))

    pl.loop(0, line)(lambda j: stage_z(j, first))

    def half(k, core):
        if k < whole:
            return outs[k].at[:, rows_of(k, core)]
        cols = kinds[k][2]
        return outs[k].at[:, :, pl.ds(pl.multiple_of(core * cols, cols), cols)]

    def share(k):
        return remote(accs[k].at[spot_of(k, z, 3)], half(k, t.core), s_send.at[k], s_recv.at[k], t.partner)

    def keep(k):
        return pltpu.make_async_copy(accs[k].at[spot_of(k, z, 3)], half(k, t.core), load_sem.at[k, 0])

    for k in range(count):
        share(k).start()
        keep(k).start()

    @pl.loop(0, line)
    def _(j):
        zz = spot(j)
        for k in range(count):
            if k < whole:
                for w in range(4):
                    to_partner(k, zz * 4 + lows[w]).wait_send()
                to_b(k, zz, 0).wait_send()
                to_b(k, zz, 1).wait_send()
            to_a(k, zz).wait_send()
            pl.when(zz > z)(lambda: along(k, zz, True).wait_send())
            pl.when(zz < z)(lambda: along(k, zz, False).wait_send())

    for k in range(count):
        keep(k).wait()
        other = half(k, 1 - t.core)
        remote(other, other, s_send.at[k], s_recv.at[k], t.partner).wait_recv()
        share(k).wait_send()


def reduce_shards(parts, late, number):
    n = lax.axis_size("fsdp")
    line = n // 4
    whole = len(parts)
    kinds = [(p.shape[0], p.shape[2], p.shape[3]) for p in parts] + [p.shape[1:] for p in late]
    sizes = [(l, r // 2, c) for l, r, c in kinds[:whole]] + kinds[whole:]
    results = kinds[:whole] + [(l, r, 2 * c) for l, r, c in kinds[whole:]]
    bf = jnp.bfloat16
    count = len(kinds)
    dma = pltpu.SemaphoreType.DMA

    def room(some, *lead):
        return [pltpu.VMEM(tuple(lead) + tuple(s), bf) for s in some]

    accs = [
        pltpu.VMEM((n if k < whole else 2 * line,) + tuple(s), bf) for k, s in enumerate(sizes)
    ]
    return pl.pallas_call(
        functools.partial(reduce_kernel, kinds, whole),
        out_shape=tuple(jax.ShapeDtypeStruct(r, bf) for r in results),
        in_specs=[pl.BlockSpec(memory_space=pl.ANY)] * count,
        out_specs=tuple([pl.BlockSpec(memory_space=pl.ANY)] * count),
        scratch_shapes=accs
        + room(sizes, line)
        + room(sizes, 2, line)
        + room(sizes[:whole], n)
        + room(sizes[:whole], 2 * line)
        + [
            dma((count, n)),
            dma((count, n)),
            dma((count, n)),
            dma((count, 2 * line)),
            dma((count, 2 * line)),
            dma((count, line)),
            dma((count, line)),
            dma((count, 2, line)),
            dma((count, 2, line)),
            dma((count,)),
            dma((count,)),
        ],
        compiler_params=pltpu.CompilerParams(
            collective_id=number, has_side_effects=True, vmem_limit_bytes=60 * 2**20
        ),
    )(*parts, *late)


def exchange_kernel(offsets, rows, count, x_ref, o_ref, send, recv):
    core = lax.axis_index("dp")
    place = lax.axis_index("fsdp")
    pieces = []
    for k, offset in enumerate(offsets):
        first, cut = offset // rows, offset % rows
        for part, (gap, low, high, to) in enumerate(
            ((first, cut, rows, 0), (first + 1, 0, cut, rows - cut))
        ):
            if high > low:
                pieces.append((k, part, gap, low, high - low, to))
    gaps = sorted({abs(p[2]) for p in pieces} - {0})
    gaps = [-g for g in gaps] + gaps
    barrier = pltpu.get_barrier_semaphore()

    def present(gap):
        return jnp.logical_and(place + gap >= 0, place + gap < count)

    met = jnp.int32(0)
    for gap in gaps:
        met = met + jnp.where(present(gap), 1, 0)

        @pl.when(present(gap))
        def _():
            pl.semaphore_signal(
                barrier, inc=1, device_id=(core, place + gap), device_id_type=MESH
            )

    pl.semaphore_wait(barrier, met)

    def piece(k, part, gap, low, size, to):
        return pltpu.make_async_remote_copy(
            src_ref=x_ref.at[k, pl.ds(low, size)],
            dst_ref=o_ref.at[k, pl.ds(to, size)],
            send_sem=send.at[k, part],
            recv_sem=recv.at[k, part],
            device_id=(core, place - gap),
            device_id_type=MESH,
        )

    for p in pieces:
        k, part, gap, low, size, to = p
        if gap == 0:
            o_ref[k, to : to + size] = x_ref[k, low : low + size]
        else:
            pl.when(present(-gap))(lambda p=p: piece(*p).start())
    for p in pieces:
        if p[2]:
            pl.when(present(p[2]))(lambda p=p: piece(*p).wait_recv())
    for p in pieces:
        if p[2]:
            pl.when(present(-p[2]))(lambda p=p: piece(*p).wait_send())


def exchange(x, offsets, number):
    entries, rows = x.shape[:2]
    return pl.pallas_call(
        functools.partial(exchange_kernel, offsets, rows, lax.axis_size("fsdp")),
        out_shape=jax.ShapeDtypeStruct(x.shape, x.dtype),
        in_specs=[pl.BlockSpec(memory_space=pltpu.VMEM)],
        out_specs=pl.BlockSpec(memory_space=pltpu.VMEM),
        scratch_shapes=[
            pltpu.SemaphoreType.DMA((entries, 2)),
            pltpu.SemaphoreType.DMA((entries, 2)),
        ],
        compiler_params=pltpu.CompilerParams(
            collective_id=number, has_side_effects=True, vmem_limit_bytes=32 * 2**20
        ),
    )(x)


def plane_signal(line, core, z, low):
    barrier = pltpu.get_barrier_semaphore()
    me = low * 2 + core
    for s in range(1, 8):
        other = (me + s) % 8
        pl.semaphore_signal(
            barrier, inc=1, device_id=(other % 2, z * 4 + other // 2), device_id_type=MESH
        )

    @pl.loop(1, line)
    def _(s):
        pl.semaphore_signal(
            barrier, inc=1, device_id=(core, ((z + s) % line) * 4 + low), device_id_type=MESH
        )


def plane_scratch(line, shape):
    dma = pltpu.SemaphoreType.DMA
    return [
        pltpu.VMEM((8,) + shape, jnp.float32),
        pltpu.VMEM(shape, jnp.float32),
        pltpu.VMEM((line,) + shape, jnp.float32),
        dma((8,)),
        dma,
        dma((line,)),
        dma,
    ]


def plane_sum(line, fill, room, meanwhile=None, later=None):
    near, part, far, n_send, n_recv, f_send, f_recv = room
    core = lax.axis_index("dp")
    place = lax.axis_index("fsdp")
    z, low = place // 4, place % 4
    me = low * 2 + core

    def to_beside(s):
        other = (me + s) % 8
        return pltpu.make_async_remote_copy(
            src_ref=near.at[me],
            dst_ref=near.at[me],
            send_sem=n_send.at[s],
            recv_sem=n_recv,
            device_id=(other % 2, z * 4 + other // 2),
            device_id_type=MESH,
        )

    def to_away(s):
        return pltpu.make_async_remote_copy(
            src_ref=part,
            dst_ref=far.at[z],
            send_sem=f_send.at[s],
            recv_sem=f_recv,
            device_id=(core, ((z + s) % line) * 4 + low),
            device_id_type=MESH,
        )

    fill(near.at[me])
    for s in range(1, 8):
        to_beside(s).start()
    if meanwhile is not None:
        meanwhile()
    seven = near.at[pl.ds(0, 7)]
    pltpu.make_async_copy(seven, seven, n_recv).wait()
    total = jnp.sum(near[...], axis=0)
    part[...] = total
    pl.loop(1, line)(lambda s: to_away(s).start())
    far[z] = total
    if later is not None:
        later()
    rest = far.at[pl.ds(0, line - 1)]
    pltpu.make_async_copy(rest, rest, f_recv).wait()
    result = jnp.sum(far[...], axis=0)
    for s in range(1, 8):
        to_beside(s).wait_send()
    pl.loop(1, line)(lambda s: to_away(s).wait_send())
    return result


def row_pieces(offset, rows):
    first, cut = offset // rows, offset % rows
    pieces = [(first, cut, rows - cut, 0)]
    if cut:
        pieces.append((first + 1, 0, cut, rows - cut))
    return pieces


def row_gaps(offsets, rows):
    gaps = {abs(p[0]) for o in offsets for p in row_pieces(o, rows)} - {0}
    return sorted(-g for g in gaps) + sorted(gaps)


def greet_rows(gaps, count):
    barrier = pltpu.get_barrier_semaphore()
    core = lax.axis_index("dp")
    place = lax.axis_index("fsdp")
    met = jnp.int32(0)
    for gap in gaps:
        here = jnp.logical_and(place + gap >= 0, place + gap < count)
        met = met + jnp.where(here, 1, 0)

        @pl.when(here)
        def _():
            pl.semaphore_signal(
                barrier, inc=1, device_id=(core, place + gap), device_id_type=MESH
            )

    return met


class Rows:
    def __init__(self, offsets, rows, cols, count, x_ref, o_ref, send, recv):
        self.core = lax.axis_index("dp")
        self.place = lax.axis_index("fsdp")
        self.rows, self.cols, self.count = rows, cols, count
        self.offsets, self.x_ref, self.o_ref = offsets, x_ref, o_ref
        self.send, self.recv = send, recv

    def present(self, gap):
        return jnp.logical_and(self.place + gap >= 0, self.place + gap < self.count)

    def copies(self, k):
        for part, (gap, low, size, to) in enumerate(row_pieces(self.offsets[k], self.rows)):
            yield gap, low, size, to, pltpu.make_async_remote_copy(
                src_ref=self.x_ref.at[k, pl.ds(low * self.cols, size * self.cols)],
                dst_ref=self.o_ref.at[k, pl.ds(to * self.cols, size * self.cols)],
                send_sem=self.send.at[k, part],
                recv_sem=self.recv.at[k, part],
                device_id=(self.core, self.place - gap),
                device_id_type=MESH,
            )

    def start(self, k):
        for gap, low, size, to, copy in self.copies(k):
            if gap == 0:
                cols = self.cols
                self.o_ref[k, to * cols : (to + size) * cols] = self.x_ref[
                    k, low * cols : (low + size) * cols
                ]
            else:
                pl.when(self.present(-gap))(copy.start)

    def wait_recv(self, k):
        for gap, _, _, _, copy in self.copies(k):
            if gap:
                pl.when(self.present(gap))(copy.wait_recv)

    def wait_send(self, k):
        for gap, _, _, _, copy in self.copies(k):
            if gap:
                pl.when(self.present(-gap))(copy.wait_send)


def heads_kernel(
    rates, rows, cols, count,
    x_ref, xt_o, wa_ref, wb_ref, cot_o, par_ref, mask_ref,
    g_ref, own_ref, got_ref, late_ref, sums_ref, sq_ref,
    wv, out_rows, in_rows, resp, dn, taps, g_room, dw_room, xt_ref, cot_ref, late_sem,
    w_sem, f_send, f_recv, e_send, e_recv, g_sem, dw_sem, hand_sem, got_sem, *rooms,
):
    px = rows * cols
    heads = len(rates)
    width = par_ref.shape[1]
    line = count // 4
    core = lax.axis_index("dp")
    place = lax.axis_index("fsdp")
    z, low = place // 4, place % 4
    one, two = rooms[:7], rooms[7:]

    def w_copy(t, k):
        early = wa_ref.shape[0] // 9
        src = wa_ref.at[t * 9 + k] if t < early else wb_ref.at[(t - early) * 9 + k]
        return pltpu.make_async_copy(
            src, wv.at[t, :, k * width : (k + 1) * width], w_sem.at[t * 9 + k]
        )

    for t in reversed(range(heads)):
        for k in range(9):
            w_copy(t, k).start()
    fetched = [
        pltpu.make_async_copy(cot_o, cot_ref, late_sem.at[0]),
        pltpu.make_async_copy(xt_o, xt_ref, late_sem.at[1]),
    ]
    for c in fetched:
        c.start()
    fwd = Rows([o for r in rates for o in (-r, r)], rows, cols, count, out_rows, in_rows, f_send, f_recv)
    bwd = Rows([o for r in rates for o in (r, -r)], rows, cols, count, out_rows, in_rows, e_send, e_recv)
    plane_signal(line, core, z, low)
    met = greet_rows(row_gaps(fwd.offsets, rows), count)
    barrier = pltpu.get_barrier_semaphore()

    def mask(t, k):
        return mask_ref[t, :, k : k + 1]

    @pl.loop(0, heads)
    def _(step):
        t = heads - 1 - step
        rate = 12 * (t + 1)
        for j in (0, 2, 1):
            summed = None
            for c in range(3):
                k = 3 * j + c
                pltpu.make_async_copy(
                    wa_ref.at[k], wv.at[t, :, k * width : (k + 1) * width], w_sem.at[t * 9 + k]
                ).wait()
                prod = jnp.dot(
                    x_ref[...], wv[t, :, k * width : (k + 1) * width], preferred_element_type=jnp.float32
                )
                if c == 0:
                    summed = jnp.where(mask(t, 1) > 0, pltpu.roll(prod, rate, 0), 0.0)
                elif c == 1:
                    summed = summed + jnp.where(mask(t, 0) > 0, prod, 0.0)
                else:
                    summed = summed + jnp.where(mask(t, 2) > 0, pltpu.roll(prod, px - rate, 0), 0.0)
            if j == 1:
                resp[t] = summed
                continue
            out_rows[t * 2 + j // 2] = summed.astype(jnp.bfloat16)
            if j == 0:

                @pl.when(step == 0)
                def _():
                    pl.semaphore_wait(barrier, 7 + line - 1 + met)

            for h in range(heads):
                pl.when(t == h)(lambda: fwd.start(2 * h + j // 2))

    def stats(ref):
        for h in range(heads):
            total = resp[h]
            for j in (0, 1):
                fwd.wait_recv(2 * h + j)
                total = total + jnp.where(
                    mask(h, 3 + j) > 0, in_rows[2 * h + j].astype(jnp.float32), 0.0
                )
            resp[h] = total
            kept = total * mask(h, 0)
            ref[2 * h : 2 * h + 1] = jnp.sum(kept, axis=0, keepdims=True)
            ref[2 * h + 1 : 2 * h + 2] = jnp.sum(kept * total, axis=0, keepdims=True)

    sums = plane_sum(line, stats, one)
    for c in fetched:
        c.wait()
    pixels = par_ref[2 * heads : 2 * heads + 1]
    inverses = []

    def grads(ref):
        for h in range(heads):
            mean = sums[2 * h : 2 * h + 1] / pixels
            var = sums[2 * h + 1 : 2 * h + 2] / pixels - mean * mean
            inverse = lax.rsqrt(var + norm_epsilon)
            inverses.append(inverse)
            scaled = (resp[h] - mean) * inverse
            normed = scaled * par_ref[2 * h : 2 * h + 1] + par_ref[2 * h + 1 : 2 * h + 2]
            s = jax.nn.sigmoid(normed)
            d = cot_ref[h].astype(jnp.float32) * (s * (1.0 + normed * (1.0 - s))) * mask(h, 0)
            resp[h] = scaled
            dn[h] = d
            ref[2 * h : 2 * h + 1] = jnp.sum(d, axis=0, keepdims=True)
            ref[2 * h + 1 : 2 * h + 2] = jnp.sum(d * scaled, axis=0, keepdims=True)

    back = plane_sum(line, grads, two)
    sums_ref[...] = back
    for h in range(heads):
        fwd.wait_send(2 * h)
        fwd.wait_send(2 * h + 1)
        e = (
            mask(h, 0)
            * (inverses[h] * par_ref[2 * h : 2 * h + 1])
            * (dn[h] - back[2 * h : 2 * h + 1] / pixels - resp[h] * (back[2 * h + 1 : 2 * h + 2] / pixels))
        )
        dn[h] = e
        out_rows[2 * h] = jnp.where(mask(h, 3) > 0, e, 0.0).astype(jnp.bfloat16)
        out_rows[2 * h + 1] = jnp.where(mask(h, 4) > 0, e, 0.0).astype(jnp.bfloat16)
        bwd.start(2 * h)
        bwd.start(2 * h + 1)

    def g_copy(t):
        return pltpu.make_async_copy(g_room, g_ref.at[t], g_sem)

    half = width // 2

    def lanes(owner):
        return pl.ds(pl.multiple_of(owner * half, half), half)

    def keep(slot, at):
        return pltpu.make_async_copy(
            dw_room.at[slot, :, lanes(core)], own_ref.at[at], dw_sem.at[slot]
        )

    def hand(slot, at):
        return pltpu.make_async_remote_copy(
            src_ref=dw_room.at[slot, :, lanes(1 - core)],
            dst_ref=got_ref.at[at],
            send_sem=hand_sem.at[slot],
            recv_sem=got_sem,
            device_id=(1 - core, place),
            device_id_type=MESH,
        )

    def put(slot, at):
        return pltpu.make_async_copy(
            dw_room.at[slot], late_ref.at[at - own_ref.shape[0]], dw_sem.at[slot]
        )

    def handed(t):
        return (t + 1) * 9 <= own_ref.shape[0]

    def dw_start(slot, t, k):
        at = t * 9 + k

        @pl.when(handed(t))
        def _():
            keep(slot, at).start()
            hand(slot, at).start()

        pl.when(jnp.logical_not(handed(t)))(lambda: put(slot, at).start())

    def dw_wait(slot, t):
        @pl.when(handed(t))
        def _():
            keep(slot, 0).wait()
            hand(slot, 0).wait_send()

        pl.when(jnp.logical_not(handed(t)))(lambda: put(slot, own_ref.shape[0]).wait())

    def weigh(t, k, number, before):
        slot = lax.rem(number, 2)
        pl.when(number >= 2)(lambda: dw_wait(slot, before))
        dw_room[slot] = jnp.dot(
            xt_ref[...],
            taps[:, pl.ds(pl.multiple_of(k * width, width), width)],
            preferred_element_type=jnp.float32,
        ).astype(jnp.bfloat16)
        dw_start(slot, t, k)

    def spread(t, j, arrived):
        rate = 12 * (t + 1)
        for c in range(3):
            if c == 0:
                tap = pltpu.roll(jnp.where(mask(t, 1) > 0, arrived, 0.0), px - rate, 0)
            elif c == 1:
                tap = jnp.where(mask(t, 0) > 0, arrived, 0.0)
            else:
                tap = pltpu.roll(jnp.where(mask(t, 2) > 0, arrived, 0.0), rate, 0)
            k = 3 * j + c
            taps[:, k * width : (k + 1) * width] = tap.astype(jnp.bfloat16)

    tiles = wv.shape[1] // width
    sq_ref[...] = jnp.zeros_like(sq_ref)

    def center(t):
        spread(t, 1, dn[t].astype(jnp.bfloat16).astype(jnp.float32))

    @pl.loop(0, heads)
    def _(t):
        center(t)
        pl.loop(0, 3)(lambda k: weigh(t, 3 + k, t * 3 + k, t - jnp.where(k < 2, 1, 0)))

    @pl.loop(0, heads)
    def _(t):
        center(t)
        for h in range(heads):
            @pl.when(t == h)
            def _():
                bwd.wait_recv(2 * h)
                bwd.wait_recv(2 * h + 1)

        spread(t, 0, jnp.where(mask(t, 5) > 0, in_rows[2 * t].astype(jnp.float32), 0.0))
        spread(t, 2, jnp.where(mask(t, 6) > 0, in_rows[2 * t + 1].astype(jnp.float32), 0.0))

        pl.loop(0, 6)(
            lambda k: weigh(
                t,
                k + jnp.where(k >= 3, 3, 0),
                3 * heads + t * 6 + k,
                jnp.where(k < 2, jnp.where(t > 0, t - 1, heads - 1), t),
            )
        )
        pl.when(t > 0)(lambda: g_copy(t - 1).wait())
        def tile(n, square):
            cut = pl.ds(pl.multiple_of(n * width, width), width)
            g = lax.dot_general(
                taps[...], wv[t, cut, :], (((1,), (1,)), ((), ())), preferred_element_type=jnp.float32
            )
            g_room[:, cut] = g
            return square + jnp.sum(g * g, axis=0, keepdims=True)

        square = lax.fori_loop(0, tiles, tile, jnp.zeros((1, width), jnp.float32))
        sq_ref[pl.ds(t, 1)] = square
        g_copy(t).start()

    g_copy(heads - 1).wait()
    dw_wait(0, heads - 1)
    dw_wait(1, heads - 1)
    pltpu.make_async_copy(got_ref, got_ref, got_sem).wait()

    for k in range(2 * heads):
        bwd.wait_send(k)


def heads_step(trunk_out, turned, early, late, cotangent, params, masks, rates, rows, cols, handed, number):
    px, channels = trunk_out.shape
    heads, width = len(rates), early.shape[-1]
    count = lax.axis_size("fsdp")
    line = count // 4
    bf, f32 = jnp.bfloat16, jnp.float32
    dma = pltpu.SemaphoreType.DMA
    vmem = pl.BlockSpec(memory_space=pltpu.VMEM)
    hbm = pl.BlockSpec(memory_space=pl.ANY)
    return pl.pallas_call(
        functools.partial(heads_kernel, rates, rows, cols, count),
        out_shape=(
            jax.ShapeDtypeStruct((heads, px, channels), f32),
            jax.ShapeDtypeStruct((9 * handed, channels, width // 2), bf),
            jax.ShapeDtypeStruct((9 * handed, channels, width // 2), bf),
            jax.ShapeDtypeStruct((9 * (heads - handed), channels, width), bf),
            jax.ShapeDtypeStruct((2 * heads, width), f32),
            jax.ShapeDtypeStruct((8, width), f32),
        ),
        in_specs=[vmem, hbm, hbm, hbm, hbm, vmem, vmem],
        out_specs=(hbm, hbm, hbm, hbm, vmem, vmem),
        scratch_shapes=[
            pltpu.VMEM((heads, channels, 9 * width), bf),
            pltpu.VMEM((2 * heads, px, width), bf),
            pltpu.VMEM((2 * heads, px, width), bf),
            pltpu.VMEM((heads, px, width), f32),
            pltpu.VMEM((heads, px, width), f32),
            pltpu.VMEM((px, 9 * width), bf),
            pltpu.VMEM((px, channels), f32),
            pltpu.VMEM((2, channels, width), bf),
            pltpu.VMEM((channels, px), bf),
            pltpu.VMEM((heads, px, width), bf),
            dma((2,)),
            dma((9 * heads,)),
            dma((2 * heads, 2)),
            dma((2 * heads, 2)),
            dma((2 * heads, 2)),
            dma((2 * heads, 2)),
            dma,
            dma((2,)),
            dma((2,)),
            dma,
        ]
        + plane_scratch(line, (2 * heads, width))
        + plane_scratch(line, (2 * heads, width)),
        compiler_params=pltpu.CompilerParams(
            collective_id=number, has_side_effects=True, vmem_limit_bytes=62 * 2**20
        ),
    )(trunk_out, turned, early, late, cotangent, params, masks)


class Fan:
    def __init__(self, t, arrays, sends, arrives, shares, own_sem):
        self.t, self.arrays = t, arrays
        self.sends, self.arrives, self.shares, self.own_sem = sends, arrives, shares, own_sem

    def copy(self, k, kind, block, peer, own=False):
        src, place = self.arrays[k]
        dst = place(block, self.t.core)
        return pltpu.make_async_remote_copy(
            src_ref=src if own else dst,
            dst_ref=dst,
            send_sem=self.sends.at[k, kind, block],
            recv_sem=(self.shares if kind == 4 else self.arrives).at[k, block],
            device_id=peer,
            device_id_type=MESH,
        )

    def fan(self, k, block, own, down, up, a, b, finish):
        t = self.t

        def act(kind, peer):
            c = self.copy(k, kind, block, peer, own)
            c.wait_send() if finish else c.start()

        if down:
            pl.when(t.z > 0)(lambda: act(0, t.down))
        if up:
            pl.when(t.z < t.line - 1)(lambda: act(1, t.up))
        if a:
            act(2, t.a)
        if b:
            act(3, t.b)
        act(4, t.partner)

    def stay(self, k):
        src, place = self.arrays[k]
        return pltpu.make_async_copy(src, place(self.t.place, self.t.core), self.own_sem.at[k])

    def own(self, ks, finish=False):
        for k in ks:
            if not finish:
                self.stay(k).start()
            self.fan(k, self.t.place, True, True, True, True, True, finish)

    def step(self, ks, s, move, down, up, a, b, finish):
        t = self.t
        for k in ks:
            def one(block, down, up):
                if not finish:
                    self.copy(k, 0, block, t.partner).wait_recv()
                self.fan(k, block, False, down, up, a, b, finish)

            pl.when(t.z - s >= 0)(lambda: one(t.place - 4 * s + move, down, False))
            if s:
                pl.when(t.z + s < t.line)(lambda: one(t.place + 4 * s + move, False, up))

    def steps(self, ks, finish=False):
        t = self.t
        result = []
        for s in range(1, t.line):
            result.append(lambda s=s: self.along(ks, s, finish))
            result.append(lambda s=s: self.step(ks, s - 1, t.move_a, False, False, False, True, finish))
        result.append(lambda: self.step(ks, t.line - 1, t.move_a, False, False, False, True, finish))
        tail = []
        for s in range(t.line):
            tail.append(lambda s=s: self.step(ks, s, t.move_b, False, False, False, False, finish))
            tail.append(
                lambda s=s: self.step(ks, s, t.move_a + t.move_b, False, False, False, False, finish)
            )
        return result, tail

    def along(self, ks, s, finish):
        t = self.t
        for k in ks:
            def one(block, down, up):
                if not finish:
                    self.copy(k, 0, block, t.partner).wait_recv()
                self.fan(k, block, False, down, up, True, True, finish)

            pl.when(t.z - s >= 0)(lambda: one(t.place - 4 * s, False, True))
            pl.when(t.z + s < t.line)(lambda: one(t.place + 4 * s, True, False))

    def wait_shares(self, ks):
        t = self.t
        for k in ks:
            self.stay(k).wait()

        @pl.loop(0, t.count)
        def _(block):
            for k in ks:
                other = self.arrays[k][1](block, 1 - t.core)
                pltpu.make_async_remote_copy(
                    src_ref=other,
                    dst_ref=other,
                    send_sem=self.sends.at[k, 4, block],
                    recv_sem=self.shares.at[k, block],
                    device_id=t.partner,
                    device_id_type=MESH,
                ).wait_recv()

    def finish(self, ks):
        self.own(ks, True)
        first, tail = self.steps(ks, True)
        for f in first + tail:
            f()


def silu(v):
    return v * jax.nn.sigmoid(v)


def scale_rows(sums, pixels):
    mean = sums[0:1] / pixels
    var = sums[1:2] / pixels - mean * mean
    return mean, lax.rsqrt(var + norm_epsilon)


def read_params(norm_ref, crop_ref, par_ref, par3_ref, heads_ref):
    middle, width = par_ref.shape[1], heads_ref.shape[1]
    total = jnp.int32(0)
    for g in range(crop_ref.shape[0]):
        for c in range(crop_ref.shape[1]):
            total = total + crop_ref[g, c] * crop_ref[g, c]
    total = total.astype(jnp.float32)
    for k in range(2):
        for row in range(2):
            par_ref[2 * k + row : 2 * k + row + 1] = norm_ref[row : row + 1, k * middle : (k + 1) * middle]
    par_ref[4:] = jnp.full((par_ref.shape[0] - 4, middle), total)
    parts = par3_ref.shape[0] // 2
    for k in range(parts):
        at = (2 + k) * middle
        for row in range(2):
            par3_ref[2 * k + row : 2 * k + row + 1] = norm_ref[row : row + 1, at : at + middle]
    heads = heads_ref.shape[0] // 2 - 1
    for k in range(heads):
        at = (2 + parts) * middle + k * width
        for row in range(2):
            heads_ref[2 * k + row : 2 * k + row + 1] = norm_ref[row : row + 1, at : at + width]
    heads_ref[2 * heads :] = jnp.full((2, width), total)


def read_layout(crop_ref, group, row_start, total_rows, cols, rates, masks_ref, at):
    shape = masks_ref.shape[1:]
    pixel = lax.broadcasted_iota(jnp.int32, shape, 0)
    lane = lax.broadcasted_iota(jnp.int32, shape, 1)
    row = row_start + lax.div(pixel, jnp.full(shape, cols, jnp.int32))
    col = lax.rem(pixel, jnp.full(shape, cols, jnp.int32))
    top = bottom = side = jnp.zeros(shape, jnp.int32)
    start = jnp.int32(0)
    for c in range(crop_ref.shape[1]):
        height = crop_ref[group, c]
        member = jnp.logical_and(row >= start, row < start + height)
        top = jnp.where(member, start, top)
        bottom = jnp.where(member, start + height, bottom)
        side = jnp.where(member, height, side)
        start = start + height
    for k, rate in enumerate(rates):
        flags = (
            col < side,
            jnp.logical_and(col >= rate, col - rate < side),
            col + rate < side,
            jnp.logical_and(row - rate >= top, row - rate < bottom),
            jnp.logical_and(row + rate >= top, row + rate < bottom),
            row + rate < total_rows,
            row >= rate,
        )
        value = jnp.zeros(shape, jnp.float32)
        for n, flag in enumerate(flags):
            value = jnp.where(jnp.logical_and(lane == n, flag), 1.0, value)
        masks_ref[at + k] = value


def trunk_kernel(
    rates, rows, cols, count,
    x_ref, wr_s, wd_s, we_s, wh_s, norm_ref, crop_ref,
    wr_o, wd_o, we_o, wh_o, out_o, sc1_o, sc2_o, sc3_o, masks_o, turned_o, s1_ref, s2_ref, s3_ref,
    par_ref, par3_ref, heads_ref,
    wr_v, wd_v, we_v, ext, taps, out_ref, sc1_ref, sc2_ref, sc3_ref, masks_ref, turned_ref,
    sends, arrives, shares, own_sem, save_sem, h_send, h_recv, *rooms,
):
    rate = rates[-1]
    px = rows * cols
    line = count // 4
    middle = par_ref.shape[1]
    channels = out_ref.shape[1]
    t = Tree()
    one, two, three = rooms[:7], rooms[7:14], rooms[14:]
    halo = rate * cols

    def cut(start, size, step=8):
        return pl.ds(pl.multiple_of(start, step), size)

    def rows_array(shard, full):
        size = shard.shape[0]
        return (
            shard.at[cut(t.core * (size // 2), size // 2, 16)],
            lambda block, core: full.at[cut(block * size + core * (size // 2), size // 2, 16)],
        )

    half_e = we_s.shape[0] // 2
    half_h = wh_s.shape[1] // 2
    fan = Fan(
        t,
        [
            rows_array(wr_s, wr_v),
            rows_array(wd_s, wd_v),
            (
                we_s.at[cut(t.core * half_e, half_e, 16)],
                lambda block, core: we_v.at[
                    cut(core * half_e, half_e, 16), cut(block * we_s.shape[1], we_s.shape[1], 128)
                ],
            ),
            (
                wh_s.at[:, cut(t.core * half_h, half_h, 16)],
                lambda block, core: wh_o.at[:, block, cut(core * half_h, half_h, 16)],
            ),
        ],
        sends, arrives, shares, own_sem,
    )
    plane_signal(line, t.core, t.z, t.low)
    met = greet_rows((-1, 1), count)
    read_params(norm_ref, crop_ref, par_ref, par3_ref, heads_ref)
    mask_ref = masks_ref.at[len(rates) - 1]
    read_layout(crop_ref, t.core, t.place * rows, rows * count, cols, rates[-1:], masks_ref, len(rates) - 1)
    pl.semaphore_wait(pltpu.get_barrier_semaphore(), 7 + line - 1 + met)
    small, heads = (0, 1, 2), (3,)
    fan.own(small)
    first_steps, first_tail = fan.steps(small)
    for f in first_steps:
        f()
    fan.own(heads)
    read_layout(crop_ref, t.core, t.place * rows, rows * count, cols, rates[:-1], masks_ref, 0)
    for f in first_tail:
        f()
    head_steps, head_tail = fan.steps(heads)
    queue = head_steps + head_tail

    def forward(number):
        for _ in range(number):
            if queue:
                queue.pop(0)()

    pixels = par_ref[4:5]

    def mask(k):
        return mask_ref[:, k : k + 1]

    def moments_of(v, ref, at):
        kept = v * mask(0)
        ref[at : at + 1] = jnp.sum(kept, axis=0, keepdims=True)
        ref[at + 1 : at + 2] = jnp.sum(kept * v, axis=0, keepdims=True)

    fan.wait_shares((0,))
    sc1_ref[...] = jnp.dot(x_ref[...], wr_v[...], preferred_element_type=jnp.float32)
    forward(1)
    s1_ref[...] = plane_sum(line, lambda ref: moments_of(sc1_ref[...], ref, 0), one)
    mean, inverse = scale_rows(s1_ref, pixels)
    scaled = (sc1_ref[...] - mean) * inverse
    sc1_ref[...] = scaled
    ext[halo : halo + px] = silu(scaled * par_ref[0:1] + par_ref[1:2]).astype(jnp.bfloat16)

    def edge(up):
        src = ext.at[pl.ds(halo if not up else halo + px - halo, halo)]
        dst = ext.at[pl.ds(halo + px if not up else 0, halo)]
        return pltpu.make_async_remote_copy(
            src_ref=src,
            dst_ref=dst,
            send_sem=h_send.at[int(up)],
            recv_sem=h_recv.at[int(up)],
            device_id=t.at(t.place + (1 if up else -1)),
            device_id_type=MESH,
        )

    has_next, has_last = t.place < count - 1, t.place > 0
    pl.when(has_last)(lambda: edge(False).start())
    pl.when(has_next)(lambda: edge(True).start())
    fan.wait_shares((1, 2))
    forward(2)
    saves = [
        pltpu.make_async_copy(wr_v, wr_o, save_sem.at[0]),
        pltpu.make_async_copy(wd_v, wd_o, save_sem.at[1]),
        pltpu.make_async_copy(we_v, we_o, save_sem.at[2]),
    ]
    for save in saves:
        save.start()
    pl.when(has_next)(lambda: edge(False).wait_recv())
    pl.when(has_last)(lambda: edge(True).wait_recv())
    for j in range(3):
        v = ext[j * halo : j * halo + px].astype(jnp.float32)
        kept_row = 1.0 if j == 1 else mask(3 + j // 2)
        for c in range(3):
            moved = v if c == 1 else pltpu.roll(v, rate if c == 0 else px - rate, 0)
            kept = mask((1, 0, 2)[c]) * kept_row
            k = 3 * j + c
            taps[:, k * middle : (k + 1) * middle] = jnp.where(kept > 0, moved, 0.0).astype(jnp.bfloat16)
    sc2_ref[...] = jnp.dot(taps[...], wd_v[...], preferred_element_type=jnp.float32)
    forward(2)
    s2_ref[...] = plane_sum(line, lambda ref: moments_of(sc2_ref[...], ref, 0), two)
    mean, inverse = scale_rows(s2_ref, pixels)
    scaled = (sc2_ref[...] - mean) * inverse
    sc2_ref[...] = scaled
    hidden = silu(scaled * par_ref[2:3] + par_ref[3:4]).astype(jnp.bfloat16)
    forward(2)
    parts = channels // middle

    def wide(ref):
        for q in range(parts):
            third = jnp.dot(
                hidden, we_v[:, q * middle : (q + 1) * middle], preferred_element_type=jnp.float32
            )
            sc3_ref[:, q * middle : (q + 1) * middle] = third
            moments_of(third, ref, 2 * q)

    s3_ref[...] = plane_sum(line, wide, three)
    forward(1)
    for q in range(parts):
        at = slice(q * middle, (q + 1) * middle)
        mean, inverse = scale_rows(s3_ref[2 * q : 2 * q + 2], pixels)
        scaled = (sc3_ref[:, at] - mean) * inverse
        sc3_ref[:, at] = scaled
        pre = x_ref[:, at].astype(jnp.float32) + (
            scaled * par3_ref[2 * q : 2 * q + 1] + par3_ref[2 * q + 1 : 2 * q + 2]
        )
        active = silu(pre)
        out_ref[:, at] = active.astype(jnp.bfloat16)
        turned_ref[at] = active.T.astype(jnp.bfloat16)
    for k, (here, there) in enumerate(
        (
            (out_ref, out_o),
            (sc1_ref, sc1_o),
            (sc2_ref, sc2_o),
            (sc3_ref, sc3_o),
            (masks_ref, masks_o),
            (turned_ref, turned_o),
        )
    ):
        saves.append(pltpu.make_async_copy(here, there, save_sem.at[3 + k]))
        saves[-1].start()
    forward(len(queue))
    fan.wait_shares(heads)
    for save in saves:
        save.wait()
    pl.when(has_last)(lambda: edge(False).wait_send())
    pl.when(has_next)(lambda: edge(True).wait_send())
    fan.finish(small + heads)


def trunk_step(x, shards, norm_params, crop_heights, rates, rows, cols, middle, number):
    px, channels = x.shape
    count = lax.axis_size("fsdp")
    line = count // 4
    rate = rates[-1]
    bf, f32 = jnp.bfloat16, jnp.float32
    dma = pltpu.SemaphoreType.DMA
    vmem = pl.BlockSpec(memory_space=pltpu.VMEM)
    hbm = pl.BlockSpec(memory_space=pl.ANY)
    parts = channels // middle
    heads, head_rows, width = shards[3].shape
    S = jax.ShapeDtypeStruct
    return pl.pallas_call(
        functools.partial(trunk_kernel, rates, rows, cols, count),
        out_shape=(
            S((channels, middle), bf),
            S((9 * middle, middle), bf),
            S((middle, channels), bf),
            S((heads, count, head_rows, width), bf),
            S((px, channels), bf),
            S((px, middle), f32),
            S((px, middle), f32),
            S((px, channels), f32),
            S((len(rates), px, 128), f32),
            S((channels, px), bf),
            S((2, middle), f32),
            S((2, middle), f32),
            S((2 * parts, middle), f32),
            S((8, middle), f32),
            S((2 * parts, middle), f32),
            S((2 * len(rates), width), f32),
        ),
        in_specs=[vmem] + [hbm] * 4 + [vmem, pl.BlockSpec(memory_space=pltpu.SMEM)],
        out_specs=(hbm,) * 10 + (vmem,) * 6,
        scratch_shapes=[
            pltpu.VMEM((channels, middle), bf),
            pltpu.VMEM((9 * middle, middle), bf),
            pltpu.VMEM((middle, channels), bf),
            pltpu.VMEM((px + 2 * rate * cols, middle), bf),
            pltpu.VMEM((px, 9 * middle), bf),
            pltpu.VMEM((px, channels), bf),
            pltpu.VMEM((px, middle), f32),
            pltpu.VMEM((px, middle), f32),
            pltpu.VMEM((px, channels), f32),
            pltpu.VMEM((len(rates), px, 128), f32),
            pltpu.VMEM((channels, px), bf),
            dma((4, 5, count)),
            dma((4, count)),
            dma((4, count)),
            dma((4,)),
            dma((9,)),
            dma((2,)),
            dma((2,)),
        ]
        + plane_scratch(line, (2, middle))
        + plane_scratch(line, (2, middle))
        + plane_scratch(line, (2 * parts, middle)),
        compiler_params=pltpu.CompilerParams(
            collective_id=number, has_side_effects=True, vmem_limit_bytes=56 * 2**20
        ),
    )(x, *shards, norm_params, crop_heights)


FEED = {"join": 1, "pass": 1, "keep": 1, "third": 1, "d2": 1, "ge": 1, "edge": 2, "d1": 1, "gd": 1, "later3": 4, "later2": 4, "later1": 4}


def nt(a, b):
    return lax.dot_general(a, b, (((1,), (1,)), ((), ())), preferred_element_type=jnp.float32)


def tn(a, b):
    return lax.dot_general(a, b, (((0,), (0,)), ((), ())), preferred_element_type=jnp.float32)


def slope(v):
    s = jax.nn.sigmoid(v)
    return s * (1.0 + v * (1.0 - s))


def back_kernel(
    rate, rows, cols, count, heads,
    x_ref, scale_ref, sq_ref, sc1_ref, sc2_ref, par_ref, par3_ref, s1_ref, s2_ref, s3_ref, mask_ref,
    g_ref, sc3_ref, wr_ref, wd_ref, we_ref, own_ref, got_ref,
    tw_ref, bs1_ref, bs2_ref, bs3_ref, fg_ref, gr_ref, gd_ref, ge_ref, sum_ref,
    b_send, acc, b_room, extra, g_room, s_room, dpre, dthird, wr_v, wd_v, we_v, ext, taps, out_room, grad_room,
    load_sem, extra_sem, bs_sem, br_sem, g_sem, s_sem, w_sem, h_send, h_recv, out_sem, grad_sem, sum_sem, *rooms,
):
    px = rows * cols
    line = count // 4
    middle = par_ref.shape[1]
    channels = x_ref.shape[1]
    parts = channels // middle
    wide = g_room.shape[-1]
    chunks = channels // wide
    halo = rate * cols
    t = Tree()
    one, two, three, four = rooms[:7], rooms[7:14], rooms[14:21], rooms[21:]
    bf, f32 = jnp.bfloat16, jnp.float32

    weights = [
        pltpu.make_async_copy(we_ref, we_v, w_sem.at[0]),
        pltpu.make_async_copy(wd_ref, wd_v, w_sem.at[1]),
        pltpu.make_async_copy(wr_ref, wr_v, w_sem.at[2]),
    ]

    def lanes(c):
        return pl.ds(c * wide, wide)

    def g_load(c):
        return pltpu.make_async_copy(g_ref.at[:, :, lanes(c)], g_room.at[c % 2], g_sem.at[c % 2])

    def s_load(c):
        return pltpu.make_async_copy(sc3_ref.at[:, lanes(c)], s_room.at[c % 2], s_sem.at[c % 2])

    moves = (t.move_b, t.move_a + t.move_b, 0, t.move_a)

    def pair(n, w):
        block = n * 4 + t.low + moves[w]
        room = (b_send if w < 2 else acc).at[n * 2 + w % 2]
        slot = w % 2
        return (
            pltpu.make_async_copy(own_ref.at[:, block], room, load_sem.at[slot]),
            pltpu.make_async_copy(got_ref.at[:, block], extra.at[slot], extra_sem.at[slot]),
        )

    def join(n, w):
        for c in pair(n, w):
            c.wait()
        room = b_send if w < 2 else acc
        at = n * 2 + w % 2

        @pl.loop(0, heads)
        def _(h):
            room[at, h] = room[at, h] + extra[w % 2, h]

    def to_b(n, w, piece=None):
        at = (n * 2 + w,)
        if piece is not None:
            at = at + (piece[0], pl.ds(piece[1], piece[2]))
        return pltpu.make_async_remote_copy(
            src_ref=b_send.at[at],
            dst_ref=b_room.at[at],
            send_sem=bs_sem.at[n * 2 + w],
            recv_sem=br_sem.at[n * 2 + w],
            device_id=t.b,
            device_id_type=MESH,
        )

    head_rows = b_send.shape[2]
    size = head_rows // 4
    pieces = [
        to_b(n, w, (h, r, size))
        for n in range(line)
        for w in (1, 0)
        for h in range(heads)
        for r in range(0, head_rows, size)
    ]

    def feed(number):
        for _ in range(min(number, len(pieces))):
            pieces.pop(0).start()

    plane_signal(line, t.core, t.z, t.low)
    met = greet_rows((-1, 1), count)
    for w in (1, 0):
        for c in pair(0, w):
            c.start()
    for c in weights:
        c.start()
    for c in (0, 1):
        g_load(c).start()
        s_load(c).start()
    pl.semaphore_wait(pltpu.get_barrier_semaphore(), 7 + line - 1 + met)

    def squares(ref):
        ref[...] = sq_ref[...]

    def send_side():
        for n in range(line):
            for w in (1, 0):
                join(n, w)
                feed(FEED["join"])
                if n < line - 1:
                    for c in pair(n + 1, w):
                        c.start()

    square_sums = jnp.sum(plane_sum(line, squares, four, send_side), axis=1, keepdims=True)
    tw_ref[...] = scale_ref[...] / jnp.sqrt(
        square_sums / (par_ref[4:5, 0:1] * channels) + task_epsilon
    )

    for w in (3, 2):
        for c in pair(0, w):
            c.start()

    def mask(k):
        return mask_ref[mask_ref.shape[0] - 1, :, k : k + 1]

    pixels = par_ref[4:5]
    pixels_wide = pixels[:, :wide]

    def third_params(c):
        q, at = (c * wide) // middle, (c * wide) % middle
        at = slice(at, at + wide)
        return 2 * q, at

    def moved_sums(ref, row, at, d, scaled):
        ref[row : row + 1, at] = jnp.sum(d, axis=0, keepdims=True)
        ref[row + 1 : row + 2, at] = jnp.sum(d * scaled, axis=0, keepdims=True)

    def first_pass(ref):
        for c in range(chunks):
            g_load(c).wait()
            s_load(c).wait()
            row, at = third_params(c)
            total = tw_ref[0:1, 0:1] * g_room[c % 2, 0]
            for h in range(1, g_ref.shape[0]):
                total = total + tw_ref[h : h + 1, 0:1] * g_room[c % 2, h]
            scaled = s_room[c % 2]
            here = slice(c * wide, (c + 1) * wide)
            pre = x_ref[:, here].astype(f32) + (
                scaled * par3_ref[row : row + 1, at] + par3_ref[row + 1 : row + 2, at]
            )
            d = total * slope(pre)
            dpre[:, here] = d
            d = d * mask(0)
            moved_sums(ref, row, at, d, scaled)
            feed(FEED["pass"])
            if c + 2 < chunks:
                g_load(c + 2).start()
                s_load(c + 2).start()
        for c in (0, 1):
            s_load(c).start()

    def keep_rest():
        for n in range(line):
            for w in (3, 2):
                feed(FEED["keep"])
                join(n, w)
                if n < line - 1:
                    for c in pair(n + 1, w):
                        c.start()

    back3 = plane_sum(line, first_pass, three, keep_rest, lambda: feed(FEED["later3"]))
    bs3_ref[...] = back3
    for c in range(chunks):
        s_load(c).wait()
        row, at = third_params(c)
        mean = s3_ref[row : row + 1, at] / pixels_wide
        var = s3_ref[row + 1 : row + 2, at] / pixels_wide - mean * mean
        inverse = lax.rsqrt(var + norm_epsilon)
        here = slice(c * wide, (c + 1) * wide)
        v = (
            mask(0)
            * (inverse * par3_ref[row : row + 1, at])
            * (
                dpre[:, here] * mask(0)
                - back3[row : row + 1, at] / pixels_wide
                - s_room[c % 2] * (back3[row + 1 : row + 2, at] / pixels_wide)
            )
        )
        dthird[:, here] = v.astype(bf)
        feed(FEED["third"])
        if c + 2 < chunks:
            s_load(c + 2).start()
    weights[0].wait()
    scaled2 = sc2_ref[...]
    normed2 = scaled2 * par_ref[2:3] + par_ref[3:4]
    feed(FEED["d2"])
    d2 = nt(dthird[...], we_v[...]) * slope(normed2) * mask(0)

    state = []

    def put(value, *targets):
        n = len(state)
        if n >= 2:
            for c in state[n - 2]:
                c.wait()
        grad_room[n % 2] = value.astype(bf)
        cols = middle // len(targets)
        state.append(
            [
                pltpu.make_async_copy(
                    grad_room.at[n % 2, :, pl.ds(i * cols, cols)], ref, grad_sem.at[n % 2, i]
                )
                for i, ref in enumerate(targets)
            ]
        )
        for c in state[n]:
            c.start()

    hidden2 = silu(normed2).astype(bf)

    def expand_grads():
        for q in range(parts):
            feed(FEED["ge"])
            per = count // parts
            put(
                tn(hidden2, dthird[:, q * middle : (q + 1) * middle]),
                *(ge_ref.at[q * per + i] for i in range(per)),
            )

    back2 = plane_sum(
        line, lambda ref: moved_sums(ref, 0, slice(None), d2, scaled2), two, expand_grads,
        lambda: feed(FEED["later2"]),
    )
    bs2_ref[...] = back2

    def through(d, scaled, sums, back, gain):
        _, inverse = scale_rows(sums, pixels)
        return mask(0) * (inverse * gain) * (d - back[0:1] / pixels - scaled * (back[1:2] / pixels))

    ext[halo : halo + px] = through(d2, scaled2, s2_ref, back2, par_ref[2:3]).astype(bf)

    def edge(up):
        src = ext.at[pl.ds(px if up else halo, halo)]
        dst = ext.at[pl.ds(0 if up else halo + px, halo)]
        return pltpu.make_async_remote_copy(
            src_ref=src,
            dst_ref=dst,
            send_sem=h_send.at[int(up)],
            recv_sem=h_recv.at[int(up)],
            device_id=t.at(t.place + (1 if up else -1)),
            device_id_type=MESH,
        )

    has_next, has_last = t.place < count - 1, t.place > 0
    pl.when(has_last)(lambda: edge(False).start())
    pl.when(has_next)(lambda: edge(True).start())
    weights[1].wait()
    scaled1 = sc1_ref[...]
    normed1 = scaled1 * par_ref[0:1] + par_ref[1:2]
    hidden1 = silu(normed1).astype(bf)

    def spread(j):
        v = ext[(2 - j) * halo : (2 - j) * halo + px].astype(f32)
        kept_row = 1.0 if j == 1 else mask(4 if j == 0 else 3)
        for c in range(3):
            if c == 0:
                moved, kept = pltpu.roll(v, px - rate, 0), mask(2)
            elif c == 1:
                moved, kept = v, mask(0)
            else:
                moved, kept = pltpu.roll(v, rate, 0), mask(1) * mask(0)
            k = 3 * j + c
            taps[:, k * middle : (k + 1) * middle] = jnp.where(kept * kept_row > 0, moved, 0.0).astype(bf)

    def tap(k):
        return taps[:, k * middle : (k + 1) * middle]

    feed(FEED["edge"])
    spread(1)
    d1 = None
    for j in (1, 0, 2):
        if j == 0:
            pl.when(has_next)(lambda: edge(False).wait_recv())
            pl.when(has_last)(lambda: edge(True).wait_recv())
            spread(0)
            spread(2)
        for c in range(3):
            k = 3 * j + c
            feed(FEED["d1"])
            part = nt(tap(k), wd_v[k * middle : (k + 1) * middle])
            d1 = part if d1 is None else d1 + part
    d1 = d1 * slope(normed1) * mask(0)

    def dilated_grads():
        for k in range(9):
            feed(FEED["gd"])
            put(tn(hidden1, tap(k)), gd_ref.at[k])

    back1 = plane_sum(
        line, lambda ref: moved_sums(ref, 0, slice(None), d1, scaled1), one, dilated_grads,
        lambda: feed(FEED["later1"]),
    )
    bs1_ref[...] = back1
    dfirst = through(d1, scaled1, s1_ref, back1, par_ref[0:1]).astype(bf)
    feed(len(pieces))
    weights[2].wait()
    outs = []
    for q in range(parts):
        here = slice(q * middle, (q + 1) * middle)
        if q >= 2:
            outs[q - 2].wait()
        out_room[q % 2] = nt(dfirst, wr_v[here]) + dpre[:, here]
        outs.append(
            pltpu.make_async_copy(
                out_room.at[q % 2], fg_ref.at[:, pl.ds(q * middle, middle)], out_sem.at[q % 2]
            )
        )
        outs[q].start()
    for q in range(parts):
        here = slice(q * middle, (q + 1) * middle)
        put(tn(x_ref[:, here], dfirst), gr_ref.at[pl.ds(q * middle, middle)])

    def stays(n):
        return pltpu.make_async_copy(acc.at[n], sum_ref.at[n], sum_sem.at[n])

    @pl.loop(0, line)
    def _(n):
        for w in (1, 0):
            to_b(n, w).wait_recv()
            at = n * 2 + w

            @pl.loop(0, heads)
            def _(h):
                acc[at, h] = acc[at, h] + b_room[at, h]

            stays(at).start()

    for c in state[-2] + state[-1] + outs[-2:]:
        c.wait()

    @pl.loop(0, line)
    def _(n):
        for w in (1, 0):
            to_b(n, w).wait_send()
            stays(n * 2 + w).wait()

    pl.when(has_last)(lambda: edge(False).wait_send())
    pl.when(has_next)(lambda: edge(True).wait_send())


def back_step(x, task_scale, squares, scaled1, scaled2, scaled3, params, params3, sums1, sums2, sums3, masks, grads,
              wr, wd, we, own, got, rate, rows, cols, number):
    px, channels = x.shape
    count = lax.axis_size("fsdp")
    line = count // 4
    middle = params.shape[1]
    parts = channels // middle
    wide = middle // 2
    heads, _, head_rows, half = own.shape
    bf, f32 = jnp.bfloat16, jnp.float32
    dma = pltpu.SemaphoreType.DMA
    vmem = pl.BlockSpec(memory_space=pltpu.VMEM)
    hbm = pl.BlockSpec(memory_space=pl.ANY)
    S = jax.ShapeDtypeStruct
    V = pltpu.VMEM
    return pl.pallas_call(
        functools.partial(back_kernel, rate, rows, cols, count, heads),
        out_shape=(
            S(task_scale.shape, f32),
            S((2, middle), f32),
            S((2, middle), f32),
            S((2 * parts, middle), f32),
            S((px, channels), f32),
            S((channels, middle), bf),
            S((9, middle, middle), bf),
            S((count, middle, channels // count), bf),
            S((2 * line, heads, head_rows, half), bf),
        ),
        in_specs=[vmem] * 11 + [hbm] * 7,
        out_specs=(vmem,) * 4 + (hbm,) * 5,
        scratch_shapes=[
            V((2 * line, heads, head_rows, half), bf),
            V((2 * line, heads, head_rows, half), bf),
            V((2 * line, heads, head_rows, half), bf),
            V((2, heads, head_rows, half), bf),
            V((2, grads.shape[0], px, wide), f32),
            V((2, px, wide), f32),
            V((px, channels), f32),
            V((px, channels), bf),
            V((channels, middle), bf),
            V((9 * middle, middle), bf),
            V((middle, channels), bf),
            V((px + 2 * rate * cols, middle), bf),
            V((px, 9 * middle), bf),
            V((2, px, middle), f32),
            V((2, middle, middle), bf),
            dma((2,)),
            dma((2,)),
            dma((2 * line,)),
            dma((2 * line,)),
            dma((2,)),
            dma((2,)),
            dma((3,)),
            dma((2,)),
            dma((2,)),
            dma((2,)),
            dma((2, count // parts)),
            dma((2 * line,)),
        ]
        + plane_scratch(line, (2, middle))
        + plane_scratch(line, (2, middle))
        + plane_scratch(line, (2 * parts, middle))
        + plane_scratch(line, squares.shape),
        compiler_params=pltpu.CompilerParams(
            collective_id=number, has_side_effects=True, vmem_limit_bytes=63 * 2**20
        ),
    )(x, task_scale, squares, scaled1, scaled2, params, params3, sums1, sums2, sums3, masks,
      grads, scaled3, wr, wd, we, own, got)


def silu_slope(values):
    sigmoid_value = jax.nn.sigmoid(values)
    return sigmoid_value * (1.0 + values * (1.0 - sigmoid_value))


def shift_along(values, offset, axis_number):
    if offset == 0:
        return values
    length = values.shape[axis_number]
    pad_shape = list(values.shape)
    pad_shape[axis_number] = abs(offset)
    zero_block = jnp.zeros(pad_shape, values.dtype)
    if offset > 0:
        return jnp.concatenate(
            [lax.slice_in_dim(values, offset, length, axis=axis_number), zero_block], axis_number
        )
    return jnp.concatenate(
        [zero_block, lax.slice_in_dim(values, 0, length + offset, axis=axis_number)], axis_number
    )


def inside_rows(layout, offset):
    row_ids, row_top, row_bottom, row_side = layout
    return (row_ids + offset >= row_top) & (row_ids + offset < row_bottom)


def inside_cols(layout, offset, col_count):
    row_ids, row_top, row_bottom, row_side = layout
    columns = jnp.arange(col_count, dtype=jnp.int32)
    return (columns[None, :] + offset >= 0) & (columns[None, :] + offset < row_side[:, None])


def column_sums(inputs, weight, rate, layout):
    col_count = inputs.shape[1]
    products = jnp.einsum("rwc,kco->krwo", inputs, weight, preferred_element_type=jnp.float32)
    sums = []
    for row_step in range(3):
        summed = 0.0
        for col_step in range(3):
            across = (col_step - 1) * rate
            summed = summed + jnp.where(
                inside_cols(layout, across, col_count)[:, :, None],
                shift_along(products[3 * row_step + col_step], across, 1),
                0.0,
            )
        sums.append(summed)
    return sums


def dilated_forward(inputs, weights, rates, layout, number):
    outer, centers = [], []
    for weight, rate in zip(weights, rates):
        low, center, high = column_sums(inputs, weight, rate, layout)
        outer += [low.astype(jnp.bfloat16), high.astype(jnp.bfloat16)]
        centers.append(center)
    offsets = tuple(o for rate in rates for o in (-rate, rate))
    pulled = exchange(jnp.stack(outer), offsets, number)
    results = []
    for k, (center, rate) in enumerate(zip(centers, rates)):
        for j, down in ((2 * k, -rate), (2 * k + 1, rate)):
            center = center + jnp.where(
                inside_rows(layout, down)[:, None, None], pulled[j].astype(jnp.float32), 0.0
            )
        results.append(center)
    return results


def spread_taps(grads, rates, layout, number):
    row_ids = layout[0]
    row_count, col_count = grads[0].shape[:2]
    total_rows = row_count * lax.axis_size("fsdp")
    outer = []
    for grad, rate in zip(grads, rates):
        for down in (-rate, rate):
            outer.append(
                jnp.where(inside_rows(layout, down)[:, None, None], grad, jnp.bfloat16(0.0))
            )
    offsets = tuple(o for rate in rates for o in (rate, -rate))
    pulled = exchange(jnp.stack(outer), offsets, number)
    results = []
    for k, (grad, rate) in enumerate(zip(grads, rates)):
        taps = []
        for row_step in range(3):
            down = (row_step - 1) * rate
            if row_step == 1:
                arrived = grad
            else:
                there = (row_ids - down >= 0) & (row_ids - down < total_rows)
                arrived = jnp.where(
                    there[:, None, None], pulled[2 * k + row_step // 2], jnp.bfloat16(0.0)
                )
            for col_step in range(3):
                across = (col_step - 1) * rate
                kept = jnp.where(
                    inside_cols(layout, across, col_count)[:, :, None], arrived, jnp.bfloat16(0.0)
                )
                taps.append(shift_along(kept, -across, 1))
        results.append(taps)
    return results


def spread(stat):
    return stat.reshape(stat.shape[:-1] + (1, 1) + stat.shape[-1:])


def totals_of(one, two, number):
    local_sums = jnp.stack([jnp.sum(one, axis=(-3, -2)), jnp.sum(two, axis=(-3, -2))])
    flat = all_sum(local_sums.reshape(2, -1), number)
    return flat.reshape(local_sums.shape)


def moments(values, valid_mask, number):
    weighted = values * valid_mask[..., None]
    return totals_of(weighted, weighted * values, number)


def normalize(values, sums, valid_count, gain_row, bias_row):
    mean_value = sums[0] / valid_count
    variance = sums[1] / valid_count - mean_value * mean_value
    inverse = lax.rsqrt(variance + norm_epsilon)
    scaled = (values - spread(mean_value)) * spread(inverse)
    return (scaled, inverse, scaled * spread(gain_row) + spread(bias_row))


def norm_backward(grad_norm, scaled, inverse, gain_row, valid_mask, valid_count, number):
    masked = grad_norm * valid_mask[..., None]
    sums = totals_of(masked, masked * scaled, number)
    grad_values = (
        valid_mask[..., None]
        * spread(inverse * gain_row)
        * (masked - spread(sums[0] / valid_count) - scaled * spread(sums[1] / valid_count))
    )
    return (grad_values, sums)


def update(param, moment, grad):
    moment_new = momentum_decay * moment + grad
    return (param - step_rate * moment_new, moment_new)


def local(
    features,
    cotangent,
    crop_heights,
    task_scale,
    w_reduce,
    w_dilated,
    w_expand,
    w_heads,
    norm_params,
    m_reduce,
    m_dilated,
    m_expand,
    m_heads,
    norm_moment,
):
    row_count = features.shape[1]
    col_count = features.shape[2]
    channels = features.shape[3]
    middle = w_reduce.shape[1]
    head_width = w_heads.shape[2]
    head_total = w_heads.shape[0]
    group_index = lax.axis_index("dp")
    place_index = lax.axis_index("fsdp")
    group_heights = lax.dynamic_index_in_dim(crop_heights, group_index, 0, keepdims=False)
    crop_order = jnp.arange(group_heights.shape[0], dtype=jnp.int32)
    crop_ends = jnp.sum(
        jnp.where(crop_order[None, :] <= crop_order[:, None], group_heights[None, :], 0),
        axis=1,
        dtype=jnp.int32,
    )
    crop_starts = crop_ends - group_heights
    row_ids = place_index * row_count + jnp.arange(row_count, dtype=jnp.int32)
    member = (row_ids[:, None] >= crop_starts[None, :]) & (row_ids[:, None] < crop_ends[None, :])
    row_top = jnp.sum(jnp.where(member, crop_starts[None, :], 0), axis=1, dtype=jnp.int32)
    row_bottom = jnp.sum(jnp.where(member, crop_ends[None, :], 0), axis=1, dtype=jnp.int32)
    row_side = jnp.sum(jnp.where(member, group_heights[None, :], 0), axis=1, dtype=jnp.int32)
    layout = (row_ids, row_top, row_bottom, row_side)
    valid_mask = (jnp.arange(col_count, dtype=jnp.int32)[None, :] < row_side[:, None]).astype(
        jnp.float32
    )
    valid_count = jnp.sum(crop_heights * crop_heights).astype(jnp.float32)
    gain_values = norm_params[0]
    bias_values = norm_params[1]
    trunk_end = 2 * middle + channels
    inputs = features[0]
    inputs_float = inputs.astype(jnp.float32)
    place_count = lax.axis_size("fsdp")
    pixels = row_count * col_count
    half_rows = w_heads.shape[1] // 2
    heads_half = lax.dynamic_slice_in_dim(w_heads, group_index * half_rows, half_rows, 1)

    def beside(part):
        return lax.all_gather(
            part.astype(jnp.bfloat16), ("fsdp", "dp"), axis=1, tiled=True
        ).reshape(-1, channels, head_width)

    heads_late = beside(heads_half[1:])
    if place_count == 16:
        (
            reduce_low, dilated_low, expand_low, heads_early, trunk_out,
            scaled_one, scaled_two, scaled_three, masks, turned,
            sums_in_one, sums_in_two, sums_in_three, flat_params, wide_params, head_params,
        ) = trunk_step(
            inputs.reshape(pixels, channels),
            (
                w_reduce.astype(jnp.bfloat16),
                w_dilated.astype(jnp.bfloat16),
                w_expand.astype(jnp.bfloat16),
                w_heads[:1].astype(jnp.bfloat16),
            ),
            norm_params,
            crop_heights,
            head_rates + (trunk_rate,),
            row_count,
            col_count,
            middle,
            0,
        )
        heads_early = heads_early.reshape(-1, channels, head_width)
    else:
        head_gain = gain_values[trunk_end:].reshape(head_total, head_width)
        head_bias = bias_values[trunk_end:].reshape(head_total, head_width)
        head_params = jnp.concatenate(
            [
                jnp.stack([head_gain, head_bias], 1).reshape(2 * head_total, head_width),
                jnp.broadcast_to(valid_count, (2, head_width)),
            ]
        )
        total_rows = row_count * place_count
        masks = []
        for rate in head_rates + (trunk_rate,):
            flags = [
                inside_cols(layout, 0, col_count),
                inside_cols(layout, -rate, col_count),
                inside_cols(layout, rate, col_count),
            ] + [
                jnp.broadcast_to(flag[:, None], (row_count, col_count))
                for flag in (
                    inside_rows(layout, -rate),
                    inside_rows(layout, rate),
                    row_ids + rate < total_rows,
                    row_ids - rate >= 0,
                )
            ]
            flags = jnp.stack([f.reshape(pixels) for f in flags], 1).astype(jnp.float32)
            masks.append(jnp.pad(flags, ((0, 0), (0, 128 - flags.shape[1]))))
        masks = jnp.stack(masks)
        heads_early = beside(heads_half[:1])
        reduce_low, dilated_low, expand_low = (
            lax.all_gather(w.astype(jnp.bfloat16), "fsdp", axis=0)
            for w in (w_reduce, w_dilated, w_expand)
        )
        reduce_low = reduce_low.reshape(channels, middle)
        dilated_low = dilated_low.reshape(9, middle, middle)
        first = jnp.einsum("rwc,cm->rwm", inputs, reduce_low, preferred_element_type=jnp.float32)
        scaled_one, inverse_one, normed_one = normalize(
            first, moments(first, valid_mask, 1), valid_count, gain_values[:middle], bias_values[:middle]
        )
        hidden_one = jax.nn.silu(normed_one).astype(jnp.bfloat16)
        (second,) = dilated_forward(hidden_one, (dilated_low,), (trunk_rate,), layout, 2)
        scaled_two, inverse_two, normed_two = normalize(
            second,
            moments(second, valid_mask, 3),
            valid_count,
            gain_values[middle : 2 * middle],
            bias_values[middle : 2 * middle],
        )
        hidden_two = jax.nn.silu(normed_two).astype(jnp.bfloat16)
        expand_low = expand_low.transpose(1, 0, 2).reshape(middle, channels)
        third = jnp.einsum("rwm,mc->rwc", hidden_two, expand_low, preferred_element_type=jnp.float32)
        scaled_three, inverse_three, normed_three = normalize(
            third,
            moments(third, valid_mask, 4),
            valid_count,
            gain_values[2 * middle : trunk_end],
            bias_values[2 * middle : trunk_end],
        )
        pre_act = inputs_float + normed_three
        trunk_out = jax.nn.silu(pre_act).astype(jnp.bfloat16).reshape(pixels, channels)
        turned = trunk_out.T
    handed = head_total - 1
    head_grads, grads_own, grads_got, grads_late, head_sums, squares = heads_step(
        trunk_out,
        turned,
        heads_early,
        heads_late,
        cotangent.reshape(head_total, pixels, head_width),
        head_params,
        masks,
        head_rates,
        row_count,
        col_count,
        handed,
        5,
    )
    head_sums = head_sums.reshape(head_total, 2, head_width).transpose(1, 0, 2)
    shared = lax.psum_scatter(
        grads_late.reshape(-1, head_width), ("fsdp", "dp"), scatter_dimension=0, tiled=True
    )
    late_total = lax.all_gather(shared, "dp", axis=0, tiled=True)[None]
    if place_count == 16:
        (
            task_weight, back_one, back_two, back_three, features_grad, grad_reduce, grad_dilated, grad_expand, late,
        ) = back_step(
            inputs.reshape(pixels, channels),
            jnp.broadcast_to(jnp.pad(task_scale, (0, 8 - head_total))[:, None], (8, 128)),
            squares,
            scaled_one,
            scaled_two,
            scaled_three,
            flat_params,
            wide_params,
            sums_in_one,
            sums_in_two,
            sums_in_three,
            masks,
            head_grads,
            reduce_low,
            dilated_low,
            expand_low,
            grads_own.reshape(handed, place_count, -1, head_width // 2),
            grads_got.reshape(handed, place_count, -1, head_width // 2),
            trunk_rate,
            row_count,
            col_count,
            1,
        )
        task_weight = task_weight[:head_total, 0]
        features_grad = features_grad.reshape(row_count, col_count, channels)
        *trunk_totals, heads_total = reduce_shards(
            (
                grad_reduce.reshape(1, place_count, -1, middle),
                grad_dilated.reshape(1, place_count, -1, middle),
                grad_expand[None],
            ),
            (late,),
            2,
        )
        trunk_totals = [t[0] for t in trunk_totals]
        sums_one, sums_two = back_one, back_two
        sums_three = back_three.reshape(-1, 2, middle).transpose(1, 0, 2).reshape(2, channels)
    else:
        squares = jnp.sum(all_sum(squares, 9)[:head_total], axis=1)
        task_rms = jnp.sqrt(squares / (valid_count * channels) + task_epsilon)
        task_weight = task_scale / task_rms
        grad_trunk = task_weight[0] * head_grads[0]
        for k in range(1, head_total):
            grad_trunk = grad_trunk + task_weight[k] * head_grads[k]
        grad_trunk = grad_trunk.reshape(row_count, col_count, channels)
        grad_pre = grad_trunk * silu_slope(pre_act)
        grad_third, sums_three = norm_backward(
            grad_pre,
            scaled_three,
            inverse_three,
            gain_values[2 * middle : trunk_end],
            valid_mask,
            valid_count,
            11,
        )
        grad_third = grad_third.astype(jnp.bfloat16)
        grad_expand = jnp.einsum(
            "rwm,rwc->mc", hidden_two, grad_third, preferred_element_type=jnp.float32
        ).astype(jnp.bfloat16)
        grad_hidden_two = jnp.einsum(
            "rwc,mc->rwm", grad_third, expand_low, preferred_element_type=jnp.float32
        )
        grad_second, sums_two = norm_backward(
            grad_hidden_two * silu_slope(normed_two),
            scaled_two,
            inverse_two,
            gain_values[middle : 2 * middle],
            valid_mask,
            valid_count,
            12,
        )
        (taps,) = spread_taps([grad_second.astype(jnp.bfloat16)], (trunk_rate,), layout, 13)
        taps = jnp.stack(taps)
        grad_hidden_one = jnp.einsum(
            "krwo,kco->rwc", taps, dilated_low, preferred_element_type=jnp.float32
        )
        grad_dilated = jnp.einsum(
            "rwc,krwo->kco", hidden_one, taps, preferred_element_type=jnp.float32
        )
        grad_first, sums_one = norm_backward(
            grad_hidden_one * silu_slope(normed_one),
            scaled_one,
            inverse_one,
            gain_values[:middle],
            valid_mask,
            valid_count,
            14,
        )
        grad_first = grad_first.astype(jnp.bfloat16)
        grad_reduce = jnp.einsum("rwc,rwm->cm", inputs, grad_first, preferred_element_type=jnp.float32)
        features_grad = (
            jnp.einsum("rwm,cm->rwc", grad_first, reduce_low, preferred_element_type=jnp.float32)
            + grad_pre
        )
        trunk_totals = []
        for grad, axis in ((grad_reduce, 0), (grad_dilated.reshape(-1, middle), 0), (grad_expand, 1)):
            shard = lax.psum_scatter(
                grad.astype(jnp.bfloat16), "fsdp", scatter_dimension=axis, tiled=True
            )
            trunk_totals.append(lax.psum(shard, "dp"))
        shared = lax.psum_scatter(
            (grads_own + grads_got).reshape(handed, -1, head_width // 2),
            "fsdp",
            scatter_dimension=1,
            tiled=True,
        )
        heads_total = lax.all_gather(shared, "dp", axis=2, tiled=True)
    totals = tuple(t.astype(jnp.float32) for t in trunk_totals) + (
        task_weight[:, None, None]
        * jnp.concatenate([heads_total, late_total]).astype(jnp.float32),
    )
    gain_grad = jnp.concatenate(
        [sums_one[1], sums_two[1], sums_three[1], (task_weight[:, None] * head_sums[1]).reshape(-1)]
    )
    bias_grad = jnp.concatenate(
        [sums_one[0], sums_two[0], sums_three[0], (task_weight[:, None] * head_sums[0]).reshape(-1)]
    )
    norm_grad = jnp.stack([gain_grad, bias_grad])
    w_reduce_new, m_reduce_new = update(w_reduce, m_reduce, totals[0])
    w_dilated_new, m_dilated_new = update(w_dilated, m_dilated, totals[1])
    w_expand_new, m_expand_new = update(w_expand, m_expand, totals[2])
    w_heads_new, m_heads_new = update(w_heads, m_heads, totals[3])
    norm_params_new, norm_moment_new = update(norm_params, norm_moment, norm_grad)
    return (
        features_grad[None],
        w_reduce_new,
        m_reduce_new,
        w_dilated_new,
        m_dilated_new,
        w_expand_new,
        m_expand_new,
        w_heads_new,
        m_heads_new,
        norm_params_new,
        norm_moment_new,
    )


def solution(mesh):
    placed = (
        P("dp", "fsdp", None, None),
        P(None, "dp", "fsdp", None, None),
        P(),
        P(),
        P("fsdp", None),
        P("fsdp", None),
        P(None, "fsdp"),
        P(None, "fsdp", None),
        P(),
        P("fsdp", None),
        P("fsdp", None),
        P(None, "fsdp"),
        P(None, "fsdp", None),
        P(),
    )
    return jax.shard_map(
        local,
        mesh=mesh,
        in_specs=placed,
        out_specs=(
            P("dp", "fsdp", None, None),
            P("fsdp", None),
            P("fsdp", None),
            P("fsdp", None),
            P("fsdp", None),
            P(None, "fsdp"),
            P(None, "fsdp"),
            P(None, "fsdp", None),
            P(None, "fsdp", None),
            P(),
            P(),
        ),
        check_vma=False,
    )
```

```python
import functools

import jax
import jax.numpy as jnp
from jax import lax
from jax.experimental import pallas as pl
from jax.experimental.pallas import tpu as pltpu
from jax.sharding import PartitionSpec as P

MESH = pl.DeviceIdType.MESH
norm_epsilon = 1e-05
task_epsilon = 1e-06
momentum_decay = 0.9
step_rate = 0.01
trunk_rate = 4
head_rates = (12, 24, 36)

class Tree:
    def __init__(self):
        self.core = lax.axis_index("dp")
        self.place = lax.axis_index("fsdp")
        self.count = lax.axis_size("fsdp")
        self.line = self.count // 4
        self.z = self.place // 4
        self.low = self.place % 4
        self.step_a = 1 + self.core
        self.step_b = 2 - self.core
        self.move_a = self.step_a * (1 - 2 * ((self.low // self.step_a) % 2))
        self.move_b = self.step_b * (1 - 2 * ((self.low // self.step_b) % 2))

    def at(self, place):
        return (self.core, place)

    @property
    def partner(self):
        return (1 - self.core, self.place)

    @property
    def a(self):
        return self.at(self.place + self.move_a)

    @property
    def b(self):
        return self.at(self.place + self.move_b)

    @property
    def down(self):
        return self.at(self.place - 4)

    @property
    def up(self):
        return self.at(self.place + 4)

    def greet(self):
        barrier = pltpu.get_barrier_semaphore()
        for peer in (self.partner, self.a, self.b):
            pl.semaphore_signal(barrier, inc=1, device_id=peer, device_id_type=MESH)

        @pl.when(self.z > 0)
        def _():
            pl.semaphore_signal(barrier, inc=1, device_id=self.down, device_id_type=MESH)

        @pl.when(self.z < self.line - 1)
        def _():
            pl.semaphore_signal(barrier, inc=1, device_id=self.up, device_id_type=MESH)

        pl.semaphore_wait(
            barrier,
            3
            + jnp.where(self.z > 0, 1, 0)
            + jnp.where(self.z < self.line - 1, 1, 0),
        )


def plane_sum_kernel(line, x_ref, o_ref, near, part, far, n_send, n_recv, f_send, f_recv):
    core = lax.axis_index("dp")
    place = lax.axis_index("fsdp")
    z, low = place // 4, place % 4
    me = low * 2 + core

    def beside(s):
        other = (me + s) % 8
        return (other % 2, z * 4 + other // 2)

    def away(s):
        return (core, ((z + s) % line) * 4 + low)

    barrier = pltpu.get_barrier_semaphore()
    for s in range(1, 8):
        pl.semaphore_signal(barrier, inc=1, device_id=beside(s), device_id_type=MESH)

    @pl.loop(1, line)
    def _(s):
        pl.semaphore_signal(barrier, inc=1, device_id=away(s), device_id_type=MESH)

    near[me] = x_ref[...]
    pl.semaphore_wait(barrier, 7 + line - 1)

    def to_beside(s):
        return pltpu.make_async_remote_copy(src_ref=x_ref, dst_ref=near.at[me], send_sem=n_send.at[s], recv_sem=n_recv, device_id=beside(s), device_id_type=MESH)

    def to_away(s):
        return pltpu.make_async_remote_copy(src_ref=part, dst_ref=far.at[z], send_sem=f_send.at[s], recv_sem=f_recv, device_id=away(s), device_id_type=MESH)

    for s in range(1, 8):
        to_beside(s).start()
    seven = near.at[pl.ds(0, 7)]
    pltpu.make_async_copy(seven, seven, n_recv).wait()
    total = jnp.sum(near[...], axis=0)
    part[...] = total
    pl.loop(1, line)(lambda s: to_away(s).start())
    far[z] = total
    rest = far.at[pl.ds(0, line - 1)]
    pltpu.make_async_copy(rest, rest, f_recv).wait()
    o_ref[...] = jnp.sum(far[...], axis=0)
    for s in range(1, 8):
        to_beside(s).wait_send()
    pl.loop(1, line)(lambda s: to_away(s).wait_send())


def all_sum(x, number):
    line = lax.axis_size("fsdp") // 4
    dma = pltpu.SemaphoreType.DMA
    return pl.pallas_call(
        functools.partial(plane_sum_kernel, line),
        out_shape=jax.ShapeDtypeStruct(x.shape, x.dtype),
        in_specs=[pl.BlockSpec(memory_space=pltpu.VMEM)],
        out_specs=pl.BlockSpec(memory_space=pltpu.VMEM),
        scratch_shapes=[
            pltpu.VMEM((8,) + x.shape, x.dtype), pltpu.VMEM(x.shape, x.dtype), pltpu.VMEM((line,) + x.shape, x.dtype),
            dma((8,)), dma, dma((line,)), dma,
        ],
        compiler_params=pltpu.CompilerParams(collective_id=number, has_side_effects=True),
    )(x)


def reduce_kernel(kinds, whole, *refs):
    count = len(kinds)
    parts, outs = refs[:count], refs[count : 2 * count]
    scratch = refs[2 * count :]
    accs, arx, zrx = (scratch[k * count : (k + 1) * count] for k in range(3))
    prx, brx = (scratch[3 * count + k * whole : 3 * count + (k + 1) * whole] for k in range(2))
    (
        load_sem, p_send, p_recv, b_send, b_recv, a_send, a_recv, z_send, z_recv, s_send, s_recv,
    ) = scratch[3 * count + 2 * whole :]
    t = Tree()
    t.greet()
    line, z, low = t.line, t.z, t.low

    def rows_of(k, core):
        rows = kinds[k][1] // 2
        return pl.ds(pl.multiple_of(core * rows, 16), rows)

    def remote(src, dst, send, recv, peer):
        return pltpu.make_async_remote_copy(src_ref=src, dst_ref=dst, send_sem=send, recv_sem=recv, device_id=peer, device_id_type=MESH)

    def load(k, block):
        return pltpu.make_async_copy(
            parts[k].at[:, block, rows_of(k, t.core)], accs[k].at[block], load_sem.at[k, block]
        )

    def load_late(k, at):
        return pltpu.make_async_copy(parts[k].at[at], accs[k].at[at], load_sem.at[k, at])

    def spot_of(k, zz, w):
        if k < whole:
            return zz * 4 + lows[w]
        return zz * 2 + (3 - w)

    def to_partner(k, block):
        return remote(parts[k].at[:, block, rows_of(k, 1 - t.core)], prx[k].at[block], p_send.at[k, block], p_recv.at[k, block], t.partner)

    upper = z >= line // 2
    own_spot = jnp.where(upper, z, line - 1 - z)

    def spot(j):
        q = j + jnp.where(j >= own_spot, 1, 0)
        other = jnp.where(upper, q, line - 1 - q)
        return jnp.where(j == line - 1, z, other)

    lows = (low + t.move_b, low + t.move_a + t.move_b, low + t.move_a, low)

    def to_b(k, zz, which):
        return remote(accs[k].at[zz * 4 + lows[which]], brx[k].at[zz * 2 + which], b_send.at[k, zz * 2 + which], b_recv.at[k, zz * 2 + which], t.b)

    def to_a(k, zz):
        return remote(accs[k].at[spot_of(k, zz, 2)], arx[k].at[zz], a_send.at[k, zz], a_recv.at[k, zz], t.a)

    def along(k, zz, up):
        w = 1 if up else 0
        return remote(accs[k].at[spot_of(k, zz, 3)], zrx[k].at[w, zz], z_send.at[k, w, zz], z_recv.at[k, w, zz], t.up if up else t.down)

    def add(k, block, ref):
        lead = kinds[k][0]

        @pl.loop(0, lead)
        def _(h):
            accs[k][block, h] = accs[k][block, h] + ref[h]

    def begin(j):
        zz = spot(j)
        for k in range(whole, count):
            load_late(k, zz * 2).start()
            load_late(k, zz * 2 + 1).start()
        for w in range(4):
            for k in range(whole):
                to_partner(k, zz * 4 + lows[w]).start()
                load(k, zz * 4 + lows[w]).start()

    first, last = range(whole), range(whole, count)

    def send_late(j):
        zz = spot(j)
        for k in last:
            load_late(k, zz * 2 + 1).wait()
            to_a(k, zz).start()

    def stage_b(j):
        zz = spot(j)
        for w in range(4):
            for k in first:
                block = zz * 4 + lows[w]
                load(k, block).wait()
                to_partner(k, block).wait_recv()
                add(k, block, prx[k].at[block])
                if w < 2:
                    to_b(k, zz, w).start()

    def stage_a(j):
        zz = spot(j)
        for w in (1, 0):
            for k in first:
                to_b(k, zz, w).wait_recv()
                add(k, zz * 4 + lows[3 if w == 0 else 2], brx[k].at[zz * 2 + w])
                if w == 1:
                    to_a(k, zz).start()

    def stage_z(j, ks):
        zz = spot(j)
        for k in ks:
            if k >= whole:
                load_late(k, zz * 2).wait()
            to_a(k, zz).wait_recv()
            here = spot_of(k, zz, 3)
            add(k, here, arx[k].at[zz])

            @pl.when(jnp.logical_and(zz >= z, z > 0))
            def _():
                along(k, zz, True).wait_recv()
                add(k, here, zrx[k].at[1, zz])

            @pl.when(jnp.logical_and(zz <= z, z < line - 1))
            def _():
                along(k, zz, False).wait_recv()
                add(k, here, zrx[k].at[0, zz])

            @pl.when(zz > z)
            def _():
                along(k, zz, True).start()

            @pl.when(zz < z)
            def _():
                along(k, zz, False).start()

    pl.loop(0, line)(begin)
    pl.loop(0, line)(send_late)
    pl.loop(0, line)(stage_b)

    @pl.loop(0, line + 1)
    def _(j):
        pl.when(j < line)(lambda: stage_z(j, last))
        pl.when(j >= 1)(lambda: stage_a(j - 1))

    pl.loop(0, line)(lambda j: stage_z(j, first))

    def half(k, core):
        if k < whole:
            return outs[k].at[:, rows_of(k, core)]
        cols = kinds[k][2]
        return outs[k].at[:, :, pl.ds(pl.multiple_of(core * cols, cols), cols)]

    def share(k):
        return remote(accs[k].at[spot_of(k, z, 3)], half(k, t.core), s_send.at[k], s_recv.at[k], t.partner)

    def keep(k):
        return pltpu.make_async_copy(accs[k].at[spot_of(k, z, 3)], half(k, t.core), load_sem.at[k, 0])

    for k in range(count):
        share(k).start()
        keep(k).start()

    @pl.loop(0, line)
    def _(j):
        zz = spot(j)
        for k in range(count):
            if k < whole:
                for w in range(4):
                    to_partner(k, zz * 4 + lows[w]).wait_send()
                to_b(k, zz, 0).wait_send()
                to_b(k, zz, 1).wait_send()
            to_a(k, zz).wait_send()
            pl.when(zz > z)(lambda: along(k, zz, True).wait_send())
            pl.when(zz < z)(lambda: along(k, zz, False).wait_send())

    for k in range(count):
        keep(k).wait()
        other = half(k, 1 - t.core)
        remote(other, other, s_send.at[k], s_recv.at[k], t.partner).wait_recv()
        share(k).wait_send()


def reduce_shards(parts, late, number):
    n = lax.axis_size("fsdp")
    line = n // 4
    whole = len(parts)
    kinds = [(p.shape[0], p.shape[2], p.shape[3]) for p in parts] + [p.shape[1:] for p in late]
    sizes = [(l, r // 2, c) for l, r, c in kinds[:whole]] + kinds[whole:]
    results = kinds[:whole] + [(l, r, 2 * c) for l, r, c in kinds[whole:]]
    bf = jnp.bfloat16
    count = len(kinds)
    dma = pltpu.SemaphoreType.DMA

    def room(some, *lead):
        return [pltpu.VMEM(tuple(lead) + tuple(s), bf) for s in some]

    accs = [
        pltpu.VMEM((n if k < whole else 2 * line,) + tuple(s), bf) for k, s in enumerate(sizes)
    ]
    return pl.pallas_call(
        functools.partial(reduce_kernel, kinds, whole),
        out_shape=tuple(jax.ShapeDtypeStruct(r, bf) for r in results),
        in_specs=[pl.BlockSpec(memory_space=pl.ANY)] * count,
        out_specs=tuple([pl.BlockSpec(memory_space=pl.ANY)] * count),
        scratch_shapes=accs
        + room(sizes, line)
        + room(sizes, 2, line)
        + room(sizes[:whole], n)
        + room(sizes[:whole], 2 * line)
        + [
            dma((count, n)),
            dma((count, n)),
            dma((count, n)),
            dma((count, 2 * line)),
            dma((count, 2 * line)),
            dma((count, line)),
            dma((count, line)),
            dma((count, 2, line)),
            dma((count, 2, line)),
            dma((count,)),
            dma((count,)),
        ],
        compiler_params=pltpu.CompilerParams(
            collective_id=number, has_side_effects=True, vmem_limit_bytes=60 * 2**20
        ),
    )(*parts, *late)


def exchange_kernel(offsets, rows, count, x_ref, o_ref, send, recv):
    core = lax.axis_index("dp")
    place = lax.axis_index("fsdp")
    pieces = []
    for k, offset in enumerate(offsets):
        first, cut = offset // rows, offset % rows
        for part, (gap, low, high, to) in enumerate(
            ((first, cut, rows, 0), (first + 1, 0, cut, rows - cut))
        ):
            if high > low:
                pieces.append((k, part, gap, low, high - low, to))
    gaps = sorted({abs(p[2]) for p in pieces} - {0})
    gaps = [-g for g in gaps] + gaps
    barrier = pltpu.get_barrier_semaphore()

    def present(gap):
        return jnp.logical_and(place + gap >= 0, place + gap < count)

    met = jnp.int32(0)
    for gap in gaps:
        met = met + jnp.where(present(gap), 1, 0)

        @pl.when(present(gap))
        def _():
            pl.semaphore_signal(
                barrier, inc=1, device_id=(core, place + gap), device_id_type=MESH
            )

    pl.semaphore_wait(barrier, met)

    def piece(k, part, gap, low, size, to):
        return pltpu.make_async_remote_copy(
            src_ref=x_ref.at[k, pl.ds(low, size)],
            dst_ref=o_ref.at[k, pl.ds(to, size)],
            send_sem=send.at[k, part],
            recv_sem=recv.at[k, part],
            device_id=(core, place - gap),
            device_id_type=MESH,
        )

    for p in pieces:
        k, part, gap, low, size, to = p
        if gap == 0:
            o_ref[k, to : to + size] = x_ref[k, low : low + size]
        else:
            pl.when(present(-gap))(lambda p=p: piece(*p).start())
    for p in pieces:
        if p[2]:
            pl.when(present(p[2]))(lambda p=p: piece(*p).wait_recv())
    for p in pieces:
        if p[2]:
            pl.when(present(-p[2]))(lambda p=p: piece(*p).wait_send())


def exchange(x, offsets, number):
    entries, rows = x.shape[:2]
    return pl.pallas_call(
        functools.partial(exchange_kernel, offsets, rows, lax.axis_size("fsdp")),
        out_shape=jax.ShapeDtypeStruct(x.shape, x.dtype),
        in_specs=[pl.BlockSpec(memory_space=pltpu.VMEM)],
        out_specs=pl.BlockSpec(memory_space=pltpu.VMEM),
        scratch_shapes=[
            pltpu.SemaphoreType.DMA((entries, 2)),
            pltpu.SemaphoreType.DMA((entries, 2)),
        ],
        compiler_params=pltpu.CompilerParams(
            collective_id=number, has_side_effects=True, vmem_limit_bytes=32 * 2**20
        ),
    )(x)


def plane_signal(line, core, z, low):
    barrier = pltpu.get_barrier_semaphore()
    me = low * 2 + core
    for s in range(1, 8):
        other = (me + s) % 8
        pl.semaphore_signal(
            barrier, inc=1, device_id=(other % 2, z * 4 + other // 2), device_id_type=MESH
        )

    @pl.loop(1, line)
    def _(s):
        pl.semaphore_signal(
            barrier, inc=1, device_id=(core, ((z + s) % line) * 4 + low), device_id_type=MESH
        )


def plane_scratch(line, shape):
    dma = pltpu.SemaphoreType.DMA
    return [
        pltpu.VMEM((8,) + shape, jnp.float32),
        pltpu.VMEM(shape, jnp.float32),
        pltpu.VMEM((line,) + shape, jnp.float32),
        dma((8,)),
        dma,
        dma((line,)),
        dma,
    ]


def plane_sum(line, fill, room, meanwhile=None, later=None):
    near, part, far, n_send, n_recv, f_send, f_recv = room
    core = lax.axis_index("dp")
    place = lax.axis_index("fsdp")
    z, low = place // 4, place % 4
    me = low * 2 + core

    def to_beside(s):
        other = (me + s) % 8
        return pltpu.make_async_remote_copy(
            src_ref=near.at[me],
            dst_ref=near.at[me],
            send_sem=n_send.at[s],
            recv_sem=n_recv,
            device_id=(other % 2, z * 4 + other // 2),
            device_id_type=MESH,
        )

    def to_away(s):
        return pltpu.make_async_remote_copy(
            src_ref=part,
            dst_ref=far.at[z],
            send_sem=f_send.at[s],
            recv_sem=f_recv,
            device_id=(core, ((z + s) % line) * 4 + low),
            device_id_type=MESH,
        )

    fill(near.at[me])
    for s in range(1, 8):
        to_beside(s).start()
    if meanwhile is not None:
        meanwhile()
    seven = near.at[pl.ds(0, 7)]
    pltpu.make_async_copy(seven, seven, n_recv).wait()
    total = jnp.sum(near[...], axis=0)
    part[...] = total
    pl.loop(1, line)(lambda s: to_away(s).start())
    far[z] = total
    if later is not None:
        later()
    rest = far.at[pl.ds(0, line - 1)]
    pltpu.make_async_copy(rest, rest, f_recv).wait()
    result = jnp.sum(far[...], axis=0)
    for s in range(1, 8):
        to_beside(s).wait_send()
    pl.loop(1, line)(lambda s: to_away(s).wait_send())
    return result


def row_pieces(offset, rows):
    first, cut = offset // rows, offset % rows
    pieces = [(first, cut, rows - cut, 0)]
    if cut:
        pieces.append((first + 1, 0, cut, rows - cut))
    return pieces


def row_gaps(offsets, rows):
    gaps = {abs(p[0]) for o in offsets for p in row_pieces(o, rows)} - {0}
    return sorted(-g for g in gaps) + sorted(gaps)


def greet_rows(gaps, count):
    barrier = pltpu.get_barrier_semaphore()
    core = lax.axis_index("dp")
    place = lax.axis_index("fsdp")
    met = jnp.int32(0)
    for gap in gaps:
        here = jnp.logical_and(place + gap >= 0, place + gap < count)
        met = met + jnp.where(here, 1, 0)

        @pl.when(here)
        def _():
            pl.semaphore_signal(
                barrier, inc=1, device_id=(core, place + gap), device_id_type=MESH
            )

    return met


class Rows:
    def __init__(self, offsets, rows, cols, count, x_ref, o_ref, send, recv):
        self.core = lax.axis_index("dp")
        self.place = lax.axis_index("fsdp")
        self.rows, self.cols, self.count = rows, cols, count
        self.offsets, self.x_ref, self.o_ref = offsets, x_ref, o_ref
        self.send, self.recv = send, recv

    def present(self, gap):
        return jnp.logical_and(self.place + gap >= 0, self.place + gap < self.count)

    def copies(self, k):
        for part, (gap, low, size, to) in enumerate(row_pieces(self.offsets[k], self.rows)):
            yield gap, low, size, to, pltpu.make_async_remote_copy(
                src_ref=self.x_ref.at[k, pl.ds(low * self.cols, size * self.cols)],
                dst_ref=self.o_ref.at[k, pl.ds(to * self.cols, size * self.cols)],
                send_sem=self.send.at[k, part],
                recv_sem=self.recv.at[k, part],
                device_id=(self.core, self.place - gap),
                device_id_type=MESH,
            )

    def start(self, k):
        for gap, low, size, to, copy in self.copies(k):
            if gap == 0:
                cols = self.cols
                self.o_ref[k, to * cols : (to + size) * cols] = self.x_ref[
                    k, low * cols : (low + size) * cols
                ]
            else:
                pl.when(self.present(-gap))(copy.start)

    def wait_recv(self, k):
        for gap, _, _, _, copy in self.copies(k):
            if gap:
                pl.when(self.present(gap))(copy.wait_recv)

    def wait_send(self, k):
        for gap, _, _, _, copy in self.copies(k):
            if gap:
                pl.when(self.present(-gap))(copy.wait_send)


def heads_kernel(
    rates, rows, cols, count,
    x_ref, xt_o, wa_ref, wb_ref, cot_o, par_ref, mask_ref,
    g_ref, own_ref, got_ref, late_ref, sums_ref, sq_ref,
    wv, out_rows, in_rows, resp, dn, taps, g_room, dw_room, xt_ref, cot_ref, late_sem,
    w_sem, f_send, f_recv, e_send, e_recv, g_sem, dw_sem, hand_sem, got_sem, *rooms,
):
    px = rows * cols
    heads = len(rates)
    width = par_ref.shape[1]
    line = count // 4
    core = lax.axis_index("dp")
    place = lax.axis_index("fsdp")
    z, low = place // 4, place % 4
    one, two = rooms[:7], rooms[7:]

    def w_copy(t, k):
        early = wa_ref.shape[0] // 9
        src = wa_ref.at[t * 9 + k] if t < early else wb_ref.at[(t - early) * 9 + k]
        return pltpu.make_async_copy(
            src, wv.at[t, :, k * width : (k + 1) * width], w_sem.at[t * 9 + k]
        )

    for t in reversed(range(heads)):
        for k in range(9):
            w_copy(t, k).start()
    fetched = [
        pltpu.make_async_copy(cot_o, cot_ref, late_sem.at[0]),
        pltpu.make_async_copy(xt_o, xt_ref, late_sem.at[1]),
    ]
    for c in fetched:
        c.start()
    fwd = Rows([o for r in rates for o in (-r, r)], rows, cols, count, out_rows, in_rows, f_send, f_recv)
    bwd = Rows([o for r in rates for o in (r, -r)], rows, cols, count, out_rows, in_rows, e_send, e_recv)
    plane_signal(line, core, z, low)
    met = greet_rows(row_gaps(fwd.offsets, rows), count)
    barrier = pltpu.get_barrier_semaphore()

    def mask(t, k):
        return mask_ref[t, :, k : k + 1]

    @pl.loop(0, heads)
    def _(step):
        t = heads - 1 - step
        rate = 12 * (t + 1)
        for j in (0, 2, 1):
            summed = None
            for c in range(3):
                k = 3 * j + c
                pltpu.make_async_copy(
                    wa_ref.at[k], wv.at[t, :, k * width : (k + 1) * width], w_sem.at[t * 9 + k]
                ).wait()
                prod = jnp.dot(
                    x_ref[...], wv[t, :, k * width : (k + 1) * width], preferred_element_type=jnp.float32
                )
                if c == 0:
                    summed = jnp.where(mask(t, 1) > 0, pltpu.roll(prod, rate, 0), 0.0)
                elif c == 1:
                    summed = summed + jnp.where(mask(t, 0) > 0, prod, 0.0)
                else:
                    summed = summed + jnp.where(mask(t, 2) > 0, pltpu.roll(prod, px - rate, 0), 0.0)
            if j == 1:
                resp[t] = summed
                continue
            out_rows[t * 2 + j // 2] = summed.astype(jnp.bfloat16)
            if j == 0:

                @pl.when(step == 0)
                def _():
                    pl.semaphore_wait(barrier, 7 + line - 1 + met)

            for h in range(heads):
                pl.when(t == h)(lambda: fwd.start(2 * h + j // 2))

    def stats(ref):
        for h in range(heads):
            total = resp[h]
            for j in (0, 1):
                fwd.wait_recv(2 * h + j)
                total = total + jnp.where(
                    mask(h, 3 + j) > 0, in_rows[2 * h + j].astype(jnp.float32), 0.0
                )
            resp[h] = total
            kept = total * mask(h, 0)
            ref[2 * h : 2 * h + 1] = jnp.sum(kept, axis=0, keepdims=True)
            ref[2 * h + 1 : 2 * h + 2] = jnp.sum(kept * total, axis=0, keepdims=True)

    sums = plane_sum(line, stats, one)
    for c in fetched:
        c.wait()
    pixels = par_ref[2 * heads : 2 * heads + 1]
    inverses = []

    def grads(ref):
        for h in range(heads):
            mean = sums[2 * h : 2 * h + 1] / pixels
            var = sums[2 * h + 1 : 2 * h + 2] / pixels - mean * mean
            inverse = lax.rsqrt(var + norm_epsilon)
            inverses.append(inverse)
            scaled = (resp[h] - mean) * inverse
            normed = scaled * par_ref[2 * h : 2 * h + 1] + par_ref[2 * h + 1 : 2 * h + 2]
            s = jax.nn.sigmoid(normed)
            d = cot_ref[h].astype(jnp.float32) * (s * (1.0 + normed * (1.0 - s))) * mask(h, 0)
            resp[h] = scaled
            dn[h] = d
            ref[2 * h : 2 * h + 1] = jnp.sum(d, axis=0, keepdims=True)
            ref[2 * h + 1 : 2 * h + 2] = jnp.sum(d * scaled, axis=0, keepdims=True)

    back = plane_sum(line, grads, two)
    sums_ref[...] = back
    for h in range(heads):
        fwd.wait_send(2 * h)
        fwd.wait_send(2 * h + 1)
        e = (
            mask(h, 0)
            * (inverses[h] * par_ref[2 * h : 2 * h + 1])
            * (dn[h] - back[2 * h : 2 * h + 1] / pixels - resp[h] * (back[2 * h + 1 : 2 * h + 2] / pixels))
        )
        dn[h] = e
        out_rows[2 * h] = jnp.where(mask(h, 3) > 0, e, 0.0).astype(jnp.bfloat16)
        out_rows[2 * h + 1] = jnp.where(mask(h, 4) > 0, e, 0.0).astype(jnp.bfloat16)
        bwd.start(2 * h)
        bwd.start(2 * h + 1)

    def g_copy(t):
        return pltpu.make_async_copy(g_room, g_ref.at[t], g_sem)

    half = width // 2

    def lanes(owner):
        return pl.ds(pl.multiple_of(owner * half, half), half)

    def keep(slot, at):
        return pltpu.make_async_copy(
            dw_room.at[slot, :, lanes(core)], own_ref.at[at], dw_sem.at[slot]
        )

    def hand(slot, at):
        return pltpu.make_async_remote_copy(
            src_ref=dw_room.at[slot, :, lanes(1 - core)],
            dst_ref=got_ref.at[at],
            send_sem=hand_sem.at[slot],
            recv_sem=got_sem,
            device_id=(1 - core, place),
            device_id_type=MESH,
        )

    def put(slot, at):
        return pltpu.make_async_copy(
            dw_room.at[slot], late_ref.at[at - own_ref.shape[0]], dw_sem.at[slot]
        )

    def handed(t):
        return (t + 1) * 9 <= own_ref.shape[0]

    def dw_start(slot, t, k):
        at = t * 9 + k

        @pl.when(handed(t))
        def _():
            keep(slot, at).start()
            hand(slot, at).start()

        pl.when(jnp.logical_not(handed(t)))(lambda: put(slot, at).start())

    def dw_wait(slot, t):
        @pl.when(handed(t))
        def _():
            keep(slot, 0).wait()
            hand(slot, 0).wait_send()

        pl.when(jnp.logical_not(handed(t)))(lambda: put(slot, own_ref.shape[0]).wait())

    def weigh(t, k, number, before):
        slot = lax.rem(number, 2)
        pl.when(number >= 2)(lambda: dw_wait(slot, before))
        dw_room[slot] = jnp.dot(
            xt_ref[...],
            taps[:, pl.ds(pl.multiple_of(k * width, width), width)],
            preferred_element_type=jnp.float32,
        ).astype(jnp.bfloat16)
        dw_start(slot, t, k)

    def spread(t, j, arrived):
        rate = 12 * (t + 1)
        for c in range(3):
            if c == 0:
                tap = pltpu.roll(jnp.where(mask(t, 1) > 0, arrived, 0.0), px - rate, 0)
            elif c == 1:
                tap = jnp.where(mask(t, 0) > 0, arrived, 0.0)
            else:
                tap = pltpu.roll(jnp.where(mask(t, 2) > 0, arrived, 0.0), rate, 0)
            k = 3 * j + c
            taps[:, k * width : (k + 1) * width] = tap.astype(jnp.bfloat16)

    tiles = wv.shape[1] // width
    sq_ref[...] = jnp.zeros_like(sq_ref)

    def center(t):
        spread(t, 1, dn[t].astype(jnp.bfloat16).astype(jnp.float32))

    @pl.loop(0, heads)
    def _(t):
        center(t)
        pl.loop(0, 3)(lambda k: weigh(t, 3 + k, t * 3 + k, t - jnp.where(k < 2, 1, 0)))

    @pl.loop(0, heads)
    def _(t):
        center(t)
        for h in range(heads):
            @pl.when(t == h)
            def _():
                bwd.wait_recv(2 * h)
                bwd.wait_recv(2 * h + 1)

        spread(t, 0, jnp.where(mask(t, 5) > 0, in_rows[2 * t].astype(jnp.float32), 0.0))
        spread(t, 2, jnp.where(mask(t, 6) > 0, in_rows[2 * t + 1].astype(jnp.float32), 0.0))

        pl.loop(0, 6)(
            lambda k: weigh(
                t,
                k + jnp.where(k >= 3, 3, 0),
                3 * heads + t * 6 + k,
                jnp.where(k < 2, jnp.where(t > 0, t - 1, heads - 1), t),
            )
        )
        pl.when(t > 0)(lambda: g_copy(t - 1).wait())
        def tile(n, square):
            cut = pl.ds(pl.multiple_of(n * width, width), width)
            g = lax.dot_general(
                taps[...], wv[t, cut, :], (((1,), (1,)), ((), ())), preferred_element_type=jnp.float32
            )
            g_room[:, cut] = g.astype(jnp.bfloat16)
            return square + jnp.sum(g * g, axis=0, keepdims=True)

        square = lax.fori_loop(0, tiles, tile, jnp.zeros((1, width), jnp.float32))
        sq_ref[pl.ds(t, 1)] = square
        g_copy(t).start()

    g_copy(heads - 1).wait()
    dw_wait(0, heads - 1)
    dw_wait(1, heads - 1)
    pltpu.make_async_copy(got_ref, got_ref, got_sem).wait()

    for k in range(2 * heads):
        bwd.wait_send(k)


def heads_step(trunk_out, turned, early, late, cotangent, params, masks, rates, rows, cols, handed, number):
    px, channels = trunk_out.shape
    heads, width = len(rates), early.shape[-1]
    count = lax.axis_size("fsdp")
    line = count // 4
    bf, f32 = jnp.bfloat16, jnp.float32
    dma = pltpu.SemaphoreType.DMA
    vmem = pl.BlockSpec(memory_space=pltpu.VMEM)
    hbm = pl.BlockSpec(memory_space=pl.ANY)
    return pl.pallas_call(
        functools.partial(heads_kernel, rates, rows, cols, count),
        out_shape=(
            jax.ShapeDtypeStruct((heads, px, channels), bf),
            jax.ShapeDtypeStruct((9 * handed, channels, width // 2), bf),
            jax.ShapeDtypeStruct((9 * handed, channels, width // 2), bf),
            jax.ShapeDtypeStruct((9 * (heads - handed), channels, width), bf),
            jax.ShapeDtypeStruct((2 * heads, width), f32),
            jax.ShapeDtypeStruct((8, width), f32),
        ),
        in_specs=[vmem, hbm, hbm, hbm, hbm, vmem, vmem],
        out_specs=(hbm, hbm, hbm, hbm, vmem, vmem),
        scratch_shapes=[
            pltpu.VMEM((heads, channels, 9 * width), bf),
            pltpu.VMEM((2 * heads, px, width), bf),
            pltpu.VMEM((2 * heads, px, width), bf),
            pltpu.VMEM((heads, px, width), f32),
            pltpu.VMEM((heads, px, width), f32),
            pltpu.VMEM((px, 9 * width), bf),
            pltpu.VMEM((px, channels), bf),
            pltpu.VMEM((2, channels, width), bf),
            pltpu.VMEM((channels, px), bf),
            pltpu.VMEM((heads, px, width), bf),
            dma((2,)),
            dma((9 * heads,)),
            dma((2 * heads, 2)),
            dma((2 * heads, 2)),
            dma((2 * heads, 2)),
            dma((2 * heads, 2)),
            dma,
            dma((2,)),
            dma((2,)),
            dma,
        ]
        + plane_scratch(line, (2 * heads, width))
        + plane_scratch(line, (2 * heads, width)),
        compiler_params=pltpu.CompilerParams(
            collective_id=number, has_side_effects=True, vmem_limit_bytes=62 * 2**20
        ),
    )(trunk_out, turned, early, late, cotangent, params, masks)


class Fan:
    def __init__(self, t, arrays, sends, arrives, shares, own_sem):
        self.t, self.arrays = t, arrays
        self.sends, self.arrives, self.shares, self.own_sem = sends, arrives, shares, own_sem

    def copy(self, k, kind, block, peer, own=False):
        src, place = self.arrays[k]
        dst = place(block, self.t.core)
        return pltpu.make_async_remote_copy(
            src_ref=src if own else dst,
            dst_ref=dst,
            send_sem=self.sends.at[k, kind, block],
            recv_sem=(self.shares if kind == 4 else self.arrives).at[k, block],
            device_id=peer,
            device_id_type=MESH,
        )

    def fan(self, k, block, own, down, up, a, b, finish):
        t = self.t

        def act(kind, peer):
            c = self.copy(k, kind, block, peer, own)
            c.wait_send() if finish else c.start()

        if down:
            pl.when(t.z > 0)(lambda: act(0, t.down))
        if up:
            pl.when(t.z < t.line - 1)(lambda: act(1, t.up))
        if a:
            act(2, t.a)
        if b:
            act(3, t.b)
        act(4, t.partner)

    def stay(self, k):
        src, place = self.arrays[k]
        return pltpu.make_async_copy(src, place(self.t.place, self.t.core), self.own_sem.at[k])

    def own(self, ks, finish=False):
        for k in ks:
            if not finish:
                self.stay(k).start()
            self.fan(k, self.t.place, True, True, True, True, True, finish)

    def step(self, ks, s, move, down, up, a, b, finish):
        t = self.t
        for k in ks:
            def one(block, down, up):
                if not finish:
                    self.copy(k, 0, block, t.partner).wait_recv()
                self.fan(k, block, False, down, up, a, b, finish)

            pl.when(t.z - s >= 0)(lambda: one(t.place - 4 * s + move, down, False))
            if s:
                pl.when(t.z + s < t.line)(lambda: one(t.place + 4 * s + move, False, up))

    def steps(self, ks, finish=False):
        t = self.t
        result = []
        for s in range(1, t.line):
            result.append(lambda s=s: self.along(ks, s, finish))
            result.append(lambda s=s: self.step(ks, s - 1, t.move_a, False, False, False, True, finish))
        result.append(lambda: self.step(ks, t.line - 1, t.move_a, False, False, False, True, finish))
        tail = []
        for s in range(t.line):
            tail.append(lambda s=s: self.step(ks, s, t.move_b, False, False, False, False, finish))
            tail.append(
                lambda s=s: self.step(ks, s, t.move_a + t.move_b, False, False, False, False, finish)
            )
        return result, tail

    def along(self, ks, s, finish):
        t = self.t
        for k in ks:
            def one(block, down, up):
                if not finish:
                    self.copy(k, 0, block, t.partner).wait_recv()
                self.fan(k, block, False, down, up, True, True, finish)

            pl.when(t.z - s >= 0)(lambda: one(t.place - 4 * s, False, True))
            pl.when(t.z + s < t.line)(lambda: one(t.place + 4 * s, True, False))

    def wait_shares(self, ks):
        t = self.t
        for k in ks:
            self.stay(k).wait()

        @pl.loop(0, t.count)
        def _(block):
            for k in ks:
                other = self.arrays[k][1](block, 1 - t.core)
                pltpu.make_async_remote_copy(
                    src_ref=other,
                    dst_ref=other,
                    send_sem=self.sends.at[k, 4, block],
                    recv_sem=self.shares.at[k, block],
                    device_id=t.partner,
                    device_id_type=MESH,
                ).wait_recv()

    def finish(self, ks):
        self.own(ks, True)
        first, tail = self.steps(ks, True)
        for f in first + tail:
            f()


def silu(v):
    return v * jax.nn.sigmoid(v)


def scale_rows(sums, pixels):
    mean = sums[0:1] / pixels
    var = sums[1:2] / pixels - mean * mean
    return mean, lax.rsqrt(var + norm_epsilon)


def read_params(norm_ref, crop_ref, par_ref, par3_ref, heads_ref):
    middle, width = par_ref.shape[1], heads_ref.shape[1]
    total = jnp.int32(0)
    for g in range(crop_ref.shape[0]):
        for c in range(crop_ref.shape[1]):
            total = total + crop_ref[g, c] * crop_ref[g, c]
    total = total.astype(jnp.float32)
    for k in range(2):
        for row in range(2):
            par_ref[2 * k + row : 2 * k + row + 1] = norm_ref[row : row + 1, k * middle : (k + 1) * middle]
    par_ref[4:] = jnp.full((par_ref.shape[0] - 4, middle), total)
    parts = par3_ref.shape[0] // 2
    for k in range(parts):
        at = (2 + k) * middle
        for row in range(2):
            par3_ref[2 * k + row : 2 * k + row + 1] = norm_ref[row : row + 1, at : at + middle]
    heads = heads_ref.shape[0] // 2 - 1
    for k in range(heads):
        at = (2 + parts) * middle + k * width
        for row in range(2):
            heads_ref[2 * k + row : 2 * k + row + 1] = norm_ref[row : row + 1, at : at + width]
    heads_ref[2 * heads :] = jnp.full((2, width), total)


def read_layout(crop_ref, group, row_start, total_rows, cols, rates, masks_ref, at):
    shape = masks_ref.shape[1:]
    pixel = lax.broadcasted_iota(jnp.int32, shape, 0)
    lane = lax.broadcasted_iota(jnp.int32, shape, 1)
    row = row_start + lax.div(pixel, jnp.full(shape, cols, jnp.int32))
    col = lax.rem(pixel, jnp.full(shape, cols, jnp.int32))
    top = bottom = side = jnp.zeros(shape, jnp.int32)
    start = jnp.int32(0)
    for c in range(crop_ref.shape[1]):
        height = crop_ref[group, c]
        member = jnp.logical_and(row >= start, row < start + height)
        top = jnp.where(member, start, top)
        bottom = jnp.where(member, start + height, bottom)
        side = jnp.where(member, height, side)
        start = start + height
    for k, rate in enumerate(rates):
        flags = (
            col < side,
            jnp.logical_and(col >= rate, col - rate < side),
            col + rate < side,
            jnp.logical_and(row - rate >= top, row - rate < bottom),
            jnp.logical_and(row + rate >= top, row + rate < bottom),
            row + rate < total_rows,
            row >= rate,
        )
        value = jnp.zeros(shape, jnp.float32)
        for n, flag in enumerate(flags):
            value = jnp.where(jnp.logical_and(lane == n, flag), 1.0, value)
        masks_ref[at + k] = value


def trunk_kernel(
    rates, rows, cols, count,
    x_ref, wr_s, wd_s, we_s, wh_s, norm_ref, crop_ref,
    wr_o, wd_o, we_o, wh_o, out_o, sc1_o, sc2_o, sc3_o, masks_o, turned_o, s1_ref, s2_ref, s3_ref,
    par_ref, par3_ref, heads_ref,
    wr_v, wd_v, we_v, ext, taps, out_ref, sc1_ref, sc2_ref, sc3_ref, masks_ref, turned_ref,
    sends, arrives, shares, own_sem, save_sem, h_send, h_recv, *rooms,
):
    rate = rates[-1]
    px = rows * cols
    line = count // 4
    middle = par_ref.shape[1]
    channels = out_ref.shape[1]
    t = Tree()
    one, two, three = rooms[:7], rooms[7:14], rooms[14:]
    halo = rate * cols

    def cut(start, size, step=8):
        return pl.ds(pl.multiple_of(start, step), size)

    def rows_array(shard, full):
        size = shard.shape[0]
        return (
            shard.at[cut(t.core * (size // 2), size // 2, 16)],
            lambda block, core: full.at[cut(block * size + core * (size // 2), size // 2, 16)],
        )

    half_e = we_s.shape[0] // 2
    half_h = wh_s.shape[1] // 2
    fan = Fan(
        t,
        [
            rows_array(wr_s, wr_v),
            rows_array(wd_s, wd_v),
            (
                we_s.at[cut(t.core * half_e, half_e, 16)],
                lambda block, core: we_v.at[
                    cut(core * half_e, half_e, 16), cut(block * we_s.shape[1], we_s.shape[1], 128)
                ],
            ),
            (
                wh_s.at[:, cut(t.core * half_h, half_h, 16)],
                lambda block, core: wh_o.at[:, block, cut(core * half_h, half_h, 16)],
            ),
        ],
        sends, arrives, shares, own_sem,
    )
    plane_signal(line, t.core, t.z, t.low)
    met = greet_rows((-1, 1), count)
    read_params(norm_ref, crop_ref, par_ref, par3_ref, heads_ref)
    mask_ref = masks_ref.at[len(rates) - 1]
    read_layout(crop_ref, t.core, t.place * rows, rows * count, cols, rates[-1:], masks_ref, len(rates) - 1)
    pl.semaphore_wait(pltpu.get_barrier_semaphore(), 7 + line - 1 + met)
    small, heads = (0, 1, 2), (3,)
    fan.own(small)
    first_steps, first_tail = fan.steps(small)
    for f in first_steps:
        f()
    fan.own(heads)
    read_layout(crop_ref, t.core, t.place * rows, rows * count, cols, rates[:-1], masks_ref, 0)
    for f in first_tail:
        f()
    head_steps, head_tail = fan.steps(heads)
    queue = head_steps + head_tail

    def forward(number):
        for _ in range(number):
            if queue:
                queue.pop(0)()

    pixels = par_ref[4:5]

    def mask(k):
        return mask_ref[:, k : k + 1]

    def moments_of(v, ref, at):
        kept = v * mask(0)
        ref[at : at + 1] = jnp.sum(kept, axis=0, keepdims=True)
        ref[at + 1 : at + 2] = jnp.sum(kept * v, axis=0, keepdims=True)

    fan.wait_shares((0,))
    sc1_ref[...] = jnp.dot(x_ref[...], wr_v[...], preferred_element_type=jnp.float32)
    forward(1)
    s1_ref[...] = plane_sum(line, lambda ref: moments_of(sc1_ref[...], ref, 0), one)
    mean, inverse = scale_rows(s1_ref, pixels)
    scaled = (sc1_ref[...] - mean) * inverse
    sc1_ref[...] = scaled
    ext[halo : halo + px] = silu(scaled * par_ref[0:1] + par_ref[1:2]).astype(jnp.bfloat16)

    def edge(up):
        src = ext.at[pl.ds(halo if not up else halo + px - halo, halo)]
        dst = ext.at[pl.ds(halo + px if not up else 0, halo)]
        return pltpu.make_async_remote_copy(
            src_ref=src,
            dst_ref=dst,
            send_sem=h_send.at[int(up)],
            recv_sem=h_recv.at[int(up)],
            device_id=t.at(t.place + (1 if up else -1)),
            device_id_type=MESH,
        )

    has_next, has_last = t.place < count - 1, t.place > 0
    pl.when(has_last)(lambda: edge(False).start())
    pl.when(has_next)(lambda: edge(True).start())
    fan.wait_shares((1, 2))
    forward(2)
    saves = [
        pltpu.make_async_copy(wr_v, wr_o, save_sem.at[0]),
        pltpu.make_async_copy(wd_v, wd_o, save_sem.at[1]),
        pltpu.make_async_copy(we_v, we_o, save_sem.at[2]),
    ]
    for save in saves:
        save.start()
    pl.when(has_next)(lambda: edge(False).wait_recv())
    pl.when(has_last)(lambda: edge(True).wait_recv())
    for j in range(3):
        v = ext[j * halo : j * halo + px].astype(jnp.float32)
        kept_row = 1.0 if j == 1 else mask(3 + j // 2)
        for c in range(3):
            moved = v if c == 1 else pltpu.roll(v, rate if c == 0 else px - rate, 0)
            kept = mask((1, 0, 2)[c]) * kept_row
            k = 3 * j + c
            taps[:, k * middle : (k + 1) * middle] = jnp.where(kept > 0, moved, 0.0).astype(jnp.bfloat16)
    sc2_ref[...] = jnp.dot(taps[...], wd_v[...], preferred_element_type=jnp.float32)
    forward(2)
    s2_ref[...] = plane_sum(line, lambda ref: moments_of(sc2_ref[...], ref, 0), two)
    mean, inverse = scale_rows(s2_ref, pixels)
    scaled = (sc2_ref[...] - mean) * inverse
    sc2_ref[...] = scaled
    hidden = silu(scaled * par_ref[2:3] + par_ref[3:4]).astype(jnp.bfloat16)
    forward(2)
    parts = channels // middle

    def wide(ref):
        for q in range(parts):
            third = jnp.dot(
                hidden, we_v[:, q * middle : (q + 1) * middle], preferred_element_type=jnp.float32
            )
            sc3_ref[:, q * middle : (q + 1) * middle] = third
            moments_of(third, ref, 2 * q)

    s3_ref[...] = plane_sum(line, wide, three)
    forward(1)
    for q in range(parts):
        at = slice(q * middle, (q + 1) * middle)
        mean, inverse = scale_rows(s3_ref[2 * q : 2 * q + 2], pixels)
        scaled = (sc3_ref[:, at] - mean) * inverse
        sc3_ref[:, at] = scaled
        pre = x_ref[:, at].astype(jnp.float32) + (
            scaled * par3_ref[2 * q : 2 * q + 1] + par3_ref[2 * q + 1 : 2 * q + 2]
        )
        active = silu(pre)
        out_ref[:, at] = active.astype(jnp.bfloat16)
        turned_ref[at] = active.T.astype(jnp.bfloat16)
    for k, (here, there) in enumerate(
        (
            (out_ref, out_o),
            (sc1_ref, sc1_o),
            (sc2_ref, sc2_o),
            (sc3_ref, sc3_o),
            (masks_ref, masks_o),
            (turned_ref, turned_o),
        )
    ):
        saves.append(pltpu.make_async_copy(here, there, save_sem.at[3 + k]))
        saves[-1].start()
    forward(len(queue))
    fan.wait_shares(heads)
    for save in saves:
        save.wait()
    pl.when(has_last)(lambda: edge(False).wait_send())
    pl.when(has_next)(lambda: edge(True).wait_send())
    fan.finish(small + heads)


def trunk_step(x, shards, norm_params, crop_heights, rates, rows, cols, middle, number):
    px, channels = x.shape
    count = lax.axis_size("fsdp")
    line = count // 4
    rate = rates[-1]
    bf, f32 = jnp.bfloat16, jnp.float32
    dma = pltpu.SemaphoreType.DMA
    vmem = pl.BlockSpec(memory_space=pltpu.VMEM)
    hbm = pl.BlockSpec(memory_space=pl.ANY)
    parts = channels // middle
    heads, head_rows, width = shards[3].shape
    S = jax.ShapeDtypeStruct
    return pl.pallas_call(
        functools.partial(trunk_kernel, rates, rows, cols, count),
        out_shape=(
            S((channels, middle), bf),
            S((9 * middle, middle), bf),
            S((middle, channels), bf),
            S((heads, count, head_rows, width), bf),
            S((px, channels), bf),
            S((px, middle), f32),
            S((px, middle), f32),
            S((px, channels), f32),
            S((len(rates), px, 128), f32),
            S((channels, px), bf),
            S((2, middle), f32),
            S((2, middle), f32),
            S((2 * parts, middle), f32),
            S((8, middle), f32),
            S((2 * parts, middle), f32),
            S((2 * len(rates), width), f32),
        ),
        in_specs=[vmem] + [hbm] * 4 + [vmem, pl.BlockSpec(memory_space=pltpu.SMEM)],
        out_specs=(hbm,) * 10 + (vmem,) * 6,
        scratch_shapes=[
            pltpu.VMEM((channels, middle), bf),
            pltpu.VMEM((9 * middle, middle), bf),
            pltpu.VMEM((middle, channels), bf),
            pltpu.VMEM((px + 2 * rate * cols, middle), bf),
            pltpu.VMEM((px, 9 * middle), bf),
            pltpu.VMEM((px, channels), bf),
            pltpu.VMEM((px, middle), f32),
            pltpu.VMEM((px, middle), f32),
            pltpu.VMEM((px, channels), f32),
            pltpu.VMEM((len(rates), px, 128), f32),
            pltpu.VMEM((channels, px), bf),
            dma((4, 5, count)),
            dma((4, count)),
            dma((4, count)),
            dma((4,)),
            dma((9,)),
            dma((2,)),
            dma((2,)),
        ]
        + plane_scratch(line, (2, middle))
        + plane_scratch(line, (2, middle))
        + plane_scratch(line, (2 * parts, middle)),
        compiler_params=pltpu.CompilerParams(
            collective_id=number, has_side_effects=True, vmem_limit_bytes=56 * 2**20
        ),
    )(x, *shards, norm_params, crop_heights)


FEED = {"join": 1, "pass": 1, "keep": 1, "third": 1, "d2": 1, "ge": 1, "edge": 2, "d1": 1, "gd": 1, "later3": 4, "later2": 4, "later1": 4}


def nt(a, b):
    return lax.dot_general(a, b, (((1,), (1,)), ((), ())), preferred_element_type=jnp.float32)


def tn(a, b):
    return lax.dot_general(a, b, (((0,), (0,)), ((), ())), preferred_element_type=jnp.float32)


def slope(v):
    s = jax.nn.sigmoid(v)
    return s * (1.0 + v * (1.0 - s))


def back_kernel(
    rate, rows, cols, count, heads,
    x_o, scale_ref, sq_ref, sc1_o, sc2_o, par_ref, par3_ref, s1_ref, s2_ref, s3_ref, mask_ref,
    g_ref, sc3_ref, wr_ref, wd_ref, we_ref, own_ref, got_ref,
    tw_ref, bs1_ref, bs2_ref, bs3_ref, fg_ref, gr_ref, gd_ref, ge_ref, sum_ref,
    b_send, acc, b_room, extra, g_room, s_room, dpre, dthird, wr_v, wd_v, we_v, ext, taps, out_room, grad_room,
    x_ref, sc1_ref, sc2_ref, in_sem, load_sem, extra_sem, bs_sem, br_sem, g_sem, s_sem, w_sem, h_send, h_recv, out_sem, grad_sem, sum_sem, *rooms,
):
    px = rows * cols
    line = count // 4
    middle = par_ref.shape[1]
    channels = x_ref.shape[1]
    parts = channels // middle
    wide = g_room.shape[-1]
    chunks = channels // wide
    halo = rate * cols
    t = Tree()
    one, two, three, four = rooms[:7], rooms[7:14], rooms[14:21], rooms[21:]
    bf, f32 = jnp.bfloat16, jnp.float32

    weights = [
        pltpu.make_async_copy(we_ref, we_v, w_sem.at[0]),
        pltpu.make_async_copy(wd_ref, wd_v, w_sem.at[1]),
        pltpu.make_async_copy(wr_ref, wr_v, w_sem.at[2]),
    ]

    def lanes(c):
        return pl.ds(c * wide, wide)

    def g_load(c):
        return pltpu.make_async_copy(g_ref.at[:, :, lanes(c)], g_room.at[c % 2], g_sem.at[c % 2])

    def s_load(c):
        return pltpu.make_async_copy(sc3_ref.at[:, lanes(c)], s_room.at[c % 2], s_sem.at[c % 2])

    moves = (t.move_b, t.move_a + t.move_b, 0, t.move_a)

    def pair(n, w):
        block = n * 4 + t.low + moves[w]
        room = (b_send if w < 2 else acc).at[n * 2 + w % 2]
        slot = w % 2
        return (
            pltpu.make_async_copy(own_ref.at[:, block], room, load_sem.at[slot]),
            pltpu.make_async_copy(got_ref.at[:, block], extra.at[slot], extra_sem.at[slot]),
        )

    def join(n, w):
        for c in pair(n, w):
            c.wait()
        room = b_send if w < 2 else acc
        at = n * 2 + w % 2

        @pl.loop(0, heads)
        def _(h):
            room[at, h] = room[at, h] + extra[w % 2, h]

    def to_b(n, w, piece=None):
        at = (n * 2 + w,)
        if piece is not None:
            at = at + (piece[0], pl.ds(piece[1], piece[2]))
        return pltpu.make_async_remote_copy(
            src_ref=b_send.at[at],
            dst_ref=b_room.at[at],
            send_sem=bs_sem.at[n * 2 + w],
            recv_sem=br_sem.at[n * 2 + w],
            device_id=t.b,
            device_id_type=MESH,
        )

    head_rows = b_send.shape[2]
    size = head_rows // 4
    pieces = [
        to_b(n, w, (h, r, size))
        for n in range(line)
        for w in (1, 0)
        for h in range(heads)
        for r in range(0, head_rows, size)
    ]

    def feed(number):
        for _ in range(min(number, len(pieces))):
            pieces.pop(0).start()

    plane_signal(line, t.core, t.z, t.low)
    met = greet_rows((-1, 1), count)
    for w in (1, 0):
        for c in pair(0, w):
            c.start()
    fetched = [
        pltpu.make_async_copy(x_o, x_ref, in_sem.at[0]),
        pltpu.make_async_copy(sc1_o, sc1_ref, in_sem.at[1]),
        pltpu.make_async_copy(sc2_o, sc2_ref, in_sem.at[2]),
    ]
    for c in fetched + weights:
        c.start()
    for c in (0, 1):
        g_load(c).start()
        s_load(c).start()
    pl.semaphore_wait(pltpu.get_barrier_semaphore(), 7 + line - 1 + met)

    def squares(ref):
        ref[...] = sq_ref[...]

    def send_side():
        for n in range(line):
            for w in (1, 0):
                join(n, w)
                feed(FEED["join"])
                if n < line - 1:
                    for c in pair(n + 1, w):
                        c.start()

    square_sums = jnp.sum(plane_sum(line, squares, four, send_side), axis=1, keepdims=True)
    tw_ref[...] = scale_ref[...] / jnp.sqrt(
        square_sums / (par_ref[4:5, 0:1] * channels) + task_epsilon
    )

    for w in (3, 2):
        for c in pair(0, w):
            c.start()

    def mask(k):
        return mask_ref[mask_ref.shape[0] - 1, :, k : k + 1]

    pixels = par_ref[4:5]
    pixels_wide = pixels[:, :wide]

    def third_params(c):
        q, at = (c * wide) // middle, (c * wide) % middle
        at = slice(at, at + wide)
        return 2 * q, at

    def moved_sums(ref, row, at, d, scaled):
        ref[row : row + 1, at] = jnp.sum(d, axis=0, keepdims=True)
        ref[row + 1 : row + 2, at] = jnp.sum(d * scaled, axis=0, keepdims=True)

    for c in fetched:
        c.wait()

    def first_pass(ref):
        for c in range(chunks):
            g_load(c).wait()
            s_load(c).wait()
            row, at = third_params(c)
            total = tw_ref[0:1, 0:1] * g_room[c % 2, 0].astype(f32)
            for h in range(1, g_ref.shape[0]):
                total = total + tw_ref[h : h + 1, 0:1] * g_room[c % 2, h].astype(f32)
            scaled = s_room[c % 2]
            here = slice(c * wide, (c + 1) * wide)
            pre = x_ref[:, here].astype(f32) + (
                scaled * par3_ref[row : row + 1, at] + par3_ref[row + 1 : row + 2, at]
            )
            d = total * slope(pre)
            dpre[:, here] = d
            d = d * mask(0)
            moved_sums(ref, row, at, d, scaled)
            feed(FEED["pass"])
            if c + 2 < chunks:
                g_load(c + 2).start()
                s_load(c + 2).start()
        for c in (0, 1):
            s_load(c).start()

    def keep_rest():
        for n in range(line):
            for w in (3, 2):
                feed(FEED["keep"])
                join(n, w)
                if n < line - 1:
                    for c in pair(n + 1, w):
                        c.start()

    back3 = plane_sum(line, first_pass, three, keep_rest, lambda: feed(FEED["later3"]))
    bs3_ref[...] = back3
    for c in range(chunks):
        s_load(c).wait()
        row, at = third_params(c)
        mean = s3_ref[row : row + 1, at] / pixels_wide
        var = s3_ref[row + 1 : row + 2, at] / pixels_wide - mean * mean
        inverse = lax.rsqrt(var + norm_epsilon)
        here = slice(c * wide, (c + 1) * wide)
        v = (
            mask(0)
            * (inverse * par3_ref[row : row + 1, at])
            * (
                dpre[:, here] * mask(0)
                - back3[row : row + 1, at] / pixels_wide
                - s_room[c % 2] * (back3[row + 1 : row + 2, at] / pixels_wide)
            )
        )
        dthird[:, here] = v.astype(bf)
        feed(FEED["third"])
        if c + 2 < chunks:
            s_load(c + 2).start()
    weights[0].wait()
    scaled2 = sc2_ref[...]
    normed2 = scaled2 * par_ref[2:3] + par_ref[3:4]
    feed(FEED["d2"])
    d2 = nt(dthird[...], we_v[...]) * slope(normed2) * mask(0)

    state = []

    def put(value, *targets):
        n = len(state)
        if n >= 2:
            for c in state[n - 2]:
                c.wait()
        grad_room[n % 2] = value.astype(bf)
        cols = middle // len(targets)
        state.append(
            [
                pltpu.make_async_copy(
                    grad_room.at[n % 2, :, pl.ds(i * cols, cols)], ref, grad_sem.at[n % 2, i]
                )
                for i, ref in enumerate(targets)
            ]
        )
        for c in state[n]:
            c.start()

    hidden2 = silu(normed2).astype(bf)

    def expand_grads():
        for q in range(parts):
            feed(FEED["ge"])
            per = count // parts
            put(
                tn(hidden2, dthird[:, q * middle : (q + 1) * middle]),
                *(ge_ref.at[q * per + i] for i in range(per)),
            )

    back2 = plane_sum(
        line, lambda ref: moved_sums(ref, 0, slice(None), d2, scaled2), two, expand_grads,
        lambda: feed(FEED["later2"]),
    )
    bs2_ref[...] = back2

    def through(d, scaled, sums, back, gain):
        _, inverse = scale_rows(sums, pixels)
        return mask(0) * (inverse * gain) * (d - back[0:1] / pixels - scaled * (back[1:2] / pixels))

    ext[halo : halo + px] = through(d2, scaled2, s2_ref, back2, par_ref[2:3]).astype(bf)

    def edge(up):
        src = ext.at[pl.ds(px if up else halo, halo)]
        dst = ext.at[pl.ds(0 if up else halo + px, halo)]
        return pltpu.make_async_remote_copy(
            src_ref=src,
            dst_ref=dst,
            send_sem=h_send.at[int(up)],
            recv_sem=h_recv.at[int(up)],
            device_id=t.at(t.place + (1 if up else -1)),
            device_id_type=MESH,
        )

    has_next, has_last = t.place < count - 1, t.place > 0
    pl.when(has_last)(lambda: edge(False).start())
    pl.when(has_next)(lambda: edge(True).start())
    weights[1].wait()
    scaled1 = sc1_ref[...]
    normed1 = scaled1 * par_ref[0:1] + par_ref[1:2]
    hidden1 = silu(normed1).astype(bf)

    def spread(j):
        v = ext[(2 - j) * halo : (2 - j) * halo + px].astype(f32)
        kept_row = 1.0 if j == 1 else mask(4 if j == 0 else 3)
        for c in range(3):
            if c == 0:
                moved, kept = pltpu.roll(v, px - rate, 0), mask(2)
            elif c == 1:
                moved, kept = v, mask(0)
            else:
                moved, kept = pltpu.roll(v, rate, 0), mask(1) * mask(0)
            k = 3 * j + c
            taps[:, k * middle : (k + 1) * middle] = jnp.where(kept * kept_row > 0, moved, 0.0).astype(bf)

    def tap(k):
        return taps[:, k * middle : (k + 1) * middle]

    feed(FEED["edge"])
    spread(1)
    d1 = None
    for j in (1, 0, 2):
        if j == 0:
            pl.when(has_next)(lambda: edge(False).wait_recv())
            pl.when(has_last)(lambda: edge(True).wait_recv())
            spread(0)
            spread(2)
        for c in range(3):
            k = 3 * j + c
            feed(FEED["d1"])
            part = nt(tap(k), wd_v[k * middle : (k + 1) * middle])
            d1 = part if d1 is None else d1 + part
    d1 = d1 * slope(normed1) * mask(0)

    def dilated_grads():
        for k in range(9):
            feed(FEED["gd"])
            put(tn(hidden1, tap(k)), gd_ref.at[k])

    back1 = plane_sum(
        line, lambda ref: moved_sums(ref, 0, slice(None), d1, scaled1), one, dilated_grads,
        lambda: feed(FEED["later1"]),
    )
    bs1_ref[...] = back1
    dfirst = through(d1, scaled1, s1_ref, back1, par_ref[0:1]).astype(bf)
    feed(len(pieces))
    weights[2].wait()
    outs = []
    for q in range(parts):
        here = slice(q * middle, (q + 1) * middle)
        if q >= 2:
            outs[q - 2].wait()
        out_room[q % 2] = nt(dfirst, wr_v[here]) + dpre[:, here]
        outs.append(
            pltpu.make_async_copy(
                out_room.at[q % 2], fg_ref.at[:, pl.ds(q * middle, middle)], out_sem.at[q % 2]
            )
        )
        outs[q].start()
    for q in range(parts):
        here = slice(q * middle, (q + 1) * middle)
        put(tn(x_ref[:, here], dfirst), gr_ref.at[pl.ds(q * middle, middle)])

    def stays(n):
        return pltpu.make_async_copy(acc.at[n], sum_ref.at[n], sum_sem.at[n])

    @pl.loop(0, line)
    def _(n):
        for w in (1, 0):
            to_b(n, w).wait_recv()
            at = n * 2 + w

            @pl.loop(0, heads)
            def _(h):
                acc[at, h] = acc[at, h] + b_room[at, h]

            stays(at).start()

    for c in state[-2] + state[-1] + outs[-2:]:
        c.wait()

    @pl.loop(0, line)
    def _(n):
        for w in (1, 0):
            to_b(n, w).wait_send()
            stays(n * 2 + w).wait()

    pl.when(has_last)(lambda: edge(False).wait_send())
    pl.when(has_next)(lambda: edge(True).wait_send())


def back_step(x, task_scale, squares, scaled1, scaled2, scaled3, params, params3, sums1, sums2, sums3, masks, grads,
              wr, wd, we, own, got, rate, rows, cols, number):
    px, channels = x.shape
    count = lax.axis_size("fsdp")
    line = count // 4
    middle = params.shape[1]
    parts = channels // middle
    wide = middle // 2
    heads, _, head_rows, half = own.shape
    bf, f32 = jnp.bfloat16, jnp.float32
    dma = pltpu.SemaphoreType.DMA
    vmem = pl.BlockSpec(memory_space=pltpu.VMEM)
    hbm = pl.BlockSpec(memory_space=pl.ANY)
    S = jax.ShapeDtypeStruct
    V = pltpu.VMEM
    return pl.pallas_call(
        functools.partial(back_kernel, rate, rows, cols, count, heads),
        out_shape=(
            S(task_scale.shape, f32),
            S((2, middle), f32),
            S((2, middle), f32),
            S((2 * parts, middle), f32),
            S((px, channels), f32),
            S((channels, middle), bf),
            S((9, middle, middle), bf),
            S((count, middle, channels // count), bf),
            S((2 * line, heads, head_rows, half), bf),
        ),
        in_specs=[hbm, vmem, vmem, hbm, hbm] + [vmem] * 6 + [hbm] * 7,
        out_specs=(vmem,) * 4 + (hbm,) * 5,
        scratch_shapes=[
            V((2 * line, heads, head_rows, half), bf),
            V((2 * line, heads, head_rows, half), bf),
            V((2 * line, heads, head_rows, half), bf),
            V((2, heads, head_rows, half), bf),
            V((2, grads.shape[0], px, wide), bf),
            V((2, px, wide), f32),
            V((px, channels), f32),
            V((px, channels), bf),
            V((channels, middle), bf),
            V((9 * middle, middle), bf),
            V((middle, channels), bf),
            V((px + 2 * rate * cols, middle), bf),
            V((px, 9 * middle), bf),
            V((2, px, middle), f32),
            V((2, middle, middle), bf),
            V((px, channels), bf),
            V((px, middle), f32),
            V((px, middle), f32),
            dma((3,)),
            dma((2,)),
            dma((2,)),
            dma((2 * line,)),
            dma((2 * line,)),
            dma((2,)),
            dma((2,)),
            dma((3,)),
            dma((2,)),
            dma((2,)),
            dma((2,)),
            dma((2, count // parts)),
            dma((2 * line,)),
        ]
        + plane_scratch(line, (2, middle))
        + plane_scratch(line, (2, middle))
        + plane_scratch(line, (2 * parts, middle))
        + plane_scratch(line, squares.shape),
        compiler_params=pltpu.CompilerParams(
            collective_id=number, has_side_effects=True, vmem_limit_bytes=63 * 2**20
        ),
    )(x, task_scale, squares, scaled1, scaled2, params, params3, sums1, sums2, sums3, masks,
      grads, scaled3, wr, wd, we, own, got)


def silu_slope(values):
    sigmoid_value = jax.nn.sigmoid(values)
    return sigmoid_value * (1.0 + values * (1.0 - sigmoid_value))


def shift_along(values, offset, axis_number):
    if offset == 0:
        return values
    length = values.shape[axis_number]
    pad_shape = list(values.shape)
    pad_shape[axis_number] = abs(offset)
    zero_block = jnp.zeros(pad_shape, values.dtype)
    if offset > 0:
        return jnp.concatenate(
            [lax.slice_in_dim(values, offset, length, axis=axis_number), zero_block], axis_number
        )
    return jnp.concatenate(
        [zero_block, lax.slice_in_dim(values, 0, length + offset, axis=axis_number)], axis_number
    )


def inside_rows(layout, offset):
    row_ids, row_top, row_bottom, row_side = layout
    return (row_ids + offset >= row_top) & (row_ids + offset < row_bottom)


def inside_cols(layout, offset, col_count):
    row_ids, row_top, row_bottom, row_side = layout
    columns = jnp.arange(col_count, dtype=jnp.int32)
    return (columns[None, :] + offset >= 0) & (columns[None, :] + offset < row_side[:, None])


def column_sums(inputs, weight, rate, layout):
    col_count = inputs.shape[1]
    products = jnp.einsum("rwc,kco->krwo", inputs, weight, preferred_element_type=jnp.float32)
    sums = []
    for row_step in range(3):
        summed = 0.0
        for col_step in range(3):
            across = (col_step - 1) * rate
            summed = summed + jnp.where(
                inside_cols(layout, across, col_count)[:, :, None],
                shift_along(products[3 * row_step + col_step], across, 1),
                0.0,
            )
        sums.append(summed)
    return sums


def dilated_forward(inputs, weights, rates, layout, number):
    outer, centers = [], []
    for weight, rate in zip(weights, rates):
        low, center, high = column_sums(inputs, weight, rate, layout)
        outer += [low.astype(jnp.bfloat16), high.astype(jnp.bfloat16)]
        centers.append(center)
    offsets = tuple(o for rate in rates for o in (-rate, rate))
    pulled = exchange(jnp.stack(outer), offsets, number)
    results = []
    for k, (center, rate) in enumerate(zip(centers, rates)):
        for j, down in ((2 * k, -rate), (2 * k + 1, rate)):
            center = center + jnp.where(
                inside_rows(layout, down)[:, None, None], pulled[j].astype(jnp.float32), 0.0
            )
        results.append(center)
    return results


def spread_taps(grads, rates, layout, number):
    row_ids = layout[0]
    row_count, col_count = grads[0].shape[:2]
    total_rows = row_count * lax.axis_size("fsdp")
    outer = []
    for grad, rate in zip(grads, rates):
        for down in (-rate, rate):
            outer.append(
                jnp.where(inside_rows(layout, down)[:, None, None], grad, jnp.bfloat16(0.0))
            )
    offsets = tuple(o for rate in rates for o in (rate, -rate))
    pulled = exchange(jnp.stack(outer), offsets, number)
    results = []
    for k, (grad, rate) in enumerate(zip(grads, rates)):
        taps = []
        for row_step in range(3):
            down = (row_step - 1) * rate
            if row_step == 1:
                arrived = grad
            else:
                there = (row_ids - down >= 0) & (row_ids - down < total_rows)
                arrived = jnp.where(
                    there[:, None, None], pulled[2 * k + row_step // 2], jnp.bfloat16(0.0)
                )
            for col_step in range(3):
                across = (col_step - 1) * rate
                kept = jnp.where(
                    inside_cols(layout, across, col_count)[:, :, None], arrived, jnp.bfloat16(0.0)
                )
                taps.append(shift_along(kept, -across, 1))
        results.append(taps)
    return results


def spread(stat):
    return stat.reshape(stat.shape[:-1] + (1, 1) + stat.shape[-1:])


def totals_of(one, two, number):
    local_sums = jnp.stack([jnp.sum(one, axis=(-3, -2)), jnp.sum(two, axis=(-3, -2))])
    flat = all_sum(local_sums.reshape(2, -1), number)
    return flat.reshape(local_sums.shape)


def moments(values, valid_mask, number):
    weighted = values * valid_mask[..., None]
    return totals_of(weighted, weighted * values, number)


def normalize(values, sums, valid_count, gain_row, bias_row):
    mean_value = sums[0] / valid_count
    variance = sums[1] / valid_count - mean_value * mean_value
    inverse = lax.rsqrt(variance + norm_epsilon)
    scaled = (values - spread(mean_value)) * spread(inverse)
    return (scaled, inverse, scaled * spread(gain_row) + spread(bias_row))


def norm_backward(grad_norm, scaled, inverse, gain_row, valid_mask, valid_count, number):
    masked = grad_norm * valid_mask[..., None]
    sums = totals_of(masked, masked * scaled, number)
    grad_values = (
        valid_mask[..., None]
        * spread(inverse * gain_row)
        * (masked - spread(sums[0] / valid_count) - scaled * spread(sums[1] / valid_count))
    )
    return (grad_values, sums)


def update(param, moment, grad):
    moment_new = momentum_decay * moment + grad
    return (param - step_rate * moment_new, moment_new)


def local(
    features,
    cotangent,
    crop_heights,
    task_scale,
    w_reduce,
    w_dilated,
    w_expand,
    w_heads,
    norm_params,
    m_reduce,
    m_dilated,
    m_expand,
    m_heads,
    norm_moment,
):
    row_count = features.shape[1]
    col_count = features.shape[2]
    channels = features.shape[3]
    middle = w_reduce.shape[1]
    head_width = w_heads.shape[2]
    head_total = w_heads.shape[0]
    group_index = lax.axis_index("dp")
    place_index = lax.axis_index("fsdp")
    group_heights = lax.dynamic_index_in_dim(crop_heights, group_index, 0, keepdims=False)
    crop_order = jnp.arange(group_heights.shape[0], dtype=jnp.int32)
    crop_ends = jnp.sum(
        jnp.where(crop_order[None, :] <= crop_order[:, None], group_heights[None, :], 0),
        axis=1,
        dtype=jnp.int32,
    )
    crop_starts = crop_ends - group_heights
    row_ids = place_index * row_count + jnp.arange(row_count, dtype=jnp.int32)
    member = (row_ids[:, None] >= crop_starts[None, :]) & (row_ids[:, None] < crop_ends[None, :])
    row_top = jnp.sum(jnp.where(member, crop_starts[None, :], 0), axis=1, dtype=jnp.int32)
    row_bottom = jnp.sum(jnp.where(member, crop_ends[None, :], 0), axis=1, dtype=jnp.int32)
    row_side = jnp.sum(jnp.where(member, group_heights[None, :], 0), axis=1, dtype=jnp.int32)
    layout = (row_ids, row_top, row_bottom, row_side)
    valid_mask = (jnp.arange(col_count, dtype=jnp.int32)[None, :] < row_side[:, None]).astype(
        jnp.float32
    )
    valid_count = jnp.sum(crop_heights * crop_heights).astype(jnp.float32)
    gain_values = norm_params[0]
    bias_values = norm_params[1]
    trunk_end = 2 * middle + channels
    inputs = features[0]
    inputs_float = inputs.astype(jnp.float32)
    place_count = lax.axis_size("fsdp")
    pixels = row_count * col_count
    half_rows = w_heads.shape[1] // 2
    heads_half = lax.dynamic_slice_in_dim(w_heads, group_index * half_rows, half_rows, 1)

    def beside(part):
        return lax.all_gather(
            part.astype(jnp.bfloat16), ("fsdp", "dp"), axis=1, tiled=True
        ).reshape(-1, channels, head_width)

    heads_late = beside(heads_half[1:])
    if place_count == 16:
        (
            reduce_low, dilated_low, expand_low, heads_early, trunk_out,
            scaled_one, scaled_two, scaled_three, masks, turned,
            sums_in_one, sums_in_two, sums_in_three, flat_params, wide_params, head_params,
        ) = trunk_step(
            inputs.reshape(pixels, channels),
            (
                w_reduce.astype(jnp.bfloat16),
                w_dilated.astype(jnp.bfloat16),
                w_expand.astype(jnp.bfloat16),
                w_heads[:1].astype(jnp.bfloat16),
            ),
            norm_params,
            crop_heights,
            head_rates + (trunk_rate,),
            row_count,
            col_count,
            middle,
            0,
        )
        heads_early = heads_early.reshape(-1, channels, head_width)
    else:
        head_gain = gain_values[trunk_end:].reshape(head_total, head_width)
        head_bias = bias_values[trunk_end:].reshape(head_total, head_width)
        head_params = jnp.concatenate(
            [
                jnp.stack([head_gain, head_bias], 1).reshape(2 * head_total, head_width),
                jnp.broadcast_to(valid_count, (2, head_width)),
            ]
        )
        total_rows = row_count * place_count
        masks = []
        for rate in head_rates + (trunk_rate,):
            flags = [
                inside_cols(layout, 0, col_count),
                inside_cols(layout, -rate, col_count),
                inside_cols(layout, rate, col_count),
            ] + [
                jnp.broadcast_to(flag[:, None], (row_count, col_count))
                for flag in (
                    inside_rows(layout, -rate),
                    inside_rows(layout, rate),
                    row_ids + rate < total_rows,
                    row_ids - rate >= 0,
                )
            ]
            flags = jnp.stack([f.reshape(pixels) for f in flags], 1).astype(jnp.float32)
            masks.append(jnp.pad(flags, ((0, 0), (0, 128 - flags.shape[1]))))
        masks = jnp.stack(masks)
        heads_early = beside(heads_half[:1])
        reduce_low, dilated_low, expand_low = (
            lax.all_gather(w.astype(jnp.bfloat16), "fsdp", axis=0)
            for w in (w_reduce, w_dilated, w_expand)
        )
        reduce_low = reduce_low.reshape(channels, middle)
        dilated_low = dilated_low.reshape(9, middle, middle)
        first = jnp.einsum("rwc,cm->rwm", inputs, reduce_low, preferred_element_type=jnp.float32)
        scaled_one, inverse_one, normed_one = normalize(
            first, moments(first, valid_mask, 1), valid_count, gain_values[:middle], bias_values[:middle]
        )
        hidden_one = jax.nn.silu(normed_one).astype(jnp.bfloat16)
        (second,) = dilated_forward(hidden_one, (dilated_low,), (trunk_rate,), layout, 2)
        scaled_two, inverse_two, normed_two = normalize(
            second,
            moments(second, valid_mask, 3),
            valid_count,
            gain_values[middle : 2 * middle],
            bias_values[middle : 2 * middle],
        )
        hidden_two = jax.nn.silu(normed_two).astype(jnp.bfloat16)
        expand_low = expand_low.transpose(1, 0, 2).reshape(middle, channels)
        third = jnp.einsum("rwm,mc->rwc", hidden_two, expand_low, preferred_element_type=jnp.float32)
        scaled_three, inverse_three, normed_three = normalize(
            third,
            moments(third, valid_mask, 4),
            valid_count,
            gain_values[2 * middle : trunk_end],
            bias_values[2 * middle : trunk_end],
        )
        pre_act = inputs_float + normed_three
        trunk_out = jax.nn.silu(pre_act).astype(jnp.bfloat16).reshape(pixels, channels)
        turned = trunk_out.T
    handed = head_total - 1
    head_grads, grads_own, grads_got, grads_late, head_sums, squares = heads_step(
        trunk_out,
        turned,
        heads_early,
        heads_late,
        cotangent.reshape(head_total, pixels, head_width),
        head_params,
        masks,
        head_rates,
        row_count,
        col_count,
        handed,
        5,
    )
    head_sums = head_sums.reshape(head_total, 2, head_width).transpose(1, 0, 2)
    shared = lax.psum_scatter(
        grads_late.reshape(-1, head_width), ("fsdp", "dp"), scatter_dimension=0, tiled=True
    )
    late_total = lax.all_gather(shared, "dp", axis=0, tiled=True)[None]
    if place_count == 16:
        (
            task_weight, back_one, back_two, back_three, features_grad, grad_reduce, grad_dilated, grad_expand, late,
        ) = back_step(
            inputs.reshape(pixels, channels),
            jnp.broadcast_to(jnp.pad(task_scale, (0, 8 - head_total))[:, None], (8, 128)),
            squares,
            scaled_one,
            scaled_two,
            scaled_three,
            flat_params,
            wide_params,
            sums_in_one,
            sums_in_two,
            sums_in_three,
            masks,
            head_grads,
            reduce_low,
            dilated_low,
            expand_low,
            grads_own.reshape(handed, place_count, -1, head_width // 2),
            grads_got.reshape(handed, place_count, -1, head_width // 2),
            trunk_rate,
            row_count,
            col_count,
            1,
        )
        task_weight = task_weight[:head_total, 0]
        features_grad = features_grad.reshape(row_count, col_count, channels)
        *trunk_totals, heads_total = reduce_shards(
            (
                grad_reduce.reshape(1, place_count, -1, middle),
                grad_dilated.reshape(1, place_count, -1, middle),
                grad_expand[None],
            ),
            (late,),
            2,
        )
        trunk_totals = [t[0] for t in trunk_totals]
        sums_one, sums_two = back_one, back_two
        sums_three = back_three.reshape(-1, 2, middle).transpose(1, 0, 2).reshape(2, channels)
    else:
        squares = jnp.sum(all_sum(squares, 9)[:head_total], axis=1)
        task_rms = jnp.sqrt(squares / (valid_count * channels) + task_epsilon)
        task_weight = task_scale / task_rms
        head_grads = head_grads.astype(jnp.float32)
        grad_trunk = task_weight[0] * head_grads[0]
        for k in range(1, head_total):
            grad_trunk = grad_trunk + task_weight[k] * head_grads[k]
        grad_trunk = grad_trunk.reshape(row_count, col_count, channels)
        grad_pre = grad_trunk * silu_slope(pre_act)
        grad_third, sums_three = norm_backward(
            grad_pre,
            scaled_three,
            inverse_three,
            gain_values[2 * middle : trunk_end],
            valid_mask,
            valid_count,
            11,
        )
        grad_third = grad_third.astype(jnp.bfloat16)
        grad_expand = jnp.einsum(
            "rwm,rwc->mc", hidden_two, grad_third, preferred_element_type=jnp.float32
        ).astype(jnp.bfloat16)
        grad_hidden_two = jnp.einsum(
            "rwc,mc->rwm", grad_third, expand_low, preferred_element_type=jnp.float32
        )
        grad_second, sums_two = norm_backward(
            grad_hidden_two * silu_slope(normed_two),
            scaled_two,
            inverse_two,
            gain_values[middle : 2 * middle],
            valid_mask,
            valid_count,
            12,
        )
        (taps,) = spread_taps([grad_second.astype(jnp.bfloat16)], (trunk_rate,), layout, 13)
        taps = jnp.stack(taps)
        grad_hidden_one = jnp.einsum(
            "krwo,kco->rwc", taps, dilated_low, preferred_element_type=jnp.float32
        )
        grad_dilated = jnp.einsum(
            "rwc,krwo->kco", hidden_one, taps, preferred_element_type=jnp.float32
        )
        grad_first, sums_one = norm_backward(
            grad_hidden_one * silu_slope(normed_one),
            scaled_one,
            inverse_one,
            gain_values[:middle],
            valid_mask,
            valid_count,
            14,
        )
        grad_first = grad_first.astype(jnp.bfloat16)
        grad_reduce = jnp.einsum("rwc,rwm->cm", inputs, grad_first, preferred_element_type=jnp.float32)
        features_grad = (
            jnp.einsum("rwm,cm->rwc", grad_first, reduce_low, preferred_element_type=jnp.float32)
            + grad_pre
        )
        trunk_totals = []
        for grad, axis in ((grad_reduce, 0), (grad_dilated.reshape(-1, middle), 0), (grad_expand, 1)):
            shard = lax.psum_scatter(
                grad.astype(jnp.bfloat16), "fsdp", scatter_dimension=axis, tiled=True
            )
            trunk_totals.append(lax.psum(shard, "dp"))
        shared = lax.psum_scatter(
            (grads_own + grads_got).reshape(handed, -1, head_width // 2),
            "fsdp",
            scatter_dimension=1,
            tiled=True,
        )
        heads_total = lax.all_gather(shared, "dp", axis=2, tiled=True)
    totals = tuple(t.astype(jnp.float32) for t in trunk_totals) + (
        task_weight[:, None, None]
        * jnp.concatenate([heads_total, late_total]).astype(jnp.float32),
    )
    gain_grad = jnp.concatenate(
        [sums_one[1], sums_two[1], sums_three[1], (task_weight[:, None] * head_sums[1]).reshape(-1)]
    )
    bias_grad = jnp.concatenate(
        [sums_one[0], sums_two[0], sums_three[0], (task_weight[:, None] * head_sums[0]).reshape(-1)]
    )
    norm_grad = jnp.stack([gain_grad, bias_grad])
    w_reduce_new, m_reduce_new = update(w_reduce, m_reduce, totals[0])
    w_dilated_new, m_dilated_new = update(w_dilated, m_dilated, totals[1])
    w_expand_new, m_expand_new = update(w_expand, m_expand, totals[2])
    w_heads_new, m_heads_new = update(w_heads, m_heads, totals[3])
    norm_params_new, norm_moment_new = update(norm_params, norm_moment, norm_grad)
    return (
        features_grad[None],
        w_reduce_new,
        m_reduce_new,
        w_dilated_new,
        m_dilated_new,
        w_expand_new,
        m_expand_new,
        w_heads_new,
        m_heads_new,
        norm_params_new,
        norm_moment_new,
    )


def solution(mesh):
    placed = (
        P("dp", "fsdp", None, None),
        P(None, "dp", "fsdp", None, None),
        P(),
        P(),
        P("fsdp", None),
        P("fsdp", None),
        P(None, "fsdp"),
        P(None, "fsdp", None),
        P(),
        P("fsdp", None),
        P("fsdp", None),
        P(None, "fsdp"),
        P(None, "fsdp", None),
        P(),
    )
    return jax.shard_map(
        local,
        mesh=mesh,
        in_specs=placed,
        out_specs=(
            P("dp", "fsdp", None, None),
            P("fsdp", None),
            P("fsdp", None),
            P("fsdp", None),
            P("fsdp", None),
            P(None, "fsdp"),
            P(None, "fsdp"),
            P(None, "fsdp", None),
            P(None, "fsdp", None),
            P(),
            P(),
        ),
        check_vma=False,
    )
```
